32 devices in a mesh: wide: 8 (over z, y), narrow: 4 (over x, core).
Axes of the slice: x: 2, y: 2, z: 4, core: 2. Of those that a mesh axis runs over, the one named last changes fastest.
Arguments:
- tokens: bfloat16 [64, 512, 768], P(('wide', 'narrow')), may hold values from -6 to 6
- segment_ids: int32 [64, 512], P(('wide', 'narrow')), may hold values from 0 to 3, never falling along the last dimension, each value on 1 to 256 neighbouring positions
- cotangent: bfloat16 [64, 512, 768], P(('wide', 'narrow')), may hold values from -6 to 6
- blocks: float32 [12, 768, 768], P(None, ('wide', 'narrow'))
- vectors: float32 [13, 768], P(None, ('wide', 'narrow'))
- stat_left: float32 [32, 768, 768], P(('wide', 'narrow'))
- stat_right: float32 [32, 768, 768], P(('wide', 'narrow'))
- root_left: float32 [32, 768, 768], P(('wide', 'narrow'))
- root_right: float32 [32, 768, 768], P(('wide', 'narrow'))
- vec_stat: float32 [13, 768], P(None, ('wide', 'narrow')), may hold values from 0.5 to 4
- owners: int32 [12], replicated, may hold values from 0 to 31, as said below
Outputs:
- output: bfloat16 [64, 512, 768], P(('wide', 'narrow'))
- grad_tokens: bfloat16 [64, 512, 768], P(('wide', 'narrow'))
- clipped_blocks: float32 [12, 768, 768], P(None, ('wide', 'narrow'))
- clipped_vectors: float32 [13, 768], P(None, ('wide', 'narrow'))
- grad_norm: float32 [], replicated
- new_left: float32 [32, 768, 768], P(('wide', 'narrow'))
- new_right: float32 [32, 768, 768], P(('wide', 'narrow'))
- new_vec_stat: float32 [13, 768], P(None, ('wide', 'narrow'))
- new_blocks: float32 [12, 768, 768], P(None, ('wide', 'narrow'))
- new_vectors: float32 [13, 768], P(None, ('wide', 'narrow'))
- blocks_copy: bfloat16 [12, 768, 768], P(None, ('wide', 'narrow'))
- vectors_copy: bfloat16 [13, 768], P(None, ('wide', 'narrow'))
The draws below stay inside these ranges and needn't reach their ends.
Inputs may be any that keep to these rules, and one draw needn't show every extreme that they name: `owners`: distinct device numbers; device 0 and device 32 - 1 are always among them. `segment_ids`: within each row never falling, each segment at most 256 tokens.
All inputs are finite; a program needn't handle non-finite values.
Results may differ from the reference program's by a relative error of at most 0.007.
The reference program's roundings to bfloat16 on the way count: a program that leaves them out, or rounds other values in their place, can miss the bound.
Values may be sent and summed in bfloat16 or wider, within the bound.
No kernel may reach another device: no remote copies, remote signals or barrier semaphores. Data moves between devices by JAX's collectives and lax.ppermute only.
A program may use at most 256 MiB of HBM per device.

```python
import math
import jax
import jax.numpy as jnp
import numpy as np
from jax import lax

D = 768
H = 12
HD = 64
FF = 3072
ROT = 16
SEQ = 512
SEGS = 4
SLOTS = 32
ROWS = 64
BLOCKS = 12
VEC = 13
NPARAM = 7087872


def scaled_identity(key, low_end, high_end):
    factor_key, noise_key = jax.random.split(key)
    factor = jnp.exp(jax.random.uniform(factor_key, (SLOTS, 1, 1), jnp.float32, math.log(low_end), math.log(high_end)))
    noise = jax.random.normal(noise_key, (SLOTS, D, D), jnp.float32)
    symmetric = (noise + jnp.swapaxes(noise, 1, 2)) * 0.014
    return factor * jnp.eye(D, dtype=jnp.float32)[None] + symmetric


def draw_stat_left(key, part):
    return scaled_identity(jax.random.fold_in(key, 11), 0.5, 2.0)


def draw_stat_right(key, part):
    return scaled_identity(jax.random.fold_in(key, 12), 0.5, 2.0)


def draw_root_left(key, part):
    return scaled_identity(jax.random.fold_in(key, 13), 0.7, 1.4)


def draw_root_right(key, part):
    return scaled_identity(jax.random.fold_in(key, 14), 0.7, 1.4)


def draw_blocks(key, part):
    inner = jax.random.fold_in(key, 15)
    base = jax.random.normal(inner, (BLOCKS, D, D), jnp.float32)
    index = jnp.arange(BLOCKS)
    factor = jnp.where(index < 2, 1.3, jnp.where(index == 3, 4.0, 1.0)).astype(jnp.float32)
    return base * factor[:, None, None] / math.sqrt(D)


def draw_vectors(key, part):
    inner = jax.random.fold_in(key, 16)
    base = jax.random.normal(inner, (VEC, D), jnp.float32)
    index = jnp.arange(VEC)[:, None]
    gains = (index == 0) | (index == 2)
    return jnp.where(gains, 1.0 + 0.1 * base, 0.3 * base)


def draw_owners(key, part):
    first_key, second_key = jax.random.split(jax.random.fold_in(key, 17))
    middle = jax.random.permutation(first_key, SLOTS - 2)[:BLOCKS - 2] + 1
    listed = jnp.concatenate([jnp.array([0, SLOTS - 1], jnp.int32), middle.astype(jnp.int32)])
    return jax.random.permutation(second_key, listed)


def block_scale(own_key, extent, shards, smallest, top_value):
    level, own = 1.0, jax.random.fold_in(own_key, 6)
    for dim, blocks in shards:
        steps = jnp.exp(jax.random.uniform(jax.random.fold_in(own, dim), (blocks,), jnp.float32, smallest / len(shards), top_value / len(shards)))
        level = level * jnp.repeat(steps, extent[dim] // blocks).reshape([-1 if axis == dim else 1 for axis in range(len(extent))])
    return level


def split_up(amount, total, bound, lean):
    portions = [(1 << 20) // math.isqrt(grade ** lean) + 1 for grade in range(2, amount + 1)]
    surplus, counts = total - bound - (amount - 1), [1] * (amount - 1)
    while surplus > 0:
        free = [i for i in range(amount - 1) if counts[i] < bound]
        mass, remaining = sum([portions[i] for i in free]), surplus
        for i in free:
            extra = min(bound - counts[i], max(1, remaining * portions[i] // mass), surplus)
            counts[i] = counts[i] + extra
            surplus = surplus - extra
    return np.array([bound] + counts)


def uneven(own_key, amount, total, limit, slope):
    if amount == 2:
        one = jax.random.randint(own_key, (), max(1, total - limit), min(limit, total - 1) + 1)
        return jnp.stack([one, total - one])
    tallies = jnp.asarray(split_up(amount, total, limit, slope), jnp.int32)
    pairs = (amount - 1) // 2
    donor, taker = tallies[1:1 + 2 * pairs:2], tallies[2:2 + 2 * pairs:2]
    room = jnp.minimum(donor - 1, limit - taker)
    moved = jax.random.randint(jax.random.fold_in(own_key, 1), (pairs,), 0, 1 << 20) % (room + 1)
    tallies = tallies.at[1:1 + 2 * pairs:2].set(donor - moved).at[2:2 + 2 * pairs:2].set(taker + moved)
    return tallies[jax.random.permutation(jax.random.fold_in(own_key, 2), amount)]


def gaussian(rng, dims, scale, most, shards=(), kind=jnp.bfloat16):
    values = jax.random.normal(rng, dims, jnp.float32) * scale
    if len(shards) > 0:
        values = block_scale(rng, dims, shards, -0.22, 0.18) * values
    return jnp.clip(values, min=-most, max=most).astype(kind)


def setup_inputs(seed: int = 0) -> dict:
    seeds = jax.random.split(jax.random.key(seed), 12)
    tokens = gaussian(seeds[0], (ROWS, SEQ, D), 1.0, 6.0, ((0, 32),))
    segment_ids = jax.vmap(lambda own: jnp.searchsorted(jnp.cumsum(uneven(own, SEGS, SEQ, SEQ // 2, 0)), jnp.arange(SEQ), side="right"))(jax.random.split(seeds[1], ROWS)).reshape((ROWS, SEQ)).astype(jnp.int32)
    cotangent = gaussian(seeds[2], (ROWS, SEQ, D), 1.0, 6.0, ((0, 32),))
    blocks = draw_blocks(jax.random.fold_in(seeds[11], 71), 0)
    vectors = draw_vectors(jax.random.fold_in(seeds[11], 71), 0)
    stat_left = draw_stat_left(jax.random.fold_in(seeds[11], 71), 0)
    stat_right = draw_stat_right(jax.random.fold_in(seeds[11], 71), 0)
    root_left = draw_root_left(jax.random.fold_in(seeds[11], 71), 0)
    root_right = draw_root_right(jax.random.fold_in(seeds[11], 71), 0)
    vec_stat = jnp.clip(jnp.exp(math.log(4.0) - 2.0794415 * jax.random.uniform(seeds[9], (VEC, D), jnp.float32) ** block_scale(seeds[9], (VEC, D), ((1, 32),), -0.2, 0.2)), 0.5, 4.0)
    owners = draw_owners(jax.random.fold_in(seeds[11], 71), 0)
    return dict(tokens=tokens, segment_ids=segment_ids, cotangent=cotangent, blocks=blocks, vectors=vectors, stat_left=stat_left, stat_right=stat_right, root_left=root_left, root_right=root_right, vec_stat=vec_stat, owners=owners)


highest = lax.Precision.HIGHEST
clip_level = 1.0
matrix_rate = 0.03
vector_rate = 0.2
decay_beta = 0.5
norm_epsilon = 1e-05

@jax.custom_vjp
def low(v):
    return lax.optimization_barrier(v.astype(jnp.bfloat16)).astype(jnp.float32)

@jax.custom_vjp
def low_back(v):
    return v

def low_keep(v):
    return (low(v), None)

def low_pass(kept, grad):
    return (grad,)

def back_keep(v):
    return (v, None)

def back_low(kept, grad):
    return (low(grad),)
low.defvjp(low_keep, low_pass)
low_back.defvjp(back_keep, back_low)

def layer_norm(values, gain, shift):
    centre = lax.optimization_barrier(jnp.mean(values, axis=-1, keepdims=True))
    centred = values - centre
    spread = lax.optimization_barrier(jnp.mean(centred * centred, axis=-1, keepdims=True))
    return centred * lax.rsqrt(spread + norm_epsilon) * gain + shift

def rotary_tables(segment_ids):
    length = segment_ids.shape[-1]
    places = jnp.broadcast_to(jnp.arange(length, dtype=jnp.int32), segment_ids.shape)
    earlier = jnp.concatenate([segment_ids[..., :1] - 1, segment_ids[..., :-1]], axis=-1)
    starts = lax.cummax(jnp.where(segment_ids != earlier, places, 0), axis=segment_ids.ndim - 1)
    offset = (places - starts).astype(jnp.float32)
    half_rot = ROT // 2
    rates = jnp.power(10000.0, -2.0 * jnp.arange(half_rot, dtype=jnp.float32) / ROT)
    angles = offset[..., None] * rates
    angles = jnp.concatenate([angles, angles], axis=-1)
    return (jnp.cos(angles), jnp.sin(angles))

def rotate(values, cosine, sine):
    rotary_part = values[..., :ROT]
    first_half = rotary_part[..., :ROT // 2]
    second_half = rotary_part[..., ROT // 2:]
    turned = jnp.concatenate([-second_half, first_half], axis=-1)
    return jnp.concatenate([rotary_part * cosine + turned * sine, values[..., ROT:]], axis=-1)

def causal_mask(segment_row):
    places = jnp.arange(segment_row.shape[0])
    return (segment_row[:, None] == segment_row[None, :]) & (places[:, None] >= places[None, :])

def row_forward(weights, vecs, row_tokens, segment_row):
    length = row_tokens.shape[0]
    splits = FF // D
    normed_one = layer_norm(row_tokens, vecs[0], vecs[1])
    projected = jnp.einsum('nd,kde->nke', low(normed_one), weights[0:3], precision=highest) + vecs[4:7][None]
    projected = low_back(projected).reshape(length, 3, H, HD)
    cosine, sine = rotary_tables(segment_row)
    cosine = cosine[:, None, :]
    sine = sine[:, None, :]
    queries = low(rotate(projected[:, 0], cosine, sine))
    keys_rot = low(rotate(projected[:, 1], cosine, sine))
    values_low = low(projected[:, 2])
    scores = low_back(jnp.einsum('qhd,khd->hqk', queries, keys_rot, precision=highest) * 0.125)
    scores = jnp.where(causal_mask(segment_row)[None], scores, -1e+30)
    soft_weights = jax.nn.softmax(scores, axis=-1)
    mixed = jnp.einsum('hqk,khd->qhd', low(soft_weights), values_low, precision=highest).reshape(length, D)
    attended = jnp.dot(low(low_back(mixed)), weights[3], precision=highest) + vecs[7]
    normed_two = layer_norm(row_tokens, vecs[2], vecs[3])
    hidden_pre = jnp.einsum('nd,kdf->nkf', low(normed_two), weights[4:4 + splits], precision=highest)
    hidden_pre = low_back(hidden_pre + vecs[8:8 + splits][None])
    activated = low(jax.nn.gelu(hidden_pre, approximate=False))
    feed = jnp.einsum('nkf,kfd->nd', activated, weights[4 + splits:4 + 2 * splits], precision=highest) + vecs[8 + splits]
    return row_tokens + attended + feed

def reference(tokens, segment_ids, cotangent, blocks, vectors, stat_left, stat_right, root_left, root_right, vec_stat, owners):

    def forward(blocks_in, vectors_in, tokens_in):
        weights = low(blocks_in)
        vecs = low(vectors_in)

        def one_row(row_pair):
            return row_forward(weights, vecs, row_pair[0], row_pair[1])
        return lax.map(jax.checkpoint(one_row), (tokens_in, segment_ids))
    output, pullback = jax.vjp(forward, blocks, vectors, tokens.astype(jnp.float32))
    grad_blocks, grad_vectors, grad_input = pullback(cotangent.astype(jnp.float32))
    squares = jnp.sum(grad_blocks * grad_blocks) + jnp.sum(grad_vectors * grad_vectors)
    grad_norm = jnp.sqrt(squares)
    factor = jnp.minimum(1.0, clip_level / grad_norm)
    clipped_blocks = grad_blocks * factor
    clipped_vectors = grad_vectors * factor
    root_count = math.sqrt(NPARAM)
    scaled_blocks = clipped_blocks * root_count

    def per_block(carry, items):
        left_all, right_all = carry
        owner_index, scaled, weight = items
        owner_index = owner_index.astype(jnp.int32)
        left_old = lax.dynamic_index_in_dim(left_all, owner_index, 0, keepdims=False)
        right_old = lax.dynamic_index_in_dim(right_all, owner_index, 0, keepdims=False)
        left_root = lax.dynamic_index_in_dim(root_left, owner_index, 0, keepdims=False)
        right_root = lax.dynamic_index_in_dim(root_right, owner_index, 0, keepdims=False)
        left_next = decay_beta * left_old + (1.0 - decay_beta) * (jnp.dot(scaled, scaled.T, precision=highest) / D)
        right_next = decay_beta * right_old + (1.0 - decay_beta) * (jnp.dot(scaled.T, scaled, precision=highest) / D)
        precond = jnp.dot(jnp.dot(left_root, scaled, precision=highest), right_root, precision=highest)
        left_all = lax.dynamic_update_index_in_dim(left_all, left_next, owner_index, 0)
        right_all = lax.dynamic_update_index_in_dim(right_all, right_next, owner_index, 0)
        return ((left_all, right_all), weight - matrix_rate * precond)
    (new_left, new_right), new_blocks = lax.scan(per_block, (stat_left, stat_right), (owners, scaled_blocks, blocks))
    scaled_vectors = clipped_vectors * root_count
    new_vec_stat = decay_beta * vec_stat + (1.0 - decay_beta) * (scaled_vectors * scaled_vectors)
    new_vectors = vectors - vector_rate * scaled_vectors * lax.rsqrt(new_vec_stat)
    return (output.astype(jnp.bfloat16), grad_input.astype(jnp.bfloat16), clipped_blocks, clipped_vectors, grad_norm, new_left, new_right, new_vec_stat, new_blocks, new_vectors, new_blocks.astype(jnp.bfloat16), new_vectors.astype(jnp.bfloat16))
```

```python
import functools
import math

import jax
import jax.numpy as jnp
from jax import lax
from jax.experimental import pallas as pl
from jax.experimental.pallas import tpu as pltpu
from jax.sharding import PartitionSpec as P

H = 12
FF = 3072
ROT = 16
NPARAM = 7087872
LONGEST = 256

clip_level = 1.0
matrix_rate = 0.03
vector_rate = 0.2
decay_beta = 0.5
norm_epsilon = 1e-05

f32 = jnp.float32
bf16 = jnp.bfloat16
AXES = ("wide", "narrow")
LANES = 128
MIB = 2**20

NN = (((1,), (0,)), ((), ()))
NT = (((1,), (1,)), ((), ()))
TN = (((0,), (0,)), ((), ()))


def mm(left, right, dims):
    return lax.dot_general(left, right, dims, preferred_element_type=f32)


def call(body, flops, moved, vmem=60, **rest):
    grid = rest["grid_spec"].grid if "grid_spec" in rest else rest.get("grid", ())
    return pl.pallas_call(
        body,
        compiler_params=pltpu.CompilerParams(
            vmem_limit_bytes=vmem * MIB,
            dimension_semantics=("arbitrary",) * len(grid),
        ),
        cost_estimate=pl.CostEstimate(
            flops=int(flops), bytes_accessed=int(moved), transcendentals=0
        ),
        **rest,
    )


def sub_sum(values):
    return jnp.sum(values.reshape(-1, 8, values.shape[-1]), axis=0)


def rotary_tables(segment_ids):
    rows, length = segment_ids.shape
    start = jnp.sum(
        (segment_ids[:, None, :] < segment_ids[:, :, None]).astype(jnp.int32), axis=-1
    )
    offset = (jnp.arange(length, dtype=jnp.int32)[None] - start).astype(f32).reshape(-1, 1)
    half = ROT // 2
    lane = jnp.arange(LANES) % 64
    rates = jnp.power(10000.0, -2.0 * jnp.arange(half, dtype=f32) / ROT)
    angle = offset * jnp.where(lane < ROT, rates[lane % half], 0.0)[None]
    cosine, sine = jnp.cos(angle), jnp.sin(angle)
    first = jnp.where(lane[None] < half, -sine, 0.0)
    second = jnp.where((lane[None] >= half) & (lane[None] < ROT), sine, 0.0)
    return cosine, first, second


def rotate(values, cosine, first, second):
    parts = []
    for at in range(0, values.shape[1], LANES):
        part = values[:, at : at + LANES]
        parts.append(
            part * cosine
            + pltpu.roll(part, LANES - ROT // 2, 1) * first
            + pltpu.roll(part, ROT // 2, 1) * second
        )
    return jnp.concatenate(parts, axis=1)


def rotate_back(values, cosine, first, second):
    return (
        values * cosine
        - pltpu.roll(values, LANES - ROT // 2, 1) * first
        - pltpu.roll(values, ROT // 2, 1) * second
    )


def project_body(a1_ref, dy_ref, w_ref, vec_ref, c_ref, a_ref, b_ref, q_ref, k_ref, v_ref, do_ref):
    a1, tables = a1_ref[...], (c_ref[...], a_ref[...], b_ref[...])
    q_ref[...] = rotate(mm(a1, w_ref[0], NN) + vec_ref[4:5, :], *tables).astype(bf16)
    k_ref[...] = rotate(mm(a1, w_ref[1], NN) + vec_ref[5:6, :], *tables).astype(bf16)
    v_ref[...] = (mm(a1, w_ref[2], NN) + vec_ref[6:7, :]).astype(bf16)
    do_ref[...] = mm(dy_ref[...], w_ref[3], NT).astype(bf16)


def project(a1, dy, weights, vecs, tables, step=256):
    count, width = a1.shape
    token = pl.BlockSpec((step, width), lambda i: (i, 0))
    table = pl.BlockSpec((step, LANES), lambda i: (i, 0))
    return call(
        project_body,
        8 * count * width * width,
        12 * count * width + 8 * width * width,
        grid=(count // step,),
        in_specs=[
            token,
            token,
            pl.BlockSpec((4, width, width), lambda i: (0, 0, 0)),
            pl.BlockSpec(vecs.shape, lambda i: (0, 0)),
            table,
            table,
            table,
        ],
        out_specs=[token] * 4,
        out_shape=[jax.ShapeDtypeStruct((count, width), bf16)] * 4,
    )(a1, dy, weights, vecs, *tables)


def attend_body(
    col_ref, row_ref, q_ref, k_ref, v_ref, do_ref, c_ref, a_ref, b_ref,
    o_ref, g_ref, sum_ref, mask_ref, dk_acc, dv_acc, *, block,
):
    length = q_ref.shape[0]
    steps = length // block

    def reach(i):
        return max(0, (i * block - (LONGEST - 1)) // block * block), (i + 1) * block

    @pl.when(pl.program_id(1) == 0)
    def _():
        for i in range(steps):
            lo, hi = reach(i)
            key = lax.broadcasted_iota(jnp.int32, (hi - lo, block), 0) + lo
            query = lax.broadcasted_iota(jnp.int32, (hi - lo, block), 1) + i * block
            same = col_ref[lo:hi, :] == row_ref[0, :, i * block : hi]
            mask = jnp.where(same & (key <= query), 0.0, -jnp.inf)
            mask_ref[i, 0 : hi - lo, 0:block] = mask
            mask_ref[i, 0 : hi - lo, block:] = mask

    low = lax.broadcasted_iota(jnp.int32, (1, LANES), 1) < 64
    eighth = jnp.asarray(0.125, bf16)
    zero = jnp.zeros((), bf16)
    keys, values, grads = k_ref[...], v_ref[...], do_ref[...]
    queries = q_ref[...] * eighth
    keys_t, values_t = (keys * eighth).T, values.T

    def both(part):
        return jnp.concatenate([jnp.where(low, part, zero), jnp.where(low, zero, part)], axis=0)

    def unstack(part):
        return jnp.concatenate([part[0:64, 0:block], part[64:, block:]], axis=0).T

    dk_acc[...] = jnp.zeros_like(dk_acc)
    dv_acc[...] = jnp.zeros_like(dv_acc)
    q_sum = jnp.zeros((8, LANES), f32)
    for i in range(steps):
        lo, hi = reach(i)
        here = slice(i * block, hi)
        q2, do2 = both(queries[here]), both(grads[here])
        scores = mm(keys[lo:hi], q2, NT) + mask_ref[i, 0 : hi - lo, :]
        raised = jnp.exp(scores - jnp.max(scores, axis=0, keepdims=True))
        soft = raised * (1.0 / jnp.sum(raised, axis=0, keepdims=True))
        d_soft = mm(values[lo:hi], do2, NT)
        inner = jnp.sum(soft * d_soft, axis=0, keepdims=True)
        soft_low = soft.astype(bf16)
        d_scores = (soft * (d_soft - inner)).astype(bf16)
        o_ref[here, :] = unstack(mm(values_t[:, lo:hi], soft_low, NN)).astype(bf16)
        dq = rotate_back(
            unstack(mm(keys_t[:, lo:hi], d_scores, NN)), c_ref[here, :], a_ref[here, :], b_ref[here, :]
        ).astype(bf16)
        g_ref[0, here, :] = dq
        q_sum = q_sum + sub_sum(dq.astype(f32))
        dk_acc[lo:hi, :] += mm(d_scores, q2, NN)
        dv_acc[lo:hi, :] += mm(soft_low, do2, NN)
    dk = rotate_back(dk_acc[...], c_ref[...], a_ref[...], b_ref[...]).astype(bf16)
    dv = dv_acc[...].astype(bf16)
    g_ref[1] = dk
    g_ref[2] = dv
    sum_ref[0] = q_sum
    sum_ref[1] = sub_sum(dk.astype(f32))
    sum_ref[2] = sub_sum(dv.astype(f32))


def attend(segment_ids, q, k, v, do, tables, block=256):
    rows, length = segment_ids.shape
    count, width = q.shape
    block = min(block, length)
    token = pl.BlockSpec((length, LANES), lambda r, h: (r, h))
    table = pl.BlockSpec((length, LANES), lambda r, h: (r, 0))
    return call(
        functools.partial(attend_body, block=block),
        24 * count * length * width,
        24 * count * width,
        grid=(rows, width // LANES),
        in_specs=[
            pl.BlockSpec((length, 1), lambda r, h: (r, 0)),
            pl.BlockSpec((1, 1, length), lambda r, h: (r, 0, 0)),
            token,
            token,
            token,
            token,
            table,
            table,
            table,
        ],
        out_specs=[
            token,
            pl.BlockSpec((3, length, LANES), lambda r, h: (0, r, h)),
            pl.BlockSpec((3, 8, LANES), lambda r, h: (0, r, h)),
        ],
        out_shape=[
            jax.ShapeDtypeStruct((count, width), bf16),
            jax.ShapeDtypeStruct((3, count, width), bf16),
            jax.ShapeDtypeStruct((3, 8 * rows, width), f32),
        ],
        scratch_shapes=[
            pltpu.VMEM((length // block, length, 2 * block), f32),
            pltpu.VMEM((length, LANES), f32),
            pltpu.VMEM((length, LANES), f32),
        ],
    )(
        segment_ids.reshape(-1, 1),
        segment_ids.reshape(rows, 1, length),
        q,
        k,
        v,
        do,
        *tables,
    )


def put_grad(grad, core, outs, index, shard):
    if len(outs) == 1:
        outs[0][index] = grad
        return
    width = grad.shape[1]
    parts = grad.reshape(-1, 2, shard, width)
    even = parts[:, 0].reshape(-1, width).astype(bf16)
    odd = parts[:, 1].reshape(-1, width).astype(bf16)
    keep_ref, send_ref = outs

    @pl.when(core == 0)
    def _():
        keep_ref[index] = even
        send_ref[index] = odd

    @pl.when(core != 0)
    def _():
        keep_ref[index] = odd
        send_ref[index] = even


def grad_shapes(blocks, width, paired):
    if paired:
        return [jax.ShapeDtypeStruct((blocks, width // 2, width), bf16)] * 2
    return [jax.ShapeDtypeStruct((blocks, width, width), f32)]


def attn_grad_body(core_ref, a1_ref, o_ref, g_ref, dy_ref, *outs, shard):
    b = pl.program_id(0)

    @pl.when(b < 3)
    def _():
        put_grad(mm(a1_ref[...], g_ref[0], TN), core_ref[0], outs, 0, shard)

    @pl.when(b == 3)
    def _():
        put_grad(mm(o_ref[...], dy_ref[...], TN), core_ref[0], outs, 0, shard)


def attn_grads(core, a1, o, g, dy, shard, paired):
    count, width = a1.shape
    whole = pl.BlockSpec((count, width), lambda b, s: (0, 0))
    shapes = grad_shapes(4, width, paired)
    return call(
        functools.partial(attn_grad_body, shard=shard),
        8 * count * width * width,
        12 * count * width + 8 * width * width,
        grid_spec=pltpu.PrefetchScalarGridSpec(
            num_scalar_prefetch=1,
            grid=(4,),
            in_specs=[
                whole,
                whole,
                pl.BlockSpec((1, count, width), lambda b, s: (jnp.minimum(b, 2), 0, 0)),
                whole,
            ],
            out_specs=[pl.BlockSpec((1, *s.shape[1:]), lambda b, s: (b, 0, 0)) for s in shapes],
        ),
        out_shape=shapes,
    )(core, a1, o, g, dy)


def gelu_parts(u):
    raised = jnp.exp(-0.5 * (u * u))
    t = 1.0 / (1.0 + (0.3275911 * math.sqrt(0.5)) * jnp.abs(u))
    poly = 1.061405429 * t - 1.453152027
    poly = poly * t + 1.421413741
    poly = poly * t - 0.284496736
    poly = (poly * t + 0.254829592) * t
    tail = 0.5 * poly * raised
    return jnp.where(u < 0, tail, 1.0 - tail), raised * (1.0 / math.sqrt(2.0 * math.pi))


def mlp_body(core_ref, a2_ref, dy_ref, wu_ref, wd_ref, bu_ref, e_ref, du_ref, sum_ref, *rest, steps, shard):
    *outs, up_acc, down_acc, sum_acc = rest
    i = pl.program_id(1)
    a2, dy = a2_ref[...], dy_ref[...]
    u = mm(a2, wu_ref[0], NN) + bu_ref[0]
    de = mm(dy, wd_ref[0], NT)
    dist, density = gelu_parts(u)
    e = (u * dist).astype(bf16)
    du = (de * (dist + u * density)).astype(bf16)
    e_ref[0] = e
    du_ref[0] = du
    up, down = mm(a2, du, TN), mm(e, dy, TN)
    part = sub_sum(du.astype(f32))

    @pl.when(i == 0)
    def _():
        up_acc[...] = up
        down_acc[...] = down
        sum_acc[...] = part

    @pl.when((i > 0) & (i < steps - 1))
    def _():
        up_acc[...] += up
        down_acc[...] += down
        sum_acc[...] += part

    @pl.when(i == steps - 1)
    def _():
        put_grad(up_acc[...] + up, core_ref[0], outs, (0, 0), shard)
        put_grad(down_acc[...] + down, core_ref[0], outs, (1, 0), shard)
        sum_ref[0] = sum_acc[...] + part


def mlp(core, a2, dy, ups, downs, biases, shard, paired, step=512):
    blocks = len(ups)
    count, width = a2.shape
    steps = count // step
    wu, wd, bu = jnp.stack(ups), jnp.stack(downs), jnp.stack(biases)[:, None, :]
    token = pl.BlockSpec((step, width), lambda j, i, s: (i, 0))
    weight = pl.BlockSpec((1, width, width), lambda j, i, s: (j, 0, 0))
    hidden = pl.BlockSpec((1, step, width), lambda j, i, s: (j, i, 0))
    shapes = [
        jax.ShapeDtypeStruct((2, blocks, *s.shape[1:]), s.dtype)
        for s in grad_shapes(blocks, width, paired)
    ]
    return call(
        functools.partial(mlp_body, steps=steps, shard=shard),
        blocks * 8 * count * width * width,
        blocks * (8 * count * width + 8 * width * width),
        grid_spec=pltpu.PrefetchScalarGridSpec(
            num_scalar_prefetch=1,
            grid=(blocks, steps),
            in_specs=[
                token,
                token,
                weight,
                weight,
                pl.BlockSpec((1, 1, width), lambda j, i, s: (j, 0, 0)),
            ],
            out_specs=[hidden, hidden, pl.BlockSpec((1, 8, width), lambda j, i, s: (j, 0, 0))]
            + [pl.BlockSpec((2, 1, *s.shape[2:]), lambda j, i, s: (0, j, 0, 0)) for s in shapes],
            scratch_shapes=[
                pltpu.VMEM((width, width), f32),
                pltpu.VMEM((width, width), f32),
                pltpu.VMEM((8, width), f32),
            ],
        ),
        out_shape=[
            jax.ShapeDtypeStruct((blocks, count, width), bf16),
            jax.ShapeDtypeStruct((blocks, count, width), bf16),
            jax.ShapeDtypeStruct((blocks, 8, width), f32),
            *shapes,
        ],
    )(core, a2, dy, wu, wd, bu)


def norm_back(grad, unit, scale, gain):
    grad = grad * gain
    first = jnp.mean(grad, axis=1, keepdims=True)
    second = jnp.mean(grad * unit, axis=1, keepdims=True)
    return scale * (grad - first - unit * second)


def finish_body(*refs, splits, parts):
    x_ref, dy_ref, o_ref, g_ref, *refs = refs
    e_refs, du_refs, refs = refs[:parts], refs[parts : 2 * parts], refs[2 * parts :]
    wa_ref, wm_ref, vec_ref, out_ref, grad_ref, sum_ref = refs
    per = splits // parts
    x, dy = x_ref[...].astype(f32), dy_ref[...].astype(f32)
    acc = mm(o_ref[...], wa_ref[3], NN)
    for j in range(splits):
        acc = acc + mm(e_refs[j // per][j % per], wm_ref[splits + j], NN)
    out_ref[...] = (x + acc + (vec_ref[7:8, :] + vec_ref[8 + splits : 9 + splits, :])).astype(bf16)
    one = mm(g_ref[0], wa_ref[0], NT) + mm(g_ref[1], wa_ref[1], NT) + mm(g_ref[2], wa_ref[2], NT)
    two = mm(du_refs[0][0], wm_ref[0], NT)
    for j in range(1, splits):
        two = two + mm(du_refs[j // per][j % per], wm_ref[j], NT)
    centred = x - jnp.mean(x, axis=1, keepdims=True)
    scale = lax.rsqrt(jnp.mean(centred * centred, axis=1, keepdims=True) + norm_epsilon)
    unit = centred * scale
    grad_ref[...] = (
        dy
        + norm_back(one, unit, scale, vec_ref[0:1, :])
        + norm_back(two, unit, scale, vec_ref[2:3, :])
    ).astype(bf16)
    sums = [sub_sum(t) for t in (one * unit, one, two * unit, two, dy)]

    @pl.when(pl.program_id(0) == 0)
    def _():
        for n, s in enumerate(sums):
            sum_ref[n] = s

    @pl.when(pl.program_id(0) > 0)
    def _():
        for n, s in enumerate(sums):
            sum_ref[n] += s


def finish(x, dy, o, g, es, dus, wa, wm, vecs, step=256):
    count, width = x.shape
    parts = len(es)
    splits = sum(e.shape[0] for e in es)
    token = pl.BlockSpec((step, width), lambda i: (i, 0))

    def stacked(n):
        return pl.BlockSpec((n, step, width), lambda i: (0, i, 0))

    def resident(w):
        return pl.BlockSpec(w.shape, lambda i: (0, 0, 0), pipeline_mode=pl.Buffered(1))

    return call(
        functools.partial(finish_body, splits=splits, parts=parts),
        24 * count * width * width,
        36 * count * width + 24 * width * width,
        grid=(count // step,),
        in_specs=[token, token, token, stacked(3)]
        + [stacked(e.shape[0]) for e in es]
        + [stacked(d.shape[0]) for d in dus]
        + [resident(wa), resident(wm), pl.BlockSpec(vecs.shape, lambda i: (0, 0))],
        out_specs=[token, token, pl.BlockSpec((5, 8, width), lambda i: (0, 0, 0))],
        out_shape=[
            jax.ShapeDtypeStruct((count, width), bf16),
            jax.ShapeDtypeStruct((count, width), bf16),
            jax.ShapeDtypeStruct((5, 8, width), f32),
        ],
    )(x, dy, o, g, *es, *dus, wa, wm, vecs)


def grid_places():
    wide, narrow = lax.axis_index("wide"), lax.axis_index("narrow")
    return wide // 2, wide % 2, narrow // 2, narrow % 2


def to_place(move):
    pairs = []
    for z in range(4):
        for y in range(2):
            for x in range(2):
                for c in range(2):
                    a, b, d, e = move(z, y, x, c)
                    pairs.append((((z * 2 + y) * 2 + x) * 2 + c, ((a * 2 + b) * 2 + d) * 2 + e))
    return pairs


def over_c(value):
    return lax.ppermute(value, AXES, to_place(lambda z, y, x, c: (z, y, x, 1 - c)))


def over_x(value):
    return lax.ppermute(value, AXES, to_place(lambda z, y, x, c: (z, y, 1 - x, c)))


def over_y(value):
    return lax.ppermute(value, AXES, to_place(lambda z, y, x, c: (z, 1 - y, x, c)))


def over_z(value, by):
    return lax.ppermute(value, AXES, to_place(lambda z, y, x, c: ((z + by) % 4, y, x, c)))


def gather_order_body(place_ref, a_ref, ac_ref, b_ref, bc_ref, w_ref, v_ref, *, blocks, shard):
    t = pl.program_id(0)
    y, x, c = place_ref[1], place_ref[2], place_ref[3]
    half = a_ref.shape[-1]
    rows = blocks * shard
    for yt in range(2):
        for xt in range(2):
            ry, rx = y ^ yt, x ^ xt
            for at, own_ref, other_ref, i, j in (
                (0, a_ref, ac_ref, ry, rx),
                (half, b_ref, bc_ref, rx, ry),
            ):
                own, other = own_ref[i, j, 0], other_ref[i, j, 0]
                first = jnp.where(c == 0, own, other)
                second = jnp.where(c == 0, other, own)
                for n in range(blocks):
                    piece = jnp.concatenate(
                        [first[n * shard : (n + 1) * shard], second[n * shard : (n + 1) * shard]], axis=0
                    )
                    base = (yt * 2 + xt) * 2 * shard
                    w_ref[n, base : base + 2 * shard, at : at + half] = piece
                v_ref[0, yt, xt, 0, :, at : at + half] = first[rows:]
                v_ref[0, yt, xt, 1, :, at : at + half] = second[rows:]


def gather_staged(shards, extra):
    blocks, shard, width = shards.shape
    z, y, x, c = grid_places()
    own = jnp.concatenate([shards.reshape(blocks * shard, width), extra], axis=0)
    line = jnp.stack([own] + [over_z(own, s) for s in (1, 2, 3)])
    half = width // 2
    a, b = line[:, :, :half], line[:, :, half:]
    a, b = jnp.stack([a, over_x(a)]), jnp.stack([b, over_y(b)])
    a, b = jnp.stack([a, over_y(a)]), jnp.stack([b, over_x(b)])
    ac, bc = over_c(a), over_c(b)
    rows = own.shape[0]
    small = extra.shape[0]
    piece = pl.BlockSpec((2, 2, 1, rows, half), lambda t, s: (0, 0, lax.rem(s[0] - t + 4, 4), 0, 0))
    weights, rest = call(
        functools.partial(gather_order_body, blocks=blocks, shard=shard),
        0,
        64 * rows * width * 4,
        grid_spec=pltpu.PrefetchScalarGridSpec(
            num_scalar_prefetch=1,
            grid=(4,),
            in_specs=[piece] * 4,
            out_specs=[
                pl.BlockSpec((blocks, width // 4, width), lambda t, s: (0, t, 0)),
                pl.BlockSpec((1, 2, 2, 2, small, width), lambda t, s: (t, 0, 0, 0, 0, 0)),
            ],
        ),
        out_shape=[
            jax.ShapeDtypeStruct((blocks, width, width), bf16),
            jax.ShapeDtypeStruct((4, 2, 2, 2, small, width), bf16),
        ],
    )(jnp.stack([z, y, x, c]).astype(jnp.int32), a, ac, b, bc)
    return weights, rest.reshape(32, small, width)


def split_one_body(place_ref, keep_ref, got_ref, ka_ref, sa_ref, kb_ref, sb_ref):
    y, x = place_ref[1], place_ref[2]
    half = ka_ref.shape[-1]

    def total(yi, xi, lo):
        return keep_ref[0, :, yi, xi, :, lo : lo + half].astype(f32) + got_ref[0, :, yi, xi, :, lo : lo + half].astype(f32)

    for i in range(2):
        ka_ref[0, :, i] = total(i, x, 0)
        sa_ref[0, :, i] = total(i, 1 - x, 0).astype(bf16)
        kb_ref[0, :, i] = total(y, i, half)
        sb_ref[0, :, i] = total(1 - y, i, half).astype(bf16)


def split_two_body(place_ref, ka_ref, ga_ref, kb_ref, gb_ref, ka2_ref, sa2_ref, kb2_ref, sb2_ref):
    y, x = place_ref[1], place_ref[2]
    for mine, k_ref, g_ref, k2_ref, s2_ref in (
        (y, ka_ref, ga_ref, ka2_ref, sa2_ref),
        (x, kb_ref, gb_ref, kb2_ref, sb2_ref),
    ):
        k2_ref[0] = k_ref[0, :, mine] + g_ref[0, :, mine].astype(f32)
        s2_ref[0] = (k_ref[0, :, 1 - mine] + g_ref[0, :, 1 - mine].astype(f32)).astype(bf16)


def split_three_body(place_ref, ka_ref, ga_ref, kb_ref, gb_ref, keep_ref, *send_refs):
    z = place_ref[0]
    half = ka_ref.shape[-1]
    for s in range(4):
        at = lax.rem(z + s, 4)
        for lo, k_ref, g_ref in ((0, ka_ref, ga_ref), (half, kb_ref, gb_ref)):
            value = k_ref[0, at] + g_ref[0, at].astype(f32)
            if s == 0:
                keep_ref[0, :, lo : lo + half] = value
            else:
                send_refs[s - 1][0, :, lo : lo + half] = value.astype(bf16)


def staged(body, place, operands, shapes):
    def spec(s):
        n = len(s.shape)
        return pl.BlockSpec((1, *s.shape[1:]), lambda b, p: (b,) + (0,) * (n - 1))

    moved = sum(v.size * v.dtype.itemsize for v in operands) * 2
    return call(
        body,
        0,
        moved,
        grid_spec=pltpu.PrefetchScalarGridSpec(
            num_scalar_prefetch=1,
            grid=(operands[0].shape[0],),
            in_specs=[spec(v) for v in operands],
            out_specs=[spec(s) for s in shapes],
        ),
        out_shape=shapes,
    )(place, *operands)


def reduce_staged(keep, send, shard):
    blocks, rows, width = keep.shape
    half = width // 2
    place = jnp.stack(grid_places()).astype(jnp.int32)
    got = over_c(send)
    full = (blocks, 4, 2, 2, shard, width)

    def shape(middle, wide, kind):
        return jax.ShapeDtypeStruct((blocks, *middle, shard, wide), kind)

    ka, sa, kb, sb = staged(
        split_one_body,
        place,
        [keep.reshape(full), got.reshape(full)],
        [shape((4, 2), half, k) for k in (f32, bf16, f32, bf16)],
    )
    ga, gb = over_x(sa), over_y(sb)
    ka, sa, kb, sb = staged(
        split_two_body, place, [ka, ga, kb, gb], [shape((4,), half, k) for k in (f32, bf16, f32, bf16)]
    )
    ga, gb = over_y(sa), over_x(sb)
    own, *sends = staged(
        split_three_body, place, [ka, ga, kb, gb], [shape((), width, k) for k in (f32, bf16, bf16, bf16)]
    )
    return [own] + [over_z(v, s) for s, v in zip((1, 2, 3), sends)]


def pack_body(slot_ref, *refs, groups, per):
    terms, (shard_ref, out_ref, square_ref) = refs[: groups * per], refs[groups * per :]
    blocks = terms[0].shape[0]
    total = jnp.zeros(square_ref.shape, f32)
    for n in range(groups):
        for b in range(blocks):
            value = terms[n * per][b]
            for m in range(1, per):
                value = value + terms[n * per + m][b].astype(f32)
            shard_ref[n * blocks + b] = value
            total = total + value * value
    square_ref[...] = total

    def one(j, carry):
        b = slot_ref[j]

        @pl.when(b >= 0)
        def _():
            out_ref[j] = shard_ref[jnp.maximum(b, 0)].astype(bf16)

        @pl.when(b < 0)
        def _():
            out_ref[j] = jnp.zeros(out_ref.shape[1:], bf16)

        return carry

    lax.fori_loop(0, out_ref.shape[0], one, 0)


def pack(slots, groups):
    per = len(groups[0])
    blocks, shard, width = groups[0][0].shape
    count = slots.shape[0]
    whole = [v for g in groups for v in g]
    vmem = pl.BlockSpec(memory_space=pltpu.VMEM)
    return call(
        functools.partial(pack_body, groups=len(groups), per=per),
        0,
        sum(v.size * v.dtype.itemsize for v in whole) * 2,
        in_specs=[pl.BlockSpec(memory_space=pltpu.SMEM)] + [vmem] * len(whole),
        out_specs=[vmem] * 3,
        out_shape=[
            jax.ShapeDtypeStruct((blocks * len(groups), shard, width), f32),
            jax.ShapeDtypeStruct((count, shard, width), bf16),
            jax.ShapeDtypeStruct((shard, width), f32),
        ],
    )(slots, *whole)


def precondition_body(scale_ref, s_ref, l_ref, r_ref, p_ref, s_low, r_low):
    @pl.when(pl.program_id(0) == 0)
    def _():
        s_low[...] = (s_ref[...].astype(f32) * scale_ref[0]).astype(bf16)
        r_low[...] = r_ref[...].astype(bf16)

    left = mm(l_ref[...].astype(bf16), s_low[...], NN)
    p_ref[...] = (scale_ref[1] * mm(left.astype(bf16), r_low[...], NN)).astype(bf16)


def precondition(scales, block, left, right, step=256):
    width = block.shape[0]
    whole = pl.BlockSpec((width, width), lambda i: (0, 0))
    rows = pl.BlockSpec((step, width), lambda i: (i, 0))
    return call(
        precondition_body,
        4 * width**3,
        12 * width**2,
        grid=(width // step,),
        in_specs=[pl.BlockSpec(memory_space=pltpu.SMEM), whole, rows, whole],
        out_specs=rows,
        out_shape=jax.ShapeDtypeStruct((width, width), bf16),
        scratch_shapes=[pltpu.VMEM((width, width), bf16), pltpu.VMEM((width, width), bf16)],
    )(scales, block, left, right)


def statistics_body(has_ref, scale_ref, s_ref, l_ref, r_ref, nl_ref, nr_ref, s_low, *, step):
    i = pl.program_id(0)
    width = s_ref.shape[0]

    @pl.when(i == 0)
    def _():
        s_low[...] = (s_ref[...].astype(f32) * scale_ref[0]).astype(bf16)

    factor = (1.0 - decay_beta) * (scale_ref[1] * scale_ref[1] / width)
    at = pl.multiple_of(i * step, step)

    @pl.when(has_ref[0] != 0)
    def _():
        nl_ref[...] = decay_beta * l_ref[...] + factor * mm(s_low[pl.ds(at, step), :], s_low[...], NT)
        nr_ref[...] = decay_beta * r_ref[...] + factor * mm(s_low[:, pl.ds(at, step)], s_low[...], TN)

    @pl.when(has_ref[0] == 0)
    def _():
        nl_ref[...] = l_ref[...]
        nr_ref[...] = r_ref[...]


def statistics(has, scales, block, left, right, step=256):
    width = block.shape[0]
    whole = pl.BlockSpec((width, width), lambda i: (0, 0))
    rows = pl.BlockSpec((step, width), lambda i: (i, 0))
    smem = pl.BlockSpec(memory_space=pltpu.SMEM)
    return call(
        functools.partial(statistics_body, step=step),
        4 * width**3,
        18 * width**2,
        grid=(width // step,),
        in_specs=[smem, smem, whole, rows, rows],
        out_specs=[rows, rows],
        out_shape=[jax.ShapeDtypeStruct((width, width), f32)] * 2,
        scratch_shapes=[pltpu.VMEM((width, width), bf16)],
    )(has, scales, block, left, right)


def update_body(owner_ref, factor_ref, p_ref, shard_ref, block_ref, clip_ref, new_ref, copy_ref):
    for b in range(shard_ref.shape[0]):
        clip_ref[b] = shard_ref[b] * factor_ref[0]
        value = block_ref[b] - matrix_rate * p_ref[owner_ref[b]].astype(f32)
        new_ref[b] = value
        copy_ref[b] = value.astype(bf16)


def update(owners, factor, returned, shards, blocks):
    smem, vmem = pl.BlockSpec(memory_space=pltpu.SMEM), pl.BlockSpec(memory_space=pltpu.VMEM)
    return call(
        update_body,
        0,
        returned.size * 2 + shards.size * 18,
        in_specs=[smem, smem, vmem, vmem, vmem],
        out_specs=[vmem] * 3,
        out_shape=[
            jax.ShapeDtypeStruct(shards.shape, f32),
            jax.ShapeDtypeStruct(shards.shape, f32),
            jax.ShapeDtypeStruct(shards.shape, bf16),
        ],
    )(owners, factor, returned, shards, blocks)


def layer_inputs(tokens, vecs):
    values = tokens.astype(f32)
    centred = values - jnp.mean(values, axis=-1, keepdims=True)
    spread = jnp.mean(centred * centred, axis=-1, keepdims=True)
    unit = centred * lax.rsqrt(spread + norm_epsilon)
    one = (unit * vecs[0] + vecs[1]).astype(bf16)
    two = (unit * vecs[2] + vecs[3]).astype(bf16)
    return one, two


def to_all(value):
    return lax.all_to_all(value, AXES, split_axis=0, concat_axis=0, tiled=True)


def per_device(
    tokens,
    segment_ids,
    cotangent,
    blocks,
    vectors,
    stat_left,
    stat_right,
    root_left,
    root_right,
    vec_stat,
    owners,
    *,
    paired,
):
    rows_here, seq_len, width = tokens.shape
    count = rows_here * seq_len
    splits = FF // width
    slot_count = lax.axis_size(AXES)
    my_index = lax.axis_index(AXES)
    shard = width // slot_count
    vec_rows = vectors.shape[0]

    low_blocks, low_vectors = blocks.astype(bf16), vectors.astype(bf16)
    mlp_weights = lax.all_gather(low_blocks[4:], AXES, axis=1, tiled=True)
    if paired:
        flat = low_vectors.reshape(-1)
        extra = jnp.zeros((8, width), bf16).at[0, : flat.shape[0]].set(flat)
        attn_weights, rest = gather_staged(low_blocks[:4], extra)
        rest = rest[:, 0, : flat.shape[0]].reshape(slot_count, vec_rows, shard)
        vecs = rest.transpose(1, 0, 2).reshape(vec_rows, width).astype(f32)
    else:
        attn_weights = lax.all_gather(low_blocks[:4], AXES, axis=1, tiled=True)
        vecs = lax.all_gather(low_vectors, AXES, axis=1, tiled=True).astype(f32)

    flat_tokens = tokens.reshape(count, width)
    dy = cotangent.reshape(count, width)
    tables = rotary_tables(segment_ids)
    a1, a2 = layer_inputs(flat_tokens, vecs)
    core = (my_index % 2).astype(jnp.int32).reshape(1)

    q, k, v, do = project(a1, dy, attn_weights, vecs, tables)
    o, g, attn_sums = attend(segment_ids, q, k, v, do, tables)
    groups = [attn_grads(core, a1, o, g, dy, shard, paired)]
    es, dus, up_sums = [], [], []
    half = splits // 2
    for first in range(0, splits, half):
        which = range(first, first + half)
        e, du, up_sum, *grads = mlp(
            core,
            a2,
            dy,
            [mlp_weights[j] for j in which],
            [mlp_weights[splits + j] for j in which],
            [vecs[8 + j] for j in which],
            shard,
            paired,
        )
        es.append(e)
        dus.append(du)
        up_sums.append(up_sum)
        groups.append([v.reshape(-1, *v.shape[2:]) for v in grads])
    out, grad_in, sums = finish(flat_tokens, dy, o, g, es, dus, attn_weights, mlp_weights, vecs)

    if paired:
        terms = [reduce_staged(*group, shard) for group in groups]
    else:
        terms = [
            [lax.psum_scatter(group[0], AXES, scatter_dimension=1, tiled=True)] for group in groups
        ]
    order = [0, 1, 2, 3]
    for first in range(0, splits, half):
        order += [4 + first + j for j in range(half)] + [4 + splits + first + j for j in range(half)]

    sums = jnp.sum(sums, axis=1)
    qkv_sums = jnp.sum(attn_sums, axis=1)
    up_sums = jnp.sum(jnp.concatenate(up_sums, axis=0), axis=1)
    grad_vectors = jnp.concatenate([sums[:4], qkv_sums, sums[4:5], up_sums, sums[4:5]], axis=0)
    by_slot = grad_vectors.reshape(vec_rows, slot_count, shard).transpose(1, 0, 2)
    shard_vectors = jnp.sum(to_all(by_slot.reshape(slot_count, -1)), axis=0).reshape(vec_rows, shard)

    ordered = owners[jnp.asarray(order)]
    slot_ids = jnp.arange(slot_count, dtype=jnp.int32)
    match = ordered[None, :] == slot_ids[:, None]
    slots = jnp.sum(jnp.where(match, jnp.arange(1, len(order) + 1, dtype=jnp.int32)[None], 0), axis=1) - 1
    has_block = jnp.any(owners == my_index)
    shards, outgoing, squares = pack(slots, terms)
    local = jnp.sum(squares) + jnp.sum(shard_vectors * shard_vectors)
    everywhere = to_all(jnp.broadcast_to(local, (slot_count, LANES)))
    grad_norm = jnp.sqrt(jnp.sum(everywhere[:, 0]))
    factor = jnp.minimum(1.0, clip_level / grad_norm)
    root_count = math.sqrt(NPARAM)

    scale = factor * root_count
    power = jnp.exp2(jnp.floor(jnp.log2(jnp.maximum(scale, 1e-30)))).astype(bf16).astype(f32)
    scales = jnp.stack([power, scale / power])
    owned = to_all(outgoing).reshape(width, width)
    precond = precondition(scales, owned, root_left[0], root_right[0])
    returned = to_all(precond.reshape(slot_count, shard, width))
    new_left, new_right = statistics(
        has_block.astype(jnp.int32).reshape(1), scales, owned, stat_left[0], stat_right[0]
    )
    inverse = [order.index(b) for b in range(len(order))]
    shards = jnp.stack([shards[i] for i in inverse])
    clipped_blocks, new_blocks, blocks_copy = update(owners, factor.reshape(1), returned, shards, blocks)
    clipped_vectors = shard_vectors * factor
    scaled_vectors = clipped_vectors * root_count
    new_vec_stat = decay_beta * vec_stat + (1.0 - decay_beta) * (scaled_vectors * scaled_vectors)
    new_vectors = vectors - vector_rate * scaled_vectors * lax.rsqrt(new_vec_stat)
    return (
        out.reshape(tokens.shape),
        grad_in.reshape(tokens.shape),
        clipped_blocks,
        clipped_vectors,
        grad_norm,
        new_left[None],
        new_right[None],
        new_vec_stat,
        new_blocks,
        new_vectors,
        blocks_copy,
        new_vectors.astype(bf16),
    )


def solution(mesh):
    rows = P(AXES, None, None)
    split_rows = P(None, AXES, None)
    split_columns = P(None, AXES)
    paired = dict(mesh.shape) == {"wide": 8, "narrow": 4}
    return jax.shard_map(
        functools.partial(per_device, paired=paired),
        mesh=mesh,
        in_specs=(
            rows, P(AXES, None), rows, split_rows, split_columns,
            rows, rows, rows, rows, split_columns, P(),
        ),
        out_specs=(
            rows, rows, split_rows, split_columns, P(), rows, rows,
            split_columns, split_rows, split_columns, split_rows, split_columns,
        ),
        check_vma=False,
    )
```

```python
import functools
import math

import jax
import jax.numpy as jnp
from jax import lax
from jax.experimental import pallas as pl
from jax.experimental.pallas import tpu as pltpu
from jax.sharding import PartitionSpec as P

H = 12
FF = 3072
ROT = 16
NPARAM = 7087872
LONGEST = 256

clip_level = 1.0
matrix_rate = 0.03
vector_rate = 0.2
decay_beta = 0.5
norm_epsilon = 1e-05

f32 = jnp.float32
bf16 = jnp.bfloat16
AXES = ("wide", "narrow")
LANES = 128
MIB = 2**20

NN = (((1,), (0,)), ((), ()))
NT = (((1,), (1,)), ((), ()))
TN = (((0,), (0,)), ((), ()))


def mm(left, right, dims):
    return lax.dot_general(left, right, dims, preferred_element_type=f32)


def call(body, flops, moved, vmem=60, after=(), **rest):
    spec = rest.pop("grid_spec", None)
    grid = spec.grid if spec is not None else rest.get("grid", ())
    later = len(after)
    if later:
        held = [pl.BlockSpec(memory_space=pl.ANY)] * later
        if spec is not None:
            first = spec.num_scalar_prefetch + len(spec.in_specs)
            spec = pltpu.PrefetchScalarGridSpec(
                num_scalar_prefetch=spec.num_scalar_prefetch,
                grid=spec.grid,
                in_specs=list(spec.in_specs) + held,
                out_specs=spec.out_specs,
                scratch_shapes=spec.scratch_shapes,
            )
        else:
            first = len(rest["in_specs"])
            rest["in_specs"] = list(rest["in_specs"]) + held
        inner = body

        def body(*refs):
            inner(*refs[:first], *refs[first + later :])

    if spec is not None:
        rest["grid_spec"] = spec
    made = pl.pallas_call(
        body,
        compiler_params=pltpu.CompilerParams(
            vmem_limit_bytes=vmem * MIB,
            dimension_semantics=("arbitrary",) * len(grid),
        ),
        cost_estimate=pl.CostEstimate(
            flops=int(flops), bytes_accessed=int(moved), transcendentals=0
        ),
        **rest,
    )
    return lambda *operands: made(*operands, *after)


def sub_sum(values):
    return jnp.sum(values.reshape(-1, 8, values.shape[-1]), axis=0)


def rotary_tables(segment_ids):
    rows, length = segment_ids.shape
    start = jnp.sum(
        (segment_ids[:, None, :] < segment_ids[:, :, None]).astype(jnp.int32), axis=-1
    )
    offset = (jnp.arange(length, dtype=jnp.int32)[None] - start).astype(f32).reshape(-1, 1)
    half = ROT // 2
    lane = jnp.arange(LANES) % 64
    rates = jnp.power(10000.0, -2.0 * jnp.arange(half, dtype=f32) / ROT)
    angle = offset * jnp.where(lane < ROT, rates[lane % half], 0.0)[None]
    cosine, sine = jnp.cos(angle), jnp.sin(angle)
    first = jnp.where(lane[None] < half, -sine, 0.0)
    second = jnp.where((lane[None] >= half) & (lane[None] < ROT), sine, 0.0)
    return cosine, first, second


def rotate(values, cosine, first, second):
    parts = []
    for at in range(0, values.shape[1], LANES):
        part = values[:, at : at + LANES]
        parts.append(
            part * cosine
            + pltpu.roll(part, LANES - ROT // 2, 1) * first
            + pltpu.roll(part, ROT // 2, 1) * second
        )
    return jnp.concatenate(parts, axis=1)


def rotate_back(values, cosine, first, second):
    return (
        values * cosine
        - pltpu.roll(values, LANES - ROT // 2, 1) * first
        - pltpu.roll(values, ROT // 2, 1) * second
    )


def project_body(a1_ref, dy_ref, w_ref, vec_ref, c_ref, a_ref, b_ref, q_ref, k_ref, v_ref, do_ref):
    a1, tables = a1_ref[...], (c_ref[...], a_ref[...], b_ref[...])
    q_ref[...] = rotate(mm(a1, w_ref[0], NN) + vec_ref[4:5, :], *tables).astype(bf16)
    k_ref[...] = rotate(mm(a1, w_ref[1], NN) + vec_ref[5:6, :], *tables).astype(bf16)
    v_ref[...] = (mm(a1, w_ref[2], NN) + vec_ref[6:7, :]).astype(bf16)
    do_ref[...] = mm(dy_ref[...], w_ref[3], NT).astype(bf16)


def project(a1, dy, weights, vecs, tables, after=(), step=256):
    count, width = a1.shape
    token = pl.BlockSpec((step, width), lambda i: (i, 0))
    table = pl.BlockSpec((step, LANES), lambda i: (i, 0))
    return call(
        project_body,
        8 * count * width * width,
        12 * count * width + 8 * width * width,
        grid=(count // step,),
        in_specs=[
            token,
            token,
            pl.BlockSpec((4, width, width), lambda i: (0, 0, 0)),
            pl.BlockSpec(vecs.shape, lambda i: (0, 0)),
            table,
            table,
            table,
        ],
        out_specs=[token] * 4,
        out_shape=[jax.ShapeDtypeStruct((count, width), bf16)] * 4,
    )(a1, dy, weights, vecs, *tables)


def attend_body(
    col_ref, row_ref, q_ref, k_ref, v_ref, do_ref, c_ref, a_ref, b_ref,
    o_ref, g_ref, sum_ref, mask_ref, dk_acc, dv_acc, *, block,
):
    length = q_ref.shape[0]
    steps = length // block

    def reach(i):
        return max(0, (i * block - (LONGEST - 1)) // block * block), (i + 1) * block

    @pl.when(pl.program_id(1) == 0)
    def _():
        for i in range(steps):
            lo, hi = reach(i)
            key = lax.broadcasted_iota(jnp.int32, (hi - lo, block), 0) + lo
            query = lax.broadcasted_iota(jnp.int32, (hi - lo, block), 1) + i * block
            same = col_ref[lo:hi, :] == row_ref[0, :, i * block : hi]
            mask = jnp.where(same & (key <= query), 0.0, -jnp.inf)
            mask_ref[i, 0 : hi - lo, 0:block] = mask
            mask_ref[i, 0 : hi - lo, block:] = mask

    low = lax.broadcasted_iota(jnp.int32, (1, LANES), 1) < 64
    eighth = jnp.asarray(0.125, bf16)
    zero = jnp.zeros((), bf16)
    keys, values, grads = k_ref[...], v_ref[...], do_ref[...]
    queries = q_ref[...] * eighth
    keys_t, values_t = (keys * eighth).T, values.T

    def both(part):
        return jnp.concatenate([jnp.where(low, part, zero), jnp.where(low, zero, part)], axis=0)

    def unstack(part):
        return jnp.concatenate([part[0:64, 0:block], part[64:, block:]], axis=0).T

    dk_acc[...] = jnp.zeros_like(dk_acc)
    dv_acc[...] = jnp.zeros_like(dv_acc)
    q_sum = jnp.zeros((8, LANES), f32)
    for i in range(steps):
        lo, hi = reach(i)
        here = slice(i * block, hi)
        q2, do2 = both(queries[here]), both(grads[here])
        scores = mm(keys[lo:hi], q2, NT) + mask_ref[i, 0 : hi - lo, :]
        raised = jnp.exp(scores - jnp.max(scores, axis=0, keepdims=True))
        soft = raised * (1.0 / jnp.sum(raised, axis=0, keepdims=True))
        d_soft = mm(values[lo:hi], do2, NT)
        inner = jnp.sum(soft * d_soft, axis=0, keepdims=True)
        soft_low = soft.astype(bf16)
        d_scores = (soft * (d_soft - inner)).astype(bf16)
        o_ref[here, :] = unstack(mm(values_t[:, lo:hi], soft_low, NN)).astype(bf16)
        dq = rotate_back(
            unstack(mm(keys_t[:, lo:hi], d_scores, NN)), c_ref[here, :], a_ref[here, :], b_ref[here, :]
        ).astype(bf16)
        g_ref[0, here, :] = dq
        q_sum = q_sum + sub_sum(dq.astype(f32))
        dk_acc[lo:hi, :] += mm(d_scores, q2, NN)
        dv_acc[lo:hi, :] += mm(soft_low, do2, NN)
    dk = rotate_back(dk_acc[...], c_ref[...], a_ref[...], b_ref[...]).astype(bf16)
    dv = dv_acc[...].astype(bf16)
    g_ref[1] = dk
    g_ref[2] = dv
    sum_ref[0] = q_sum
    sum_ref[1] = sub_sum(dk.astype(f32))
    sum_ref[2] = sub_sum(dv.astype(f32))


def attend(segment_ids, q, k, v, do, tables, block=256):
    rows, length = segment_ids.shape
    count, width = q.shape
    block = min(block, length)
    token = pl.BlockSpec((length, LANES), lambda r, h: (r, h))
    table = pl.BlockSpec((length, LANES), lambda r, h: (r, 0))
    return call(
        functools.partial(attend_body, block=block),
        24 * count * length * width,
        24 * count * width,
        grid=(rows, width // LANES),
        in_specs=[
            pl.BlockSpec((length, 1), lambda r, h: (r, 0)),
            pl.BlockSpec((1, 1, length), lambda r, h: (r, 0, 0)),
            token,
            token,
            token,
            token,
            table,
            table,
            table,
        ],
        out_specs=[
            token,
            pl.BlockSpec((3, length, LANES), lambda r, h: (0, r, h)),
            pl.BlockSpec((3, 8, LANES), lambda r, h: (0, r, h)),
        ],
        out_shape=[
            jax.ShapeDtypeStruct((count, width), bf16),
            jax.ShapeDtypeStruct((3, count, width), bf16),
            jax.ShapeDtypeStruct((3, 8 * rows, width), f32),
        ],
        scratch_shapes=[
            pltpu.VMEM((length // block, length, 2 * block), f32),
            pltpu.VMEM((length, LANES), f32),
            pltpu.VMEM((length, LANES), f32),
        ],
    )(
        segment_ids.reshape(-1, 1),
        segment_ids.reshape(rows, 1, length),
        q,
        k,
        v,
        do,
        *tables,
    )


def put_grad(grad, core, outs, index, shard):
    if len(outs) == 1:
        outs[0][index] = grad
        return
    width = grad.shape[1]
    parts = grad.reshape(-1, 2, shard, width)
    even = parts[:, 0].reshape(-1, width).astype(bf16)
    odd = parts[:, 1].reshape(-1, width).astype(bf16)
    keep_ref, send_ref = outs

    @pl.when(core == 0)
    def _():
        keep_ref[index] = even
        send_ref[index] = odd

    @pl.when(core != 0)
    def _():
        keep_ref[index] = odd
        send_ref[index] = even


def grad_shapes(blocks, width, paired):
    if paired:
        return [jax.ShapeDtypeStruct((blocks, width // 2, width), bf16)] * 2
    return [jax.ShapeDtypeStruct((blocks, width, width), f32)]


def attn_grad_body(core_ref, a1_ref, o_ref, g_ref, dy_ref, *outs, shard):
    b = pl.program_id(0)

    @pl.when(b < 3)
    def _():
        put_grad(mm(a1_ref[...], g_ref[0], TN), core_ref[0], outs, 0, shard)

    @pl.when(b == 3)
    def _():
        put_grad(mm(o_ref[...], dy_ref[...], TN), core_ref[0], outs, 0, shard)


def attn_grads(core, a1, o, g, dy, shard, paired):
    count, width = a1.shape
    whole = pl.BlockSpec((count, width), lambda b, s: (0, 0))
    shapes = grad_shapes(4, width, paired)
    return call(
        functools.partial(attn_grad_body, shard=shard),
        8 * count * width * width,
        12 * count * width + 8 * width * width,
        grid_spec=pltpu.PrefetchScalarGridSpec(
            num_scalar_prefetch=1,
            grid=(4,),
            in_specs=[
                whole,
                whole,
                pl.BlockSpec((1, count, width), lambda b, s: (jnp.minimum(b, 2), 0, 0)),
                whole,
            ],
            out_specs=[pl.BlockSpec((1, *s.shape[1:]), lambda b, s: (b, 0, 0)) for s in shapes],
        ),
        out_shape=shapes,
    )(core, a1, o, g, dy)


def gelu_parts(u):
    raised = jnp.exp(-0.5 * (u * u))
    t = 1.0 / (1.0 + (0.3275911 * math.sqrt(0.5)) * jnp.abs(u))
    poly = 1.061405429 * t - 1.453152027
    poly = poly * t + 1.421413741
    poly = poly * t - 0.284496736
    poly = (poly * t + 0.254829592) * t
    tail = 0.5 * poly * raised
    return jnp.where(u < 0, tail, 1.0 - tail), raised * (1.0 / math.sqrt(2.0 * math.pi))


def mlp_body(core_ref, a2_ref, dy_ref, wu_ref, wd_ref, bu_ref, e_ref, du_ref, sum_ref, *rest, steps, shard):
    *outs, up_acc, down_acc, sum_acc = rest
    i = pl.program_id(0)
    a2, dy = a2_ref[...], dy_ref[...]
    u = mm(a2, wu_ref[0], NN) + bu_ref[0]
    de = mm(dy, wd_ref[0], NT)
    dist, density = gelu_parts(u)
    e = (u * dist).astype(bf16)
    du = (de * (dist + u * density)).astype(bf16)
    e_ref[...] = e
    du_ref[...] = du
    up, down = mm(a2, du, TN), mm(e, dy, TN)
    part = sub_sum(du.astype(f32))

    @pl.when(i == 0)
    def _():
        up_acc[...] = up
        down_acc[...] = down
        sum_acc[...] = part

    @pl.when((i > 0) & (i < steps - 1))
    def _():
        up_acc[...] += up
        down_acc[...] += down
        sum_acc[...] += part

    @pl.when(i == steps - 1)
    def _():
        put_grad(up_acc[...] + up, core_ref[0], outs, 0, shard)
        put_grad(down_acc[...] + down, core_ref[0], outs, 1, shard)
        sum_ref[...] = sum_acc[...] + part


def mlp(j, core, a2, dy, weights, vecs, shard, paired, after=(), step=512):
    count, width = a2.shape
    splits = weights.shape[0] // 2
    steps = count // step
    token = pl.BlockSpec((step, width), lambda i, s: (i, 0))
    shapes = grad_shapes(2, width, paired)
    return call(
        functools.partial(mlp_body, steps=steps, shard=shard),
        8 * count * width * width,
        8 * count * width + 8 * width * width,
        after=after,
        grid_spec=pltpu.PrefetchScalarGridSpec(
            num_scalar_prefetch=1,
            grid=(steps,),
            in_specs=[
                token,
                token,
                pl.BlockSpec((1, width, width), lambda i, s: (j, 0, 0)),
                pl.BlockSpec((1, width, width), lambda i, s: (splits + j, 0, 0)),
                pl.BlockSpec((1, 1, width), lambda i, s: (8 + j, 0, 0)),
            ],
            out_specs=[token, token, pl.BlockSpec((8, width), lambda i, s: (0, 0))]
            + [pl.BlockSpec(s.shape, lambda i, s: (0, 0, 0)) for s in shapes],
            scratch_shapes=[
                pltpu.VMEM((width, width), f32),
                pltpu.VMEM((width, width), f32),
                pltpu.VMEM((8, width), f32),
            ],
        ),
        out_shape=[
            jax.ShapeDtypeStruct((count, width), bf16),
            jax.ShapeDtypeStruct((count, width), bf16),
            jax.ShapeDtypeStruct((8, width), f32),
            *shapes,
        ],
    )(core, a2, dy, weights, weights, vecs[:, None, :])


def norm_back(grad, unit, scale, gain):
    grad = grad * gain
    first = jnp.mean(grad, axis=1, keepdims=True)
    second = jnp.mean(grad * unit, axis=1, keepdims=True)
    return scale * (grad - first - unit * second)


def output_body(x_ref, o_ref, *refs, splits):
    e_refs, (wo_ref, wm_ref, vec_ref, out_ref) = refs[:splits], refs[splits:]
    acc = mm(o_ref[...], wo_ref[0], NN)
    for j in range(splits):
        acc = acc + mm(e_refs[j][...], wm_ref[j], NN)
    bias = vec_ref[7:8, :] + vec_ref[8 + splits : 9 + splits, :]
    out_ref[...] = (x_ref[...].astype(f32) + acc + bias).astype(bf16)


def output(x, o, es, wa, wm, vecs, after=(), step=256):
    count, width = x.shape
    splits = len(es)
    token = pl.BlockSpec((step, width), lambda i: (i, 0))
    once = pl.Buffered(1)
    return call(
        functools.partial(output_body, splits=splits),
        10 * count * width * width,
        14 * count * width + 10 * width * width,
        after=after,
        grid=(count // step,),
        in_specs=[token, token]
        + [token] * splits
        + [
            pl.BlockSpec((1, width, width), lambda i: (3, 0, 0), pipeline_mode=once),
            pl.BlockSpec((splits, width, width), lambda i: (1, 0, 0), pipeline_mode=once),
            pl.BlockSpec(vecs.shape, lambda i: (0, 0)),
        ],
        out_specs=token,
        out_shape=jax.ShapeDtypeStruct((count, width), bf16),
    )(x, o, *es, wa, wm, vecs)


def input_grad_body(x_ref, dy_ref, g_ref, *refs, splits):
    du_refs, (wa_ref, wm_ref, vec_ref, grad_ref, sum_ref) = refs[:splits], refs[splits:]
    x, dy = x_ref[...].astype(f32), dy_ref[...].astype(f32)
    two = mm(du_refs[0][...], wm_ref[0], NT)
    for j in range(1, splits):
        two = two + mm(du_refs[j][...], wm_ref[j], NT)
    one = mm(g_ref[0], wa_ref[0], NT) + mm(g_ref[1], wa_ref[1], NT) + mm(g_ref[2], wa_ref[2], NT)
    centred = x - jnp.mean(x, axis=1, keepdims=True)
    scale = lax.rsqrt(jnp.mean(centred * centred, axis=1, keepdims=True) + norm_epsilon)
    unit = centred * scale
    grad_ref[...] = (
        dy
        + norm_back(one, unit, scale, vec_ref[0:1, :])
        + norm_back(two, unit, scale, vec_ref[2:3, :])
    ).astype(bf16)
    sums = [sub_sum(t) for t in (one * unit, one, two * unit, two, dy)]

    @pl.when(pl.program_id(0) == 0)
    def _():
        for n, s in enumerate(sums):
            sum_ref[n] = s

    @pl.when(pl.program_id(0) > 0)
    def _():
        for n, s in enumerate(sums):
            sum_ref[n] += s


def input_grad(x, dy, g, dus, wa, wm, vecs, after=(), step=256):
    count, width = x.shape
    splits = len(dus)
    token = pl.BlockSpec((step, width), lambda i: (i, 0))
    once = pl.Buffered(1)
    return call(
        functools.partial(input_grad_body, splits=splits),
        14 * count * width * width,
        20 * count * width + 14 * width * width,
        after=after,
        grid=(count // step,),
        in_specs=[token, token, pl.BlockSpec((3, step, width), lambda i: (0, i, 0))]
        + [token] * splits
        + [
            pl.BlockSpec((3, width, width), lambda i: (0, 0, 0), pipeline_mode=once),
            pl.BlockSpec((splits, width, width), lambda i: (0, 0, 0), pipeline_mode=once),
            pl.BlockSpec(vecs.shape, lambda i: (0, 0)),
        ],
        out_specs=[token, pl.BlockSpec((5, 8, width), lambda i: (0, 0, 0))],
        out_shape=[
            jax.ShapeDtypeStruct((count, width), bf16),
            jax.ShapeDtypeStruct((5, 8, width), f32),
        ],
    )(x, dy, g, *dus, wa, wm, vecs)


def grid_places():
    wide, narrow = lax.axis_index("wide"), lax.axis_index("narrow")
    return wide // 2, wide % 2, narrow // 2, narrow % 2


def to_place(move):
    pairs = []
    for z in range(4):
        for y in range(2):
            for x in range(2):
                for c in range(2):
                    a, b, d, e = move(z, y, x, c)
                    pairs.append((((z * 2 + y) * 2 + x) * 2 + c, ((a * 2 + b) * 2 + d) * 2 + e))
    return pairs


def over_c(value):
    return lax.ppermute(value, AXES, to_place(lambda z, y, x, c: (z, y, x, 1 - c)))


def over_x(value):
    return lax.ppermute(value, AXES, to_place(lambda z, y, x, c: (z, y, 1 - x, c)))


def over_y(value):
    return lax.ppermute(value, AXES, to_place(lambda z, y, x, c: (z, 1 - y, x, c)))


def over_z(value, by):
    return lax.ppermute(value, AXES, to_place(lambda z, y, x, c: ((z + by) % 4, y, x, c)))


def gather_order_body(place_ref, *refs):
    z, y, x, c = place_ref[0], place_ref[1], place_ref[2], place_ref[3]
    out_ref = refs[-1]
    near = pl.program_id(0)
    blocks = out_ref.shape[0]
    half = blocks // 2
    for rc in range(2):
        own, by_x, by_y, lower, upper = refs[rc * 5 : rc * 5 + 5]
        for ry in range(2):
            for rx in range(2):
                at = ((y ^ ry) * 2 + (x ^ rx)) * 2 + (c ^ rc)
                for n in range(blocks):
                    if ry == 0 or rx == 0:
                        ref, m = (own if rx == 0 else by_x) if ry == 0 else by_y, n
                    else:
                        ref, m = (lower, n) if n < half else (upper, n - half)
                    out_ref[n, at] = ref[m, 0]


def gather_staged(shards, after=()):
    blocks, shard, width = shards.shape
    half = blocks // 2
    z, y, x, c = grid_places()
    own = jnp.stack([shards] + [over_z(shards, s) for s in (1, 2, 3)], axis=1)
    by_x, by_y = over_x(own), over_y(own)
    lower, upper = over_y(by_x[:half]), over_x(by_y[half:])
    here = [own, by_x, by_y, lower, upper]
    pieces = here + [over_c(v) for v in here]

    def piece(v):
        return pl.BlockSpec((v.shape[0], 1, shard, width), lambda t, s: (0, lax.rem(s[0] - t + 4, 4), 0, 0))

    weights = call(
        gather_order_body,
        0,
        64 * blocks * shard * width * 2,
        after=after,
        grid_spec=pltpu.PrefetchScalarGridSpec(
            num_scalar_prefetch=1,
            grid=(4,),
            in_specs=[piece(v) for v in pieces],
            out_specs=pl.BlockSpec((blocks, 8, shard, width), lambda t, s: (0, t, 0, 0)),
        ),
        out_shape=jax.ShapeDtypeStruct((blocks, 32, shard, width), bf16),
    )(jnp.stack([z, y, x, c]).astype(jnp.int32), *pieces)
    return weights.reshape(blocks, width, width)


def core_sum_body(place_ref, keep_ref, got_ref, own_ref, send_ref):
    x = place_ref[2]
    for ref, at in ((own_ref, x), (send_ref, 1 - x)):
        ref[...] = (keep_ref[:, :, at].astype(f32) + got_ref[:, :, at].astype(f32)).astype(ref.dtype)


def core_sum(keep, got, shard, after=()):
    blocks, rows, width = keep.shape
    wide = rows // (2 * shard)
    place = jnp.stack(grid_places()).astype(jnp.int32)
    whole = pl.BlockSpec((1, wide, 2, shard, width), lambda b, p: (b, 0, 0, 0, 0))
    part = pl.BlockSpec((1, wide, shard, width), lambda b, p: (b, 0, 0, 0))
    return call(
        core_sum_body,
        0,
        keep.size * 7,
        after=after,
        grid_spec=pltpu.PrefetchScalarGridSpec(
            num_scalar_prefetch=1, grid=(blocks,), in_specs=[whole, whole], out_specs=[part, part]
        ),
        out_shape=[
            jax.ShapeDtypeStruct((blocks, wide, shard, width), f32),
            jax.ShapeDtypeStruct((blocks, wide, shard, width), bf16),
        ],
    )(place, keep.reshape(blocks, wide, 2, shard, width), got.reshape(blocks, wide, 2, shard, width))


def pair_sum_body(own_ref, got_ref, out_ref):
    for n in range(own_ref.shape[0]):
        out_ref[:, n] = (own_ref[n] + got_ref[n].astype(f32)).astype(bf16)


def pair_sum(own, got, after=()):
    blocks, wide, shard, width = own.shape
    part = pl.BlockSpec((blocks, wide // 2, shard, width), lambda t: (0, t, 0, 0))
    return call(
        pair_sum_body,
        0,
        own.size * 8,
        after=after,
        grid=(2,),
        in_specs=[part, part],
        out_specs=pl.BlockSpec((wide // 2, blocks, shard, width), lambda t: (t, 0, 0, 0)),
        out_shape=jax.ShapeDtypeStruct((wide, blocks, shard, width), bf16),
    )(own, got)


def over_wide(value):
    return lax.all_to_all(value, "wide", split_axis=0, concat_axis=0, tiled=True)


def pack_body(slot_ref, *refs, orders):
    terms, (shard_ref, out_ref, square_ref) = refs[: len(orders)], refs[len(orders) :]
    total = jnp.zeros(square_ref.shape, f32)
    for ref, order in zip(terms, orders):
        for m, b in enumerate(order):
            value = ref[0, m].astype(f32)
            for t in range(1, ref.shape[0]):
                value = value + ref[t, m].astype(f32)
            shard_ref[b] = value
            total = total + value * value
    square_ref[...] = total

    def one(j, carry):
        b = slot_ref[j]

        @pl.when(b >= 0)
        def _():
            out_ref[j] = shard_ref[jnp.maximum(b, 0)].astype(bf16)

        @pl.when(b < 0)
        def _():
            out_ref[j] = jnp.zeros(out_ref.shape[1:], bf16)

        return carry

    lax.fori_loop(0, out_ref.shape[0], one, 0)


def pack(slots, terms, orders, after=()):
    _, _, shard, width = terms[0].shape
    vmem = pl.BlockSpec(memory_space=pltpu.VMEM)
    return call(
        functools.partial(pack_body, orders=orders),
        0,
        sum(v.size * v.dtype.itemsize for v in terms) * 2,
        after=after,
        in_specs=[pl.BlockSpec(memory_space=pltpu.SMEM)] + [vmem] * len(terms),
        out_specs=[vmem] * 3,
        out_shape=[
            jax.ShapeDtypeStruct((sum(map(len, orders)), shard, width), f32),
            jax.ShapeDtypeStruct((slots.shape[0], shard, width), bf16),
            jax.ShapeDtypeStruct((shard, width), f32),
        ],
    )(slots, *terms)


def precondition_body(scale_ref, s_ref, l_ref, r_ref, p_ref, s_low, r_low):
    @pl.when(pl.program_id(0) == 0)
    def _():
        s_low[...] = (s_ref[...].astype(f32) * scale_ref[0]).astype(bf16)
        r_low[...] = r_ref[...].astype(bf16)

    left = mm(l_ref[...].astype(bf16), s_low[...], NN)
    p_ref[...] = (scale_ref[1] * mm(left.astype(bf16), r_low[...], NN)).astype(bf16)


def precondition(scales, block, left, right, step=256):
    width = block.shape[0]
    whole = pl.BlockSpec((width, width), lambda i: (0, 0))
    rows = pl.BlockSpec((step, width), lambda i: (i, 0))
    return call(
        precondition_body,
        4 * width**3,
        12 * width**2,
        grid=(width // step,),
        in_specs=[pl.BlockSpec(memory_space=pltpu.SMEM), whole, rows, whole],
        out_specs=rows,
        out_shape=jax.ShapeDtypeStruct((width, width), bf16),
        scratch_shapes=[pltpu.VMEM((width, width), bf16), pltpu.VMEM((width, width), bf16)],
    )(scales, block, left, right)


def statistics_body(has_ref, scale_ref, s_ref, l_ref, r_ref, nl_ref, nr_ref, s_low, *, step):
    i = pl.program_id(0)
    width = s_ref.shape[0]

    @pl.when(i == 0)
    def _():
        s_low[...] = (s_ref[...].astype(f32) * scale_ref[0]).astype(bf16)

    factor = (1.0 - decay_beta) * (scale_ref[1] * scale_ref[1] / width)
    at = pl.multiple_of(i * step, step)

    @pl.when(has_ref[0] != 0)
    def _():
        nl_ref[...] = decay_beta * l_ref[...] + factor * mm(s_low[pl.ds(at, step), :], s_low[...], NT)
        nr_ref[...] = decay_beta * r_ref[...] + factor * mm(s_low[:, pl.ds(at, step)], s_low[...], TN)

    @pl.when(has_ref[0] == 0)
    def _():
        nl_ref[...] = l_ref[...]
        nr_ref[...] = r_ref[...]


def statistics(has, scales, block, left, right, step=256):
    width = block.shape[0]
    whole = pl.BlockSpec((width, width), lambda i: (0, 0))
    rows = pl.BlockSpec((step, width), lambda i: (i, 0))
    smem = pl.BlockSpec(memory_space=pltpu.SMEM)
    return call(
        functools.partial(statistics_body, step=step),
        4 * width**3,
        18 * width**2,
        grid=(width // step,),
        in_specs=[smem, smem, whole, rows, rows],
        out_specs=[rows, rows],
        out_shape=[jax.ShapeDtypeStruct((width, width), f32)] * 2,
        scratch_shapes=[pltpu.VMEM((width, width), bf16)],
    )(has, scales, block, left, right)


def update_body(owner_ref, factor_ref, p_ref, shard_ref, block_ref, clip_ref, new_ref, copy_ref):
    for b in range(shard_ref.shape[0]):
        clip_ref[b] = shard_ref[b] * factor_ref[0]
        value = block_ref[b] - matrix_rate * p_ref[owner_ref[b]].astype(f32)
        new_ref[b] = value
        copy_ref[b] = value.astype(bf16)


def update(owners, factor, returned, shards, blocks):
    smem, vmem = pl.BlockSpec(memory_space=pltpu.SMEM), pl.BlockSpec(memory_space=pltpu.VMEM)
    return call(
        update_body,
        0,
        returned.size * 2 + shards.size * 18,
        in_specs=[smem, smem, vmem, vmem, vmem],
        out_specs=[vmem] * 3,
        out_shape=[
            jax.ShapeDtypeStruct(shards.shape, f32),
            jax.ShapeDtypeStruct(shards.shape, f32),
            jax.ShapeDtypeStruct(shards.shape, bf16),
        ],
    )(owners, factor, returned, shards, blocks)


def layer_inputs(tokens, vecs):
    values = tokens.astype(f32)
    centred = values - jnp.mean(values, axis=-1, keepdims=True)
    spread = jnp.mean(centred * centred, axis=-1, keepdims=True)
    unit = centred * lax.rsqrt(spread + norm_epsilon)
    one = (unit * vecs[0] + vecs[1]).astype(bf16)
    two = (unit * vecs[2] + vecs[3]).astype(bf16)
    return one, two


def to_all(value):
    return lax.all_to_all(value, AXES, split_axis=0, concat_axis=0, tiled=True)


def per_device(
    tokens,
    segment_ids,
    cotangent,
    blocks,
    vectors,
    stat_left,
    stat_right,
    root_left,
    root_right,
    vec_stat,
    owners,
    *,
    paired,
):
    rows_here, seq_len, width = tokens.shape
    count = rows_here * seq_len
    splits = FF // width
    slot_count = lax.axis_size(AXES)
    my_index = lax.axis_index(AXES)
    shard = width // slot_count
    vec_rows = vectors.shape[0]

    low_blocks, low_vectors = blocks.astype(bf16), vectors.astype(bf16)
    everyone = jnp.broadcast_to(low_vectors.reshape(1, -1), (slot_count, vec_rows * shard))
    vecs = to_all(everyone).reshape(slot_count, vec_rows, shard)
    vecs = vecs.transpose(1, 0, 2).reshape(vec_rows, width).astype(f32)
    mlp_weights = lax.all_gather(low_blocks[4:], AXES, axis=1, tiled=True)

    flat_tokens = tokens.reshape(count, width)
    dy = cotangent.reshape(count, width)
    tables = rotary_tables(segment_ids)
    a1, a2 = layer_inputs(flat_tokens, vecs)
    core = (my_index % 2).astype(jnp.int32).reshape(1)
    if paired:
        attn_weights = gather_staged(low_blocks[:4], after=(*tables, a1, a2))
    else:
        attn_weights = lax.all_gather(low_blocks[:4], AXES, axis=1, tiled=True)

    q, k, v, do = project(a1, dy, attn_weights, vecs, tables)
    o, g, attn_sums = attend(segment_ids, q, k, v, do, tables)
    orders = [list(range(4))] + [[4 + j, 4 + splits + j] for j in range(splits)]
    grads = [attn_grads(core, a1, o, g, dy, shard, paired)]
    es, dus, up_sums, terms = [], [], [], []
    at_core, at_pair = [], []
    after = (grads[0][0],)
    for j in range(splits):
        e, du, up_sum, *grad = mlp(j, core, a2, dy, mlp_weights, vecs, shard, paired, after=after)
        es.append(e)
        dus.append(du)
        up_sums.append(up_sum)
        grads.append(grad)
        if paired:
            after = ()
            if at_core:
                terms.append(over_wide(made := pair_sum(*at_core.pop(), after=(e,))))
                after += (made,)
            keep, send = grads[j]
            own, send = core_sum(keep, over_c(send), shard, after=(e,))
            at_core.append((own, over_x(send)))
            after += (own,)
        else:
            after = (e,)
    if paired:
        terms.append(over_wide(made := pair_sum(*at_core.pop(), after=(es[-1],))))
        keep, send = grads[splits]
        own, send = core_sum(keep, over_c(send), shard, after=(made,))
        out = output(flat_tokens, o, es, attn_weights, mlp_weights, vecs, after=(made, own))
        terms.append(over_wide(made := pair_sum(own, over_x(send), after=(out,))))
        after = (made,)
    else:
        out = output(flat_tokens, o, es, attn_weights, mlp_weights, vecs)
        terms = [
            lax.psum_scatter(grad[0], AXES, scatter_dimension=1, tiled=True)[None] for grad in grads
        ]
        after = ()
    grad_in, sums = input_grad(flat_tokens, dy, g, dus, attn_weights, mlp_weights, vecs, after=after)

    sums = jnp.sum(sums, axis=1)
    qkv_sums = jnp.sum(attn_sums, axis=1)
    up_sums = jnp.sum(jnp.stack(up_sums), axis=1)
    grad_vectors = jnp.concatenate([sums[:4], qkv_sums, sums[4:5], up_sums, sums[4:5]], axis=0)
    by_slot = grad_vectors.reshape(vec_rows, slot_count, shard).transpose(1, 0, 2)
    shard_vectors = jnp.sum(to_all(by_slot.reshape(slot_count, -1)), axis=0).reshape(vec_rows, shard)

    slot_ids = jnp.arange(slot_count, dtype=jnp.int32)
    match = owners[None, :] == slot_ids[:, None]
    slots = jnp.sum(jnp.where(match, jnp.arange(1, owners.shape[0] + 1, dtype=jnp.int32)[None], 0), axis=1) - 1
    has_block = jnp.any(owners == my_index)
    shards, outgoing, squares = pack(slots, terms, orders, after=(grad_in,))
    local = jnp.sum(squares) + jnp.sum(shard_vectors * shard_vectors)
    everywhere = to_all(jnp.broadcast_to(local, (slot_count, LANES)))
    grad_norm = jnp.sqrt(jnp.sum(everywhere[:, 0]))
    factor = jnp.minimum(1.0, clip_level / grad_norm)
    root_count = math.sqrt(NPARAM)

    scale = factor * root_count
    power = jnp.exp2(jnp.floor(jnp.log2(jnp.maximum(scale, 1e-30)))).astype(bf16).astype(f32)
    scales = jnp.stack([power, scale / power])
    owned = to_all(outgoing).reshape(width, width)
    precond = precondition(scales, owned, root_left[0], root_right[0])
    returned = to_all(precond.reshape(slot_count, shard, width))
    new_left, new_right = statistics(
        has_block.astype(jnp.int32).reshape(1), scales, owned, stat_left[0], stat_right[0]
    )
    clipped_blocks, new_blocks, blocks_copy = update(owners, factor.reshape(1), returned, shards, blocks)
    clipped_vectors = shard_vectors * factor
    scaled_vectors = clipped_vectors * root_count
    new_vec_stat = decay_beta * vec_stat + (1.0 - decay_beta) * (scaled_vectors * scaled_vectors)
    new_vectors = vectors - vector_rate * scaled_vectors * lax.rsqrt(new_vec_stat)
    return (
        out.reshape(tokens.shape),
        grad_in.reshape(tokens.shape),
        clipped_blocks,
        clipped_vectors,
        grad_norm,
        new_left[None],
        new_right[None],
        new_vec_stat,
        new_blocks,
        new_vectors,
        blocks_copy,
        new_vectors.astype(bf16),
    )


def solution(mesh):
    rows = P(AXES, None, None)
    split_rows = P(None, AXES, None)
    split_columns = P(None, AXES)
    paired = dict(mesh.shape) == {"wide": 8, "narrow": 4}
    return jax.shard_map(
        functools.partial(per_device, paired=paired),
        mesh=mesh,
        in_specs=(
            rows, P(AXES, None), rows, split_rows, split_columns,
            rows, rows, rows, rows, split_columns, P(),
        ),
        out_specs=(
            rows, rows, split_rows, split_columns, P(), rows, rows,
            split_columns, split_rows, split_columns, split_rows, split_columns,
        ),
        check_vma=False,
    )
```

```python
import functools
import math

import jax
import jax.numpy as jnp
from jax import lax
from jax.experimental import pallas as pl
from jax.experimental.pallas import tpu as pltpu
from jax.sharding import PartitionSpec as P

H = 12
FF = 3072
ROT = 16
NPARAM = 7087872
LONGEST = 256

clip_level = 1.0
matrix_rate = 0.03
vector_rate = 0.2
decay_beta = 0.5
norm_epsilon = 1e-05

f32 = jnp.float32
bf16 = jnp.bfloat16
AXES = ("wide", "narrow")
LANES = 128
MIB = 2**20

NN = (((1,), (0,)), ((), ()))
NT = (((1,), (1,)), ((), ()))
TN = (((0,), (0,)), ((), ()))


def mm(left, right, dims):
    return lax.dot_general(left, right, dims, preferred_element_type=f32)


def call(body, flops, moved, vmem=60, after=(), **rest):
    spec = rest.pop("grid_spec", None)
    grid = spec.grid if spec is not None else rest.get("grid", ())
    later = len(after)
    if later:
        held = [pl.BlockSpec(memory_space=pl.ANY)] * later
        if spec is not None:
            first = spec.num_scalar_prefetch + len(spec.in_specs)
            spec = pltpu.PrefetchScalarGridSpec(
                num_scalar_prefetch=spec.num_scalar_prefetch,
                grid=spec.grid,
                in_specs=list(spec.in_specs) + held,
                out_specs=spec.out_specs,
                scratch_shapes=spec.scratch_shapes,
            )
        else:
            first = len(rest["in_specs"])
            rest["in_specs"] = list(rest["in_specs"]) + held
        inner = body

        def body(*refs):
            inner(*refs[:first], *refs[first + later :])

    if spec is not None:
        rest["grid_spec"] = spec
    made = pl.pallas_call(
        body,
        compiler_params=pltpu.CompilerParams(
            vmem_limit_bytes=vmem * MIB,
            dimension_semantics=("arbitrary",) * len(grid),
        ),
        cost_estimate=pl.CostEstimate(
            flops=int(flops), bytes_accessed=int(moved), transcendentals=0
        ),
        **rest,
    )
    return lambda *operands: made(*operands, *after)


def hosted(body, steps, place, operands, in_specs, outs, out_specs, scratch=(), riders=(), after=(), flops=0, moved=0):
    counts = [len(operands), len(outs)]
    more_in = [v for r in riders for v in r.ins]
    more_out = [v for r in riders for v in r.outs]

    def whole(place_ref, *refs):
        ins, refs = refs[: counts[0] + len(more_in)], refs[counts[0] + len(more_in) :]
        results, refs = refs[: counts[1] + len(more_out)], refs[counts[1] + len(more_out) :]
        body(place_ref, *ins[: counts[0]], *results[: counts[1]], *refs)
        ins, results = ins[counts[0] :], results[counts[1] :]
        for r in riders:
            r.body(place_ref, steps, ins[: len(r.ins)], results[: len(r.outs)])
            ins, results = ins[len(r.ins) :], results[len(r.outs) :]

    made = call(
        whole,
        flops,
        moved + sum(v.size * v.dtype.itemsize for v in more_in) * 2,
        after=after,
        grid_spec=pltpu.PrefetchScalarGridSpec(
            num_scalar_prefetch=1,
            grid=(steps,),
            in_specs=list(in_specs) + [v for r in riders for v in r.in_specs(steps)],
            out_specs=list(out_specs) + [v for r in riders for v in r.out_specs(steps)],
            scratch_shapes=list(scratch),
        ),
        out_shape=list(outs) + more_out,
    )(place, *operands, *more_in)
    results, rest = made[: counts[1]], made[counts[1] :]
    ridden = []
    for r in riders:
        ridden.append(rest[: len(r.outs)])
        rest = rest[len(r.outs) :]
    return results, ridden


def sub_sum(values):
    return jnp.sum(values.reshape(-1, 8, values.shape[-1]), axis=0)


def rotary_tables(segment_ids):
    rows, length = segment_ids.shape
    start = jnp.sum(
        (segment_ids[:, None, :] < segment_ids[:, :, None]).astype(jnp.int32), axis=-1
    )
    offset = (jnp.arange(length, dtype=jnp.int32)[None] - start).astype(f32).reshape(-1, 1)
    half = ROT // 2
    lane = jnp.arange(LANES) % 64
    rates = jnp.power(10000.0, -2.0 * jnp.arange(half, dtype=f32) / ROT)
    angle = offset * jnp.where(lane < ROT, rates[lane % half], 0.0)[None]
    cosine, sine = jnp.cos(angle), jnp.sin(angle)
    first = jnp.where(lane[None] < half, -sine, 0.0)
    second = jnp.where((lane[None] >= half) & (lane[None] < ROT), sine, 0.0)
    return cosine, first, second


def rotate(values, cosine, first, second):
    parts = []
    for at in range(0, values.shape[1], LANES):
        part = values[:, at : at + LANES]
        parts.append(
            part * cosine
            + pltpu.roll(part, LANES - ROT // 2, 1) * first
            + pltpu.roll(part, ROT // 2, 1) * second
        )
    return jnp.concatenate(parts, axis=1)


def rotate_back(values, cosine, first, second):
    return (
        values * cosine
        - pltpu.roll(values, LANES - ROT // 2, 1) * first
        - pltpu.roll(values, ROT // 2, 1) * second
    )


def project_body(a1_ref, dy_ref, w_ref, vec_ref, c_ref, a_ref, b_ref, q_ref, k_ref, v_ref, do_ref):
    a1, tables = a1_ref[...], (c_ref[...], a_ref[...], b_ref[...])
    q_ref[...] = rotate(mm(a1, w_ref[0], NN) + vec_ref[4:5, :], *tables).astype(bf16)
    k_ref[...] = rotate(mm(a1, w_ref[1], NN) + vec_ref[5:6, :], *tables).astype(bf16)
    v_ref[...] = (mm(a1, w_ref[2], NN) + vec_ref[6:7, :]).astype(bf16)
    do_ref[...] = mm(dy_ref[...], w_ref[3], NT).astype(bf16)


def project(a1, dy, weights, vecs, tables, after=(), step=256):
    count, width = a1.shape
    token = pl.BlockSpec((step, width), lambda i: (i, 0))
    table = pl.BlockSpec((step, LANES), lambda i: (i, 0))
    return call(
        project_body,
        8 * count * width * width,
        12 * count * width + 8 * width * width,
        grid=(count // step,),
        in_specs=[
            token,
            token,
            pl.BlockSpec((4, width, width), lambda i: (0, 0, 0)),
            pl.BlockSpec(vecs.shape, lambda i: (0, 0)),
            table,
            table,
            table,
        ],
        out_specs=[token] * 4,
        out_shape=[jax.ShapeDtypeStruct((count, width), bf16)] * 4,
    )(a1, dy, weights, vecs, *tables)


def attend_body(
    col_ref, row_ref, q_ref, k_ref, v_ref, do_ref, c_ref, a_ref, b_ref,
    o_ref, g_ref, sum_ref, mask_ref, dk_acc, dv_acc, *, block,
):
    length = q_ref.shape[0]
    steps = length // block

    def reach(i):
        return max(0, (i * block - (LONGEST - 1)) // block * block), (i + 1) * block

    @pl.when(pl.program_id(1) == 0)
    def _():
        for i in range(steps):
            lo, hi = reach(i)
            key = lax.broadcasted_iota(jnp.int32, (hi - lo, block), 0) + lo
            query = lax.broadcasted_iota(jnp.int32, (hi - lo, block), 1) + i * block
            same = col_ref[lo:hi, :] == row_ref[0, :, i * block : hi]
            mask = jnp.where(same & (key <= query), 0.0, -jnp.inf)
            mask_ref[i, 0 : hi - lo, 0:block] = mask
            mask_ref[i, 0 : hi - lo, block:] = mask

    low = lax.broadcasted_iota(jnp.int32, (1, LANES), 1) < 64
    eighth = jnp.asarray(0.125, bf16)
    zero = jnp.zeros((), bf16)
    keys, values, grads = k_ref[...], v_ref[...], do_ref[...]
    queries = q_ref[...] * eighth
    keys_t, values_t = (keys * eighth).T, values.T

    def both(part):
        return jnp.concatenate([jnp.where(low, part, zero), jnp.where(low, zero, part)], axis=0)

    def unstack(part):
        return jnp.concatenate([part[0:64, 0:block], part[64:, block:]], axis=0).T

    dk_acc[...] = jnp.zeros_like(dk_acc)
    dv_acc[...] = jnp.zeros_like(dv_acc)
    q_sum = jnp.zeros((8, LANES), f32)
    for i in range(steps):
        lo, hi = reach(i)
        here = slice(i * block, hi)
        q2, do2 = both(queries[here]), both(grads[here])
        scores = mm(keys[lo:hi], q2, NT) + mask_ref[i, 0 : hi - lo, :]
        raised = jnp.exp(scores - jnp.max(scores, axis=0, keepdims=True))
        soft = raised * (1.0 / jnp.sum(raised, axis=0, keepdims=True))
        d_soft = mm(values[lo:hi], do2, NT)
        inner = jnp.sum(soft * d_soft, axis=0, keepdims=True)
        soft_low = soft.astype(bf16)
        d_scores = (soft * (d_soft - inner)).astype(bf16)
        o_ref[here, :] = unstack(mm(values_t[:, lo:hi], soft_low, NN)).astype(bf16)
        dq = rotate_back(
            unstack(mm(keys_t[:, lo:hi], d_scores, NN)), c_ref[here, :], a_ref[here, :], b_ref[here, :]
        ).astype(bf16)
        g_ref[0, here, :] = dq
        q_sum = q_sum + sub_sum(dq.astype(f32))
        dk_acc[lo:hi, :] += mm(d_scores, q2, NN)
        dv_acc[lo:hi, :] += mm(soft_low, do2, NN)
    dk = rotate_back(dk_acc[...], c_ref[...], a_ref[...], b_ref[...]).astype(bf16)
    dv = dv_acc[...].astype(bf16)
    g_ref[1] = dk
    g_ref[2] = dv
    sum_ref[0] = q_sum
    sum_ref[1] = sub_sum(dk.astype(f32))
    sum_ref[2] = sub_sum(dv.astype(f32))


def attend(segment_ids, q, k, v, do, tables, block=256):
    rows, length = segment_ids.shape
    count, width = q.shape
    block = min(block, length)
    token = pl.BlockSpec((length, LANES), lambda r, h: (r, h))
    table = pl.BlockSpec((length, LANES), lambda r, h: (r, 0))
    return call(
        functools.partial(attend_body, block=block),
        24 * count * length * width,
        24 * count * width,
        grid=(rows, width // LANES),
        in_specs=[
            pl.BlockSpec((length, 1), lambda r, h: (r, 0)),
            pl.BlockSpec((1, 1, length), lambda r, h: (r, 0, 0)),
            token,
            token,
            token,
            token,
            table,
            table,
            table,
        ],
        out_specs=[
            token,
            pl.BlockSpec((3, length, LANES), lambda r, h: (0, r, h)),
            pl.BlockSpec((3, 8, LANES), lambda r, h: (0, r, h)),
        ],
        out_shape=[
            jax.ShapeDtypeStruct((count, width), bf16),
            jax.ShapeDtypeStruct((3, count, width), bf16),
            jax.ShapeDtypeStruct((3, 8 * rows, width), f32),
        ],
        scratch_shapes=[
            pltpu.VMEM((length // block, length, 2 * block), f32),
            pltpu.VMEM((length, LANES), f32),
            pltpu.VMEM((length, LANES), f32),
        ],
    )(
        segment_ids.reshape(-1, 1),
        segment_ids.reshape(rows, 1, length),
        q,
        k,
        v,
        do,
        *tables,
    )


def put_grad(grad, core, outs, index, shard):
    if len(outs) == 1:
        outs[0][index] = grad
        return
    width = grad.shape[1]
    parts = grad.reshape(-1, 2, shard, width)
    even = parts[:, 0].reshape(-1, width).astype(bf16)
    odd = parts[:, 1].reshape(-1, width).astype(bf16)
    keep_ref, send_ref = outs

    @pl.when(core == 0)
    def _():
        keep_ref[index] = even
        send_ref[index] = odd

    @pl.when(core != 0)
    def _():
        keep_ref[index] = odd
        send_ref[index] = even


def grad_shapes(blocks, width, paired):
    if paired:
        return [jax.ShapeDtypeStruct((blocks, width // 2, width), bf16)] * 2
    return [jax.ShapeDtypeStruct((blocks, width, width), f32)]


def attn_grad_body(place_ref, a1_ref, o_ref, g_ref, dy_ref, *outs, shard):
    b = pl.program_id(0)

    @pl.when(b < 3)
    def _():
        put_grad(mm(a1_ref[...], g_ref[0], TN), place_ref[3], outs, 0, shard)

    @pl.when(b == 3)
    def _():
        put_grad(mm(o_ref[...], dy_ref[...], TN), place_ref[3], outs, 0, shard)


def attn_grads(place, a1, o, g, dy, shard, paired):
    count, width = a1.shape
    whole = pl.BlockSpec((count, width), lambda b, s: (0, 0))
    shapes = grad_shapes(4, width, paired)
    return call(
        functools.partial(attn_grad_body, shard=shard),
        8 * count * width * width,
        12 * count * width + 8 * width * width,
        grid_spec=pltpu.PrefetchScalarGridSpec(
            num_scalar_prefetch=1,
            grid=(4,),
            in_specs=[
                whole,
                whole,
                pl.BlockSpec((1, count, width), lambda b, s: (jnp.minimum(b, 2), 0, 0)),
                whole,
            ],
            out_specs=[pl.BlockSpec((1, *s.shape[1:]), lambda b, s: (b, 0, 0)) for s in shapes],
        ),
        out_shape=shapes,
    )(place, a1, o, g, dy)


def gelu_parts(u):
    raised = jnp.exp(-0.5 * (u * u))
    t = 1.0 / (1.0 + (0.3275911 * math.sqrt(0.5)) * jnp.abs(u))
    poly = 1.061405429 * t - 1.453152027
    poly = poly * t + 1.421413741
    poly = poly * t - 0.284496736
    poly = (poly * t + 0.254829592) * t
    tail = 0.5 * poly * raised
    return jnp.where(u < 0, tail, 1.0 - tail), raised * (1.0 / math.sqrt(2.0 * math.pi))


def mlp_body(place_ref, a2_ref, dy_ref, wu_ref, wd_ref, bu_ref, e_ref, du_ref, sum_ref, *rest, steps, shard):
    *outs, up_acc, down_acc, sum_acc = rest
    i = pl.program_id(0)
    a2, dy = a2_ref[...], dy_ref[...]
    u = mm(a2, wu_ref[0], NN) + bu_ref[0]
    de = mm(dy, wd_ref[0], NT)
    dist, density = gelu_parts(u)
    e = (u * dist).astype(bf16)
    du = (de * (dist + u * density)).astype(bf16)
    e_ref[...] = e
    du_ref[...] = du
    up, down = mm(a2, du, TN), mm(e, dy, TN)
    part = sub_sum(du.astype(f32))

    @pl.when(i == 0)
    def _():
        up_acc[...] = up
        down_acc[...] = down
        sum_acc[...] = part

    @pl.when((i > 0) & (i < steps - 1))
    def _():
        up_acc[...] += up
        down_acc[...] += down
        sum_acc[...] += part

    @pl.when(i == steps - 1)
    def _():
        put_grad(up_acc[...] + up, place_ref[3], outs, 0, shard)
        put_grad(down_acc[...] + down, place_ref[3], outs, 1, shard)
        sum_ref[...] = sum_acc[...] + part


def mlp(j, place, a2, dy, weights, vecs, shard, paired, riders=(), after=(), step=512):
    count, width = a2.shape
    splits = weights.shape[0] // 2
    steps = count // step
    token = pl.BlockSpec((step, width), lambda i, s: (i, 0))
    shapes = grad_shapes(2, width, paired)
    return hosted(
        functools.partial(mlp_body, steps=steps, shard=shard),
        steps,
        place,
        [a2, dy, weights, weights, vecs[:, None, :]],
        [
            token,
            token,
            pl.BlockSpec((1, width, width), lambda i, s: (j, 0, 0)),
            pl.BlockSpec((1, width, width), lambda i, s: (splits + j, 0, 0)),
            pl.BlockSpec((1, 1, width), lambda i, s: (8 + j, 0, 0)),
        ],
        [
            jax.ShapeDtypeStruct((count, width), bf16),
            jax.ShapeDtypeStruct((count, width), bf16),
            jax.ShapeDtypeStruct((8, width), f32),
            *shapes,
        ],
        [token, token, pl.BlockSpec((8, width), lambda i, s: (0, 0))]
        + [pl.BlockSpec(s.shape, lambda i, s: (0, 0, 0)) for s in shapes],
        [pltpu.VMEM((width, width), f32), pltpu.VMEM((width, width), f32), pltpu.VMEM((8, width), f32)],
        riders,
        after,
        8 * count * width * width,
        8 * count * width + 8 * width * width,
    )


def norm_back(grad, unit, scale, gain):
    grad = grad * gain
    first = jnp.mean(grad, axis=1, keepdims=True)
    second = jnp.mean(grad * unit, axis=1, keepdims=True)
    return scale * (grad - first - unit * second)


def output_body(place_ref, x_ref, o_ref, *refs, splits):
    e_refs, (wo_ref, wm_ref, vec_ref, out_ref) = refs[:splits], refs[splits:]
    acc = mm(o_ref[...], wo_ref[0], NN)
    for j in range(splits):
        acc = acc + mm(e_refs[j][...], wm_ref[j], NN)
    bias = vec_ref[7:8, :] + vec_ref[8 + splits : 9 + splits, :]
    out_ref[...] = (x_ref[...].astype(f32) + acc + bias).astype(bf16)


def resident(blocks, width, at):
    return pl.BlockSpec((blocks, width, width), lambda i, s: (at, 0, 0), pipeline_mode=pl.Buffered(1))


def output(place, x, o, es, wa, wm, vecs, riders=(), after=(), step=256):
    count, width = x.shape
    splits = len(es)
    token = pl.BlockSpec((step, width), lambda i, s: (i, 0))
    return hosted(
        functools.partial(output_body, splits=splits),
        count // step,
        place,
        [x, o, *es, wa, wm, vecs],
        [token] * (2 + splits)
        + [resident(1, width, 3), resident(splits, width, 1), pl.BlockSpec(vecs.shape, lambda i, s: (0, 0))],
        [jax.ShapeDtypeStruct((count, width), bf16)],
        [token],
        (),
        riders,
        after,
        10 * count * width * width,
        14 * count * width + 10 * width * width,
    )


def normed(x):
    centred = x - jnp.mean(x, axis=1, keepdims=True)
    scale = lax.rsqrt(jnp.mean(centred * centred, axis=1, keepdims=True) + norm_epsilon)
    return centred * scale, scale


def add_sums(sum_ref, sums):
    sums = [sub_sum(t) for t in sums]

    @pl.when(pl.program_id(0) == 0)
    def _():
        for n, s in enumerate(sums):
            sum_ref[n] = s

    @pl.when(pl.program_id(0) > 0)
    def _():
        for n, s in enumerate(sums):
            sum_ref[n] += s


def grad_two_body(place_ref, x_ref, dy_ref, *refs, splits):
    du_refs, (wm_ref, vec_ref, part_ref, sum_ref) = refs[:splits], refs[splits:]
    dy = dy_ref[...].astype(f32)
    grad = mm(du_refs[0][...], wm_ref[0], NT)
    for j in range(1, splits):
        grad = grad + mm(du_refs[j][...], wm_ref[j], NT)
    unit, scale = normed(x_ref[...].astype(f32))
    part_ref[...] = dy + norm_back(grad, unit, scale, vec_ref[2:3, :])
    add_sums(sum_ref, (grad * unit, grad, dy))


def grad_two(place, x, dy, dus, wm, vecs, riders=(), after=(), step=256):
    count, width = x.shape
    splits = len(dus)
    token = pl.BlockSpec((step, width), lambda i, s: (i, 0))
    return hosted(
        functools.partial(grad_two_body, splits=splits),
        count // step,
        place,
        [x, dy, *dus, wm, vecs],
        [token] * (2 + splits) + [resident(splits, width, 0), pl.BlockSpec(vecs.shape, lambda i, s: (0, 0))],
        [jax.ShapeDtypeStruct((count, width), f32), jax.ShapeDtypeStruct((3, 8, width), f32)],
        [token, pl.BlockSpec((3, 8, width), lambda i, s: (0, 0, 0))],
        (),
        riders,
        after,
        8 * count * width * width,
        16 * count * width + 8 * width * width,
    )


def grad_one_body(place_ref, x_ref, part_ref, g_ref, wa_ref, vec_ref, grad_ref, sum_ref):
    grad = mm(g_ref[0], wa_ref[0], NT) + mm(g_ref[1], wa_ref[1], NT) + mm(g_ref[2], wa_ref[2], NT)
    unit, scale = normed(x_ref[...].astype(f32))
    grad_ref[...] = (part_ref[...] + norm_back(grad, unit, scale, vec_ref[0:1, :])).astype(bf16)
    add_sums(sum_ref, (grad * unit, grad))


def grad_one(place, x, part, g, wa, vecs, riders=(), after=(), step=256):
    count, width = x.shape
    token = pl.BlockSpec((step, width), lambda i, s: (i, 0))
    return hosted(
        grad_one_body,
        count // step,
        place,
        [x, part, g, wa, vecs],
        [
            token,
            token,
            pl.BlockSpec((3, step, width), lambda i, s: (0, i, 0)),
            resident(3, width, 0),
            pl.BlockSpec(vecs.shape, lambda i, s: (0, 0)),
        ],
        [jax.ShapeDtypeStruct((count, width), bf16), jax.ShapeDtypeStruct((2, 8, width), f32)],
        [token, pl.BlockSpec((2, 8, width), lambda i, s: (0, 0, 0))],
        (),
        riders,
        after,
        6 * count * width * width,
        14 * count * width + 6 * width * width,
    )


def grid_places():
    wide, narrow = lax.axis_index("wide"), lax.axis_index("narrow")
    return wide // 2, wide % 2, narrow // 2, narrow % 2


def to_place(move):
    pairs = []
    for z in range(4):
        for y in range(2):
            for x in range(2):
                for c in range(2):
                    a, b, d, e = move(z, y, x, c)
                    pairs.append((((z * 2 + y) * 2 + x) * 2 + c, ((a * 2 + b) * 2 + d) * 2 + e))
    return pairs


def over_c(value):
    return lax.ppermute(value, AXES, to_place(lambda z, y, x, c: (z, y, x, 1 - c)))


def over_x(value):
    return lax.ppermute(value, AXES, to_place(lambda z, y, x, c: (z, y, 1 - x, c)))


def over_y(value):
    return lax.ppermute(value, AXES, to_place(lambda z, y, x, c: (z, 1 - y, x, c)))


def over_z(value, by):
    return lax.ppermute(value, AXES, to_place(lambda z, y, x, c: ((z + by) % 4, y, x, c)))


def gather_order_body(place_ref, *refs):
    z, y, x, c = place_ref[0], place_ref[1], place_ref[2], place_ref[3]
    out_ref = refs[-1]
    blocks = out_ref.shape[0]
    near = lax.rem(z - pl.program_id(0) + 4, 4) < 2
    for rc in range(2):
        own, by_x, by_y, lower, upper = refs[rc * 5 : rc * 5 + 5]
        at = (y * 2 + x) * 2 + (c ^ rc)
        for n in range(blocks):
            out_ref[n, at] = own[0, n]
            out_ref[n, at ^ 2] = by_x[0, n]
            out_ref[n, at ^ 4] = by_y[0, n]

        @pl.when(near)
        def _(lower=lower, at=at):
            for n in range(blocks):
                out_ref[n, at ^ 6] = lower[0, n]

        @pl.when(jnp.logical_not(near))
        def _(upper=upper, at=at):
            for n in range(blocks):
                out_ref[n, at ^ 6] = upper[0, n]


def gather_staged(place, shards, after=()):
    blocks, shard, width = shards.shape
    own = jnp.stack([shards] + [over_z(shards, s) for s in (1, 2, 3)])
    by_x, by_y = over_x(own), over_y(own)
    lower, upper = over_y(by_x[:2]), over_x(by_y[2:])
    here = [own, by_x, by_y, lower, upper]
    pieces = here + [over_c(v) for v in here]

    def piece(first, count):
        def index(t, s):
            apart = lax.rem(s[0] - t + 4, 4)
            return (jnp.clip(apart - first, 0, count - 1), 0, 0, 0)

        return pl.BlockSpec((1, blocks, shard, width), index)

    weights = call(
        gather_order_body,
        0,
        64 * blocks * shard * width * 2,
        after=after,
        grid_spec=pltpu.PrefetchScalarGridSpec(
            num_scalar_prefetch=1,
            grid=(4,),
            in_specs=([piece(0, 4)] * 3 + [piece(0, 2), piece(2, 2)]) * 2,
            out_specs=pl.BlockSpec((blocks, 8, shard, width), lambda t, s: (0, t, 0, 0)),
        ),
        out_shape=jax.ShapeDtypeStruct((blocks, 32, shard, width), bf16),
    )(place, *pieces)
    return weights.reshape(blocks, width, width)


class CoreSum:
    def __init__(self, keep, got, shard):
        blocks, rows, width = keep.shape
        self.shape = (blocks, rows // (2 * shard), 2, shard, width)
        self.ins = [keep.reshape(self.shape), got.reshape(self.shape)]
        part = (blocks, self.shape[1], shard, width)
        self.outs = [jax.ShapeDtypeStruct(part, f32), jax.ShapeDtypeStruct(part, bf16)]

    def in_specs(self, steps):
        b, w, two, s, d = self.shape
        return [pl.BlockSpec((b, w // steps, two, s, d), lambda i, p: (0, i, 0, 0, 0))] * 2

    def out_specs(self, steps):
        b, w, _, s, d = self.shape
        return [pl.BlockSpec((b, w // steps, s, d), lambda i, p: (0, i, 0, 0))] * 2

    def body(self, place_ref, steps, ins, outs):
        x = place_ref[2]
        for ref, at in zip(outs, (x, 1 - x)):
            ref[...] = (ins[0][:, :, at].astype(f32) + ins[1][:, :, at].astype(f32)).astype(ref.dtype)


class AcrossSum:
    def __init__(self, own, got):
        blocks, wide, shard, width = own.shape
        self.shape = (blocks, wide // 2, 2, shard, width)
        self.ins = [own.reshape(self.shape), got.reshape(self.shape)]
        part = (blocks, wide // 2, shard, width)
        self.outs = [jax.ShapeDtypeStruct(part, f32), jax.ShapeDtypeStruct(part, bf16)]

    in_specs = CoreSum.in_specs
    out_specs = CoreSum.out_specs

    def body(self, place_ref, steps, ins, outs):
        y = place_ref[1]
        for ref, at in zip(outs, (y, 1 - y)):
            ref[...] = (ins[0][:, :, at] + ins[1][:, :, at].astype(f32)).astype(ref.dtype)


class LineSum:
    def __init__(self, *chunks):
        self.ins = [v for chunk in chunks for v in chunk]
        self.wide, shard, width = chunks[0][0].shape[1:]
        self.part = (sum(own.shape[0] for own, _ in chunks), shard, width)
        self.outs = [jax.ShapeDtypeStruct(self.part, f32)] + [jax.ShapeDtypeStruct(self.part, bf16)] * 3

    def in_specs(self, steps):
        return [
            pl.BlockSpec((v.shape[0], self.wide // steps, *v.shape[2:]), lambda i, p: (0, i, 0, 0))
            for v in self.ins
        ]

    def out_specs(self, steps):
        return [pl.BlockSpec(self.part, lambda i, p: (0, 0, 0))] * 4

    def body(self, place_ref, steps, ins, outs):
        each = self.wide // steps
        for n in range(each):
            apart = lax.rem(pl.program_id(0) * each + n - place_ref[0] + 4, 4)
            first = 0
            for own, got in zip(ins[::2], ins[1::2]):
                value = own[:, n] + got[:, n].astype(f32)
                for s, ref in enumerate(outs):

                    @pl.when(apart == s)
                    def _(ref=ref, value=value, first=first):
                        ref[first : first + value.shape[0]] = value.astype(ref.dtype)

                first += own.shape[0]


def pack_body(slot_ref, *refs, orders, per):
    terms, (shard_ref, out_ref, square_ref) = refs[: len(orders) * per], refs[len(orders) * per :]
    total = jnp.zeros(square_ref.shape, f32)
    for n, order in enumerate(orders):
        for m, b in enumerate(order):
            value = terms[n * per][m]
            for t in range(1, per):
                value = value + terms[n * per + t][m].astype(f32)
            shard_ref[b] = value
            total = total + value * value
    square_ref[...] = total

    def one(j, carry):
        b = slot_ref[j]

        @pl.when(b >= 0)
        def _():
            out_ref[j] = shard_ref[jnp.maximum(b, 0)].astype(bf16)

        @pl.when(b < 0)
        def _():
            out_ref[j] = jnp.zeros(out_ref.shape[1:], bf16)

        return carry

    lax.fori_loop(0, out_ref.shape[0], one, 0)


def pack(slots, terms, orders, after=()):
    per = len(terms[0])
    _, shard, width = terms[0][0].shape
    terms = [v for t in terms for v in t]
    vmem = pl.BlockSpec(memory_space=pltpu.VMEM)
    return call(
        functools.partial(pack_body, orders=orders, per=per),
        0,
        sum(v.size * v.dtype.itemsize for v in terms) * 2,
        after=after,
        in_specs=[pl.BlockSpec(memory_space=pltpu.SMEM)] + [vmem] * len(terms),
        out_specs=[vmem] * 3,
        out_shape=[
            jax.ShapeDtypeStruct((sum(map(len, orders)), shard, width), f32),
            jax.ShapeDtypeStruct((slots.shape[0], shard, width), bf16),
            jax.ShapeDtypeStruct((shard, width), f32),
        ],
    )(slots, *terms)


def precondition_body(scale_ref, s_ref, l_ref, r_ref, p_ref, s_low, r_low):
    @pl.when(pl.program_id(0) == 0)
    def _():
        s_low[...] = (s_ref[...].astype(f32) * scale_ref[0]).astype(bf16)
        r_low[...] = r_ref[...].astype(bf16)

    left = mm(l_ref[...].astype(bf16), s_low[...], NN)
    p_ref[...] = (scale_ref[1] * mm(left.astype(bf16), r_low[...], NN)).astype(bf16)


def precondition(scales, block, left, right, step=256):
    width = block.shape[0]
    whole = pl.BlockSpec((width, width), lambda i: (0, 0))
    rows = pl.BlockSpec((step, width), lambda i: (i, 0))
    return call(
        precondition_body,
        4 * width**3,
        12 * width**2,
        grid=(width // step,),
        in_specs=[pl.BlockSpec(memory_space=pltpu.SMEM), whole, rows, whole],
        out_specs=rows,
        out_shape=jax.ShapeDtypeStruct((width, width), bf16),
        scratch_shapes=[pltpu.VMEM((width, width), bf16), pltpu.VMEM((width, width), bf16)],
    )(scales, block, left, right)


def statistics_body(has_ref, scale_ref, s_ref, l_ref, r_ref, nl_ref, nr_ref, s_low, *, step):
    i = pl.program_id(0)
    width = s_ref.shape[0]

    @pl.when(i == 0)
    def _():
        s_low[...] = (s_ref[...].astype(f32) * scale_ref[0]).astype(bf16)

    factor = (1.0 - decay_beta) * (scale_ref[1] * scale_ref[1] / width)
    at = pl.multiple_of(i * step, step)

    @pl.when(has_ref[0] != 0)
    def _():
        nl_ref[...] = decay_beta * l_ref[...] + factor * mm(s_low[pl.ds(at, step), :], s_low[...], NT)
        nr_ref[...] = decay_beta * r_ref[...] + factor * mm(s_low[:, pl.ds(at, step)], s_low[...], TN)

    @pl.when(has_ref[0] == 0)
    def _():
        nl_ref[...] = l_ref[...]
        nr_ref[...] = r_ref[...]


def statistics(has, scales, block, left, right, step=256):
    width = block.shape[0]
    whole = pl.BlockSpec((width, width), lambda i: (0, 0))
    rows = pl.BlockSpec((step, width), lambda i: (i, 0))
    smem = pl.BlockSpec(memory_space=pltpu.SMEM)
    return call(
        functools.partial(statistics_body, step=step),
        4 * width**3,
        18 * width**2,
        grid=(width // step,),
        in_specs=[smem, smem, whole, rows, rows],
        out_specs=[rows, rows],
        out_shape=[jax.ShapeDtypeStruct((width, width), f32)] * 2,
        scratch_shapes=[pltpu.VMEM((width, width), bf16)],
    )(has, scales, block, left, right)


def update_body(owner_ref, factor_ref, p_ref, shard_ref, block_ref, clip_ref, new_ref, copy_ref):
    for b in range(shard_ref.shape[0]):
        clip_ref[b] = shard_ref[b] * factor_ref[0]
        value = block_ref[b] - matrix_rate * p_ref[owner_ref[b]].astype(f32)
        new_ref[b] = value
        copy_ref[b] = value.astype(bf16)


def update(owners, factor, returned, shards, blocks):
    smem, vmem = pl.BlockSpec(memory_space=pltpu.SMEM), pl.BlockSpec(memory_space=pltpu.VMEM)
    return call(
        update_body,
        0,
        returned.size * 2 + shards.size * 18,
        in_specs=[smem, smem, vmem, vmem, vmem],
        out_specs=[vmem] * 3,
        out_shape=[
            jax.ShapeDtypeStruct(shards.shape, f32),
            jax.ShapeDtypeStruct(shards.shape, f32),
            jax.ShapeDtypeStruct(shards.shape, bf16),
        ],
    )(owners, factor, returned, shards, blocks)


def layer_inputs(tokens, vecs):
    values = tokens.astype(f32)
    centred = values - jnp.mean(values, axis=-1, keepdims=True)
    spread = jnp.mean(centred * centred, axis=-1, keepdims=True)
    unit = centred * lax.rsqrt(spread + norm_epsilon)
    one = (unit * vecs[0] + vecs[1]).astype(bf16)
    two = (unit * vecs[2] + vecs[3]).astype(bf16)
    return one, two


def to_all(value):
    return lax.all_to_all(value, AXES, split_axis=0, concat_axis=0, tiled=True)


def per_device(
    tokens,
    segment_ids,
    cotangent,
    blocks,
    vectors,
    stat_left,
    stat_right,
    root_left,
    root_right,
    vec_stat,
    owners,
    *,
    paired,
):
    rows_here, seq_len, width = tokens.shape
    count = rows_here * seq_len
    splits = FF // width
    slot_count = lax.axis_size(AXES)
    my_index = lax.axis_index(AXES)
    shard = width // slot_count
    vec_rows = vectors.shape[0]

    low_blocks, low_vectors = blocks.astype(bf16), vectors.astype(bf16)
    everyone = jnp.broadcast_to(low_vectors.reshape(1, -1), (slot_count, vec_rows * shard))
    vecs = to_all(everyone).reshape(slot_count, vec_rows, shard)
    vecs = vecs.transpose(1, 0, 2).reshape(vec_rows, width).astype(f32)
    mlp_weights = lax.all_gather(low_blocks[4:], AXES, axis=1, tiled=True)

    flat_tokens = tokens.reshape(count, width)
    dy = cotangent.reshape(count, width)
    tables = rotary_tables(segment_ids)
    a1, a2 = layer_inputs(flat_tokens, vecs)
    place = jnp.stack(grid_places()).astype(jnp.int32)
    if paired:
        attn_weights = gather_staged(place, low_blocks[:4], after=(*tables, a1, a2))
    else:
        attn_weights = lax.all_gather(low_blocks[:4], AXES, axis=1, tiled=True)

    q, k, v, do = project(a1, dy, attn_weights, vecs, tables)
    o, g, attn_sums = attend(segment_ids, q, k, v, do, tables)
    chunks = [list(range(4))] + [[4 + j, 4 + splits + j] for j in range(splits)]
    grads = [attn_grads(place, a1, o, g, dy, shard, paired)]
    es, dus, up_sums = [], [], []
    sent = [None] * len(chunks)
    orders, terms = [], []

    def ride(stages):
        if not paired:
            return []
        made = []
        for which, stage in stages:
            if stage == 0:
                made.append(CoreSum(grads[which[0]][0], sent[which[0]], shard))
            elif stage == 1:
                made.append(AcrossSum(*sent[which[0]]))
            else:
                made.append(LineSum(*[sent[n] for n in which]))
        return made

    def send(stages, ridden):
        for (which, stage), (own, *rest) in zip(stages, ridden):
            if stage < 2:
                sent[which[0]] = (own, (over_x, over_y)[stage](rest[0]))
            else:
                orders.append([b for n in which for b in chunks[n]])
                terms.append([own] + [over_z(v, s) for s, v in zip((1, 2, 3), rest)])

    def in_hidden(j):
        done = [([0], 2)] if j == 3 else []
        return done + [([n], j - 1 - n) for n in range(j) if j - 1 - n < 2]

    if paired:
        sent[0] = over_c(grads[0][1])
    after = (grads[0][0],)
    for j in range(splits):
        stages = in_hidden(j)
        (e, du, up_sum, *grad), ridden = mlp(
            j, place, a2, dy, mlp_weights, vecs, shard, paired, riders=ride(stages), after=after
        )
        after = (e,)
        es.append(e)
        dus.append(du)
        up_sums.append(up_sum)
        grads.append(grad)
        if paired:
            sent[j + 1] = over_c(grad[1])
            send(stages, ridden)
    stages = [([2], 1), ([3], 0), ([4], 0)]
    (out,), ridden = output(
        place, flat_tokens, o, es, attn_weights, mlp_weights, vecs, riders=ride(stages), after=after
    )
    send(stages, ridden)
    stages = [([1, 2], 2), ([3], 1), ([4], 1)]
    (part, two_sums), ridden = grad_two(
        place, flat_tokens, dy, dus, mlp_weights, vecs, riders=ride(stages), after=(out,)
    )
    send(stages, ridden)
    stages = [([3, 4], 2)]
    (grad_in, one_sums), ridden = grad_one(
        place, flat_tokens, part, g, attn_weights, vecs, riders=ride(stages)
    )
    send(stages, ridden)
    if not paired:
        orders = chunks
        terms = [[lax.psum_scatter(grad[0], AXES, scatter_dimension=1, tiled=True)] for grad in grads]

    one_sums, two_sums = jnp.sum(one_sums, axis=1), jnp.sum(two_sums, axis=1)
    qkv_sums = jnp.sum(attn_sums, axis=1)
    up_sums = jnp.sum(jnp.stack(up_sums), axis=1)
    bias_sum = two_sums[2:]
    grad_vectors = jnp.concatenate(
        [one_sums, two_sums[:2], qkv_sums, bias_sum, up_sums, bias_sum], axis=0
    )
    by_slot = grad_vectors.reshape(vec_rows, slot_count, shard).transpose(1, 0, 2)
    shard_vectors = jnp.sum(to_all(by_slot.reshape(slot_count, -1)), axis=0).reshape(vec_rows, shard)

    slot_ids = jnp.arange(slot_count, dtype=jnp.int32)
    match = owners[None, :] == slot_ids[:, None]
    slots = jnp.sum(jnp.where(match, jnp.arange(1, owners.shape[0] + 1, dtype=jnp.int32)[None], 0), axis=1) - 1
    has_block = jnp.any(owners == my_index)
    shards, outgoing, squares = pack(slots, terms, orders, after=(grad_in,))
    local = jnp.sum(squares) + jnp.sum(shard_vectors * shard_vectors)
    everywhere = to_all(jnp.broadcast_to(local, (slot_count, LANES)))
    grad_norm = jnp.sqrt(jnp.sum(everywhere[:, 0]))
    factor = jnp.minimum(1.0, clip_level / grad_norm)
    root_count = math.sqrt(NPARAM)

    scale = factor * root_count
    power = jnp.exp2(jnp.floor(jnp.log2(jnp.maximum(scale, 1e-30)))).astype(bf16).astype(f32)
    scales = jnp.stack([power, scale / power])
    owned = to_all(outgoing).reshape(width, width)
    precond = precondition(scales, owned, root_left[0], root_right[0])
    returned = to_all(precond.reshape(slot_count, shard, width))
    new_left, new_right = statistics(
        has_block.astype(jnp.int32).reshape(1), scales, owned, stat_left[0], stat_right[0]
    )
    clipped_blocks, new_blocks, blocks_copy = update(owners, factor.reshape(1), returned, shards, blocks)
    clipped_vectors = shard_vectors * factor
    scaled_vectors = clipped_vectors * root_count
    new_vec_stat = decay_beta * vec_stat + (1.0 - decay_beta) * (scaled_vectors * scaled_vectors)
    new_vectors = vectors - vector_rate * scaled_vectors * lax.rsqrt(new_vec_stat)
    return (
        out.reshape(tokens.shape),
        grad_in.reshape(tokens.shape),
        clipped_blocks,
        clipped_vectors,
        grad_norm,
        new_left[None],
        new_right[None],
        new_vec_stat,
        new_blocks,
        new_vectors,
        blocks_copy,
        new_vectors.astype(bf16),
    )


def solution(mesh):
    rows = P(AXES, None, None)
    split_rows = P(None, AXES, None)
    split_columns = P(None, AXES)
    paired = dict(mesh.shape) == {"wide": 8, "narrow": 4}
    return jax.shard_map(
        functools.partial(per_device, paired=paired),
        mesh=mesh,
        in_specs=(
            rows, P(AXES, None), rows, split_rows, split_columns,
            rows, rows, rows, rows, split_columns, P(),
        ),
        out_specs=(
            rows, rows, split_rows, split_columns, P(), rows, rows,
            split_columns, split_rows, split_columns, split_rows, split_columns,
        ),
        check_vma=False,
    )
```

```python
import functools
import math

import jax
import jax.numpy as jnp
from jax import lax
from jax.experimental import pallas as pl
from jax.experimental.pallas import tpu as pltpu
from jax.sharding import PartitionSpec as P

H = 12
FF = 3072
ROT = 16
NPARAM = 7087872
LONGEST = 256

clip_level = 1.0
matrix_rate = 0.03
vector_rate = 0.2
decay_beta = 0.5
norm_epsilon = 1e-05

f32 = jnp.float32
bf16 = jnp.bfloat16
AXES = ("wide", "narrow")
LANES = 128
MIB = 2**20

NN = (((1,), (0,)), ((), ()))
NT = (((1,), (1,)), ((), ()))
TN = (((0,), (0,)), ((), ()))


def mm(left, right, dims):
    return lax.dot_general(left, right, dims, preferred_element_type=f32)


def call(body, flops, moved, vmem=60, after=(), **rest):
    spec = rest.pop("grid_spec", None)
    grid = spec.grid if spec is not None else rest.get("grid", ())
    later = len(after)
    if later:
        held = [pl.BlockSpec(memory_space=pl.ANY)] * later
        if spec is not None:
            first = spec.num_scalar_prefetch + len(spec.in_specs)
            spec = pltpu.PrefetchScalarGridSpec(
                num_scalar_prefetch=spec.num_scalar_prefetch,
                grid=spec.grid,
                in_specs=list(spec.in_specs) + held,
                out_specs=spec.out_specs,
                scratch_shapes=spec.scratch_shapes,
            )
        else:
            first = len(rest["in_specs"])
            rest["in_specs"] = list(rest["in_specs"]) + held
        inner = body

        def body(*refs):
            inner(*refs[:first], *refs[first + later :])

    if spec is not None:
        rest["grid_spec"] = spec
    made = pl.pallas_call(
        body,
        compiler_params=pltpu.CompilerParams(
            vmem_limit_bytes=vmem * MIB,
            dimension_semantics=("arbitrary",) * len(grid),
        ),
        cost_estimate=pl.CostEstimate(
            flops=int(flops), bytes_accessed=int(moved), transcendentals=0
        ),
        **rest,
    )
    return lambda *operands: made(*operands, *after)


def sub_sum(values):
    return jnp.sum(values.reshape(-1, 8, values.shape[-1]), axis=0)


def rotary_tables(segment_ids):
    rows, length = segment_ids.shape
    start = jnp.sum(
        (segment_ids[:, None, :] < segment_ids[:, :, None]).astype(jnp.int32), axis=-1
    )
    offset = (jnp.arange(length, dtype=jnp.int32)[None] - start).astype(f32).reshape(-1, 1)
    half = ROT // 2
    lane = jnp.arange(LANES) % 64
    rates = jnp.power(10000.0, -2.0 * jnp.arange(half, dtype=f32) / ROT)
    angle = offset * jnp.where(lane < ROT, rates[lane % half], 0.0)[None]
    cosine, sine = jnp.cos(angle), jnp.sin(angle)
    first = jnp.where(lane[None] < half, -sine, 0.0)
    second = jnp.where((lane[None] >= half) & (lane[None] < ROT), sine, 0.0)
    return cosine, first, second


def rotate(values, cosine, first, second):
    parts = []
    for at in range(0, values.shape[1], LANES):
        part = values[:, at : at + LANES]
        parts.append(
            part * cosine
            + pltpu.roll(part, LANES - ROT // 2, 1) * first
            + pltpu.roll(part, ROT // 2, 1) * second
        )
    return jnp.concatenate(parts, axis=1)


def rotate_back(values, cosine, first, second):
    return (
        values * cosine
        - pltpu.roll(values, LANES - ROT // 2, 1) * first
        - pltpu.roll(values, ROT // 2, 1) * second
    )


def project_body(a1_ref, dy_ref, w_ref, vec_ref, c_ref, a_ref, b_ref, q_ref, k_ref, v_ref, do_ref):
    a1, tables = a1_ref[...], (c_ref[...], a_ref[...], b_ref[...])
    q_ref[...] = rotate(mm(a1, w_ref[0], NN) + vec_ref[4:5, :], *tables).astype(bf16)
    k_ref[...] = rotate(mm(a1, w_ref[1], NN) + vec_ref[5:6, :], *tables).astype(bf16)
    v_ref[...] = (mm(a1, w_ref[2], NN) + vec_ref[6:7, :]).astype(bf16)
    do_ref[...] = mm(dy_ref[...], w_ref[3], NT).astype(bf16)


def project(a1, dy, weights, vecs, tables, after=(), step=256):
    count, width = a1.shape
    token = pl.BlockSpec((step, width), lambda i: (i, 0))
    table = pl.BlockSpec((step, LANES), lambda i: (i, 0))
    return call(
        project_body,
        8 * count * width * width,
        12 * count * width + 8 * width * width,
        grid=(count // step,),
        in_specs=[
            token,
            token,
            pl.BlockSpec((4, width, width), lambda i: (0, 0, 0)),
            pl.BlockSpec(vecs.shape, lambda i: (0, 0)),
            table,
            table,
            table,
        ],
        out_specs=[token] * 4,
        out_shape=[jax.ShapeDtypeStruct((count, width), bf16)] * 4,
    )(a1, dy, weights, vecs, *tables)


def attend_body(
    col_ref, row_ref, q_ref, k_ref, v_ref, do_ref, c_ref, a_ref, b_ref,
    o_ref, g_ref, sum_ref, mask_ref, dk_acc, dv_acc, *, block,
):
    length = q_ref.shape[0]
    steps = length // block

    def reach(i):
        return max(0, (i * block - (LONGEST - 1)) // block * block), (i + 1) * block

    @pl.when(pl.program_id(1) == 0)
    def _():
        for i in range(steps):
            lo, hi = reach(i)
            key = lax.broadcasted_iota(jnp.int32, (hi - lo, block), 0) + lo
            query = lax.broadcasted_iota(jnp.int32, (hi - lo, block), 1) + i * block
            same = col_ref[lo:hi, :] == row_ref[0, :, i * block : hi]
            mask = jnp.where(same & (key <= query), 0.0, -jnp.inf)
            mask_ref[i, 0 : hi - lo, 0:block] = mask
            mask_ref[i, 0 : hi - lo, block:] = mask

    low = lax.broadcasted_iota(jnp.int32, (1, LANES), 1) < 64
    eighth = jnp.asarray(0.125, bf16)
    zero = jnp.zeros((), bf16)
    keys, values, grads = k_ref[...], v_ref[...], do_ref[...]
    queries = q_ref[...] * eighth
    keys_t, values_t = (keys * eighth).T, values.T

    def both(part):
        return jnp.concatenate([jnp.where(low, part, zero), jnp.where(low, zero, part)], axis=0)

    def unstack(part):
        return jnp.concatenate([part[0:64, 0:block], part[64:, block:]], axis=0).T

    dk_acc[...] = jnp.zeros_like(dk_acc)
    dv_acc[...] = jnp.zeros_like(dv_acc)
    q_sum = jnp.zeros((8, LANES), f32)
    for i in range(steps):
        lo, hi = reach(i)
        here = slice(i * block, hi)
        q2, do2 = both(queries[here]), both(grads[here])
        scores = mm(keys[lo:hi], q2, NT) + mask_ref[i, 0 : hi - lo, :]
        raised = jnp.exp(scores - jnp.max(scores, axis=0, keepdims=True))
        soft = raised * (1.0 / jnp.sum(raised, axis=0, keepdims=True))
        d_soft = mm(values[lo:hi], do2, NT)
        inner = jnp.sum(soft * d_soft, axis=0, keepdims=True)
        soft_low = soft.astype(bf16)
        d_scores = (soft * (d_soft - inner)).astype(bf16)
        o_ref[here, :] = unstack(mm(values_t[:, lo:hi], soft_low, NN)).astype(bf16)
        dq = rotate_back(
            unstack(mm(keys_t[:, lo:hi], d_scores, NN)), c_ref[here, :], a_ref[here, :], b_ref[here, :]
        ).astype(bf16)
        g_ref[0, here, :] = dq
        q_sum = q_sum + sub_sum(dq.astype(f32))
        dk_acc[lo:hi, :] += mm(d_scores, q2, NN)
        dv_acc[lo:hi, :] += mm(soft_low, do2, NN)
    dk = rotate_back(dk_acc[...], c_ref[...], a_ref[...], b_ref[...]).astype(bf16)
    dv = dv_acc[...].astype(bf16)
    g_ref[1] = dk
    g_ref[2] = dv
    sum_ref[0] = q_sum
    sum_ref[1] = sub_sum(dk.astype(f32))
    sum_ref[2] = sub_sum(dv.astype(f32))


def attend(segment_ids, q, k, v, do, tables, block=256):
    rows, length = segment_ids.shape
    count, width = q.shape
    block = min(block, length)
    token = pl.BlockSpec((length, LANES), lambda r, h: (r, h))
    table = pl.BlockSpec((length, LANES), lambda r, h: (r, 0))
    return call(
        functools.partial(attend_body, block=block),
        24 * count * length * width,
        24 * count * width,
        grid=(rows, width // LANES),
        in_specs=[
            pl.BlockSpec((length, 1), lambda r, h: (r, 0)),
            pl.BlockSpec((1, 1, length), lambda r, h: (r, 0, 0)),
            token,
            token,
            token,
            token,
            table,
            table,
            table,
        ],
        out_specs=[
            token,
            pl.BlockSpec((3, length, LANES), lambda r, h: (0, r, h)),
            pl.BlockSpec((3, 8, LANES), lambda r, h: (0, r, h)),
        ],
        out_shape=[
            jax.ShapeDtypeStruct((count, width), bf16),
            jax.ShapeDtypeStruct((3, count, width), bf16),
            jax.ShapeDtypeStruct((3, 8 * rows, width), f32),
        ],
        scratch_shapes=[
            pltpu.VMEM((length // block, length, 2 * block), f32),
            pltpu.VMEM((length, LANES), f32),
            pltpu.VMEM((length, LANES), f32),
        ],
    )(
        segment_ids.reshape(-1, 1),
        segment_ids.reshape(rows, 1, length),
        q,
        k,
        v,
        do,
        *tables,
    )


def half_grads_body(place_ref, *refs, first):
    l1o, l1p, l2o, l2p, r1o, r1p, r2o, r2p, ka_ref, sa_ref, kb_ref, sb_ref, acc = refs
    n = pl.program_id(0)
    y, x = place_ref[1], place_ref[2]
    half = ka_ref.shape[-1]

    @pl.when(n < first)
    def _():
        acc[...] = (mm(l1o[...], r1o[0], TN) + mm(l1p[...], r1p[0], TN)).reshape(acc.shape)

    @pl.when(n >= first)
    def _():
        acc[...] = (mm(l2o[0], r2o[...], TN) + mm(l2p[0], r2p[...], TN)).reshape(acc.shape)

    for ref, at in ((ka_ref, x), (sa_ref, 1 - x)):
        ref[0] = acc[:, :, at, :, :, :half].astype(ref.dtype)
    for ref, at in ((kb_ref, y), (sb_ref, 1 - y)):
        ref[0] = acc[:, at, :, :, :, half:].astype(ref.dtype)


def half_grads(place, left_one, left_two, right_one, right_two, shard, after=()):
    count, width = left_one[0].shape
    first, second = right_one[0].shape[0], left_two[0].shape[0]
    half = width // 2
    blocks = first + second
    one = pl.BlockSpec((count, half), lambda n, s: (0, s[3]))
    two = pl.BlockSpec((1, count, half), lambda n, s: (jnp.maximum(n - first, 0), 0, s[3]))
    part = pl.BlockSpec((1, 2, 2, 2, shard, half), lambda n, s: (n, 0, 0, 0, 0, 0))
    shape = (blocks, 2, 2, 2, shard, half)
    return call(
        functools.partial(half_grads_body, first=first),
        blocks * 2 * count * width * width,
        blocks * 4 * count * width,
        after=after,
        grid_spec=pltpu.PrefetchScalarGridSpec(
            num_scalar_prefetch=1,
            grid=(blocks,),
            in_specs=[one, one, two, two]
            + [pl.BlockSpec((1, count, width), lambda n, s: (jnp.minimum(n, first - 1), 0, 0))] * 2
            + [pl.BlockSpec((count, width), lambda n, s: (0, 0))] * 2,
            out_specs=[part] * 4,
            scratch_shapes=[pltpu.VMEM((2, 2, 2, 2, shard, width), f32)],
        ),
        out_shape=[jax.ShapeDtypeStruct(shape, k) for k in (f32, bf16, f32, bf16)],
    )(place, *left_one, *left_two, *right_one, *right_two)


def full_grads(left_one, left_two, right_one, right_two):
    one = jnp.einsum("td,nte->nde", left_one, right_one, preferred_element_type=f32)
    two = jnp.einsum("ntd,te->nde", left_two, right_two, preferred_element_type=f32)
    return jnp.concatenate([one, two], axis=0)


def gelu_parts(u):
    raised = jnp.exp(-0.5 * (u * u))
    t = 1.0 / (1.0 + (0.3275911 * math.sqrt(0.5)) * jnp.abs(u))
    poly = 1.061405429 * t - 1.453152027
    poly = poly * t + 1.421413741
    poly = poly * t - 0.284496736
    poly = (poly * t + 0.254829592) * t
    tail = 0.5 * poly * raised
    return jnp.where(u < 0, tail, 1.0 - tail), raised * (1.0 / math.sqrt(2.0 * math.pi))


def hidden_body(a2_ref, dy_ref, wu_ref, wd_ref, bu_ref, e_ref, du_ref, sum_ref):
    u = mm(a2_ref[...], wu_ref[0], NN) + bu_ref[0]
    de = mm(dy_ref[...], wd_ref[0], NT)
    dist, density = gelu_parts(u)
    e_ref[0] = (u * dist).astype(bf16)
    du = (de * (dist + u * density)).astype(bf16)
    du_ref[0] = du
    part = sub_sum(du.astype(f32))

    @pl.when(pl.program_id(1) == 0)
    def _():
        sum_ref[0] = part

    @pl.when(pl.program_id(1) > 0)
    def _():
        sum_ref[0] += part


def hidden(first, blocks, a2, dy, weights, vecs, after=(), step=512):
    count, width = a2.shape
    splits = weights.shape[0] // 2
    token = pl.BlockSpec((step, width), lambda j, i: (i, 0))
    out = pl.BlockSpec((1, step, width), lambda j, i: (j, i, 0))
    return call(
        hidden_body,
        blocks * 4 * count * width * width,
        blocks * (8 * count * width + 4 * width * width),
        after=after,
        grid=(blocks, count // step),
        in_specs=[
            token,
            token,
            pl.BlockSpec((1, width, width), lambda j, i: (first + j, 0, 0)),
            pl.BlockSpec((1, width, width), lambda j, i: (splits + first + j, 0, 0)),
            pl.BlockSpec((1, 1, width), lambda j, i: (8 + first + j, 0, 0)),
        ],
        out_specs=[out, out, pl.BlockSpec((1, 8, width), lambda j, i: (j, 0, 0))],
        out_shape=[
            jax.ShapeDtypeStruct((blocks, count, width), bf16),
            jax.ShapeDtypeStruct((blocks, count, width), bf16),
            jax.ShapeDtypeStruct((blocks, 8, width), f32),
        ],
    )(a2, dy, weights, weights, vecs[:, None, :])


def norm_back(grad, unit, scale, gain):
    grad = grad * gain
    first = jnp.mean(grad, axis=1, keepdims=True)
    second = jnp.mean(grad * unit, axis=1, keepdims=True)
    return scale * (grad - first - unit * second)


def hidden_sum(hidden_refs, w_ref, at, dims, acc):
    for ref in hidden_refs:
        for m in range(ref.shape[0]):
            part = mm(ref[m], w_ref[at], dims)
            acc = part if acc is None else acc + part
            at += 1
    return acc


def output_body(x_ref, o_ref, *refs, splits):
    *e_refs, wo_ref, wm_ref, vec_ref, out_ref = refs
    acc = hidden_sum(e_refs, wm_ref, 0, NN, mm(o_ref[...], wo_ref[0], NN))
    bias = vec_ref[7:8, :] + vec_ref[8 + splits : 9 + splits, :]
    out_ref[...] = (x_ref[...].astype(f32) + acc + bias).astype(bf16)


def resident(blocks, width, at):
    return pl.BlockSpec((blocks, width, width), lambda i: (at, 0, 0), pipeline_mode=pl.Buffered(1))


def stacked(value, step):
    return pl.BlockSpec((value.shape[0], step, value.shape[2]), lambda i: (0, i, 0))


def output(x, o, es, wa, wm, vecs, after=(), step=256):
    count, width = x.shape
    splits = wm.shape[0] // 2
    token = pl.BlockSpec((step, width), lambda i: (i, 0))
    return call(
        functools.partial(output_body, splits=splits),
        10 * count * width * width,
        14 * count * width + 10 * width * width,
        after=after,
        grid=(count // step,),
        in_specs=[token, token]
        + [stacked(e, step) for e in es]
        + [resident(1, width, 3), resident(splits, width, 1), pl.BlockSpec(vecs.shape, lambda i: (0, 0))],
        out_specs=token,
        out_shape=jax.ShapeDtypeStruct((count, width), bf16),
    )(x, o, *es, wa, wm, vecs)


def normed(x):
    centred = x - jnp.mean(x, axis=1, keepdims=True)
    scale = lax.rsqrt(jnp.mean(centred * centred, axis=1, keepdims=True) + norm_epsilon)
    return centred * scale, scale


def add_sums(sum_ref, sums):
    sums = [sub_sum(t) for t in sums]

    @pl.when(pl.program_id(0) == 0)
    def _():
        for n, s in enumerate(sums):
            sum_ref[n] = s

    @pl.when(pl.program_id(0) > 0)
    def _():
        for n, s in enumerate(sums):
            sum_ref[n] += s


def grad_two_body(x_ref, dy_ref, *refs):
    *du_refs, wm_ref, vec_ref, part_ref, sum_ref = refs
    dy = dy_ref[...].astype(f32)
    grad = hidden_sum(du_refs, wm_ref, 0, NT, None)
    unit, scale = normed(x_ref[...].astype(f32))
    part_ref[...] = dy + norm_back(grad, unit, scale, vec_ref[2:3, :])
    add_sums(sum_ref, (grad * unit, grad, dy))


def grad_two(x, dy, dus, wm, vecs, after=(), step=256):
    count, width = x.shape
    splits = wm.shape[0] // 2
    token = pl.BlockSpec((step, width), lambda i: (i, 0))
    return call(
        grad_two_body,
        8 * count * width * width,
        16 * count * width + 8 * width * width,
        after=after,
        grid=(count // step,),
        in_specs=[token, token]
        + [stacked(d, step) for d in dus]
        + [resident(splits, width, 0), pl.BlockSpec(vecs.shape, lambda i: (0, 0))],
        out_specs=[token, pl.BlockSpec((3, 8, width), lambda i: (0, 0, 0))],
        out_shape=[jax.ShapeDtypeStruct((count, width), f32), jax.ShapeDtypeStruct((3, 8, width), f32)],
    )(x, dy, *dus, wm, vecs)


def grad_one_body(x_ref, part_ref, g_ref, wa_ref, vec_ref, grad_ref, sum_ref):
    grad = mm(g_ref[0], wa_ref[0], NT) + mm(g_ref[1], wa_ref[1], NT) + mm(g_ref[2], wa_ref[2], NT)
    unit, scale = normed(x_ref[...].astype(f32))
    grad_ref[...] = (part_ref[...] + norm_back(grad, unit, scale, vec_ref[0:1, :])).astype(bf16)
    add_sums(sum_ref, (grad * unit, grad))


def grad_one(x, part, g, wa, vecs, after=(), step=256):
    count, width = x.shape
    token = pl.BlockSpec((step, width), lambda i: (i, 0))
    return call(
        grad_one_body,
        6 * count * width * width,
        14 * count * width + 6 * width * width,
        after=after,
        grid=(count // step,),
        in_specs=[
            token,
            token,
            stacked(g, step),
            resident(3, width, 0),
            pl.BlockSpec(vecs.shape, lambda i: (0, 0)),
        ],
        out_specs=[token, pl.BlockSpec((2, 8, width), lambda i: (0, 0, 0))],
        out_shape=[jax.ShapeDtypeStruct((count, width), bf16), jax.ShapeDtypeStruct((2, 8, width), f32)],
    )(x, part, g, wa, vecs)


def grid_places():
    wide, narrow = lax.axis_index("wide"), lax.axis_index("narrow")
    return wide // 2, wide % 2, narrow // 2, narrow % 2


def to_place(move):
    pairs = []
    for z in range(4):
        for y in range(2):
            for x in range(2):
                for c in range(2):
                    a, b, d, e = move(z, y, x, c)
                    pairs.append((((z * 2 + y) * 2 + x) * 2 + c, ((a * 2 + b) * 2 + d) * 2 + e))
    return pairs


def over_c(value):
    return lax.ppermute(value, AXES, to_place(lambda z, y, x, c: (z, y, x, 1 - c)))


def over_x(value):
    return lax.ppermute(value, AXES, to_place(lambda z, y, x, c: (z, y, 1 - x, c)))


def over_y(value):
    return lax.ppermute(value, AXES, to_place(lambda z, y, x, c: (z, 1 - y, x, c)))


def over_z(value, by):
    return lax.ppermute(value, AXES, to_place(lambda z, y, x, c: ((z + by) % 4, y, x, c)))


def gather_order_body(place_ref, *refs):
    z, y, x, c = place_ref[0], place_ref[1], place_ref[2], place_ref[3]
    out_ref = refs[-1]
    blocks = out_ref.shape[0]
    near = lax.rem(z - pl.program_id(0) + 4, 4) < 2
    for rc in range(2):
        own, by_x, by_y, lower, upper = refs[rc * 5 : rc * 5 + 5]
        at = (y * 2 + x) * 2 + (c ^ rc)
        for n in range(blocks):
            out_ref[n, at] = own[0, n]
            out_ref[n, at ^ 2] = by_x[0, n]
            out_ref[n, at ^ 4] = by_y[0, n]

        @pl.when(near)
        def _(lower=lower, at=at):
            for n in range(blocks):
                out_ref[n, at ^ 6] = lower[0, n]

        @pl.when(jnp.logical_not(near))
        def _(upper=upper, at=at):
            for n in range(blocks):
                out_ref[n, at ^ 6] = upper[0, n]


def gather_staged(place, shards, after=()):
    blocks, shard, width = shards.shape
    own = jnp.stack([shards] + [over_z(shards, s) for s in (1, 2, 3)])
    by_x, by_y = over_x(own), over_y(own)
    lower, upper = over_y(by_x[:2]), over_x(by_y[2:])
    here = [own, by_x, by_y, lower, upper]
    pieces = here + [over_c(v) for v in here]

    def piece(first, count):
        def index(t, s):
            apart = lax.rem(s[0] - t + 4, 4)
            return (jnp.clip(apart - first, 0, count - 1), 0, 0, 0)

        return pl.BlockSpec((1, blocks, shard, width), index)

    weights = call(
        gather_order_body,
        0,
        64 * blocks * shard * width * 2,
        after=after,
        grid_spec=pltpu.PrefetchScalarGridSpec(
            num_scalar_prefetch=1,
            grid=(4,),
            in_specs=([piece(0, 4)] * 3 + [piece(0, 2), piece(2, 2)]) * 2,
            out_specs=pl.BlockSpec((blocks, 8, shard, width), lambda t, s: (0, t, 0, 0)),
        ),
        out_shape=jax.ShapeDtypeStruct((blocks, 32, shard, width), bf16),
    )(place, *pieces)
    return weights.reshape(blocks, width, width)


def chip_pair_body(place_ref, ka_ref, ga_ref, kb_ref, gb_ref, ka2_ref, sa_ref, kb2_ref, sb_ref):
    y, x = place_ref[1], place_ref[2]
    for mine, k_ref, g_ref, k2_ref, s2_ref in (
        (y, ka_ref, ga_ref, ka2_ref, sa_ref),
        (x, kb_ref, gb_ref, kb2_ref, sb_ref),
    ):
        k2_ref[...] = k_ref[:, :, mine] + g_ref[:, :, mine].astype(f32)
        s2_ref[...] = (k_ref[:, :, 1 - mine] + g_ref[:, :, 1 - mine].astype(f32)).astype(bf16)


def plane_body(place_ref, ka_ref, ga_ref, kb_ref, gb_ref, *out_refs):
    half = ka_ref.shape[-1]
    for m, ref in enumerate(out_refs):
        at = place_ref[0] ^ m
        for lo, k_ref, g_ref in ((0, ka_ref, ga_ref), (half, kb_ref, gb_ref)):
            ref[:, :, lo : lo + half] = (k_ref[:, at >> 1, at & 1] + g_ref[:, at >> 1, at & 1].astype(f32)).astype(
                bf16
            )


def summed(body, place, operands, shapes, after, steps=2):
    def spec(s):
        n = len(s.shape)
        return pl.BlockSpec((s.shape[0] // steps, *s.shape[1:]), lambda b, p: (b,) + (0,) * (n - 1))

    return call(
        body,
        0,
        sum(v.size * v.dtype.itemsize for v in operands) * 2,
        after=after,
        grid_spec=pltpu.PrefetchScalarGridSpec(
            num_scalar_prefetch=1,
            grid=(steps,),
            in_specs=[spec(v) for v in operands],
            out_specs=[spec(s) for s in shapes],
        ),
        out_shape=shapes,
    )(place, *operands)


class Reduction:
    def __init__(self, place, ka, sa, kb, sb):
        self.place, self.made = place, ka
        self.held = (ka, over_x(sa), kb, over_y(sb))

    def first(self, after):
        blocks, two, _, c, shard, half = self.held[0].shape
        shapes = [jax.ShapeDtypeStruct((blocks, two, c, shard, half), k) for k in (f32, bf16, f32, bf16)]
        ka, sa, kb, sb = summed(chip_pair_body, self.place, self.held, shapes, after)
        self.held = (ka, over_y(sa), kb, over_x(sb))
        self.made = ka

    def second(self, after):
        blocks, _, _, shard, half = self.held[0].shape
        shapes = [jax.ShapeDtypeStruct((blocks, shard, 2 * half), bf16)] * 4
        parts = summed(plane_body, self.place, self.held, shapes, after)
        self.made = parts[0]
        self.terms = [
            lax.ppermute(
                v, AXES, to_place(lambda z, y, x, c, m=m: (2 * c + ((z ^ m) >> 1), y, x, (z ^ m) & 1))
            )
            for m, v in enumerate(parts)
        ]


def everywhere(value):
    for move in (
        lambda z, y, x, c: (z, y, x, 1 - c),
        lambda z, y, x, c: (z, y, 1 - x, c),
        lambda z, y, x, c: (z, 1 - y, x, c),
        lambda z, y, x, c: (z ^ 1, y, x, c),
        lambda z, y, x, c: (3 - z, y, x, c),
    ):
        value = value + lax.ppermute(value, AXES, to_place(move))
    return value


def pack_body(slot_ref, *refs, orders, per):
    terms, (shard_ref, out_ref, square_ref) = refs[: len(orders) * per], refs[len(orders) * per :]
    total = jnp.zeros(square_ref.shape, f32)
    for n, order in enumerate(orders):
        for m, b in enumerate(order):
            value = terms[n * per][m].astype(f32)
            for t in range(1, per):
                value = value + terms[n * per + t][m].astype(f32)
            shard_ref[b] = value
            total = total + value * value
    square_ref[...] = total

    def one(j, carry):
        b = slot_ref[j]

        @pl.when(b >= 0)
        def _():
            out_ref[j] = shard_ref[jnp.maximum(b, 0)].astype(bf16)

        @pl.when(b < 0)
        def _():
            out_ref[j] = jnp.zeros(out_ref.shape[1:], bf16)

        return carry

    lax.fori_loop(0, out_ref.shape[0], one, 0)


def pack(slots, terms, orders, after=()):
    per = len(terms[0])
    _, shard, width = terms[0][0].shape
    terms = [v for t in terms for v in t]
    vmem = pl.BlockSpec(memory_space=pltpu.VMEM)
    return call(
        functools.partial(pack_body, orders=orders, per=per),
        0,
        sum(v.size * v.dtype.itemsize for v in terms) * 2,
        after=after,
        in_specs=[pl.BlockSpec(memory_space=pltpu.SMEM)] + [vmem] * len(terms),
        out_specs=[vmem] * 3,
        out_shape=[
            jax.ShapeDtypeStruct((sum(map(len, orders)), shard, width), f32),
            jax.ShapeDtypeStruct((slots.shape[0], shard, width), bf16),
            jax.ShapeDtypeStruct((shard, width), f32),
        ],
    )(slots, *terms)


def precondition_body(scale_ref, s_ref, l_ref, r_ref, p_ref, s_low, r_low):
    @pl.when(pl.program_id(0) == 0)
    def _():
        s_low[...] = (s_ref[...].astype(f32) * scale_ref[0]).astype(bf16)
        r_low[...] = r_ref[...].astype(bf16)

    left = mm(l_ref[...].astype(bf16), s_low[...], NN)
    p_ref[...] = (scale_ref[1] * mm(left.astype(bf16), r_low[...], NN)).astype(bf16)


def precondition(scales, block, left, right, step=256):
    width = block.shape[0]
    whole = pl.BlockSpec((width, width), lambda i: (0, 0))
    rows = pl.BlockSpec((step, width), lambda i: (i, 0))
    return call(
        precondition_body,
        4 * width**3,
        12 * width**2,
        grid=(width // step,),
        in_specs=[pl.BlockSpec(memory_space=pltpu.SMEM), whole, rows, whole],
        out_specs=rows,
        out_shape=jax.ShapeDtypeStruct((width, width), bf16),
        scratch_shapes=[pltpu.VMEM((width, width), bf16), pltpu.VMEM((width, width), bf16)],
    )(scales, block, left, right)


def statistics_body(has_ref, scale_ref, s_ref, l_ref, r_ref, nl_ref, nr_ref, s_low, *, step):
    i = pl.program_id(0)
    width = s_ref.shape[0]

    @pl.when(i == 0)
    def _():
        s_low[...] = (s_ref[...].astype(f32) * scale_ref[0]).astype(bf16)

    factor = (1.0 - decay_beta) * (scale_ref[1] * scale_ref[1] / width)
    at = pl.multiple_of(i * step, step)

    @pl.when(has_ref[0] != 0)
    def _():
        nl_ref[...] = decay_beta * l_ref[...] + factor * mm(s_low[pl.ds(at, step), :], s_low[...], NT)
        nr_ref[...] = decay_beta * r_ref[...] + factor * mm(s_low[:, pl.ds(at, step)], s_low[...], TN)

    @pl.when(has_ref[0] == 0)
    def _():
        nl_ref[...] = l_ref[...]
        nr_ref[...] = r_ref[...]


def statistics(has, scales, block, left, right, step=256):
    width = block.shape[0]
    whole = pl.BlockSpec((width, width), lambda i: (0, 0))
    rows = pl.BlockSpec((step, width), lambda i: (i, 0))
    smem = pl.BlockSpec(memory_space=pltpu.SMEM)
    return call(
        functools.partial(statistics_body, step=step),
        4 * width**3,
        18 * width**2,
        grid=(width // step,),
        in_specs=[smem, smem, whole, rows, rows],
        out_specs=[rows, rows],
        out_shape=[jax.ShapeDtypeStruct((width, width), f32)] * 2,
        scratch_shapes=[pltpu.VMEM((width, width), bf16)],
    )(has, scales, block, left, right)


def update_body(owner_ref, factor_ref, p_ref, shard_ref, block_ref, clip_ref, new_ref, copy_ref):
    for b in range(shard_ref.shape[0]):
        clip_ref[b] = shard_ref[b] * factor_ref[0]
        value = block_ref[b] - matrix_rate * p_ref[owner_ref[b]].astype(f32)
        new_ref[b] = value
        copy_ref[b] = value.astype(bf16)


def update(owners, factor, returned, shards, blocks):
    smem, vmem = pl.BlockSpec(memory_space=pltpu.SMEM), pl.BlockSpec(memory_space=pltpu.VMEM)
    return call(
        update_body,
        0,
        returned.size * 2 + shards.size * 18,
        in_specs=[smem, smem, vmem, vmem, vmem],
        out_specs=[vmem] * 3,
        out_shape=[
            jax.ShapeDtypeStruct(shards.shape, f32),
            jax.ShapeDtypeStruct(shards.shape, f32),
            jax.ShapeDtypeStruct(shards.shape, bf16),
        ],
    )(owners, factor, returned, shards, blocks)


def layer_inputs(tokens, vecs):
    values = tokens.astype(f32)
    centred = values - jnp.mean(values, axis=-1, keepdims=True)
    spread = jnp.mean(centred * centred, axis=-1, keepdims=True)
    unit = centred * lax.rsqrt(spread + norm_epsilon)
    one = (unit * vecs[0] + vecs[1]).astype(bf16)
    two = (unit * vecs[2] + vecs[3]).astype(bf16)
    return one, two


def to_all(value):
    return lax.all_to_all(value, AXES, split_axis=0, concat_axis=0, tiled=True)


def per_device(
    tokens,
    segment_ids,
    cotangent,
    blocks,
    vectors,
    stat_left,
    stat_right,
    root_left,
    root_right,
    vec_stat,
    owners,
    *,
    paired,
):
    rows_here, seq_len, width = tokens.shape
    count = rows_here * seq_len
    splits = FF // width
    slot_count = lax.axis_size(AXES)
    my_index = lax.axis_index(AXES)
    shard = width // slot_count
    vec_rows = vectors.shape[0]

    low_blocks, low_vectors = blocks.astype(bf16), vectors.astype(bf16)
    everyone = jnp.broadcast_to(low_vectors.reshape(1, -1), (slot_count, vec_rows * shard))
    vecs = to_all(everyone).reshape(slot_count, vec_rows, shard)
    vecs = vecs.transpose(1, 0, 2).reshape(vec_rows, width).astype(f32)
    mlp_weights = lax.all_gather(low_blocks[4:], AXES, axis=1, tiled=True)

    flat_tokens = tokens.reshape(count, width)
    dy = cotangent.reshape(count, width)
    tables = rotary_tables(segment_ids)
    a1, a2 = layer_inputs(flat_tokens, vecs)
    place = jnp.stack(grid_places()).astype(jnp.int32)
    if paired:
        attn_weights = gather_staged(place, low_blocks[:4], after=(*tables, a1, a2))
    else:
        attn_weights = lax.all_gather(low_blocks[:4], AXES, axis=1, tiled=True)

    q, k, v, do = project(a1, dy, attn_weights, vecs, tables)
    o, g, attn_sums = attend(segment_ids, q, k, v, do, tables)
    half = splits // 2
    orders = [list(range(4))]
    for first in (0, half):
        orders.append([base + first + j for base in (4, 4 + splits) for j in range(half)])
    if paired:

        def pair(v):
            return v, over_c(v)

        a1s, a2s, dys = pair(a1), pair(a2), pair(dy)
        os, gs = pair(o[None]), pair(g)
        e0, du0, up_sum0 = hidden(0, half, a2, dy, mlp_weights, vecs, after=(o,))
        es, dus = [pair(e0)], [pair(du0)]
        attn = Reduction(place, *half_grads(place, a1s, os, gs, dys, shard, after=(e0,)))
        e1, du1, up_sum1 = hidden(half, half, a2, dy, mlp_weights, vecs, after=(attn.made,))
        es.append(pair(e1))
        dus.append(pair(du1))
        low = Reduction(place, *half_grads(place, a2s, es[0], dus[0], dys, shard, after=(e1,)))
        attn.first(after=(low.made,))
        high = Reduction(place, *half_grads(place, a2s, es[1], dus[1], dys, shard, after=(attn.made,)))
        out = output(flat_tokens, o, [e0, e1], attn_weights, mlp_weights, vecs, after=(high.made,))
        low.first(after=(out,))
        attn.second(after=(low.made,))
        part, two_sums = grad_two(flat_tokens, dy, [du0, du1], mlp_weights, vecs, after=(attn.made,))
        high.first(after=(part,))
        low.second(after=(high.made,))
        grad_in, one_sums = grad_one(flat_tokens, part, g, attn_weights, vecs, after=(low.made,))
        high.second(after=(grad_in,))
        terms = [r.terms for r in (attn, low, high)]
    else:
        e0, du0, up_sum0 = hidden(0, half, a2, dy, mlp_weights, vecs)
        e1, du1, up_sum1 = hidden(half, half, a2, dy, mlp_weights, vecs)
        grads = [
            full_grads(a1, o[None], g, dy),
            full_grads(a2, e0, du0, dy),
            full_grads(a2, e1, du1, dy),
        ]
        terms = [[lax.psum_scatter(v, AXES, scatter_dimension=1, tiled=True)] for v in grads]
        out = output(flat_tokens, o, [e0, e1], attn_weights, mlp_weights, vecs)
        part, two_sums = grad_two(flat_tokens, dy, [du0, du1], mlp_weights, vecs)
        grad_in, one_sums = grad_one(flat_tokens, part, g, attn_weights, vecs)
    up_sums = [up_sum0, up_sum1]

    one_sums, two_sums = jnp.sum(one_sums, axis=1), jnp.sum(two_sums, axis=1)
    qkv_sums = jnp.sum(attn_sums, axis=1)
    up_sums = jnp.sum(jnp.concatenate(up_sums, axis=0), axis=1)
    bias_sum = two_sums[2:]
    grad_vectors = jnp.concatenate(
        [one_sums, two_sums[:2], qkv_sums, bias_sum, up_sums, bias_sum], axis=0
    )
    by_slot = grad_vectors.reshape(vec_rows, slot_count, shard).transpose(1, 0, 2)
    shard_vectors = jnp.sum(to_all(by_slot.reshape(slot_count, -1)), axis=0).reshape(vec_rows, shard)

    slot_ids = jnp.arange(slot_count, dtype=jnp.int32)
    match = owners[None, :] == slot_ids[:, None]
    slots = jnp.sum(jnp.where(match, jnp.arange(1, owners.shape[0] + 1, dtype=jnp.int32)[None], 0), axis=1) - 1
    has_block = jnp.any(owners == my_index)
    shards, outgoing, squares = pack(slots, terms, orders, after=(grad_in,))
    local = jnp.sum(squares) + jnp.sum(shard_vectors * shard_vectors)
    if paired:
        square_sum = everywhere(jnp.broadcast_to(local, (8, LANES)))[0, 0]
    else:
        square_sum = jnp.sum(to_all(jnp.broadcast_to(local, (slot_count, LANES)))[:, 0])
    grad_norm = jnp.sqrt(square_sum)
    factor = jnp.minimum(1.0, clip_level / grad_norm)
    root_count = math.sqrt(NPARAM)

    scale = factor * root_count
    power = jnp.exp2(jnp.floor(jnp.log2(jnp.maximum(scale, 1e-30)))).astype(bf16).astype(f32)
    scales = jnp.stack([power, scale / power])
    owned = to_all(outgoing).reshape(width, width)
    precond = precondition(scales, owned, root_left[0], root_right[0])
    returned = to_all(precond.reshape(slot_count, shard, width))
    new_left, new_right = statistics(
        has_block.astype(jnp.int32).reshape(1), scales, owned, stat_left[0], stat_right[0]
    )
    clipped_blocks, new_blocks, blocks_copy = update(owners, factor.reshape(1), returned, shards, blocks)
    clipped_vectors = shard_vectors * factor
    scaled_vectors = clipped_vectors * root_count
    new_vec_stat = decay_beta * vec_stat + (1.0 - decay_beta) * (scaled_vectors * scaled_vectors)
    new_vectors = vectors - vector_rate * scaled_vectors * lax.rsqrt(new_vec_stat)
    return (
        out.reshape(tokens.shape),
        grad_in.reshape(tokens.shape),
        clipped_blocks,
        clipped_vectors,
        grad_norm,
        new_left[None],
        new_right[None],
        new_vec_stat,
        new_blocks,
        new_vectors,
        blocks_copy,
        new_vectors.astype(bf16),
    )


def solution(mesh):
    rows = P(AXES, None, None)
    split_rows = P(None, AXES, None)
    split_columns = P(None, AXES)
    paired = dict(mesh.shape) == {"wide": 8, "narrow": 4}
    return jax.shard_map(
        functools.partial(per_device, paired=paired),
        mesh=mesh,
        in_specs=(
            rows, P(AXES, None), rows, split_rows, split_columns,
            rows, rows, rows, rows, split_columns, P(),
        ),
        out_specs=(
            rows, rows, split_rows, split_columns, P(), rows, rows,
            split_columns, split_rows, split_columns, split_rows, split_columns,
        ),
        check_vma=False,
    )
```

```python
import functools
import math

import jax
import jax.numpy as jnp
from jax import lax
from jax.experimental import pallas as pl
from jax.experimental.pallas import tpu as pltpu
from jax.sharding import PartitionSpec as P

H = 12
FF = 3072
ROT = 16
NPARAM = 7087872
LONGEST = 256

clip_level = 1.0
matrix_rate = 0.03
vector_rate = 0.2
decay_beta = 0.5
norm_epsilon = 1e-05

f32 = jnp.float32
bf16 = jnp.bfloat16
AXES = ("wide", "narrow")
LANES = 128
MIB = 2**20

NN = (((1,), (0,)), ((), ()))
NT = (((1,), (1,)), ((), ()))
TN = (((0,), (0,)), ((), ()))


def mm(left, right, dims):
    return lax.dot_general(left, right, dims, preferred_element_type=f32)


def call(body, flops, moved, vmem=60, after=(), **rest):
    spec = rest.pop("grid_spec", None)
    grid = spec.grid if spec is not None else rest.get("grid", ())
    later = len(after)
    if later:
        held = [pl.BlockSpec(memory_space=pl.ANY)] * later
        if spec is not None:
            first = spec.num_scalar_prefetch + len(spec.in_specs)
            spec = pltpu.PrefetchScalarGridSpec(
                num_scalar_prefetch=spec.num_scalar_prefetch,
                grid=spec.grid,
                in_specs=list(spec.in_specs) + held,
                out_specs=spec.out_specs,
                scratch_shapes=spec.scratch_shapes,
            )
        else:
            first = len(rest["in_specs"])
            rest["in_specs"] = list(rest["in_specs"]) + held
        inner = body

        def body(*refs):
            inner(*refs[:first], *refs[first + later :])

    if spec is not None:
        rest["grid_spec"] = spec
    made = pl.pallas_call(
        body,
        compiler_params=pltpu.CompilerParams(
            vmem_limit_bytes=vmem * MIB,
            dimension_semantics=("arbitrary",) * len(grid),
        ),
        cost_estimate=pl.CostEstimate(
            flops=int(flops), bytes_accessed=int(moved), transcendentals=0
        ),
        **rest,
    )
    return lambda *operands: made(*operands, *after)


def sub_sum(values):
    return jnp.sum(values.reshape(-1, 8, values.shape[-1]), axis=0)


def rotary_tables(segment_ids):
    rows, length = segment_ids.shape
    start = jnp.sum(
        (segment_ids[:, None, :] < segment_ids[:, :, None]).astype(jnp.int32), axis=-1
    )
    offset = (jnp.arange(length, dtype=jnp.int32)[None] - start).astype(f32).reshape(-1, 1)
    half = ROT // 2
    lane = jnp.arange(LANES) % 64
    rates = jnp.power(10000.0, -2.0 * jnp.arange(half, dtype=f32) / ROT)
    angle = offset * jnp.where(lane < ROT, rates[lane % half], 0.0)[None]
    cosine, sine = jnp.cos(angle), jnp.sin(angle)
    first = jnp.where(lane[None] < half, -sine, 0.0)
    second = jnp.where((lane[None] >= half) & (lane[None] < ROT), sine, 0.0)
    return cosine, first, second


def rotate(values, cosine, first, second):
    parts = []
    for at in range(0, values.shape[1], LANES):
        part = values[:, at : at + LANES]
        parts.append(
            part * cosine
            + pltpu.roll(part, LANES - ROT // 2, 1) * first
            + pltpu.roll(part, ROT // 2, 1) * second
        )
    return jnp.concatenate(parts, axis=1)


def rotate_back(values, cosine, first, second):
    return (
        values * cosine
        - pltpu.roll(values, LANES - ROT // 2, 1) * first
        - pltpu.roll(values, ROT // 2, 1) * second
    )


def project_body(a1_ref, dy_ref, w_ref, vec_ref, c_ref, a_ref, b_ref, q_ref, k_ref, v_ref, do_ref):
    a1, tables = a1_ref[0], (c_ref[...], a_ref[...], b_ref[...])
    q_ref[...] = rotate(mm(a1, w_ref[0], NN) + vec_ref[4:5, :], *tables).astype(bf16)
    k_ref[...] = rotate(mm(a1, w_ref[1], NN) + vec_ref[5:6, :], *tables).astype(bf16)
    v_ref[...] = (mm(a1, w_ref[2], NN) + vec_ref[6:7, :]).astype(bf16)
    do_ref[...] = mm(dy_ref[...], w_ref[3], NT).astype(bf16)


def project(acts, dy, weights, vecs, tables, step=256):
    _, count, width = acts.shape
    token = pl.BlockSpec((step, width), lambda i: (i, 0))
    table = pl.BlockSpec((step, LANES), lambda i: (i, 0))
    return call(
        project_body,
        8 * count * width * width,
        12 * count * width + 8 * width * width,
        grid=(count // step,),
        in_specs=[
            pl.BlockSpec((1, step, width), lambda i: (0, i, 0)),
            token,
            pl.BlockSpec((4, width, width), lambda i: (0, 0, 0)),
            pl.BlockSpec(vecs.shape, lambda i: (0, 0)),
            table,
            table,
            table,
        ],
        out_specs=[token] * 4,
        out_shape=[jax.ShapeDtypeStruct((count, width), bf16)] * 4,
    )(acts, dy, weights, vecs, *tables)


def attend_body(
    col_ref, row_ref, q_ref, k_ref, v_ref, do_ref, c_ref, a_ref, b_ref,
    g_ref, sum_ref, mask_ref, dk_acc, dv_acc, *, block,
):
    length = q_ref.shape[0]
    steps = length // block

    def reach(i):
        return max(0, (i * block - (LONGEST - 1)) // block * block), (i + 1) * block

    @pl.when(pl.program_id(1) == 0)
    def _():
        for i in range(steps):
            lo, hi = reach(i)
            key = lax.broadcasted_iota(jnp.int32, (hi - lo, block), 0) + lo
            query = lax.broadcasted_iota(jnp.int32, (hi - lo, block), 1) + i * block
            same = col_ref[lo:hi, :] == row_ref[0, :, i * block : hi]
            mask = jnp.where(same & (key <= query), 0.0, -jnp.inf)
            mask_ref[i, 0 : hi - lo, 0:block] = mask
            mask_ref[i, 0 : hi - lo, block:] = mask

    low = lax.broadcasted_iota(jnp.int32, (1, LANES), 1) < 64
    eighth = jnp.asarray(0.125, bf16)
    zero = jnp.zeros((), bf16)
    keys, values, grads = k_ref[...], v_ref[...], do_ref[...]
    queries = q_ref[...] * eighth
    keys_t, values_t = (keys * eighth).T, values.T

    def both(part):
        return jnp.concatenate([jnp.where(low, part, zero), jnp.where(low, zero, part)], axis=0)

    def unstack(part):
        return jnp.concatenate([part[0:64, 0:block], part[64:, block:]], axis=0).T

    dk_acc[...] = jnp.zeros_like(dk_acc)
    dv_acc[...] = jnp.zeros_like(dv_acc)
    q_sum = jnp.zeros((8, LANES), f32)
    for i in range(steps):
        lo, hi = reach(i)
        here = slice(i * block, hi)
        q2, do2 = both(queries[here]), both(grads[here])
        scores = mm(keys[lo:hi], q2, NT) + mask_ref[i, 0 : hi - lo, :]
        raised = jnp.exp(scores - jnp.max(scores, axis=0, keepdims=True))
        soft = raised * (1.0 / jnp.sum(raised, axis=0, keepdims=True))
        d_soft = mm(values[lo:hi], do2, NT)
        inner = jnp.sum(soft * d_soft, axis=0, keepdims=True)
        soft_low = soft.astype(bf16)
        d_scores = (soft * (d_soft - inner)).astype(bf16)
        g_ref[3, here, :] = unstack(mm(values_t[:, lo:hi], soft_low, NN)).astype(bf16)
        dq = rotate_back(
            unstack(mm(keys_t[:, lo:hi], d_scores, NN)), c_ref[here, :], a_ref[here, :], b_ref[here, :]
        ).astype(bf16)
        g_ref[0, here, :] = dq
        q_sum = q_sum + sub_sum(dq.astype(f32))
        dk_acc[lo:hi, :] += mm(d_scores, q2, NN)
        dv_acc[lo:hi, :] += mm(soft_low, do2, NN)
    dk = rotate_back(dk_acc[...], c_ref[...], a_ref[...], b_ref[...]).astype(bf16)
    dv = dv_acc[...].astype(bf16)
    g_ref[1] = dk
    g_ref[2] = dv
    sum_ref[0] = q_sum
    sum_ref[1] = sub_sum(dk.astype(f32))
    sum_ref[2] = sub_sum(dv.astype(f32))


def attend(segment_ids, q, k, v, do, tables, after=(), block=256):
    rows, length = segment_ids.shape
    count, width = q.shape
    block = min(block, length)
    token = pl.BlockSpec((length, LANES), lambda r, h: (r, h))
    table = pl.BlockSpec((length, LANES), lambda r, h: (r, 0))
    return call(
        functools.partial(attend_body, block=block),
        24 * count * length * width,
        24 * count * width,
        after=after,
        grid=(rows, width // LANES),
        in_specs=[
            pl.BlockSpec((length, 1), lambda r, h: (r, 0)),
            pl.BlockSpec((1, 1, length), lambda r, h: (r, 0, 0)),
            token,
            token,
            token,
            token,
            table,
            table,
            table,
        ],
        out_specs=[
            pl.BlockSpec((4, length, LANES), lambda r, h: (0, r, h)),
            pl.BlockSpec((3, 8, LANES), lambda r, h: (0, r, h)),
        ],
        out_shape=[
            jax.ShapeDtypeStruct((4, count, width), bf16),
            jax.ShapeDtypeStruct((3, 8 * rows, width), f32),
        ],
        scratch_shapes=[
            pltpu.VMEM((length // block, length, 2 * block), f32),
            pltpu.VMEM((length, LANES), f32),
            pltpu.VMEM((length, LANES), f32),
        ],
    )(
        segment_ids.reshape(-1, 1),
        segment_ids.reshape(rows, 1, length),
        q,
        k,
        v,
        do,
        *tables,
    )


def half_grads_body(place_ref, *refs, first, second, steps):
    l1o, l1p, l2o, l2p, r1o, r1p, r2o, r2p, ka_ref, sa_ref, kb_ref, sb_ref, acc = refs
    i = pl.program_id(0)
    y, x = place_ref[1], place_ref[2]
    half = ka_ref.shape[-1]

    @pl.when(i == 0)
    def _():
        acc[...] = jnp.zeros_like(acc)

    for n in range(first + second):
        if n < first:
            part = mm(l1o[0], r1o[n], TN) + mm(l1p[0], r1p[n], TN)
        else:
            part = mm(l2o[n - first], r2o[...], TN) + mm(l2p[n - first], r2p[...], TN)
        acc[n] += part.reshape(acc.shape[1:])

    @pl.when(i == steps - 1)
    def _():
        for n in range(first + second):
            for ref, at in ((ka_ref, x), (sa_ref, 1 - x)):
                ref[n] = acc[n, :, :, at, :, :, :half].astype(ref.dtype)
            for ref, at in ((kb_ref, y), (sb_ref, 1 - y)):
                ref[n] = acc[n, :, at, :, :, :, half:].astype(ref.dtype)


def layers(part, step, lanes, half=False):
    _, first, count = part
    return pl.BlockSpec((count, step, lanes), lambda i, *s: (first // count, i, s[0][3] if half else 0))


def half_grads(place, left_one, left_two, right_one, right_two, shard, after=(), step=256):
    first, second = right_one[2], left_two[2]
    count, width = right_two[0].shape
    half = width // 2
    blocks = first + second
    steps = count // step
    shape = (blocks, 2, 2, 2, shard, half)
    out = pl.BlockSpec(shape, lambda i, s: (0, 0, 0, 0, 0, 0))
    return call(
        functools.partial(half_grads_body, first=first, second=second, steps=steps),
        blocks * 2 * count * width * width,
        blocks * 4 * count * width,
        after=after,
        grid_spec=pltpu.PrefetchScalarGridSpec(
            num_scalar_prefetch=1,
            grid=(steps,),
            in_specs=[layers(left_one, step, half, True)] * 2
            + [layers(left_two, step, half, True)] * 2
            + [layers(right_one, step, width)] * 2
            + [pl.BlockSpec((step, width), lambda i, s: (i, 0))] * 2,
            out_specs=[out] * 4,
            scratch_shapes=[pltpu.VMEM((blocks, 2, 2, 2, 2, shard, width), f32)],
        ),
        out_shape=[jax.ShapeDtypeStruct(shape, k) for k in (f32, bf16, f32, bf16)],
    )(place, *left_one[0], *left_two[0], *right_one[0], *right_two)


def full_grads(left_one, left_two, right_one, right_two):
    one = jnp.einsum("td,nte->nde", left_one, right_one, preferred_element_type=f32)
    two = jnp.einsum("ntd,te->nde", left_two, right_two, preferred_element_type=f32)
    return jnp.concatenate([one, two], axis=0)


def gelu_parts(u):
    raised = jnp.exp(-0.5 * (u * u))
    t = 1.0 / (1.0 + (0.3275911 * math.sqrt(0.5)) * jnp.abs(u))
    poly = 1.061405429 * t - 1.453152027
    poly = poly * t + 1.421413741
    poly = poly * t - 0.284496736
    poly = (poly * t + 0.254829592) * t
    tail = 0.5 * poly * raised
    return jnp.where(u < 0, tail, 1.0 - tail), raised * (1.0 / math.sqrt(2.0 * math.pi))


def hidden_body(a2_ref, dy_ref, wu_ref, wd_ref, bu_ref, out_ref, sum_ref):
    u = mm(a2_ref[0], wu_ref[0], NN) + bu_ref[0]
    de = mm(dy_ref[...], wd_ref[0], NT)
    dist, density = gelu_parts(u)
    out_ref[0, 0] = (u * dist).astype(bf16)
    du = (de * (dist + u * density)).astype(bf16)
    out_ref[1, 0] = du
    part = sub_sum(du.astype(f32))

    @pl.when(pl.program_id(1) == 0)
    def _():
        sum_ref[0] = part

    @pl.when(pl.program_id(1) > 0)
    def _():
        sum_ref[0] += part


def hidden(first, blocks, acts, dy, weights, vecs, after=(), step=512):
    _, count, width = acts.shape
    splits = weights.shape[0] // 2
    token = pl.BlockSpec((step, width), lambda j, i: (i, 0))
    both, sums = call(
        hidden_body,
        blocks * 4 * count * width * width,
        blocks * (8 * count * width + 4 * width * width),
        after=after,
        grid=(blocks, count // step),
        in_specs=[
            pl.BlockSpec((1, step, width), lambda j, i: (1, i, 0)),
            token,
            pl.BlockSpec((1, width, width), lambda j, i: (first + j, 0, 0)),
            pl.BlockSpec((1, width, width), lambda j, i: (splits + first + j, 0, 0)),
            pl.BlockSpec((1, 1, width), lambda j, i: (8 + first + j, 0, 0)),
        ],
        out_specs=[
            pl.BlockSpec((2, 1, step, width), lambda j, i: (0, j, i, 0)),
            pl.BlockSpec((1, 8, width), lambda j, i: (j, 0, 0)),
        ],
        out_shape=[
            jax.ShapeDtypeStruct((2, blocks, count, width), bf16),
            jax.ShapeDtypeStruct((blocks, 8, width), f32),
        ],
    )(acts, dy, weights, weights, vecs[:, None, :])
    return both.reshape(2 * blocks, count, width), sums


def norm_back(grad, unit, scale, gain):
    grad = grad * gain
    first = jnp.mean(grad, axis=1, keepdims=True)
    second = jnp.mean(grad * unit, axis=1, keepdims=True)
    return scale * (grad - first - unit * second)


def hidden_sum(hidden_refs, w_ref, at, dims, acc):
    for ref in hidden_refs:
        for m in range(ref.shape[0]):
            part = mm(ref[m], w_ref[at], dims)
            acc = part if acc is None else acc + part
            at += 1
    return acc


def output_body(x_ref, o_ref, *refs, splits):
    *e_refs, wo_ref, wm_ref, vec_ref, out_ref = refs
    acc = hidden_sum(e_refs, wm_ref, 0, NN, mm(o_ref[0], wo_ref[0], NN))
    bias = vec_ref[7:8, :] + vec_ref[8 + splits : 9 + splits, :]
    out_ref[...] = (x_ref[...].astype(f32) + acc + bias).astype(bf16)


def resident(blocks, width, at):
    return pl.BlockSpec((blocks, width, width), lambda i: (at, 0, 0), pipeline_mode=pl.Buffered(1))


def output(x, o, es, wa, wm, vecs, after=(), step=256):
    count, width = x.shape
    splits = wm.shape[0] // 2
    token = pl.BlockSpec((step, width), lambda i: (i, 0))
    return call(
        functools.partial(output_body, splits=splits),
        10 * count * width * width,
        14 * count * width + 10 * width * width,
        after=after,
        grid=(count // step,),
        in_specs=[token]
        + [layers(v, step, width) for v in (o, *es)]
        + [resident(1, width, 3), resident(splits, width, 1), pl.BlockSpec(vecs.shape, lambda i: (0, 0))],
        out_specs=token,
        out_shape=jax.ShapeDtypeStruct((count, width), bf16),
    )(x, *[v[0] for v in (o, *es)], wa, wm, vecs)


def normed(x):
    centred = x - jnp.mean(x, axis=1, keepdims=True)
    scale = lax.rsqrt(jnp.mean(centred * centred, axis=1, keepdims=True) + norm_epsilon)
    return centred * scale, scale


def add_sums(sum_ref, sums):
    sums = [sub_sum(t) for t in sums]

    @pl.when(pl.program_id(0) == 0)
    def _():
        for n, s in enumerate(sums):
            sum_ref[n] = s

    @pl.when(pl.program_id(0) > 0)
    def _():
        for n, s in enumerate(sums):
            sum_ref[n] += s


def grad_one_body(x_ref, dy_ref, g_ref, wa_ref, vec_ref, part_ref, sum_ref):
    dy = dy_ref[...].astype(f32)
    grad = mm(g_ref[0], wa_ref[0], NT) + mm(g_ref[1], wa_ref[1], NT) + mm(g_ref[2], wa_ref[2], NT)
    unit, scale = normed(x_ref[...].astype(f32))
    part_ref[...] = dy + norm_back(grad, unit, scale, vec_ref[0:1, :])
    add_sums(sum_ref, (grad * unit, grad, dy))


def grad_one(x, dy, g, wa, vecs, after=(), step=256):
    count, width = x.shape
    token = pl.BlockSpec((step, width), lambda i: (i, 0))
    return call(
        grad_one_body,
        6 * count * width * width,
        14 * count * width + 6 * width * width,
        after=after,
        grid=(count // step,),
        in_specs=[
            token,
            token,
            layers(g, step, width),
            resident(3, width, 0),
            pl.BlockSpec(vecs.shape, lambda i: (0, 0)),
        ],
        out_specs=[token, pl.BlockSpec((3, 8, width), lambda i: (0, 0, 0))],
        out_shape=[jax.ShapeDtypeStruct((count, width), f32), jax.ShapeDtypeStruct((3, 8, width), f32)],
    )(x, dy, g[0], wa, vecs)


def grad_two_body(x_ref, part_ref, *refs):
    *du_refs, wm_ref, vec_ref, grad_ref, sum_ref = refs
    grad = hidden_sum(du_refs, wm_ref, 0, NT, None)
    unit, scale = normed(x_ref[...].astype(f32))
    grad_ref[...] = (part_ref[...] + norm_back(grad, unit, scale, vec_ref[2:3, :])).astype(bf16)
    add_sums(sum_ref, (grad * unit, grad))


def grad_two(x, part, dus, wm, vecs, after=(), step=256):
    count, width = x.shape
    splits = wm.shape[0] // 2
    token = pl.BlockSpec((step, width), lambda i: (i, 0))
    return call(
        grad_two_body,
        8 * count * width * width,
        16 * count * width + 8 * width * width,
        after=after,
        grid=(count // step,),
        in_specs=[token, token]
        + [layers(v, step, width) for v in dus]
        + [resident(splits, width, 0), pl.BlockSpec(vecs.shape, lambda i: (0, 0))],
        out_specs=[token, pl.BlockSpec((2, 8, width), lambda i: (0, 0, 0))],
        out_shape=[jax.ShapeDtypeStruct((count, width), bf16), jax.ShapeDtypeStruct((2, 8, width), f32)],
    )(x, part, *[v[0] for v in dus], wm, vecs)


def grid_places():
    wide, narrow = lax.axis_index("wide"), lax.axis_index("narrow")
    return wide // 2, wide % 2, narrow // 2, narrow % 2


def to_place(move):
    pairs = []
    for z in range(4):
        for y in range(2):
            for x in range(2):
                for c in range(2):
                    a, b, d, e = move(z, y, x, c)
                    pairs.append((((z * 2 + y) * 2 + x) * 2 + c, ((a * 2 + b) * 2 + d) * 2 + e))
    return pairs


def over_c(value):
    return lax.ppermute(value, AXES, to_place(lambda z, y, x, c: (z, y, x, 1 - c)))


def over_x(value):
    return lax.ppermute(value, AXES, to_place(lambda z, y, x, c: (z, y, 1 - x, c)))


def over_y(value):
    return lax.ppermute(value, AXES, to_place(lambda z, y, x, c: (z, 1 - y, x, c)))


def over_z(value, by):
    return lax.ppermute(value, AXES, to_place(lambda z, y, x, c: ((z + by) % 4, y, x, c)))


def gather_order_body(place_ref, *refs):
    z, y, x, c = place_ref[0], place_ref[1], place_ref[2], place_ref[3]
    out_ref = refs[-1]
    blocks = out_ref.shape[0]
    near = lax.rem(z - pl.program_id(0) + 4, 4) < 2
    for rc in range(2):
        own, by_x, by_y, lower, upper = refs[rc * 5 : rc * 5 + 5]
        at = (y * 2 + x) * 2 + (c ^ rc)
        for n in range(blocks):
            out_ref[n, at] = own[0, n]
            out_ref[n, at ^ 2] = by_x[0, n]
            out_ref[n, at ^ 4] = by_y[0, n]

        @pl.when(near)
        def _(lower=lower, at=at):
            for n in range(blocks):
                out_ref[n, at ^ 6] = lower[0, n]

        @pl.when(jnp.logical_not(near))
        def _(upper=upper, at=at):
            for n in range(blocks):
                out_ref[n, at ^ 6] = upper[0, n]


def gather_staged(place, shards, after=()):
    blocks, shard, width = shards.shape
    own = jnp.stack([shards] + [over_z(shards, s) for s in (1, 2, 3)])
    by_x, by_y = over_x(own), over_y(own)
    lower, upper = over_y(by_x[:2]), over_x(by_y[2:])
    here = [own, by_x, by_y, lower, upper]
    pieces = here + [over_c(v) for v in here]

    def piece(first, count):
        def index(t, s):
            apart = lax.rem(s[0] - t + 4, 4)
            return (jnp.clip(apart - first, 0, count - 1), 0, 0, 0)

        return pl.BlockSpec((1, blocks, shard, width), index)

    weights = call(
        gather_order_body,
        0,
        64 * blocks * shard * width * 2,
        after=after,
        grid_spec=pltpu.PrefetchScalarGridSpec(
            num_scalar_prefetch=1,
            grid=(4,),
            in_specs=([piece(0, 4)] * 3 + [piece(0, 2), piece(2, 2)]) * 2,
            out_specs=pl.BlockSpec((blocks, 8, shard, width), lambda t, s: (0, t, 0, 0)),
        ),
        out_shape=jax.ShapeDtypeStruct((blocks, 32, shard, width), bf16),
    )(place, *pieces)
    return weights.reshape(blocks, width, width)


def chip_pair_body(place_ref, ka_ref, ga_ref, kb_ref, gb_ref, ka2_ref, sa_ref, kb2_ref, sb_ref):
    y, x = place_ref[1], place_ref[2]
    for mine, k_ref, g_ref, k2_ref, s2_ref in (
        (y, ka_ref, ga_ref, ka2_ref, sa_ref),
        (x, kb_ref, gb_ref, kb2_ref, sb_ref),
    ):
        k2_ref[...] = k_ref[:, :, mine] + g_ref[:, :, mine].astype(f32)
        s2_ref[...] = (k_ref[:, :, 1 - mine] + g_ref[:, :, 1 - mine].astype(f32)).astype(bf16)


def plane_body(place_ref, ka_ref, ga_ref, kb_ref, gb_ref, *out_refs):
    half = ka_ref.shape[-1]
    for m, ref in enumerate(out_refs):
        at = place_ref[0] ^ m
        for lo, k_ref, g_ref in ((0, ka_ref, ga_ref), (half, kb_ref, gb_ref)):
            ref[:, :, lo : lo + half] = (k_ref[:, at >> 1, at & 1] + g_ref[:, at >> 1, at & 1].astype(f32)).astype(
                bf16
            )


class Reduction:
    def __init__(self, ka, sa, kb, sb):
        self.made = ka
        self.held = (ka, over_x(sa), kb, over_y(sb))


def advance(place, pairs, planes, after=(), steps=2):
    blocks, *_, shard, half = (pairs + planes)[0].held[0].shape
    shapes = [jax.ShapeDtypeStruct((blocks, 2, 2, shard, half), k) for k in (f32, bf16, f32, bf16)] * len(pairs)
    if planes:
        shapes += [jax.ShapeDtypeStruct((len(planes), blocks, shard, 2 * half), bf16)] * 4
    operands = [v for r in pairs + planes for v in r.held]

    def spec(s, at=0):
        n = len(s.shape)
        block = tuple(d // steps if m == at else d for m, d in enumerate(s.shape))
        return pl.BlockSpec(block, lambda b, p: (0,) * at + (b,) + (0,) * (n - 1 - at))

    def body(place_ref, *refs):
        ins, outs = refs[: len(operands)], refs[len(operands) :]
        for n in range(len(pairs)):
            chip_pair_body(place_ref, *ins[4 * n : 4 * n + 4], *outs[4 * n : 4 * n + 4])
        for n in range(len(planes)):
            m = 4 * (len(pairs) + n)
            plane_body(place_ref, *ins[m : m + 4], *[ref.at[n] for ref in outs[4 * len(pairs) :]])

    outs = call(
        body,
        0,
        sum(v.size * v.dtype.itemsize for v in operands) * 2,
        after=after,
        grid_spec=pltpu.PrefetchScalarGridSpec(
            num_scalar_prefetch=1,
            grid=(steps,),
            in_specs=[spec(v) for v in operands],
            out_specs=[spec(s, n >= 4 * len(pairs)) for n, s in enumerate(shapes)],
        ),
        out_shape=shapes,
    )(place, *operands)
    for n, r in enumerate(pairs):
        ka, sa, kb, sb = outs[4 * n : 4 * n + 4]
        r.made = ka
        r.held = (ka, over_y(sa), kb, over_x(sb))
    terms = []
    for m, v in enumerate(outs[4 * len(pairs) :]):
        planes[0].made = v
        v = v.reshape(-1, shard, 2 * half)
        terms.append(
            lax.ppermute(
                v, AXES, to_place(lambda z, y, x, c, m=m: (2 * c + ((z ^ m) >> 1), y, x, (z ^ m) & 1))
            )
        )
    return terms


def everywhere(value):
    for move in (
        lambda z, y, x, c: (z, y, x, 1 - c),
        lambda z, y, x, c: (z, y, 1 - x, c),
        lambda z, y, x, c: (z, 1 - y, x, c),
        lambda z, y, x, c: (z ^ 1, y, x, c),
        lambda z, y, x, c: (3 - z, y, x, c),
    ):
        value = value + lax.ppermute(value, AXES, to_place(move))
    return value


def pack_body(slot_ref, *refs, orders, per):
    terms, (shard_ref, out_ref, square_ref) = refs[: len(orders) * per], refs[len(orders) * per :]
    total = jnp.zeros(square_ref.shape, f32)
    for n, order in enumerate(orders):
        for m, b in enumerate(order):
            value = terms[n * per][m].astype(f32)
            for t in range(1, per):
                value = value + terms[n * per + t][m].astype(f32)
            shard_ref[b] = value
            total = total + value * value
    square_ref[...] = total

    def one(j, carry):
        b = slot_ref[j]

        @pl.when(b >= 0)
        def _():
            out_ref[j] = shard_ref[jnp.maximum(b, 0)].astype(bf16)

        @pl.when(b < 0)
        def _():
            out_ref[j] = jnp.zeros(out_ref.shape[1:], bf16)

        return carry

    lax.fori_loop(0, out_ref.shape[0], one, 0)


def pack(slots, terms, orders, after=()):
    per = len(terms[0])
    _, shard, width = terms[0][0].shape
    terms = [v for t in terms for v in t]
    vmem = pl.BlockSpec(memory_space=pltpu.VMEM)
    return call(
        functools.partial(pack_body, orders=orders, per=per),
        0,
        sum(v.size * v.dtype.itemsize for v in terms) * 2,
        after=after,
        in_specs=[pl.BlockSpec(memory_space=pltpu.SMEM)] + [vmem] * len(terms),
        out_specs=[vmem] * 3,
        out_shape=[
            jax.ShapeDtypeStruct((sum(map(len, orders)), shard, width), f32),
            jax.ShapeDtypeStruct((slots.shape[0], shard, width), bf16),
            jax.ShapeDtypeStruct((shard, width), f32),
        ],
    )(slots, *terms)


def precondition_body(scale_ref, s_ref, l_ref, r_ref, p_ref, s_low, r_low):
    @pl.when(pl.program_id(0) == 0)
    def _():
        s_low[...] = (s_ref[...].astype(f32) * scale_ref[0]).astype(bf16)
        r_low[...] = r_ref[...].astype(bf16)

    left = mm(l_ref[...].astype(bf16), s_low[...], NN)
    p_ref[...] = (scale_ref[1] * mm(left.astype(bf16), r_low[...], NN)).astype(bf16)


def precondition(scales, block, left, right, step=256):
    width = block.shape[0]
    whole = pl.BlockSpec((width, width), lambda i: (0, 0))
    rows = pl.BlockSpec((step, width), lambda i: (i, 0))
    return call(
        precondition_body,
        4 * width**3,
        12 * width**2,
        grid=(width // step,),
        in_specs=[pl.BlockSpec(memory_space=pltpu.SMEM), whole, rows, whole],
        out_specs=rows,
        out_shape=jax.ShapeDtypeStruct((width, width), bf16),
        scratch_shapes=[pltpu.VMEM((width, width), bf16), pltpu.VMEM((width, width), bf16)],
    )(scales, block, left, right)


def statistics_body(has_ref, scale_ref, s_ref, l_ref, r_ref, nl_ref, nr_ref, s_low, *, step):
    i = pl.program_id(0)
    width = s_ref.shape[0]

    @pl.when(i == 0)
    def _():
        s_low[...] = (s_ref[...].astype(f32) * scale_ref[0]).astype(bf16)

    factor = (1.0 - decay_beta) * (scale_ref[1] * scale_ref[1] / width)
    at = pl.multiple_of(i * step, step)

    @pl.when(has_ref[0] != 0)
    def _():
        nl_ref[...] = decay_beta * l_ref[...] + factor * mm(s_low[pl.ds(at, step), :], s_low[...], NT)
        nr_ref[...] = decay_beta * r_ref[...] + factor * mm(s_low[:, pl.ds(at, step)], s_low[...], TN)

    @pl.when(has_ref[0] == 0)
    def _():
        nl_ref[...] = l_ref[...]
        nr_ref[...] = r_ref[...]


def statistics(has, scales, block, left, right, step=256):
    width = block.shape[0]
    whole = pl.BlockSpec((width, width), lambda i: (0, 0))
    rows = pl.BlockSpec((step, width), lambda i: (i, 0))
    smem = pl.BlockSpec(memory_space=pltpu.SMEM)
    return call(
        functools.partial(statistics_body, step=step),
        4 * width**3,
        18 * width**2,
        grid=(width // step,),
        in_specs=[smem, smem, whole, rows, rows],
        out_specs=[rows, rows],
        out_shape=[jax.ShapeDtypeStruct((width, width), f32)] * 2,
        scratch_shapes=[pltpu.VMEM((width, width), bf16)],
    )(has, scales, block, left, right)


def update_body(owner_ref, factor_ref, p_ref, shard_ref, block_ref, clip_ref, new_ref, copy_ref):
    for b in range(shard_ref.shape[0]):
        clip_ref[b] = shard_ref[b] * factor_ref[0]
        value = block_ref[b] - matrix_rate * p_ref[owner_ref[b]].astype(f32)
        new_ref[b] = value
        copy_ref[b] = value.astype(bf16)


def update(owners, factor, returned, shards, blocks):
    smem, vmem = pl.BlockSpec(memory_space=pltpu.SMEM), pl.BlockSpec(memory_space=pltpu.VMEM)
    return call(
        update_body,
        0,
        returned.size * 2 + shards.size * 18,
        in_specs=[smem, smem, vmem, vmem, vmem],
        out_specs=[vmem] * 3,
        out_shape=[
            jax.ShapeDtypeStruct(shards.shape, f32),
            jax.ShapeDtypeStruct(shards.shape, f32),
            jax.ShapeDtypeStruct(shards.shape, bf16),
        ],
    )(owners, factor, returned, shards, blocks)


def layer_inputs(tokens, vecs):
    values = tokens.astype(f32)
    centred = values - jnp.mean(values, axis=-1, keepdims=True)
    spread = jnp.mean(centred * centred, axis=-1, keepdims=True)
    unit = centred * lax.rsqrt(spread + norm_epsilon)
    return jnp.stack([unit * vecs[0] + vecs[1], unit * vecs[2] + vecs[3]]).astype(bf16)


def to_all(value):
    return lax.all_to_all(value, AXES, split_axis=0, concat_axis=0, tiled=True)


def per_device(
    tokens,
    segment_ids,
    cotangent,
    blocks,
    vectors,
    stat_left,
    stat_right,
    root_left,
    root_right,
    vec_stat,
    owners,
    *,
    paired,
):
    rows_here, seq_len, width = tokens.shape
    count = rows_here * seq_len
    splits = FF // width
    slot_count = lax.axis_size(AXES)
    my_index = lax.axis_index(AXES)
    shard = width // slot_count
    vec_rows = vectors.shape[0]

    low_blocks, low_vectors = blocks.astype(bf16), vectors.astype(bf16)
    everyone = jnp.broadcast_to(low_vectors.reshape(1, -1), (slot_count, vec_rows * shard))
    vecs = to_all(everyone).reshape(slot_count, vec_rows, shard)
    vecs = vecs.transpose(1, 0, 2).reshape(vec_rows, width).astype(f32)
    mlp_weights = lax.all_gather(low_blocks[4:], AXES, axis=1, tiled=True)

    flat_tokens = tokens.reshape(count, width)
    dy = cotangent.reshape(count, width)
    tables = rotary_tables(segment_ids)
    acts = layer_inputs(flat_tokens, vecs)
    place = jnp.stack(grid_places()).astype(jnp.int32)
    if paired:
        attn_weights = gather_staged(place, low_blocks[:4], after=(*tables, acts))
    else:
        attn_weights = lax.all_gather(low_blocks[:4], AXES, axis=1, tiled=True)

    def pair(v):
        return (v, over_c(v)) if paired else (v, v)

    def pair(v):
        return (v, over_c(v)) if paired else (v, v)

    q, k, v, do = project(acts, dy, attn_weights, vecs, tables)
    both_acts, dys = pair(acts), pair(dy)
    og, attn_sums = attend(segment_ids, q, k, v, do, tables, after=(both_acts[1], dys[1]))
    half = splits // 2
    orders = [list(range(4))]
    for first in (0, half):
        orders.append([base + first + j for base in (4, 4 + splits) for j in range(half)])
    if paired:
        ogs = pair(og)
        ed0, up_sum0 = hidden(0, half, acts, dy, mlp_weights, vecs, after=(og,))
        ed1, up_sum1 = hidden(half, half, acts, dy, mlp_weights, vecs, after=(ed0,))
        ed0s, ed1s = pair(ed0), pair(ed1)
        attn = Reduction(
            *half_grads(place, (both_acts, 0, 1), (ogs, 3, 1), (ogs, 0, 3), dys, shard, after=(ed1,))
        )
        low = Reduction(
            *half_grads(
                place, (both_acts, 1, 1), (ed0s, 0, half), (ed0s, half, half), dys, shard, after=(attn.made,)
            )
        )
        high = Reduction(
            *half_grads(
                place, (both_acts, 1, 1), (ed1s, 0, half), (ed1s, half, half), dys, shard, after=(low.made,)
            )
        )
        es, dus = [(v, 0, half) for v in (ed0, ed1)], [(v, half, half) for v in (ed0, ed1)]
        advance(place, [attn], [], after=(high.made,))
        out = output(flat_tokens, (og, 3, 1), es, attn_weights, mlp_weights, vecs, after=(attn.made,))
        terms = [advance(place, [low], [attn], after=(out,))]
        part, one_sums = grad_one(flat_tokens, dy, (og, 0, 3), attn_weights, vecs, after=(low.made,))
        terms.append(advance(place, [high], [low], after=(part, *terms[0])))
        terms.append(advance(place, [], [high]))
        grad_in, two_sums = grad_two(flat_tokens, part, dus, mlp_weights, vecs, after=(high.made, *terms[1]))
    else:
        ed0, up_sum0 = hidden(0, half, acts, dy, mlp_weights, vecs)
        ed1, up_sum1 = hidden(half, half, acts, dy, mlp_weights, vecs)
        grads = [
            full_grads(acts[0], og[3:], og[:3], dy),
            full_grads(acts[1], ed0[:half], ed0[half:], dy),
            full_grads(acts[1], ed1[:half], ed1[half:], dy),
        ]
        terms = [[lax.psum_scatter(v, AXES, scatter_dimension=1, tiled=True)] for v in grads]
        es, dus = [(v, 0, half) for v in (ed0, ed1)], [(v, half, half) for v in (ed0, ed1)]
        out = output(flat_tokens, (og, 3, 1), es, attn_weights, mlp_weights, vecs)
        part, one_sums = grad_one(flat_tokens, dy, (og, 0, 3), attn_weights, vecs)
        grad_in, two_sums = grad_two(flat_tokens, part, dus, mlp_weights, vecs)
    up_sums = [up_sum0, up_sum1]

    one_sums, two_sums = jnp.sum(one_sums, axis=1), jnp.sum(two_sums, axis=1)
    qkv_sums = jnp.sum(attn_sums, axis=1)
    up_sums = jnp.sum(jnp.concatenate(up_sums, axis=0), axis=1)
    bias_sum = one_sums[2:]
    grad_vectors = jnp.concatenate(
        [one_sums[:2], two_sums, qkv_sums, bias_sum, up_sums, bias_sum], axis=0
    )
    slot_ids = jnp.arange(slot_count, dtype=jnp.int32)
    match = owners[None, :] == slot_ids[:, None]
    slots = jnp.sum(jnp.where(match, jnp.arange(1, owners.shape[0] + 1, dtype=jnp.int32)[None], 0), axis=1) - 1
    has_block = jnp.any(owners == my_index)
    shards, outgoing, squares = pack(slots, terms, orders, after=(grad_in,))
    local = jnp.concatenate([grad_vectors, jnp.sum(squares, axis=0)[None], jnp.zeros((2, width), f32)])
    total = everywhere(local) if paired else lax.psum(local, AXES)
    vector_sums = total[:vec_rows]
    square_sum = jnp.sum(total[vec_rows]) + jnp.sum(vector_sums * vector_sums)
    shard_vectors = lax.dynamic_slice_in_dim(vector_sums, my_index * shard, shard, axis=1)
    grad_norm = jnp.sqrt(square_sum)
    factor = jnp.minimum(1.0, clip_level / grad_norm)
    root_count = math.sqrt(NPARAM)

    scale = factor * root_count
    power = jnp.exp2(jnp.floor(jnp.log2(jnp.maximum(scale, 1e-30)))).astype(bf16).astype(f32)
    scales = jnp.stack([power, scale / power])
    owned = to_all(outgoing).reshape(width, width)
    precond = precondition(scales, owned, root_left[0], root_right[0])
    returned = to_all(precond.reshape(slot_count, shard, width))
    new_left, new_right = statistics(
        has_block.astype(jnp.int32).reshape(1), scales, owned, stat_left[0], stat_right[0]
    )
    clipped_blocks, new_blocks, blocks_copy = update(owners, factor.reshape(1), returned, shards, blocks)
    clipped_vectors = shard_vectors * factor
    scaled_vectors = clipped_vectors * root_count
    new_vec_stat = decay_beta * vec_stat + (1.0 - decay_beta) * (scaled_vectors * scaled_vectors)
    new_vectors = vectors - vector_rate * scaled_vectors * lax.rsqrt(new_vec_stat)
    return (
        out.reshape(tokens.shape),
        grad_in.reshape(tokens.shape),
        clipped_blocks,
        clipped_vectors,
        grad_norm,
        new_left[None],
        new_right[None],
        new_vec_stat,
        new_blocks,
        new_vectors,
        blocks_copy,
        new_vectors.astype(bf16),
    )


def solution(mesh):
    rows = P(AXES, None, None)
    split_rows = P(None, AXES, None)
    split_columns = P(None, AXES)
    paired = dict(mesh.shape) == {"wide": 8, "narrow": 4}
    return jax.shard_map(
        functools.partial(per_device, paired=paired),
        mesh=mesh,
        in_specs=(
            rows, P(AXES, None), rows, split_rows, split_columns,
            rows, rows, rows, rows, split_columns, P(),
        ),
        out_specs=(
            rows, rows, split_rows, split_columns, P(), rows, rows,
            split_columns, split_rows, split_columns, split_rows, split_columns,
        ),
        check_vma=False,
    )
```

```python
import functools
import math

import jax
import jax.numpy as jnp
from jax import lax
from jax.experimental import pallas as pl
from jax.experimental.pallas import tpu as pltpu
from jax.sharding import PartitionSpec as P

H = 12
FF = 3072
ROT = 16
NPARAM = 7087872
LONGEST = 256

clip_level = 1.0
matrix_rate = 0.03
vector_rate = 0.2
decay_beta = 0.5
norm_epsilon = 1e-05

f32 = jnp.float32
bf16 = jnp.bfloat16
AXES = ("wide", "narrow")
LANES = 128
MIB = 2**20

NN = (((1,), (0,)), ((), ()))
NT = (((1,), (1,)), ((), ()))
TN = (((0,), (0,)), ((), ()))


def mm(left, right, dims):
    return lax.dot_general(left, right, dims, preferred_element_type=f32)


def call(body, flops, moved, vmem=60, after=(), **rest):
    spec = rest.pop("grid_spec", None)
    grid = spec.grid if spec is not None else rest.get("grid", ())
    later = len(after)
    if later:
        held = [pl.BlockSpec(memory_space=pl.ANY)] * later
        if spec is not None:
            first = spec.num_scalar_prefetch + len(spec.in_specs)
            spec = pltpu.PrefetchScalarGridSpec(
                num_scalar_prefetch=spec.num_scalar_prefetch,
                grid=spec.grid,
                in_specs=list(spec.in_specs) + held,
                out_specs=spec.out_specs,
                scratch_shapes=spec.scratch_shapes,
            )
        else:
            first = len(rest["in_specs"])
            rest["in_specs"] = list(rest["in_specs"]) + held
        inner = body

        def body(*refs):
            inner(*refs[:first], *refs[first + later :])

    if spec is not None:
        rest["grid_spec"] = spec
    made = pl.pallas_call(
        body,
        compiler_params=pltpu.CompilerParams(
            vmem_limit_bytes=vmem * MIB,
            dimension_semantics=("arbitrary",) * len(grid),
        ),
        cost_estimate=pl.CostEstimate(
            flops=int(flops), bytes_accessed=int(moved), transcendentals=0
        ),
        **rest,
    )
    return lambda *operands: made(*operands, *after)


def sub_sum(values):
    return jnp.sum(values.reshape(-1, 8, values.shape[-1]), axis=0)


def rotary_tables(segment_ids):
    rows, length = segment_ids.shape
    start = jnp.sum(
        (segment_ids[:, None, :] < segment_ids[:, :, None]).astype(jnp.int32), axis=-1
    )
    offset = (jnp.arange(length, dtype=jnp.int32)[None] - start).astype(f32).reshape(-1, 1)
    half = ROT // 2
    lane = jnp.arange(LANES) % 64
    rates = jnp.power(10000.0, -2.0 * jnp.arange(half, dtype=f32) / ROT)
    angle = offset * jnp.where(lane < ROT, rates[lane % half], 0.0)[None]
    cosine, sine = jnp.cos(angle), jnp.sin(angle)
    first = jnp.where(lane[None] < half, -sine, 0.0)
    second = jnp.where((lane[None] >= half) & (lane[None] < ROT), sine, 0.0)
    return cosine, first, second


def rotate(values, cosine, first, second):
    parts = []
    for at in range(0, values.shape[1], LANES):
        part = values[:, at : at + LANES]
        parts.append(
            part * cosine
            + pltpu.roll(part, LANES - ROT // 2, 1) * first
            + pltpu.roll(part, ROT // 2, 1) * second
        )
    return jnp.concatenate(parts, axis=1)


def rotate_back(values, cosine, first, second):
    return (
        values * cosine
        - pltpu.roll(values, LANES - ROT // 2, 1) * first
        - pltpu.roll(values, ROT // 2, 1) * second
    )


def project_body(a1_ref, dy_ref, w_ref, vec_ref, c_ref, a_ref, b_ref, q_ref, k_ref, v_ref, do_ref):
    a1, tables = a1_ref[0], (c_ref[...], a_ref[...], b_ref[...])
    q_ref[...] = rotate(mm(a1, w_ref[0], NN) + vec_ref[4:5, :], *tables).astype(bf16)
    k_ref[...] = rotate(mm(a1, w_ref[1], NN) + vec_ref[5:6, :], *tables).astype(bf16)
    v_ref[...] = (mm(a1, w_ref[2], NN) + vec_ref[6:7, :]).astype(bf16)
    do_ref[...] = mm(dy_ref[0], w_ref[3], NT).astype(bf16)


def project(acts, weights, vecs, tables, step=256):
    _, count, width = acts.shape
    token = pl.BlockSpec((step, width), lambda i: (i, 0))
    table = pl.BlockSpec((step, LANES), lambda i: (i, 0))
    return call(
        project_body,
        8 * count * width * width,
        12 * count * width + 8 * width * width,
        grid=(count // step,),
        in_specs=[
            pl.BlockSpec((1, step, width), lambda i: (0, i, 0)),
            pl.BlockSpec((1, step, width), lambda i: (2, i, 0)),
            pl.BlockSpec((4, width, width), lambda i: (0, 0, 0)),
            pl.BlockSpec(vecs.shape, lambda i: (0, 0)),
            table,
            table,
            table,
        ],
        out_specs=[token] * 4,
        out_shape=[jax.ShapeDtypeStruct((count, width), bf16)] * 4,
    )(acts, acts, weights, vecs, *tables)


def attend_body(
    acts_ref, col_ref, row_ref, q_ref, k_ref, v_ref, do_ref, c_ref, a_ref, b_ref,
    g_ref, sum_ref, acts_out_ref, mask_ref, dk_acc, dv_acc, *, block,
):
    length = q_ref.shape[0]
    steps = length // block

    def reach(i):
        return max(0, (i * block - (LONGEST - 1)) // block * block), (i + 1) * block

    @pl.when(pl.program_id(1) == 0)
    def _():
        for i in range(steps):
            lo, hi = reach(i)
            key = lax.broadcasted_iota(jnp.int32, (hi - lo, block), 0) + lo
            query = lax.broadcasted_iota(jnp.int32, (hi - lo, block), 1) + i * block
            same = col_ref[lo:hi, :] == row_ref[0, :, i * block : hi]
            mask = jnp.where(same & (key <= query), 0.0, -jnp.inf)
            mask_ref[i, 0 : hi - lo, 0:block] = mask
            mask_ref[i, 0 : hi - lo, block:] = mask

    low = lax.broadcasted_iota(jnp.int32, (1, LANES), 1) < 64
    eighth = jnp.asarray(0.125, bf16)
    zero = jnp.zeros((), bf16)
    keys, values, grads = k_ref[...], v_ref[...], do_ref[...]
    queries = q_ref[...] * eighth
    keys_t, values_t = (keys * eighth).T, values.T

    def both(part):
        return jnp.concatenate([jnp.where(low, part, zero), jnp.where(low, zero, part)], axis=0)

    def unstack(part):
        return jnp.concatenate([part[0:64, 0:block], part[64:, block:]], axis=0).T

    dk_acc[...] = jnp.zeros_like(dk_acc)
    dv_acc[...] = jnp.zeros_like(dv_acc)
    q_sum = jnp.zeros((8, LANES), f32)
    for i in range(steps):
        lo, hi = reach(i)
        here = slice(i * block, hi)
        q2, do2 = both(queries[here]), both(grads[here])
        scores = mm(keys[lo:hi], q2, NT) + mask_ref[i, 0 : hi - lo, :]
        raised = jnp.exp(scores - jnp.max(scores, axis=0, keepdims=True))
        soft = raised * (1.0 / jnp.sum(raised, axis=0, keepdims=True))
        d_soft = mm(values[lo:hi], do2, NT)
        inner = jnp.sum(soft * d_soft, axis=0, keepdims=True)
        soft_low = soft.astype(bf16)
        d_scores = (soft * (d_soft - inner)).astype(bf16)
        g_ref[3, here, :] = unstack(mm(values_t[:, lo:hi], soft_low, NN)).astype(bf16)
        dq = rotate_back(
            unstack(mm(keys_t[:, lo:hi], d_scores, NN)), c_ref[here, :], a_ref[here, :], b_ref[here, :]
        ).astype(bf16)
        g_ref[0, here, :] = dq
        q_sum = q_sum + sub_sum(dq.astype(f32))
        dk_acc[lo:hi, :] += mm(d_scores, q2, NN)
        dv_acc[lo:hi, :] += mm(soft_low, do2, NN)
    dk = rotate_back(dk_acc[...], c_ref[...], a_ref[...], b_ref[...]).astype(bf16)
    dv = dv_acc[...].astype(bf16)
    g_ref[1] = dk
    g_ref[2] = dv
    sum_ref[0] = q_sum
    sum_ref[1] = sub_sum(dk.astype(f32))
    sum_ref[2] = sub_sum(dv.astype(f32))


def attend(segment_ids, q, k, v, do, tables, acts, block=256):
    rows, length = segment_ids.shape
    count, width = q.shape
    block = min(block, length)
    token = pl.BlockSpec((length, LANES), lambda r, h: (r, h))
    table = pl.BlockSpec((length, LANES), lambda r, h: (r, 0))
    return call(
        functools.partial(attend_body, block=block),
        24 * count * length * width,
        24 * count * width,
        grid=(rows, width // LANES),
        input_output_aliases={0: 2},
        in_specs=[
            pl.BlockSpec(memory_space=pl.ANY),
            pl.BlockSpec((length, 1), lambda r, h: (r, 0)),
            pl.BlockSpec((1, 1, length), lambda r, h: (r, 0, 0)),
            token,
            token,
            token,
            token,
            table,
            table,
            table,
        ],
        out_specs=[
            pl.BlockSpec((4, length, LANES), lambda r, h: (0, r, h)),
            pl.BlockSpec((3, 8, LANES), lambda r, h: (0, r, h)),
            pl.BlockSpec(memory_space=pl.ANY),
        ],
        out_shape=[
            jax.ShapeDtypeStruct((4, count, width), bf16),
            jax.ShapeDtypeStruct((3, 8 * rows, width), f32),
            jax.ShapeDtypeStruct(acts.shape, acts.dtype),
        ],
        scratch_shapes=[
            pltpu.VMEM((length // block, length, 2 * block), f32),
            pltpu.VMEM((length, LANES), f32),
            pltpu.VMEM((length, LANES), f32),
        ],
    )(
        acts,
        segment_ids.reshape(-1, 1),
        segment_ids.reshape(rows, 1, length),
        q,
        k,
        v,
        do,
        *tables,
    )


def half_grads_body(place_ref, *refs, first, second, steps):
    l1o, l1p, l2o, l2p, r1o, r1p, r2o, r2p, ka_ref, sa_ref, kb_ref, sb_ref, acc = refs
    i = pl.program_id(0)
    y, x = place_ref[1], place_ref[2]
    half = ka_ref.shape[-1]

    @pl.when(i == 0)
    def _():
        acc[...] = jnp.zeros_like(acc)

    for n in range(first + second):
        if n < first:
            part = mm(l1o[0], r1o[n], TN) + mm(l1p[0], r1p[n], TN)
        else:
            part = mm(l2o[n - first], r2o[0], TN) + mm(l2p[n - first], r2p[0], TN)
        acc[n] += part.reshape(acc.shape[1:])

    @pl.when(i == steps - 1)
    def _():
        for n in range(first + second):
            for ref, at in ((ka_ref, x), (sa_ref, 1 - x)):
                ref[n] = acc[n, :, :, at, :, :, :half].astype(ref.dtype)
            for ref, at in ((kb_ref, y), (sb_ref, 1 - y)):
                ref[n] = acc[n, :, at, :, :, :, half:].astype(ref.dtype)


def layers(part, step, lanes, half=False):
    _, first, count = part
    return pl.BlockSpec((count, step, lanes), lambda i, *s: (first // count, i, s[0][3] if half else 0))


def half_grads(place, left_one, left_two, right_one, right_two, shard, after=(), step=256):
    first, second = right_one[2], left_two[2]
    _, count, width = right_two[0][0].shape
    half = width // 2
    blocks = first + second
    steps = count // step
    shape = (blocks, 2, 2, 2, shard, half)
    out = pl.BlockSpec(shape, lambda i, s: (0, 0, 0, 0, 0, 0))
    return call(
        functools.partial(half_grads_body, first=first, second=second, steps=steps),
        blocks * 2 * count * width * width,
        blocks * 4 * count * width,
        after=after,
        grid_spec=pltpu.PrefetchScalarGridSpec(
            num_scalar_prefetch=1,
            grid=(steps,),
            in_specs=[layers(left_one, step, half, True)] * 2
            + [layers(left_two, step, half, True)] * 2
            + [layers(right_one, step, width)] * 2
            + [layers(right_two, step, width)] * 2,
            out_specs=[out] * 4,
            scratch_shapes=[pltpu.VMEM((blocks, 2, 2, 2, 2, shard, width), f32)],
        ),
        out_shape=[jax.ShapeDtypeStruct(shape, k) for k in (f32, bf16, f32, bf16)],
    )(place, *left_one[0], *left_two[0], *right_one[0], *right_two[0])


def full_grads(left_one, left_two, right_one, right_two):
    one = jnp.einsum("td,nte->nde", left_one, right_one, preferred_element_type=f32)
    two = jnp.einsum("ntd,te->nde", left_two, right_two, preferred_element_type=f32)
    return jnp.concatenate([one, two], axis=0)


def gelu_parts(u):
    raised = jnp.exp(-0.5 * (u * u))
    t = 1.0 / (1.0 + (0.3275911 * math.sqrt(0.5)) * jnp.abs(u))
    poly = 1.061405429 * t - 1.453152027
    poly = poly * t + 1.421413741
    poly = poly * t - 0.284496736
    poly = (poly * t + 0.254829592) * t
    tail = 0.5 * poly * raised
    return jnp.where(u < 0, tail, 1.0 - tail), raised * (1.0 / math.sqrt(2.0 * math.pi))


def hidden_body(a2_ref, dy_ref, wu_ref, wd_ref, bu_ref, out_ref, sum_ref):
    u = mm(a2_ref[0], wu_ref[0], NN) + bu_ref[0]
    de = mm(dy_ref[0], wd_ref[0], NT)
    dist, density = gelu_parts(u)
    out_ref[0, 0] = (u * dist).astype(bf16)
    du = (de * (dist + u * density)).astype(bf16)
    out_ref[1, 0] = du
    part = sub_sum(du.astype(f32))

    @pl.when(pl.program_id(1) == 0)
    def _():
        sum_ref[0] = part

    @pl.when(pl.program_id(1) > 0)
    def _():
        sum_ref[0] += part


def hidden(first, blocks, acts, weights, vecs, after=(), step=512):
    _, count, width = acts.shape
    splits = weights.shape[0] // 2
    both, sums = call(
        hidden_body,
        blocks * 4 * count * width * width,
        blocks * (8 * count * width + 4 * width * width),
        after=after,
        grid=(blocks, count // step),
        in_specs=[
            pl.BlockSpec((1, step, width), lambda j, i: (1, i, 0)),
            pl.BlockSpec((1, step, width), lambda j, i: (2, i, 0)),
            pl.BlockSpec((1, width, width), lambda j, i: (first + j, 0, 0)),
            pl.BlockSpec((1, width, width), lambda j, i: (splits + first + j, 0, 0)),
            pl.BlockSpec((1, 1, width), lambda j, i: (8 + first + j, 0, 0)),
        ],
        out_specs=[
            pl.BlockSpec((2, 1, step, width), lambda j, i: (0, j, i, 0)),
            pl.BlockSpec((1, 8, width), lambda j, i: (j, 0, 0)),
        ],
        out_shape=[
            jax.ShapeDtypeStruct((2, blocks, count, width), bf16),
            jax.ShapeDtypeStruct((blocks, 8, width), f32),
        ],
    )(acts, acts, weights, weights, vecs[:, None, :])
    return both.reshape(2 * blocks, count, width), sums


def norm_back(grad, unit, scale, gain):
    grad = grad * gain
    first = jnp.mean(grad, axis=1, keepdims=True)
    second = jnp.mean(grad * unit, axis=1, keepdims=True)
    return scale * (grad - first - unit * second)


def hidden_sum(hidden_refs, w_ref, at, dims, acc):
    for ref in hidden_refs:
        for m in range(ref.shape[0]):
            part = mm(ref[m], w_ref[at], dims)
            acc = part if acc is None else acc + part
            at += 1
    return acc


def output_body(x_ref, o_ref, *refs, splits):
    *e_refs, wo_ref, wm_ref, vec_ref, out_ref = refs
    acc = hidden_sum(e_refs, wm_ref, 0, NN, mm(o_ref[0], wo_ref[0], NN))
    bias = vec_ref[7:8, :] + vec_ref[8 + splits : 9 + splits, :]
    out_ref[...] = (x_ref[...].astype(f32) + acc + bias).astype(bf16)


def resident(blocks, width, at):
    return pl.BlockSpec((blocks, width, width), lambda i: (at, 0, 0), pipeline_mode=pl.Buffered(1))


def output(x, o, es, wa, wm, vecs, after=(), step=256):
    count, width = x.shape
    splits = wm.shape[0] // 2
    token = pl.BlockSpec((step, width), lambda i: (i, 0))
    return call(
        functools.partial(output_body, splits=splits),
        10 * count * width * width,
        14 * count * width + 10 * width * width,
        after=after,
        grid=(count // step,),
        in_specs=[token]
        + [layers(v, step, width) for v in (o, *es)]
        + [resident(1, width, 3), resident(splits, width, 1), pl.BlockSpec(vecs.shape, lambda i: (0, 0))],
        out_specs=token,
        out_shape=jax.ShapeDtypeStruct((count, width), bf16),
    )(x, *[v[0] for v in (o, *es)], wa, wm, vecs)


def normed(x):
    centred = x - jnp.mean(x, axis=1, keepdims=True)
    scale = lax.rsqrt(jnp.mean(centred * centred, axis=1, keepdims=True) + norm_epsilon)
    return centred * scale, scale


def add_sums(sum_ref, sums):
    sums = [sub_sum(t) for t in sums]

    @pl.when(pl.program_id(0) == 0)
    def _():
        for n, s in enumerate(sums):
            sum_ref[n] = s

    @pl.when(pl.program_id(0) > 0)
    def _():
        for n, s in enumerate(sums):
            sum_ref[n] += s


def grad_one_body(x_ref, dy_ref, g_ref, wa_ref, vec_ref, part_ref, sum_ref):
    dy = dy_ref[...].astype(f32)
    grad = mm(g_ref[0], wa_ref[0], NT) + mm(g_ref[1], wa_ref[1], NT) + mm(g_ref[2], wa_ref[2], NT)
    unit, scale = normed(x_ref[...].astype(f32))
    part_ref[...] = dy + norm_back(grad, unit, scale, vec_ref[0:1, :])
    add_sums(sum_ref, (grad * unit, grad, dy))


def grad_one(x, dy, g, wa, vecs, after=(), step=256):
    count, width = x.shape
    token = pl.BlockSpec((step, width), lambda i: (i, 0))
    return call(
        grad_one_body,
        6 * count * width * width,
        14 * count * width + 6 * width * width,
        after=after,
        grid=(count // step,),
        in_specs=[
            token,
            token,
            layers(g, step, width),
            resident(3, width, 0),
            pl.BlockSpec(vecs.shape, lambda i: (0, 0)),
        ],
        out_specs=[token, pl.BlockSpec((3, 8, width), lambda i: (0, 0, 0))],
        out_shape=[jax.ShapeDtypeStruct((count, width), f32), jax.ShapeDtypeStruct((3, 8, width), f32)],
    )(x, dy, g[0], wa, vecs)


def grad_two_body(x_ref, part_ref, *refs):
    *du_refs, wm_ref, vec_ref, grad_ref, sum_ref = refs
    grad = hidden_sum(du_refs, wm_ref, 0, NT, None)
    unit, scale = normed(x_ref[...].astype(f32))
    grad_ref[...] = (part_ref[...] + norm_back(grad, unit, scale, vec_ref[2:3, :])).astype(bf16)
    add_sums(sum_ref, (grad * unit, grad))


def grad_two(x, part, dus, wm, vecs, after=(), step=256):
    count, width = x.shape
    splits = wm.shape[0] // 2
    token = pl.BlockSpec((step, width), lambda i: (i, 0))
    return call(
        grad_two_body,
        8 * count * width * width,
        16 * count * width + 8 * width * width,
        after=after,
        grid=(count // step,),
        in_specs=[token, token]
        + [layers(v, step, width) for v in dus]
        + [resident(splits, width, 0), pl.BlockSpec(vecs.shape, lambda i: (0, 0))],
        out_specs=[token, pl.BlockSpec((2, 8, width), lambda i: (0, 0, 0))],
        out_shape=[jax.ShapeDtypeStruct((count, width), bf16), jax.ShapeDtypeStruct((2, 8, width), f32)],
    )(x, part, *[v[0] for v in dus], wm, vecs)


def grid_places():
    wide, narrow = lax.axis_index("wide"), lax.axis_index("narrow")
    return wide // 2, wide % 2, narrow // 2, narrow % 2


def to_place(move):
    pairs = []
    for z in range(4):
        for y in range(2):
            for x in range(2):
                for c in range(2):
                    a, b, d, e = move(z, y, x, c)
                    pairs.append((((z * 2 + y) * 2 + x) * 2 + c, ((a * 2 + b) * 2 + d) * 2 + e))
    return pairs


def over_c(value):
    return lax.ppermute(value, AXES, to_place(lambda z, y, x, c: (z, y, x, 1 - c)))


def over_x(value):
    return lax.ppermute(value, AXES, to_place(lambda z, y, x, c: (z, y, 1 - x, c)))


def over_y(value):
    return lax.ppermute(value, AXES, to_place(lambda z, y, x, c: (z, 1 - y, x, c)))


def over_z(value, by):
    return lax.ppermute(value, AXES, to_place(lambda z, y, x, c: ((z + by) % 4, y, x, c)))


def gather_order_body(place_ref, *refs):
    z, y, x, c = place_ref[0], place_ref[1], place_ref[2], place_ref[3]
    out_ref = refs[-1]
    blocks = out_ref.shape[0]
    near = lax.rem(z - pl.program_id(0) + 4, 4) < 2
    for rc in range(2):
        own, by_x, by_y, lower, upper = refs[rc * 5 : rc * 5 + 5]
        at = (y * 2 + x) * 2 + (c ^ rc)
        for n in range(blocks):
            out_ref[n, at] = own[0, n]
            out_ref[n, at ^ 2] = by_x[0, n]
            out_ref[n, at ^ 4] = by_y[0, n]

        @pl.when(near)
        def _(lower=lower, at=at):
            for n in range(blocks):
                out_ref[n, at ^ 6] = lower[0, n]

        @pl.when(jnp.logical_not(near))
        def _(upper=upper, at=at):
            for n in range(blocks):
                out_ref[n, at ^ 6] = upper[0, n]


def gather_staged(place, shards, after=()):
    blocks, shard, width = shards.shape
    own = jnp.stack([shards] + [over_z(shards, s) for s in (1, 2, 3)])
    by_x, by_y = over_x(own), over_y(own)
    lower, upper = over_y(by_x[:2]), over_x(by_y[2:])
    here = [own, by_x, by_y, lower, upper]
    pieces = here + [over_c(v) for v in here]

    def piece(first, count):
        def index(t, s):
            apart = lax.rem(s[0] - t + 4, 4)
            return (jnp.clip(apart - first, 0, count - 1), 0, 0, 0)

        return pl.BlockSpec((1, blocks, shard, width), index)

    weights = call(
        gather_order_body,
        0,
        64 * blocks * shard * width * 2,
        after=after,
        grid_spec=pltpu.PrefetchScalarGridSpec(
            num_scalar_prefetch=1,
            grid=(4,),
            in_specs=([piece(0, 4)] * 3 + [piece(0, 2), piece(2, 2)]) * 2,
            out_specs=pl.BlockSpec((blocks, 8, shard, width), lambda t, s: (0, t, 0, 0)),
        ),
        out_shape=jax.ShapeDtypeStruct((blocks, 32, shard, width), bf16),
    )(place, *pieces)
    return weights.reshape(blocks, width, width)


def chip_pair_body(place_ref, ka_ref, ga_ref, kb_ref, gb_ref, ka2_ref, sa_ref, kb2_ref, sb_ref):
    y, x = place_ref[1], place_ref[2]
    for mine, k_ref, g_ref, k2_ref, s2_ref in (
        (y, ka_ref, ga_ref, ka2_ref, sa_ref),
        (x, kb_ref, gb_ref, kb2_ref, sb_ref),
    ):
        k2_ref[...] = k_ref[:, :, mine] + g_ref[:, :, mine].astype(f32)
        s2_ref[...] = (k_ref[:, :, 1 - mine] + g_ref[:, :, 1 - mine].astype(f32)).astype(bf16)


def plane_body(place_ref, ka_ref, ga_ref, kb_ref, gb_ref, *out_refs):
    half = ka_ref.shape[-1]
    for m, ref in enumerate(out_refs):
        at = place_ref[0] ^ m
        for lo, k_ref, g_ref in ((0, ka_ref, ga_ref), (half, kb_ref, gb_ref)):
            ref[:, :, lo : lo + half] = (k_ref[:, at >> 1, at & 1] + g_ref[:, at >> 1, at & 1].astype(f32)).astype(
                bf16
            )


class Reduction:
    def __init__(self, ka, sa, kb, sb):
        self.made = ka
        self.held = (ka, over_x(sa), kb, over_y(sb))


def advance(place, pairs, planes, after=(), steps=2):
    blocks, *_, shard, half = (pairs + planes)[0].held[0].shape
    shapes = [jax.ShapeDtypeStruct((blocks, 2, 2, shard, half), k) for k in (f32, bf16, f32, bf16)] * len(pairs)
    if planes:
        shapes += [jax.ShapeDtypeStruct((len(planes), blocks, shard, 2 * half), bf16)] * 4
    operands = [v for r in pairs + planes for v in r.held]

    def spec(s, at=0):
        n = len(s.shape)
        block = tuple(d // steps if m == at else d for m, d in enumerate(s.shape))
        return pl.BlockSpec(block, lambda b, p: (0,) * at + (b,) + (0,) * (n - 1 - at))

    def body(place_ref, *refs):
        ins, outs = refs[: len(operands)], refs[len(operands) :]
        for n in range(len(pairs)):
            chip_pair_body(place_ref, *ins[4 * n : 4 * n + 4], *outs[4 * n : 4 * n + 4])
        for n in range(len(planes)):
            m = 4 * (len(pairs) + n)
            plane_body(place_ref, *ins[m : m + 4], *[ref.at[n] for ref in outs[4 * len(pairs) :]])

    outs = call(
        body,
        0,
        sum(v.size * v.dtype.itemsize for v in operands) * 2,
        after=after,
        grid_spec=pltpu.PrefetchScalarGridSpec(
            num_scalar_prefetch=1,
            grid=(steps,),
            in_specs=[spec(v) for v in operands],
            out_specs=[spec(s, n >= 4 * len(pairs)) for n, s in enumerate(shapes)],
        ),
        out_shape=shapes,
    )(place, *operands)
    for n, r in enumerate(pairs):
        ka, sa, kb, sb = outs[4 * n : 4 * n + 4]
        r.made = ka
        r.held = (ka, over_y(sa), kb, over_x(sb))
    terms = []
    for m, v in enumerate(outs[4 * len(pairs) :]):
        planes[0].made = v
        v = v.reshape(-1, shard, 2 * half)
        terms.append(
            lax.ppermute(
                v, AXES, to_place(lambda z, y, x, c, m=m: (2 * c + ((z ^ m) >> 1), y, x, (z ^ m) & 1))
            )
        )
    return terms


def everywhere(value):
    for move in (
        lambda z, y, x, c: (z, y, x, 1 - c),
        lambda z, y, x, c: (z, y, 1 - x, c),
        lambda z, y, x, c: (z, 1 - y, x, c),
        lambda z, y, x, c: (z ^ 1, y, x, c),
        lambda z, y, x, c: (3 - z, y, x, c),
    ):
        value = value + lax.ppermute(value, AXES, to_place(move))
    return value


def pack_body(slot_ref, *refs, orders, per):
    terms, (shard_ref, out_ref, square_ref) = refs[: len(orders) * per], refs[len(orders) * per :]
    total = jnp.zeros(square_ref.shape, f32)
    for n, order in enumerate(orders):
        for m, b in enumerate(order):
            value = terms[n * per][m].astype(f32)
            for t in range(1, per):
                value = value + terms[n * per + t][m].astype(f32)
            shard_ref[b] = value
            total = total + value * value
    square_ref[...] = total

    def one(j, carry):
        b = slot_ref[j]

        @pl.when(b >= 0)
        def _():
            out_ref[j] = shard_ref[jnp.maximum(b, 0)].astype(bf16)

        @pl.when(b < 0)
        def _():
            out_ref[j] = jnp.zeros(out_ref.shape[1:], bf16)

        return carry

    lax.fori_loop(0, out_ref.shape[0], one, 0)


def pack(slots, terms, orders, after=()):
    per = len(terms[0])
    _, shard, width = terms[0][0].shape
    terms = [v for t in terms for v in t]
    vmem = pl.BlockSpec(memory_space=pltpu.VMEM)
    return call(
        functools.partial(pack_body, orders=orders, per=per),
        0,
        sum(v.size * v.dtype.itemsize for v in terms) * 2,
        after=after,
        in_specs=[pl.BlockSpec(memory_space=pltpu.SMEM)] + [vmem] * len(terms),
        out_specs=[vmem] * 3,
        out_shape=[
            jax.ShapeDtypeStruct((sum(map(len, orders)), shard, width), f32),
            jax.ShapeDtypeStruct((slots.shape[0], shard, width), bf16),
            jax.ShapeDtypeStruct((shard, width), f32),
        ],
    )(slots, *terms)


def precondition_body(scale_ref, s_ref, l_ref, r_ref, p_ref, s_low, r_low):
    @pl.when(pl.program_id(0) == 0)
    def _():
        s_low[...] = (s_ref[...].astype(f32) * scale_ref[0]).astype(bf16)
        r_low[...] = r_ref[...].astype(bf16)

    left = mm(l_ref[...].astype(bf16), s_low[...], NN)
    p_ref[...] = (scale_ref[1] * mm(left.astype(bf16), r_low[...], NN)).astype(bf16)


def precondition(scales, block, left, right, step=256):
    width = block.shape[0]
    whole = pl.BlockSpec((width, width), lambda i: (0, 0))
    rows = pl.BlockSpec((step, width), lambda i: (i, 0))
    return call(
        precondition_body,
        4 * width**3,
        12 * width**2,
        grid=(width // step,),
        in_specs=[pl.BlockSpec(memory_space=pltpu.SMEM), whole, rows, whole],
        out_specs=rows,
        out_shape=jax.ShapeDtypeStruct((width, width), bf16),
        scratch_shapes=[pltpu.VMEM((width, width), bf16), pltpu.VMEM((width, width), bf16)],
    )(scales, block, left, right)


def statistics_body(has_ref, scale_ref, s_ref, l_ref, r_ref, nl_ref, nr_ref, s_low, *, step):
    i = pl.program_id(0)
    width = s_ref.shape[0]

    @pl.when(i == 0)
    def _():
        s_low[...] = (s_ref[...].astype(f32) * scale_ref[0]).astype(bf16)

    factor = (1.0 - decay_beta) * (scale_ref[1] * scale_ref[1] / width)
    at = pl.multiple_of(i * step, step)

    @pl.when(has_ref[0] != 0)
    def _():
        nl_ref[...] = decay_beta * l_ref[...] + factor * mm(s_low[pl.ds(at, step), :], s_low[...], NT)
        nr_ref[...] = decay_beta * r_ref[...] + factor * mm(s_low[:, pl.ds(at, step)], s_low[...], TN)

    @pl.when(has_ref[0] == 0)
    def _():
        nl_ref[...] = l_ref[...]
        nr_ref[...] = r_ref[...]


def statistics(has, scales, block, left, right, step=256):
    width = block.shape[0]
    whole = pl.BlockSpec((width, width), lambda i: (0, 0))
    rows = pl.BlockSpec((step, width), lambda i: (i, 0))
    smem = pl.BlockSpec(memory_space=pltpu.SMEM)
    return call(
        functools.partial(statistics_body, step=step),
        4 * width**3,
        18 * width**2,
        grid=(width // step,),
        in_specs=[smem, smem, whole, rows, rows],
        out_specs=[rows, rows],
        out_shape=[jax.ShapeDtypeStruct((width, width), f32)] * 2,
        scratch_shapes=[pltpu.VMEM((width, width), bf16)],
    )(has, scales, block, left, right)


def update_body(owner_ref, factor_ref, p_ref, shard_ref, block_ref, clip_ref, new_ref, copy_ref):
    for b in range(shard_ref.shape[0]):
        clip_ref[b] = shard_ref[b] * factor_ref[0]
        value = block_ref[b] - matrix_rate * p_ref[owner_ref[b]].astype(f32)
        new_ref[b] = value
        copy_ref[b] = value.astype(bf16)


def update(owners, factor, returned, shards, blocks):
    smem, vmem = pl.BlockSpec(memory_space=pltpu.SMEM), pl.BlockSpec(memory_space=pltpu.VMEM)
    return call(
        update_body,
        0,
        returned.size * 2 + shards.size * 18,
        in_specs=[smem, smem, vmem, vmem, vmem],
        out_specs=[vmem] * 3,
        out_shape=[
            jax.ShapeDtypeStruct(shards.shape, f32),
            jax.ShapeDtypeStruct(shards.shape, f32),
            jax.ShapeDtypeStruct(shards.shape, bf16),
        ],
    )(owners, factor, returned, shards, blocks)


def layer_inputs(tokens, dy, vecs):
    values = tokens.astype(f32)
    centred = values - jnp.mean(values, axis=-1, keepdims=True)
    spread = jnp.mean(centred * centred, axis=-1, keepdims=True)
    unit = centred * lax.rsqrt(spread + norm_epsilon)
    norms = [(unit * vecs[n] + vecs[n + 1]).astype(bf16) for n in (0, 2)]
    return jnp.stack([*norms, dy])


def to_all(value):
    return lax.all_to_all(value, AXES, split_axis=0, concat_axis=0, tiled=True)


def per_device(
    tokens,
    segment_ids,
    cotangent,
    blocks,
    vectors,
    stat_left,
    stat_right,
    root_left,
    root_right,
    vec_stat,
    owners,
    *,
    paired,
):
    rows_here, seq_len, width = tokens.shape
    count = rows_here * seq_len
    splits = FF // width
    slot_count = lax.axis_size(AXES)
    my_index = lax.axis_index(AXES)
    shard = width // slot_count
    vec_rows = vectors.shape[0]

    low_blocks, low_vectors = blocks.astype(bf16), vectors.astype(bf16)
    everyone = jnp.broadcast_to(low_vectors.reshape(1, -1), (slot_count, vec_rows * shard))
    vecs = to_all(everyone).reshape(slot_count, vec_rows, shard)
    vecs = vecs.transpose(1, 0, 2).reshape(vec_rows, width).astype(f32)
    mlp_weights = lax.all_gather(low_blocks[4:], AXES, axis=1, tiled=True)

    flat_tokens = tokens.reshape(count, width)
    dy = cotangent.reshape(count, width)
    tables = rotary_tables(segment_ids)
    acts = layer_inputs(flat_tokens, dy, vecs)
    place = jnp.stack(grid_places()).astype(jnp.int32)
    if paired:
        attn_weights = gather_staged(place, low_blocks[:4], after=(*tables, acts))
    else:
        attn_weights = lax.all_gather(low_blocks[:4], AXES, axis=1, tiled=True)

    def pair(v):
        return (v, over_c(v)) if paired else (v, v)

    def pair(v):
        return (v, over_c(v)) if paired else (v, v)

    q, k, v, do = project(acts, attn_weights, vecs, tables)
    og, attn_sums, acts = attend(segment_ids, q, k, v, do, tables, acts)
    half = splits // 2
    orders = [list(range(4))]
    for first in (0, half):
        orders.append([base + first + j for base in (4, 4 + splits) for j in range(half)])
    if paired:
        acts_pair, og_pair = (acts, over_c(acts)), (og, over_c(og))
        dys = (acts_pair, 2, 1)
        ed0, up_sum0 = hidden(0, half, acts, mlp_weights, vecs)
        ed1, up_sum1 = hidden(half, half, acts, mlp_weights, vecs, after=(ed0, acts_pair[1]))
        pairs = [(v, over_c(v)) for v in (ed0, ed1)]
        attn = Reduction(
            *half_grads(place, (acts_pair, 0, 1), (og_pair, 3, 1), (og_pair, 0, 3), dys, shard, after=(ed1,))
        )
        low = Reduction(
            *half_grads(
                place, (acts_pair, 1, 1), (pairs[0], 0, half), (pairs[0], half, half), dys, shard, after=(attn.made,)
            )
        )
        advance(place, [attn], [], after=(low.made,))
        high = Reduction(
            *half_grads(
                place, (acts_pair, 1, 1), (pairs[1], 0, half), (pairs[1], half, half), dys, shard, after=(attn.made,)
            )
        )
        advance(place, [low], [], after=(high.made,))
        es, dus = [(v, 0, half) for v in (ed0, ed1)], [(v, half, half) for v in (ed0, ed1)]
        out = output(flat_tokens, (og, 3, 1), es, attn_weights, mlp_weights, vecs, after=(low.made,))
        terms = [advance(place, [high], [attn, low], after=(out,))]
        part, one_sums = grad_one(flat_tokens, dy, (og, 0, 3), attn_weights, vecs, after=(high.made,))
        terms.append(advance(place, [], [high], after=(part,)))
        orders = [orders[0] + orders[1], orders[2]]
        grad_in, two_sums = grad_two(flat_tokens, part, dus, mlp_weights, vecs, after=(high.made,))
    else:
        ed0, up_sum0 = hidden(0, half, acts, mlp_weights, vecs)
        ed1, up_sum1 = hidden(half, half, acts, mlp_weights, vecs)
        grads = [
            full_grads(acts[0], og[3:], og[:3], dy),
            full_grads(acts[1], ed0[:half], ed0[half:], dy),
            full_grads(acts[1], ed1[:half], ed1[half:], dy),
        ]
        terms = [[lax.psum_scatter(v, AXES, scatter_dimension=1, tiled=True)] for v in grads]
        es, dus = [(v, 0, half) for v in (ed0, ed1)], [(v, half, half) for v in (ed0, ed1)]
        out = output(flat_tokens, (og, 3, 1), es, attn_weights, mlp_weights, vecs)
        part, one_sums = grad_one(flat_tokens, dy, (og, 0, 3), attn_weights, vecs)
        grad_in, two_sums = grad_two(flat_tokens, part, dus, mlp_weights, vecs)
    up_sums = [up_sum0, up_sum1]

    one_sums, two_sums = jnp.sum(one_sums, axis=1), jnp.sum(two_sums, axis=1)
    qkv_sums = jnp.sum(attn_sums, axis=1)
    up_sums = jnp.sum(jnp.concatenate(up_sums, axis=0), axis=1)
    bias_sum = one_sums[2:]
    grad_vectors = jnp.concatenate(
        [one_sums[:2], two_sums, qkv_sums, bias_sum, up_sums, bias_sum], axis=0
    )
    slot_ids = jnp.arange(slot_count, dtype=jnp.int32)
    match = owners[None, :] == slot_ids[:, None]
    slots = jnp.sum(jnp.where(match, jnp.arange(1, owners.shape[0] + 1, dtype=jnp.int32)[None], 0), axis=1) - 1
    has_block = jnp.any(owners == my_index)
    shards, outgoing, squares = pack(slots, terms, orders, after=(grad_in,))
    local = jnp.concatenate([grad_vectors, jnp.sum(squares, axis=0)[None], jnp.zeros((2, width), f32)])
    total = everywhere(local) if paired else lax.psum(local, AXES)
    vector_sums = total[:vec_rows]
    square_sum = jnp.sum(total[vec_rows]) + jnp.sum(vector_sums * vector_sums)
    shard_vectors = lax.dynamic_slice_in_dim(vector_sums, my_index * shard, shard, axis=1)
    grad_norm = jnp.sqrt(square_sum)
    factor = jnp.minimum(1.0, clip_level / grad_norm)
    root_count = math.sqrt(NPARAM)

    scale = factor * root_count
    power = jnp.exp2(jnp.floor(jnp.log2(jnp.maximum(scale, 1e-30)))).astype(bf16).astype(f32)
    scales = jnp.stack([power, scale / power])
    owned = to_all(outgoing).reshape(width, width)
    precond = precondition(scales, owned, root_left[0], root_right[0])
    returned = to_all(precond.reshape(slot_count, shard, width))
    new_left, new_right = statistics(
        has_block.astype(jnp.int32).reshape(1), scales, owned, stat_left[0], stat_right[0]
    )
    clipped_blocks, new_blocks, blocks_copy = update(owners, factor.reshape(1), returned, shards, blocks)
    clipped_vectors = shard_vectors * factor
    scaled_vectors = clipped_vectors * root_count
    new_vec_stat = decay_beta * vec_stat + (1.0 - decay_beta) * (scaled_vectors * scaled_vectors)
    new_vectors = vectors - vector_rate * scaled_vectors * lax.rsqrt(new_vec_stat)
    return (
        out.reshape(tokens.shape),
        grad_in.reshape(tokens.shape),
        clipped_blocks,
        clipped_vectors,
        grad_norm,
        new_left[None],
        new_right[None],
        new_vec_stat,
        new_blocks,
        new_vectors,
        blocks_copy,
        new_vectors.astype(bf16),
    )


def solution(mesh):
    rows = P(AXES, None, None)
    split_rows = P(None, AXES, None)
    split_columns = P(None, AXES)
    paired = dict(mesh.shape) == {"wide": 8, "narrow": 4}
    return jax.shard_map(
        functools.partial(per_device, paired=paired),
        mesh=mesh,
        in_specs=(
            rows, P(AXES, None), rows, split_rows, split_columns,
            rows, rows, rows, rows, split_columns, P(),
        ),
        out_specs=(
            rows, rows, split_rows, split_columns, P(), rows, rows,
            split_columns, split_rows, split_columns, split_rows, split_columns,
        ),
        check_vma=False,
    )
```

```python
import functools
import math

import jax
import jax.numpy as jnp
from jax import lax
from jax.experimental import pallas as pl
from jax.experimental.pallas import tpu as pltpu
from jax.sharding import PartitionSpec as P

H = 12
FF = 3072
ROT = 16
NPARAM = 7087872
LONGEST = 256

clip_level = 1.0
matrix_rate = 0.03
vector_rate = 0.2
decay_beta = 0.5
norm_epsilon = 1e-05

f32 = jnp.float32
bf16 = jnp.bfloat16
AXES = ("wide", "narrow")
LANES = 128
MIB = 2**20

NN = (((1,), (0,)), ((), ()))
NT = (((1,), (1,)), ((), ()))
TN = (((0,), (0,)), ((), ()))


def mm(left, right, dims):
    return lax.dot_general(left, right, dims, preferred_element_type=f32)


def call(body, flops, moved, vmem=60, after=(), **rest):
    spec = rest.pop("grid_spec", None)
    grid = spec.grid if spec is not None else rest.get("grid", ())
    later = len(after)
    if later:
        held = [pl.BlockSpec(memory_space=pl.ANY)] * later
        if spec is not None:
            first = spec.num_scalar_prefetch + len(spec.in_specs)
            spec = pltpu.PrefetchScalarGridSpec(
                num_scalar_prefetch=spec.num_scalar_prefetch,
                grid=spec.grid,
                in_specs=list(spec.in_specs) + held,
                out_specs=spec.out_specs,
                scratch_shapes=spec.scratch_shapes,
            )
        else:
            first = len(rest["in_specs"])
            rest["in_specs"] = list(rest["in_specs"]) + held
        inner = body

        def body(*refs):
            inner(*refs[:first], *refs[first + later :])

    if spec is not None:
        rest["grid_spec"] = spec
    made = pl.pallas_call(
        body,
        compiler_params=pltpu.CompilerParams(
            vmem_limit_bytes=vmem * MIB,
            dimension_semantics=("arbitrary",) * len(grid),
        ),
        cost_estimate=pl.CostEstimate(
            flops=int(flops), bytes_accessed=int(moved), transcendentals=0
        ),
        **rest,
    )
    return lambda *operands: made(*operands, *after)


def sub_sum(values):
    return jnp.sum(values.reshape(-1, 8, values.shape[-1]), axis=0)


def rotary_tables(segment_ids):
    rows, length = segment_ids.shape
    start = jnp.sum(
        (segment_ids[:, None, :] < segment_ids[:, :, None]).astype(jnp.int32), axis=-1
    )
    offset = (jnp.arange(length, dtype=jnp.int32)[None] - start).astype(f32).reshape(-1, 1)
    half = ROT // 2
    lane = jnp.arange(LANES) % 64
    rates = jnp.power(10000.0, -2.0 * jnp.arange(half, dtype=f32) / ROT)
    angle = offset * jnp.where(lane < ROT, rates[lane % half], 0.0)[None]
    cosine, sine = jnp.cos(angle), jnp.sin(angle)
    first = jnp.where(lane[None] < half, -sine, 0.0)
    second = jnp.where((lane[None] >= half) & (lane[None] < ROT), sine, 0.0)
    return cosine, first, second


def rotate(values, cosine, first, second):
    parts = []
    for at in range(0, values.shape[1], LANES):
        part = values[:, at : at + LANES]
        parts.append(
            part * cosine
            + pltpu.roll(part, LANES - ROT // 2, 1) * first
            + pltpu.roll(part, ROT // 2, 1) * second
        )
    return jnp.concatenate(parts, axis=1)


def rotate_back(values, cosine, first, second):
    return (
        values * cosine
        - pltpu.roll(values, LANES - ROT // 2, 1) * first
        - pltpu.roll(values, ROT // 2, 1) * second
    )


def project_body(a1_ref, dy_ref, w_ref, vec_ref, c_ref, a_ref, b_ref, q_ref, k_ref, v_ref, do_ref):
    a1, tables = a1_ref[0], (c_ref[...], a_ref[...], b_ref[...])
    q_ref[...] = rotate(mm(a1, w_ref[0], NN) + vec_ref[4:5, :], *tables).astype(bf16)
    k_ref[...] = rotate(mm(a1, w_ref[1], NN) + vec_ref[5:6, :], *tables).astype(bf16)
    v_ref[...] = (mm(a1, w_ref[2], NN) + vec_ref[6:7, :]).astype(bf16)
    do_ref[...] = mm(dy_ref[0], w_ref[3], NT).astype(bf16)


def project(acts, weights, vecs, tables, step=256):
    _, count, width = acts.shape
    token = pl.BlockSpec((step, width), lambda i: (i, 0))
    table = pl.BlockSpec((step, LANES), lambda i: (i, 0))
    return call(
        project_body,
        8 * count * width * width,
        12 * count * width + 8 * width * width,
        grid=(count // step,),
        in_specs=[
            pl.BlockSpec((1, step, width), lambda i: (0, i, 0)),
            pl.BlockSpec((1, step, width), lambda i: (2, i, 0)),
            pl.BlockSpec((4, width, width), lambda i: (0, 0, 0)),
            pl.BlockSpec(vecs.shape, lambda i: (0, 0)),
            table,
            table,
            table,
        ],
        out_specs=[token] * 4,
        out_shape=[jax.ShapeDtypeStruct((count, width), bf16)] * 4,
    )(acts, acts, weights, vecs, *tables)


def attend_body(
    acts_ref, col_ref, row_ref, q_ref, k_ref, v_ref, do_ref, c_ref, a_ref, b_ref,
    g_ref, sum_ref, acts_out_ref, mask_ref, *, block,
):
    length = q_ref.shape[0]
    steps = length // block

    def reach(i):
        return max(0, (i * block - (LONGEST - 1)) // block * block), (i + 1) * block

    @pl.when(pl.program_id(1) == 0)
    def _():
        for i in range(steps):
            lo, hi = reach(i)
            key = lax.broadcasted_iota(jnp.int32, (hi - lo, block), 0) + lo
            query = lax.broadcasted_iota(jnp.int32, (hi - lo, block), 1) + i * block
            same = col_ref[lo:hi, :] == row_ref[0, :, i * block : hi]
            mask = jnp.where(same & (key <= query), 0.0, -jnp.inf)
            mask_ref[i, 0 : hi - lo, 0:block] = mask
            mask_ref[i, 0 : hi - lo, block:] = mask

    low = lax.broadcasted_iota(jnp.int32, (1, LANES), 1) < 64
    eighth = jnp.asarray(0.125, bf16)
    zero = jnp.zeros((), bf16)

    def both(part):
        return jnp.concatenate([jnp.where(low, part, zero), jnp.where(low, zero, part)], axis=0)

    def unstack(part):
        return jnp.concatenate([part[0:64, 0:block], part[64:, block:]], axis=0).T

    pairs = []
    for at in range(0, q_ref.shape[1], LANES):
        lanes = slice(at, at + LANES)
        keys, values = k_ref[:, lanes], v_ref[:, lanes]
        pairs.append(
            (lanes, keys, values, (keys * eighth).T, values.T, q_ref[:, lanes] * eighth, do_ref[:, lanes])
        )
    q_sums = [jnp.zeros((8, LANES), f32) for _ in pairs]
    dks = [[None] * steps for _ in pairs]
    dvs = [[None] * steps for _ in pairs]

    def add(parts, n, value):
        parts[n] = value if parts[n] is None else parts[n] + value

    for i in range(steps):
        lo, hi = reach(i)
        here = slice(i * block, hi)
        for p, (lanes, keys, values, keys_t, values_t, queries, grads) in enumerate(pairs):
            q2, do2 = both(queries[here]), both(grads[here])
            scores = mm(keys[lo:hi], q2, NT) + mask_ref[i, 0 : hi - lo, :]
            d_soft = mm(values[lo:hi], do2, NT)
            raised = jnp.exp(scores - jnp.max(scores, axis=0, keepdims=True))
            soft = raised * (1.0 / jnp.sum(raised, axis=0, keepdims=True))
            inner = jnp.sum(soft * d_soft, axis=0, keepdims=True)
            soft_low = soft.astype(bf16)
            d_scores = (soft * (d_soft - inner)).astype(bf16)
            g_ref[3, here, lanes] = unstack(mm(values_t[:, lo:hi], soft_low, NN)).astype(bf16)
            dq = rotate_back(
                unstack(mm(keys_t[:, lo:hi], d_scores, NN)), c_ref[here, :], a_ref[here, :], b_ref[here, :]
            ).astype(bf16)
            g_ref[0, here, lanes] = dq
            q_sums[p] = q_sums[p] + sub_sum(dq.astype(f32))
            dk, dv = mm(d_scores, q2, NN), mm(soft_low, do2, NN)
            for n in range(lo // block, i + 1):
                rows = slice(n * block - lo, (n + 1) * block - lo)
                add(dks[p], n, dk[rows])
                add(dvs[p], n, dv[rows])
    for p, (lanes, *_) in enumerate(pairs):
        dk = rotate_back(jnp.concatenate(dks[p], axis=0), c_ref[...], a_ref[...], b_ref[...]).astype(bf16)
        dv = jnp.concatenate(dvs[p], axis=0).astype(bf16)
        g_ref[1, :, lanes] = dk
        g_ref[2, :, lanes] = dv
        sum_ref[0, :, lanes] = q_sums[p]
        sum_ref[1, :, lanes] = sub_sum(dk.astype(f32))
        sum_ref[2, :, lanes] = sub_sum(dv.astype(f32))


def attend(segment_ids, q, k, v, do, tables, acts, block=256, lanes=3 * LANES):
    rows, length = segment_ids.shape
    count, width = q.shape
    block = min(block, length)
    token = pl.BlockSpec((length, lanes), lambda r, h: (r, h))
    table = pl.BlockSpec((length, LANES), lambda r, h: (r, 0))
    return call(
        functools.partial(attend_body, block=block),
        24 * count * length * width,
        24 * count * width,
        grid=(rows, width // lanes),
        input_output_aliases={0: 2},
        in_specs=[
            pl.BlockSpec(memory_space=pl.ANY),
            pl.BlockSpec((length, 1), lambda r, h: (r, 0)),
            pl.BlockSpec((1, 1, length), lambda r, h: (r, 0, 0)),
            token,
            token,
            token,
            token,
            table,
            table,
            table,
        ],
        out_specs=[
            pl.BlockSpec((4, length, lanes), lambda r, h: (0, r, h)),
            pl.BlockSpec((3, 8, lanes), lambda r, h: (0, r, h)),
            pl.BlockSpec(memory_space=pl.ANY),
        ],
        out_shape=[
            jax.ShapeDtypeStruct((4, count, width), bf16),
            jax.ShapeDtypeStruct((3, 8 * rows, width), f32),
            jax.ShapeDtypeStruct(acts.shape, acts.dtype),
        ],
        scratch_shapes=[pltpu.VMEM((length // block, length, 2 * block), f32)],
    )(
        acts,
        segment_ids.reshape(-1, 1),
        segment_ids.reshape(rows, 1, length),
        q,
        k,
        v,
        do,
        *tables,
    )


def half_grads_body(place_ref, *refs, first, second, steps, axes):
    l1o, l1p, l2o, l2p, r1o, r1p, r2o, r2p, *outs, acc = refs
    i = pl.program_id(0)
    y, x = place_ref[1], place_ref[2]

    @pl.when(i == 0)
    def _():
        acc[...] = jnp.zeros_like(acc)

    for n in range(first + second):
        if n < first:
            part = mm(l1o[0], r1o[n], TN) + mm(l1p[0], r1p[n], TN)
        else:
            part = mm(l2o[n - first], r2o[0], TN) + mm(l2p[n - first], r2p[0], TN)
        acc[n] += part.reshape(acc.shape[1:])

    @pl.when(i == steps - 1)
    def _():
        for n in range(first + second):
            for r, axis in enumerate(axes):
                wide = outs[0].shape[-1]
                columns = slice(r * wide, (r + 1) * wide)
                for ref, other in zip(outs[2 * r : 2 * r + 2], (0, 1)):
                    if axis == "x":
                        value = acc[n, :, :, x ^ other, :, :, columns]
                    else:
                        value = acc[n, :, y ^ other, :, :, :, columns]
                    ref[n] = value.astype(bf16)


def layers(part, step, lanes, half=False):
    _, first, count = part
    return pl.BlockSpec((count, step, lanes), lambda i, *s: (first // count, i, s[0][3] if half else 0))


def half_grads(place, left_one, left_two, right_one, right_two, shard, axes, after=(), step=256):
    first, second = right_one[2], left_two[2]
    _, count, width = right_two[0][0].shape
    half = width // 2
    blocks = first + second
    steps = count // step
    shape = (blocks, 2, 2, 2, shard, width // len(axes))
    out = pl.BlockSpec(shape, lambda i, s: (0, 0, 0, 0, 0, 0))
    return call(
        functools.partial(half_grads_body, first=first, second=second, steps=steps, axes=axes),
        blocks * 2 * count * width * width,
        blocks * 4 * count * width,
        after=after,
        grid_spec=pltpu.PrefetchScalarGridSpec(
            num_scalar_prefetch=1,
            grid=(steps,),
            in_specs=[layers(left_one, step, half, True)] * 2
            + [layers(left_two, step, half, True)] * 2
            + [layers(right_one, step, width)] * 2
            + [layers(right_two, step, width)] * 2,
            out_specs=[out] * (2 * len(axes)),
            scratch_shapes=[pltpu.VMEM((blocks, 2, 2, 2, 2, shard, width), f32)],
        ),
        out_shape=[jax.ShapeDtypeStruct(shape, bf16)] * (2 * len(axes)),
    )(place, *left_one[0], *left_two[0], *right_one[0], *right_two[0])


def full_grads(left_one, left_two, right_one, right_two):
    one = jnp.einsum("td,nte->nde", left_one, right_one, preferred_element_type=f32)
    two = jnp.einsum("ntd,te->nde", left_two, right_two, preferred_element_type=f32)
    return jnp.concatenate([one, two], axis=0)


def gelu_parts(u):
    raised = jnp.exp(-0.5 * (u * u))
    t = 1.0 / (1.0 + (0.3275911 * math.sqrt(0.5)) * jnp.abs(u))
    poly = 1.061405429 * t - 1.453152027
    poly = poly * t + 1.421413741
    poly = poly * t - 0.284496736
    poly = (poly * t + 0.254829592) * t
    tail = 0.5 * poly * raised
    return jnp.where(u < 0, tail, 1.0 - tail), raised * (1.0 / math.sqrt(2.0 * math.pi))


def hidden_body(a2_ref, dy_ref, wu_ref, wd_ref, bu_ref, out_ref, sum_ref):
    u = mm(a2_ref[0], wu_ref[0], NN) + bu_ref[0]
    de = mm(dy_ref[0], wd_ref[0], NT)
    dist, density = gelu_parts(u)
    out_ref[0, 0] = (u * dist).astype(bf16)
    du = (de * (dist + u * density)).astype(bf16)
    out_ref[1, 0] = du
    part = sub_sum(du.astype(f32))

    @pl.when(pl.program_id(1) == 0)
    def _():
        sum_ref[0] = part

    @pl.when(pl.program_id(1) > 0)
    def _():
        sum_ref[0] += part


def hidden(first, blocks, acts, weights, vecs, after=(), step=512):
    _, count, width = acts.shape
    splits = weights.shape[0] // 2
    both, sums = call(
        hidden_body,
        blocks * 4 * count * width * width,
        blocks * (8 * count * width + 4 * width * width),
        after=after,
        grid=(blocks, count // step),
        in_specs=[
            pl.BlockSpec((1, step, width), lambda j, i: (1, i, 0)),
            pl.BlockSpec((1, step, width), lambda j, i: (2, i, 0)),
            pl.BlockSpec((1, width, width), lambda j, i: (first + j, 0, 0)),
            pl.BlockSpec((1, width, width), lambda j, i: (splits + first + j, 0, 0)),
            pl.BlockSpec((1, 1, width), lambda j, i: (8 + first + j, 0, 0)),
        ],
        out_specs=[
            pl.BlockSpec((2, 1, step, width), lambda j, i: (0, j, i, 0)),
            pl.BlockSpec((1, 8, width), lambda j, i: (j, 0, 0)),
        ],
        out_shape=[
            jax.ShapeDtypeStruct((2, blocks, count, width), bf16),
            jax.ShapeDtypeStruct((blocks, 8, width), f32),
        ],
    )(acts, acts, weights, weights, vecs[:, None, :])
    return both.reshape(2 * blocks, count, width), sums


def norm_back(grad, unit, scale, gain):
    grad = grad * gain
    first = jnp.mean(grad, axis=1, keepdims=True)
    second = jnp.mean(grad * unit, axis=1, keepdims=True)
    return scale * (grad - first - unit * second)


def hidden_sum(hidden_refs, w_ref, at, dims, acc):
    for ref in hidden_refs:
        for m in range(ref.shape[0]):
            part = mm(ref[m], w_ref[at], dims)
            acc = part if acc is None else acc + part
            at += 1
    return acc


def output_body(x_ref, o_ref, *refs, splits):
    *e_refs, wo_ref, wm_ref, vec_ref, out_ref = refs
    acc = hidden_sum(e_refs, wm_ref, 0, NN, mm(o_ref[0], wo_ref[0], NN))
    bias = vec_ref[7:8, :] + vec_ref[8 + splits : 9 + splits, :]
    out_ref[...] = (x_ref[...].astype(f32) + acc + bias).astype(bf16)


def resident(blocks, width, at):
    return pl.BlockSpec((blocks, width, width), lambda i: (at, 0, 0), pipeline_mode=pl.Buffered(1))


def output(x, o, es, wa, wm, vecs, after=(), step=256):
    count, width = x.shape
    splits = wm.shape[0] // 2
    token = pl.BlockSpec((step, width), lambda i: (i, 0))
    return call(
        functools.partial(output_body, splits=splits),
        10 * count * width * width,
        14 * count * width + 10 * width * width,
        after=after,
        grid=(count // step,),
        in_specs=[token]
        + [layers(v, step, width) for v in (o, *es)]
        + [resident(1, width, 3), resident(splits, width, 1), pl.BlockSpec(vecs.shape, lambda i: (0, 0))],
        out_specs=token,
        out_shape=jax.ShapeDtypeStruct((count, width), bf16),
    )(x, *[v[0] for v in (o, *es)], wa, wm, vecs)


def normed(x):
    centred = x - jnp.mean(x, axis=1, keepdims=True)
    scale = lax.rsqrt(jnp.mean(centred * centred, axis=1, keepdims=True) + norm_epsilon)
    return centred * scale, scale


def add_sums(sum_ref, sums):
    sums = [sub_sum(t) for t in sums]

    @pl.when(pl.program_id(0) == 0)
    def _():
        for n, s in enumerate(sums):
            sum_ref[n] = s

    @pl.when(pl.program_id(0) > 0)
    def _():
        for n, s in enumerate(sums):
            sum_ref[n] += s


def grad_one_body(x_ref, dy_ref, g_ref, wa_ref, vec_ref, part_ref, sum_ref):
    dy = dy_ref[...].astype(f32)
    grad = mm(g_ref[0], wa_ref[0], NT) + mm(g_ref[1], wa_ref[1], NT) + mm(g_ref[2], wa_ref[2], NT)
    unit, scale = normed(x_ref[...].astype(f32))
    part_ref[...] = dy + norm_back(grad, unit, scale, vec_ref[0:1, :])
    add_sums(sum_ref, (grad * unit, grad, dy))


def grad_one(x, dy, g, wa, vecs, after=(), step=256):
    count, width = x.shape
    token = pl.BlockSpec((step, width), lambda i: (i, 0))
    return call(
        grad_one_body,
        6 * count * width * width,
        14 * count * width + 6 * width * width,
        after=after,
        grid=(count // step,),
        in_specs=[
            token,
            token,
            layers(g, step, width),
            resident(3, width, 0),
            pl.BlockSpec(vecs.shape, lambda i: (0, 0)),
        ],
        out_specs=[token, pl.BlockSpec((3, 8, width), lambda i: (0, 0, 0))],
        out_shape=[jax.ShapeDtypeStruct((count, width), f32), jax.ShapeDtypeStruct((3, 8, width), f32)],
    )(x, dy, g[0], wa, vecs)


def grad_two_body(x_ref, part_ref, *refs):
    *du_refs, wm_ref, vec_ref, grad_ref, sum_ref = refs
    grad = hidden_sum(du_refs, wm_ref, 0, NT, None)
    unit, scale = normed(x_ref[...].astype(f32))
    grad_ref[...] = (part_ref[...] + norm_back(grad, unit, scale, vec_ref[2:3, :])).astype(bf16)
    add_sums(sum_ref, (grad * unit, grad))


def grad_two(x, part, dus, wm, vecs, after=(), step=256):
    count, width = x.shape
    splits = wm.shape[0] // 2
    token = pl.BlockSpec((step, width), lambda i: (i, 0))
    return call(
        grad_two_body,
        8 * count * width * width,
        16 * count * width + 8 * width * width,
        after=after,
        grid=(count // step,),
        in_specs=[token, token]
        + [layers(v, step, width) for v in dus]
        + [resident(splits, width, 0), pl.BlockSpec(vecs.shape, lambda i: (0, 0))],
        out_specs=[token, pl.BlockSpec((2, 8, width), lambda i: (0, 0, 0))],
        out_shape=[jax.ShapeDtypeStruct((count, width), bf16), jax.ShapeDtypeStruct((2, 8, width), f32)],
    )(x, part, *[v[0] for v in dus], wm, vecs)


def grid_places():
    wide, narrow = lax.axis_index("wide"), lax.axis_index("narrow")
    return wide // 2, wide % 2, narrow // 2, narrow % 2


def to_place(move):
    pairs = []
    for z in range(4):
        for y in range(2):
            for x in range(2):
                for c in range(2):
                    a, b, d, e = move(z, y, x, c)
                    pairs.append((((z * 2 + y) * 2 + x) * 2 + c, ((a * 2 + b) * 2 + d) * 2 + e))
    return pairs


def over_c(value):
    return lax.ppermute(value, AXES, to_place(lambda z, y, x, c: (z, y, x, 1 - c)))


def over_x(value):
    return lax.ppermute(value, AXES, to_place(lambda z, y, x, c: (z, y, 1 - x, c)))


def over_y(value):
    return lax.ppermute(value, AXES, to_place(lambda z, y, x, c: (z, 1 - y, x, c)))


def over_z(value, by):
    return lax.ppermute(value, AXES, to_place(lambda z, y, x, c: ((z + by) % 4, y, x, c)))


def gather_order_body(place_ref, *refs):
    z, y, x, c = place_ref[0], place_ref[1], place_ref[2], place_ref[3]
    out_ref = refs[-1]
    blocks = out_ref.shape[0]
    near = lax.rem(z - pl.program_id(0) + 4, 4) < 2
    for rc in range(2):
        own, by_x, by_y, lower, upper = refs[rc * 5 : rc * 5 + 5]
        at = (y * 2 + x) * 2 + (c ^ rc)
        for n in range(blocks):
            out_ref[n, at] = own[0, n]
            out_ref[n, at ^ 2] = by_x[0, n]
            out_ref[n, at ^ 4] = by_y[0, n]

        @pl.when(near)
        def _(lower=lower, at=at):
            for n in range(blocks):
                out_ref[n, at ^ 6] = lower[0, n]

        @pl.when(jnp.logical_not(near))
        def _(upper=upper, at=at):
            for n in range(blocks):
                out_ref[n, at ^ 6] = upper[0, n]


def gather_staged(place, shards, after=()):
    blocks, shard, width = shards.shape
    own = jnp.stack([shards] + [over_z(shards, s) for s in (1, 2, 3)])
    by_x, by_y = over_x(own), over_y(own)
    lower, upper = over_y(by_x[:2]), over_x(by_y[2:])
    here = [own, by_x, by_y, lower, upper]
    pieces = here + [over_c(v) for v in here]

    def piece(first, count):
        def index(t, s):
            apart = lax.rem(s[0] - t + 4, 4)
            return (jnp.clip(apart - first, 0, count - 1), 0, 0, 0)

        return pl.BlockSpec((1, blocks, shard, width), index)

    weights = call(
        gather_order_body,
        0,
        64 * blocks * shard * width * 2,
        after=after,
        grid_spec=pltpu.PrefetchScalarGridSpec(
            num_scalar_prefetch=1,
            grid=(4,),
            in_specs=([piece(0, 4)] * 3 + [piece(0, 2), piece(2, 2)]) * 2,
            out_specs=pl.BlockSpec((blocks, 8, shard, width), lambda t, s: (0, t, 0, 0)),
        ),
        out_shape=jax.ShapeDtypeStruct((blocks, 32, shard, width), bf16),
    )(place, *pieces)
    return weights.reshape(blocks, width, width)


class Reduction:
    def __init__(self, axes, made):
        self.axes, self.made = axes, made[0]
        self.held = [
            (keep, over_x(send) if axis == "x" else over_y(send))
            for axis, keep, send in zip(axes, made[::2], made[1::2])
        ]

    def second(self, made):
        self.made = made[0]
        self.held = [
            (keep, over_y(send) if axis == "x" else over_x(send))
            for axis, keep, send in zip(self.axes, made[::2], made[1::2])
        ]


def pair_body(place_ref, r, ins, outs):
    y, x = place_ref[1], place_ref[2]
    for n, axis in enumerate(r.axes):
        keep, got = ins[2 * n : 2 * n + 2]
        for ref, other in zip(outs[2 * n : 2 * n + 2], (0, 1)):
            at = (y if axis == "x" else x) ^ other
            ref[...] = (keep[:, :, at].astype(f32) + got[:, :, at].astype(f32)).astype(bf16)


def plane_body(place_ref, r, ins, outs):
    for m, ref in enumerate(outs):
        at = place_ref[0] ^ m
        for n in range(len(r.axes)):
            keep, got = ins[2 * n : 2 * n + 2]
            wide = keep.shape[-1]
            value = keep[:, at >> 1, at & 1].astype(f32) + got[:, at >> 1, at & 1].astype(f32)
            ref[:, :, n * wide : (n + 1) * wide] = value.astype(bf16)


def advance(place, pairs, planes, after=(), steps=2):
    blocks, *_, shard, wide = (pairs + planes)[0].held[0][0].shape
    width = wide * len((pairs + planes)[0].axes)
    shapes, places = [], []
    for r in pairs:
        shapes += [jax.ShapeDtypeStruct((blocks, 2, 2, shard, width // len(r.axes)), bf16)] * (2 * len(r.axes))
    places += [0] * len(shapes)
    if planes:
        shapes += [jax.ShapeDtypeStruct((len(planes), blocks, shard, width), bf16)] * 4
        places += [1] * 4
    operands = [v for r in pairs + planes for held in r.held for v in held]

    def spec(s, at=0):
        n = len(s.shape)
        block = tuple(d // steps if m == at else d for m, d in enumerate(s.shape))
        return pl.BlockSpec(block, lambda b, p: (0,) * at + (b,) + (0,) * (n - 1 - at))

    def body(place_ref, *refs):
        ins, outs = refs[: len(operands)], refs[len(operands) :]
        for r in pairs:
            count = 2 * len(r.axes)
            pair_body(place_ref, r, ins[:count], outs[:count])
            ins, outs = ins[count:], outs[count:]
        for n, r in enumerate(planes):
            count = 2 * len(r.axes)
            plane_body(place_ref, r, ins[:count], [ref.at[n] for ref in outs])
            ins = ins[count:]

    outs = call(
        body,
        0,
        sum(v.size * v.dtype.itemsize for v in operands) * 2,
        after=after,
        grid_spec=pltpu.PrefetchScalarGridSpec(
            num_scalar_prefetch=1,
            grid=(steps,),
            in_specs=[spec(v) for v in operands],
            out_specs=[spec(s, at) for s, at in zip(shapes, places)],
        ),
        out_shape=shapes,
    )(place, *operands)
    for r in pairs:
        count = 2 * len(r.axes)
        r.second(outs[:count])
        outs = outs[count:]
    terms = []
    for m, v in enumerate(outs):
        for r in planes:
            r.made = v
        v = v.reshape(-1, shard, width)
        terms.append(
            lax.ppermute(
                v, AXES, to_place(lambda z, y, x, c, m=m: (2 * c + ((z ^ m) >> 1), y, x, (z ^ m) & 1))
            )
        )
    return terms


def everywhere(value):
    for move in (
        lambda z, y, x, c: (z, y, x, 1 - c),
        lambda z, y, x, c: (z, y, 1 - x, c),
        lambda z, y, x, c: (z, 1 - y, x, c),
        lambda z, y, x, c: (z ^ 1, y, x, c),
        lambda z, y, x, c: (3 - z, y, x, c),
    ):
        value = value + lax.ppermute(value, AXES, to_place(move))
    return value


def pack_body(slot_ref, *refs, orders, per):
    terms, (shard_ref, out_ref, square_ref) = refs[: len(orders) * per], refs[len(orders) * per :]
    total = jnp.zeros(square_ref.shape, f32)
    for n, order in enumerate(orders):
        for m, b in enumerate(order):
            value = terms[n * per][m].astype(f32)
            for t in range(1, per):
                value = value + terms[n * per + t][m].astype(f32)
            shard_ref[b] = value
            total = total + value * value
    square_ref[...] = total

    def one(j, carry):
        b = slot_ref[j]

        @pl.when(b >= 0)
        def _():
            out_ref[j] = shard_ref[jnp.maximum(b, 0)].astype(bf16)

        @pl.when(b < 0)
        def _():
            out_ref[j] = jnp.zeros(out_ref.shape[1:], bf16)

        return carry

    lax.fori_loop(0, out_ref.shape[0], one, 0)


def pack(slots, terms, orders, after=()):
    per = len(terms[0])
    _, shard, width = terms[0][0].shape
    terms = [v for t in terms for v in t]
    vmem = pl.BlockSpec(memory_space=pltpu.VMEM)
    return call(
        functools.partial(pack_body, orders=orders, per=per),
        0,
        sum(v.size * v.dtype.itemsize for v in terms) * 2,
        after=after,
        in_specs=[pl.BlockSpec(memory_space=pltpu.SMEM)] + [vmem] * len(terms),
        out_specs=[vmem] * 3,
        out_shape=[
            jax.ShapeDtypeStruct((sum(map(len, orders)), shard, width), f32),
            jax.ShapeDtypeStruct((slots.shape[0], shard, width), bf16),
            jax.ShapeDtypeStruct((shard, width), f32),
        ],
    )(slots, *terms)


def to_low_body(l_ref, r_ref, l_low, r_low):
    l_low[...] = l_ref[...].astype(bf16)
    r_low[...] = r_ref[...].astype(bf16)


def to_low(left, right, after=(), step=384):
    width = left.shape[0]
    rows = pl.BlockSpec((step, width), lambda i: (i, 0))
    return call(
        to_low_body,
        0,
        12 * width**2,
        after=after,
        grid=(width // step,),
        in_specs=[rows, rows],
        out_specs=[rows, rows],
        out_shape=[jax.ShapeDtypeStruct((width, width), bf16)] * 2,
    )(left, right)


def precondition_body(scale_ref, s_ref, l_ref, r_ref, p_ref, s_low):
    @pl.when(pl.program_id(0) == 0)
    def _():
        s_low[...] = (s_ref[...].astype(f32) * scale_ref[0]).astype(bf16)

    left = mm(l_ref[...], s_low[...], NN)
    p_ref[...] = (scale_ref[1] * mm(left.astype(bf16), r_ref[...], NN)).astype(bf16)


def precondition(scales, block, left, right, step=384):
    width = block.shape[0]
    whole = pl.BlockSpec((width, width), lambda i: (0, 0))
    rows = pl.BlockSpec((step, width), lambda i: (i, 0))
    return call(
        precondition_body,
        4 * width**3,
        8 * width**2,
        grid=(width // step,),
        in_specs=[pl.BlockSpec(memory_space=pltpu.SMEM), whole, rows, whole],
        out_specs=rows,
        out_shape=jax.ShapeDtypeStruct((width, width), bf16),
        scratch_shapes=[pltpu.VMEM((width, width), bf16)],
    )(scales, block, left, right)


def statistics_body(has_ref, scale_ref, s_ref, l_ref, r_ref, nl_ref, nr_ref, s_low, *, step):
    i = pl.program_id(0)
    width = s_ref.shape[0]

    @pl.when(i == 0)
    def _():
        s_low[...] = (s_ref[...].astype(f32) * scale_ref[0]).astype(bf16)

    factor = (1.0 - decay_beta) * (scale_ref[1] * scale_ref[1] / width)
    at = pl.multiple_of(i * step, step)

    @pl.when(has_ref[0] != 0)
    def _():
        nl_ref[...] = decay_beta * l_ref[...] + factor * mm(s_low[pl.ds(at, step), :], s_low[...], NT)
        nr_ref[...] = decay_beta * r_ref[...] + factor * mm(s_low[:, pl.ds(at, step)], s_low[...], TN)

    @pl.when(has_ref[0] == 0)
    def _():
        nl_ref[...] = l_ref[...]
        nr_ref[...] = r_ref[...]


def statistics(has, scales, block, left, right, step=256):
    width = block.shape[0]
    whole = pl.BlockSpec((width, width), lambda i: (0, 0))
    rows = pl.BlockSpec((step, width), lambda i: (i, 0))
    smem = pl.BlockSpec(memory_space=pltpu.SMEM)
    return call(
        functools.partial(statistics_body, step=step),
        4 * width**3,
        18 * width**2,
        grid=(width // step,),
        in_specs=[smem, smem, whole, rows, rows],
        out_specs=[rows, rows],
        out_shape=[jax.ShapeDtypeStruct((width, width), f32)] * 2,
        scratch_shapes=[pltpu.VMEM((width, width), bf16)],
    )(has, scales, block, left, right)


def update_body(owner_ref, factor_ref, p_ref, shard_ref, block_ref, clip_ref, new_ref, copy_ref):
    for b in range(shard_ref.shape[0]):
        clip_ref[b] = shard_ref[b] * factor_ref[0]
        value = block_ref[b] - matrix_rate * p_ref[owner_ref[b]].astype(f32)
        new_ref[b] = value
        copy_ref[b] = value.astype(bf16)


def update(owners, factor, returned, shards, blocks):
    smem, vmem = pl.BlockSpec(memory_space=pltpu.SMEM), pl.BlockSpec(memory_space=pltpu.VMEM)
    return call(
        update_body,
        0,
        returned.size * 2 + shards.size * 18,
        in_specs=[smem, smem, vmem, vmem, vmem],
        out_specs=[vmem] * 3,
        out_shape=[
            jax.ShapeDtypeStruct(shards.shape, f32),
            jax.ShapeDtypeStruct(shards.shape, f32),
            jax.ShapeDtypeStruct(shards.shape, bf16),
        ],
    )(owners, factor, returned, shards, blocks)


def layer_inputs(tokens, dy, vecs):
    values = tokens.astype(f32)
    centred = values - jnp.mean(values, axis=-1, keepdims=True)
    spread = jnp.mean(centred * centred, axis=-1, keepdims=True)
    unit = centred * lax.rsqrt(spread + norm_epsilon)
    norms = [(unit * vecs[n] + vecs[n + 1]).astype(bf16) for n in (0, 2)]
    return jnp.stack([*norms, dy])


def to_all(value):
    return lax.all_to_all(value, AXES, split_axis=0, concat_axis=0, tiled=True)


def per_device(
    tokens,
    segment_ids,
    cotangent,
    blocks,
    vectors,
    stat_left,
    stat_right,
    root_left,
    root_right,
    vec_stat,
    owners,
    *,
    paired,
):
    rows_here, seq_len, width = tokens.shape
    count = rows_here * seq_len
    splits = FF // width
    slot_count = lax.axis_size(AXES)
    my_index = lax.axis_index(AXES)
    shard = width // slot_count
    vec_rows = vectors.shape[0]

    low_blocks, low_vectors = blocks.astype(bf16), vectors.astype(bf16)
    everyone = jnp.broadcast_to(low_vectors.reshape(1, -1), (slot_count, vec_rows * shard))
    vecs = to_all(everyone).reshape(slot_count, vec_rows, shard)
    vecs = vecs.transpose(1, 0, 2).reshape(vec_rows, width).astype(f32)
    mlp_weights = lax.all_gather(low_blocks[4:], AXES, axis=1, tiled=True)

    flat_tokens = tokens.reshape(count, width)
    dy = cotangent.reshape(count, width)
    tables = rotary_tables(segment_ids)
    acts = layer_inputs(flat_tokens, dy, vecs)
    place = jnp.stack(grid_places()).astype(jnp.int32)
    if paired:
        attn_weights = gather_staged(place, low_blocks[:4], after=(*tables, acts))
    else:
        attn_weights = lax.all_gather(low_blocks[:4], AXES, axis=1, tiled=True)

    def pair(v):
        return (v, over_c(v)) if paired else (v, v)

    def pair(v):
        return (v, over_c(v)) if paired else (v, v)

    q, k, v, do = project(acts, attn_weights, vecs, tables)
    og, attn_sums, acts = attend(segment_ids, q, k, v, do, tables, acts)
    half = splits // 2
    orders = [list(range(4))]
    for first in (0, half):
        orders.append([base + first + j for base in (4, 4 + splits) for j in range(half)])
    if paired:
        acts_pair, og_pair = (acts, over_c(acts)), (og, over_c(og))
        dys = (acts_pair, 2, 1)
        ed0, up_sum0 = hidden(0, half, acts, mlp_weights, vecs)
        ed0_pair = (ed0, over_c(ed0))

        def grads(left, two, one, axes, after):
            operands = ((acts_pair, left, 1), two, one, dys, shard, axes)
            return Reduction(axes, half_grads(place, *operands, after=after))

        attn = grads(0, (og_pair, 3, 1), (og_pair, 0, 3), "x", (ed0,))
        low = grads(1, (ed0_pair, 0, half), (ed0_pair, half, half), "y", (attn.made,))
        ed1, up_sum1 = hidden(half, half, acts, mlp_weights, vecs, after=(low.made,))
        ed1_pair = (ed1, over_c(ed1))
        part, one_sums = grad_one(flat_tokens, dy, (og, 0, 3), attn_weights, vecs, after=(ed1,))
        advance(place, [attn, low], [], after=(part,))
        high = grads(1, (ed1_pair, 0, half), (ed1_pair, half, half), "xy", (low.made,))
        terms = [advance(place, [], [attn, low], after=(high.made,))]
        es, dus = [(v, 0, half) for v in (ed0, ed1)], [(v, half, half) for v in (ed0, ed1)]
        grad_in, two_sums = grad_two(flat_tokens, part, dus, mlp_weights, vecs, after=(low.made,))
        advance(place, [high], [], after=(grad_in,))
        terms.append(advance(place, [], [high]))
        orders = [orders[0] + orders[1], orders[2]]
    else:
        ed0, up_sum0 = hidden(0, half, acts, mlp_weights, vecs)
        ed1, up_sum1 = hidden(half, half, acts, mlp_weights, vecs)
        grads = [
            full_grads(acts[0], og[3:], og[:3], dy),
            full_grads(acts[1], ed0[:half], ed0[half:], dy),
            full_grads(acts[1], ed1[:half], ed1[half:], dy),
        ]
        terms = [[lax.psum_scatter(v, AXES, scatter_dimension=1, tiled=True)] for v in grads]
        es, dus = [(v, 0, half) for v in (ed0, ed1)], [(v, half, half) for v in (ed0, ed1)]
        part, one_sums = grad_one(flat_tokens, dy, (og, 0, 3), attn_weights, vecs)
        grad_in, two_sums = grad_two(flat_tokens, part, dus, mlp_weights, vecs)
    up_sums = [up_sum0, up_sum1]

    one_sums, two_sums = jnp.sum(one_sums, axis=1), jnp.sum(two_sums, axis=1)
    qkv_sums = jnp.sum(attn_sums, axis=1)
    up_sums = jnp.sum(jnp.concatenate(up_sums, axis=0), axis=1)
    bias_sum = one_sums[2:]
    grad_vectors = jnp.concatenate(
        [one_sums[:2], two_sums, qkv_sums, bias_sum, up_sums, bias_sum], axis=0
    )
    slot_ids = jnp.arange(slot_count, dtype=jnp.int32)
    match = owners[None, :] == slot_ids[:, None]
    slots = jnp.sum(jnp.where(match, jnp.arange(1, owners.shape[0] + 1, dtype=jnp.int32)[None], 0), axis=1) - 1
    has_block = jnp.any(owners == my_index)
    shards, outgoing, squares = pack(slots, terms, orders, after=(grad_in,))
    out = output(flat_tokens, (og, 3, 1), es, attn_weights, mlp_weights, vecs, after=(squares,))
    left_low, right_low = to_low(root_left[0], root_right[0], after=(out,))
    local = jnp.concatenate([grad_vectors, jnp.sum(squares, axis=0)[None], jnp.zeros((2, width), f32)])
    total = everywhere(local) if paired else lax.psum(local, AXES)
    vector_sums = total[:vec_rows]
    square_sum = jnp.sum(total[vec_rows]) + jnp.sum(vector_sums * vector_sums)
    shard_vectors = lax.dynamic_slice_in_dim(vector_sums, my_index * shard, shard, axis=1)
    grad_norm = jnp.sqrt(square_sum)
    factor = jnp.minimum(1.0, clip_level / grad_norm)
    root_count = math.sqrt(NPARAM)

    scale = factor * root_count
    power = jnp.exp2(jnp.floor(jnp.log2(jnp.maximum(scale, 1e-30)))).astype(bf16).astype(f32)
    scales = jnp.stack([power, scale / power])
    owned = to_all(outgoing).reshape(width, width)
    precond = precondition(scales, owned, left_low, right_low)
    returned = to_all(precond.reshape(slot_count, shard, width))
    new_left, new_right = statistics(
        has_block.astype(jnp.int32).reshape(1), scales, owned, stat_left[0], stat_right[0]
    )
    clipped_blocks, new_blocks, blocks_copy = update(owners, factor.reshape(1), returned, shards, blocks)
    clipped_vectors = shard_vectors * factor
    scaled_vectors = clipped_vectors * root_count
    new_vec_stat = decay_beta * vec_stat + (1.0 - decay_beta) * (scaled_vectors * scaled_vectors)
    new_vectors = vectors - vector_rate * scaled_vectors * lax.rsqrt(new_vec_stat)
    return (
        out.reshape(tokens.shape),
        grad_in.reshape(tokens.shape),
        clipped_blocks,
        clipped_vectors,
        grad_norm,
        new_left[None],
        new_right[None],
        new_vec_stat,
        new_blocks,
        new_vectors,
        blocks_copy,
        new_vectors.astype(bf16),
    )


def solution(mesh):
    rows = P(AXES, None, None)
    split_rows = P(None, AXES, None)
    split_columns = P(None, AXES)
    paired = dict(mesh.shape) == {"wide": 8, "narrow": 4}
    return jax.shard_map(
        functools.partial(per_device, paired=paired),
        mesh=mesh,
        in_specs=(
            rows, P(AXES, None), rows, split_rows, split_columns,
            rows, rows, rows, rows, split_columns, P(),
        ),
        out_specs=(
            rows, rows, split_rows, split_columns, P(), rows, rows,
            split_columns, split_rows, split_columns, split_rows, split_columns,
        ),
        check_vma=False,
    )
```

```python
import functools
import math

import jax
import jax.numpy as jnp
from jax import lax
from jax.experimental import pallas as pl
from jax.experimental.pallas import tpu as pltpu
from jax.sharding import PartitionSpec as P

H = 12
FF = 3072
ROT = 16
NPARAM = 7087872
LONGEST = 256

clip_level = 1.0
matrix_rate = 0.03
vector_rate = 0.2
decay_beta = 0.5
norm_epsilon = 1e-05

f32 = jnp.float32
bf16 = jnp.bfloat16
AXES = ("wide", "narrow")
LANES = 128
MIB = 2**20

NN = (((1,), (0,)), ((), ()))
NT = (((1,), (1,)), ((), ()))
TN = (((0,), (0,)), ((), ()))


def mm(left, right, dims):
    return lax.dot_general(left, right, dims, preferred_element_type=f32)


def call(body, flops, moved, vmem=60, after=(), **rest):
    spec = rest.pop("grid_spec", None)
    grid = spec.grid if spec is not None else rest.get("grid", ())
    later = len(after)
    if later:
        held = [pl.BlockSpec(memory_space=pl.ANY)] * later
        if spec is not None:
            first = spec.num_scalar_prefetch + len(spec.in_specs)
            spec = pltpu.PrefetchScalarGridSpec(
                num_scalar_prefetch=spec.num_scalar_prefetch,
                grid=spec.grid,
                in_specs=list(spec.in_specs) + held,
                out_specs=spec.out_specs,
                scratch_shapes=spec.scratch_shapes,
            )
        else:
            first = len(rest["in_specs"])
            rest["in_specs"] = list(rest["in_specs"]) + held
        inner = body

        def body(*refs):
            inner(*refs[:first], *refs[first + later :])

    if spec is not None:
        rest["grid_spec"] = spec
    made = pl.pallas_call(
        body,
        compiler_params=pltpu.CompilerParams(
            vmem_limit_bytes=vmem * MIB,
            dimension_semantics=("arbitrary",) * len(grid),
        ),
        cost_estimate=pl.CostEstimate(
            flops=int(flops), bytes_accessed=int(moved), transcendentals=0
        ),
        **rest,
    )
    return lambda *operands: made(*operands, *after)


def sub_sum(values):
    return jnp.sum(values.reshape(-1, 8, values.shape[-1]), axis=0)


def rotary_tables(segment_ids):
    rows, length = segment_ids.shape
    start = jnp.sum(
        (segment_ids[:, None, :] < segment_ids[:, :, None]).astype(jnp.int32), axis=-1
    )
    offset = (jnp.arange(length, dtype=jnp.int32)[None] - start).astype(f32).reshape(-1, 1)
    half = ROT // 2
    lane = jnp.arange(LANES) % 64
    rates = jnp.power(10000.0, -2.0 * jnp.arange(half, dtype=f32) / ROT)
    angle = offset * jnp.where(lane < ROT, rates[lane % half], 0.0)[None]
    cosine, sine = jnp.cos(angle), jnp.sin(angle)
    first = jnp.where(lane[None] < half, -sine, 0.0)
    second = jnp.where((lane[None] >= half) & (lane[None] < ROT), sine, 0.0)
    return cosine, first, second


def rotate(values, cosine, first, second):
    parts = []
    for at in range(0, values.shape[1], LANES):
        part = values[:, at : at + LANES]
        parts.append(
            part * cosine
            + pltpu.roll(part, LANES - ROT // 2, 1) * first
            + pltpu.roll(part, ROT // 2, 1) * second
        )
    return jnp.concatenate(parts, axis=1)


def rotate_back(values, cosine, first, second):
    return (
        values * cosine
        - pltpu.roll(values, LANES - ROT // 2, 1) * first
        - pltpu.roll(values, ROT // 2, 1) * second
    )


def assemble(place_ref, pieces, w_ref):
    z, y, x, c = place_ref[0], place_ref[1], place_ref[2], place_ref[3]
    blocks, rows = w_ref.shape[0], 2 * pieces[0].shape[2]

    def plane(t, carry):
        apart = lax.rem(z - t + 4, 4)

        def put(here, there, at, ry, rx):
            chip = (t * 2 + (y ^ ry)) * 2 + (x ^ rx)
            where = pl.ds(pl.multiple_of(chip * rows, rows), rows)
            for order, wanted in (((here, there), c == 0), ((there, here), c != 0)):

                @pl.when(wanted)
                def _(order=order):
                    for n in range(blocks):
                        w_ref[n, where, :] = jnp.concatenate([ref[at, n] for ref in order], axis=0)

        for m, (ry, rx) in enumerate(((0, 0), (0, 1), (1, 0))):
            put(pieces[m], pieces[5 + m], apart, ry, rx)
        pl.when(apart < 2)(lambda: put(pieces[3], pieces[8], apart, 1, 1))
        pl.when(apart >= 2)(lambda: put(pieces[4], pieces[9], apart - 2, 1, 1))
        return carry

    lax.fori_loop(0, 4, plane, 0)


def project_body(place_ref, x_ref, dy_ref, vec_ref, c_ref, a_ref, b_ref, *refs):
    *pieces, q_ref, k_ref, v_ref, do_ref, acts_ref, w_ref = refs

    @pl.when(pl.program_id(0) == 0)
    def _():
        if len(pieces) > 1:
            assemble(place_ref, pieces, w_ref)
        else:
            w_ref[...] = pieces[0][...]

    unit, _ = normed(x_ref[...].astype(f32))
    a1 = (unit * vec_ref[0:1, :] + vec_ref[1:2, :]).astype(bf16)
    acts_ref[0] = a1
    acts_ref[1] = (unit * vec_ref[2:3, :] + vec_ref[3:4, :]).astype(bf16)
    acts_ref[2] = dy_ref[...]
    tables = (c_ref[...], a_ref[...], b_ref[...])
    q_ref[...] = rotate(mm(a1, w_ref[0], NN) + vec_ref[4:5, :], *tables).astype(bf16)
    k_ref[...] = rotate(mm(a1, w_ref[1], NN) + vec_ref[5:6, :], *tables).astype(bf16)
    v_ref[...] = (mm(a1, w_ref[2], NN) + vec_ref[6:7, :]).astype(bf16)
    do_ref[...] = mm(dy_ref[...], w_ref[3], NT).astype(bf16)


def project(place, x, dy, pieces, vecs, tables, step=256):
    count, width = x.shape
    token = pl.BlockSpec((step, width), lambda i, s: (i, 0))
    table = pl.BlockSpec((step, LANES), lambda i, s: (i, 0))
    once = pl.Buffered(1)
    return call(
        project_body,
        8 * count * width * width,
        20 * count * width + 16 * width * width,
        grid_spec=pltpu.PrefetchScalarGridSpec(
            num_scalar_prefetch=1,
            grid=(count // step,),
            in_specs=[token, token, pl.BlockSpec(vecs.shape, lambda i, s: (0, 0)), table, table, table]
            + [pl.BlockSpec(v.shape, lambda i, s, n=v.ndim: (0,) * n, pipeline_mode=once) for v in pieces],
            out_specs=[token] * 4
            + [
                pl.BlockSpec((3, step, width), lambda i, s: (0, i, 0)),
                pl.BlockSpec((4, width, width), lambda i, s: (0, 0, 0)),
            ],
        ),
        out_shape=[jax.ShapeDtypeStruct((count, width), bf16)] * 4
        + [jax.ShapeDtypeStruct((3, count, width), bf16), jax.ShapeDtypeStruct((4, width, width), bf16)],
    )(place, x, dy, vecs, *tables, *pieces)


def attend_body(
    acts_ref, col_ref, row_ref, q_ref, k_ref, v_ref, do_ref, c_ref, a_ref, b_ref,
    g_ref, sum_ref, acts_out_ref, mask_ref, *, block,
):
    length = q_ref.shape[0]
    steps = length // block

    def reach(i):
        return max(0, (i * block - (LONGEST - 1)) // block * block), (i + 1) * block

    @pl.when(pl.program_id(1) == 0)
    def _():
        for i in range(steps):
            lo, hi = reach(i)
            key = lax.broadcasted_iota(jnp.int32, (hi - lo, block), 0) + lo
            query = lax.broadcasted_iota(jnp.int32, (hi - lo, block), 1) + i * block
            same = col_ref[lo:hi, :] == row_ref[0, :, i * block : hi]
            mask = jnp.where(same & (key <= query), 0.0, -jnp.inf)
            mask_ref[i, 0 : hi - lo, 0:block] = mask
            mask_ref[i, 0 : hi - lo, block:] = mask

    low = lax.broadcasted_iota(jnp.int32, (1, LANES), 1) < 64
    eighth = jnp.asarray(0.125, bf16)
    zero = jnp.zeros((), bf16)

    def both(part):
        return jnp.concatenate([jnp.where(low, part, zero), jnp.where(low, zero, part)], axis=0)

    def unstack(part):
        return jnp.concatenate([part[0:64, 0:block], part[64:, block:]], axis=0).T

    pairs = []
    for at in range(0, q_ref.shape[1], LANES):
        lanes = slice(at, at + LANES)
        keys, values = k_ref[:, lanes], v_ref[:, lanes]
        pairs.append(
            (lanes, keys, values, (keys * eighth).T, values.T, q_ref[:, lanes] * eighth, do_ref[:, lanes])
        )
    q_sums = [jnp.zeros((8, LANES), f32) for _ in pairs]
    dks = [[None] * steps for _ in pairs]
    dvs = [[None] * steps for _ in pairs]

    def add(parts, n, value):
        parts[n] = value if parts[n] is None else parts[n] + value

    for i in range(steps):
        lo, hi = reach(i)
        here = slice(i * block, hi)
        for p, (lanes, keys, values, keys_t, values_t, queries, grads) in enumerate(pairs):
            q2, do2 = both(queries[here]), both(grads[here])
            scores = mm(keys[lo:hi], q2, NT) + mask_ref[i, 0 : hi - lo, :]
            d_soft = mm(values[lo:hi], do2, NT)
            raised = jnp.exp(scores - jnp.max(scores, axis=0, keepdims=True))
            soft = raised * (1.0 / jnp.sum(raised, axis=0, keepdims=True))
            inner = jnp.sum(soft * d_soft, axis=0, keepdims=True)
            soft_low = soft.astype(bf16)
            d_scores = (soft * (d_soft - inner)).astype(bf16)
            g_ref[3, here, lanes] = unstack(mm(values_t[:, lo:hi], soft_low, NN)).astype(bf16)
            dq = rotate_back(
                unstack(mm(keys_t[:, lo:hi], d_scores, NN)), c_ref[here, :], a_ref[here, :], b_ref[here, :]
            ).astype(bf16)
            g_ref[0, here, lanes] = dq
            q_sums[p] = q_sums[p] + sub_sum(dq.astype(f32))
            dk, dv = mm(d_scores, q2, NN), mm(soft_low, do2, NN)
            for n in range(lo // block, i + 1):
                rows = slice(n * block - lo, (n + 1) * block - lo)
                add(dks[p], n, dk[rows])
                add(dvs[p], n, dv[rows])
    for p, (lanes, *_) in enumerate(pairs):
        dk = rotate_back(jnp.concatenate(dks[p], axis=0), c_ref[...], a_ref[...], b_ref[...]).astype(bf16)
        dv = jnp.concatenate(dvs[p], axis=0).astype(bf16)
        g_ref[1, :, lanes] = dk
        g_ref[2, :, lanes] = dv
        sum_ref[0, :, lanes] = q_sums[p]
        sum_ref[1, :, lanes] = sub_sum(dk.astype(f32))
        sum_ref[2, :, lanes] = sub_sum(dv.astype(f32))


def attend(segment_ids, q, k, v, do, tables, acts, block=256, lanes=3 * LANES):
    rows, length = segment_ids.shape
    count, width = q.shape
    block = min(block, length)
    token = pl.BlockSpec((length, lanes), lambda r, h: (r, h))
    table = pl.BlockSpec((length, LANES), lambda r, h: (r, 0))
    return call(
        functools.partial(attend_body, block=block),
        24 * count * length * width,
        24 * count * width,
        grid=(rows, width // lanes),
        input_output_aliases={0: 2},
        in_specs=[
            pl.BlockSpec(memory_space=pl.ANY),
            pl.BlockSpec((length, 1), lambda r, h: (r, 0)),
            pl.BlockSpec((1, 1, length), lambda r, h: (r, 0, 0)),
            token,
            token,
            token,
            token,
            table,
            table,
            table,
        ],
        out_specs=[
            pl.BlockSpec((4, length, lanes), lambda r, h: (0, r, h)),
            pl.BlockSpec((3, 8, lanes), lambda r, h: (0, r, h)),
            pl.BlockSpec(memory_space=pl.ANY),
        ],
        out_shape=[
            jax.ShapeDtypeStruct((4, count, width), bf16),
            jax.ShapeDtypeStruct((3, 8 * rows, width), f32),
            jax.ShapeDtypeStruct(acts.shape, acts.dtype),
        ],
        scratch_shapes=[pltpu.VMEM((length // block, length, 2 * block), f32)],
    )(
        acts,
        segment_ids.reshape(-1, 1),
        segment_ids.reshape(rows, 1, length),
        q,
        k,
        v,
        do,
        *tables,
    )


def half_grads_body(place_ref, *refs, first, second, steps, axes):
    l1o, l1p, l2o, l2p, r1o, r1p, r2o, r2p, *outs, acc = refs
    i = pl.program_id(0)
    y, x = place_ref[1], place_ref[2]

    @pl.when(i == 0)
    def _():
        acc[...] = jnp.zeros_like(acc)

    for n in range(first + second):
        if n < first:
            part = mm(l1o[0], r1o[n], TN) + mm(l1p[0], r1p[n], TN)
        else:
            part = mm(l2o[n - first], r2o[0], TN) + mm(l2p[n - first], r2p[0], TN)
        acc[n] += part.reshape(acc.shape[1:])

    @pl.when(i == steps - 1)
    def _():
        for n in range(first + second):
            for r, axis in enumerate(axes):
                wide = outs[0].shape[-1]
                columns = slice(r * wide, (r + 1) * wide)
                for ref, other in zip(outs[2 * r : 2 * r + 2], (0, 1)):
                    if axis == "x":
                        value = acc[n, :, :, x ^ other, :, :, columns]
                    else:
                        value = acc[n, :, y ^ other, :, :, :, columns]
                    ref[n] = value.astype(bf16)


def layers(part, step, lanes, half=False):
    _, first, count = part
    return pl.BlockSpec((count, step, lanes), lambda i, *s: (first // count, i, s[0][3] if half else 0))


def half_grads(place, left_one, left_two, right_one, right_two, shard, axes, after=(), step=256):
    first, second = right_one[2], left_two[2]
    _, count, width = right_two[0][0].shape
    half = width // 2
    blocks = first + second
    steps = count // step
    shape = (blocks, 2, 2, 2, shard, width // len(axes))
    out = pl.BlockSpec(shape, lambda i, s: (0, 0, 0, 0, 0, 0))
    return call(
        functools.partial(half_grads_body, first=first, second=second, steps=steps, axes=axes),
        blocks * 2 * count * width * width,
        blocks * 4 * count * width,
        after=after,
        grid_spec=pltpu.PrefetchScalarGridSpec(
            num_scalar_prefetch=1,
            grid=(steps,),
            in_specs=[layers(left_one, step, half, True)] * 2
            + [layers(left_two, step, half, True)] * 2
            + [layers(right_one, step, width)] * 2
            + [layers(right_two, step, width)] * 2,
            out_specs=[out] * (2 * len(axes)),
            scratch_shapes=[pltpu.VMEM((blocks, 2, 2, 2, 2, shard, width), f32)],
        ),
        out_shape=[jax.ShapeDtypeStruct(shape, bf16)] * (2 * len(axes)),
    )(place, *left_one[0], *left_two[0], *right_one[0], *right_two[0])


def full_grads(left_one, left_two, right_one, right_two):
    one = jnp.einsum("td,nte->nde", left_one, right_one, preferred_element_type=f32)
    two = jnp.einsum("ntd,te->nde", left_two, right_two, preferred_element_type=f32)
    return jnp.concatenate([one, two], axis=0)


def gelu_parts(u):
    raised = jnp.exp(-0.5 * (u * u))
    t = 1.0 / (1.0 + (0.3275911 * math.sqrt(0.5)) * jnp.abs(u))
    poly = 1.061405429 * t - 1.453152027
    poly = poly * t + 1.421413741
    poly = poly * t - 0.284496736
    poly = (poly * t + 0.254829592) * t
    tail = 0.5 * poly * raised
    return jnp.where(u < 0, tail, 1.0 - tail), raised * (1.0 / math.sqrt(2.0 * math.pi))


def hidden_body(a2_ref, dy_ref, wu_ref, wd_ref, bu_ref, out_ref, sum_ref):
    u = mm(a2_ref[0], wu_ref[0], NN) + bu_ref[0]
    de = mm(dy_ref[0], wd_ref[0], NT)
    dist, density = gelu_parts(u)
    out_ref[0, 0] = (u * dist).astype(bf16)
    du = (de * (dist + u * density)).astype(bf16)
    out_ref[1, 0] = du
    part = sub_sum(du.astype(f32))

    @pl.when(pl.program_id(1) == 0)
    def _():
        sum_ref[0] = part

    @pl.when(pl.program_id(1) > 0)
    def _():
        sum_ref[0] += part


def hidden(first, blocks, acts, weights, vecs, after=(), step=512):
    _, count, width = acts.shape
    splits = weights.shape[0] // 2
    both, sums = call(
        hidden_body,
        blocks * 4 * count * width * width,
        blocks * (8 * count * width + 4 * width * width),
        after=after,
        grid=(blocks, count // step),
        in_specs=[
            pl.BlockSpec((1, step, width), lambda j, i: (1, i, 0)),
            pl.BlockSpec((1, step, width), lambda j, i: (2, i, 0)),
            pl.BlockSpec((1, width, width), lambda j, i: (first + j, 0, 0)),
            pl.BlockSpec((1, width, width), lambda j, i: (splits + first + j, 0, 0)),
            pl.BlockSpec((1, 1, width), lambda j, i: (8 + first + j, 0, 0)),
        ],
        out_specs=[
            pl.BlockSpec((2, 1, step, width), lambda j, i: (0, j, i, 0)),
            pl.BlockSpec((1, 8, width), lambda j, i: (j, 0, 0)),
        ],
        out_shape=[
            jax.ShapeDtypeStruct((2, blocks, count, width), bf16),
            jax.ShapeDtypeStruct((blocks, 8, width), f32),
        ],
    )(acts, acts, weights, weights, vecs[:, None, :])
    return both.reshape(2 * blocks, count, width), sums


def norm_back(grad, unit, scale, gain):
    grad = grad * gain
    first = jnp.mean(grad, axis=1, keepdims=True)
    second = jnp.mean(grad * unit, axis=1, keepdims=True)
    return scale * (grad - first - unit * second)


def hidden_sum(hidden_refs, w_ref, at, dims, acc):
    for ref in hidden_refs:
        for m in range(ref.shape[0]):
            part = mm(ref[m], w_ref[at], dims)
            acc = part if acc is None else acc + part
            at += 1
    return acc


def output_body(x_ref, o_ref, *refs, splits):
    *e_refs, wo_ref, wm_ref, vec_ref, out_ref = refs
    acc = hidden_sum(e_refs, wm_ref, 0, NN, mm(o_ref[0], wo_ref[0], NN))
    bias = vec_ref[7:8, :] + vec_ref[8 + splits : 9 + splits, :]
    out_ref[...] = (x_ref[...].astype(f32) + acc + bias).astype(bf16)


def resident(blocks, width, at):
    return pl.BlockSpec((blocks, width, width), lambda i: (at, 0, 0), pipeline_mode=pl.Buffered(1))


def output(x, o, es, wa, wm, vecs, after=(), step=256):
    count, width = x.shape
    splits = wm.shape[0] // 2
    token = pl.BlockSpec((step, width), lambda i: (i, 0))
    return call(
        functools.partial(output_body, splits=splits),
        10 * count * width * width,
        14 * count * width + 10 * width * width,
        after=after,
        grid=(count // step,),
        in_specs=[token]
        + [layers(v, step, width) for v in (o, *es)]
        + [resident(1, width, 3), resident(splits, width, 1), pl.BlockSpec(vecs.shape, lambda i: (0, 0))],
        out_specs=token,
        out_shape=jax.ShapeDtypeStruct((count, width), bf16),
    )(x, *[v[0] for v in (o, *es)], wa, wm, vecs)


def normed(x):
    centred = x - jnp.mean(x, axis=1, keepdims=True)
    scale = lax.rsqrt(jnp.mean(centred * centred, axis=1, keepdims=True) + norm_epsilon)
    return centred * scale, scale


def add_sums(sum_ref, sums):
    sums = [sub_sum(t) for t in sums]

    @pl.when(pl.program_id(0) == 0)
    def _():
        for n, s in enumerate(sums):
            sum_ref[n] = s

    @pl.when(pl.program_id(0) > 0)
    def _():
        for n, s in enumerate(sums):
            sum_ref[n] += s


def grad_one_body(x_ref, dy_ref, g_ref, wa_ref, vec_ref, part_ref, sum_ref):
    dy = dy_ref[...].astype(f32)
    grad = mm(g_ref[0], wa_ref[0], NT) + mm(g_ref[1], wa_ref[1], NT) + mm(g_ref[2], wa_ref[2], NT)
    unit, scale = normed(x_ref[...].astype(f32))
    part_ref[...] = dy + norm_back(grad, unit, scale, vec_ref[0:1, :])
    add_sums(sum_ref, (grad * unit, grad, dy))


def grad_one(x, dy, g, wa, vecs, after=(), step=256):
    count, width = x.shape
    token = pl.BlockSpec((step, width), lambda i: (i, 0))
    return call(
        grad_one_body,
        6 * count * width * width,
        14 * count * width + 6 * width * width,
        after=after,
        grid=(count // step,),
        in_specs=[
            token,
            token,
            layers(g, step, width),
            resident(3, width, 0),
            pl.BlockSpec(vecs.shape, lambda i: (0, 0)),
        ],
        out_specs=[token, pl.BlockSpec((3, 8, width), lambda i: (0, 0, 0))],
        out_shape=[jax.ShapeDtypeStruct((count, width), f32), jax.ShapeDtypeStruct((3, 8, width), f32)],
    )(x, dy, g[0], wa, vecs)


def grad_two_body(x_ref, part_ref, *refs):
    *du_refs, wm_ref, vec_ref, grad_ref, sum_ref = refs
    grad = hidden_sum(du_refs, wm_ref, 0, NT, None)
    unit, scale = normed(x_ref[...].astype(f32))
    grad_ref[...] = (part_ref[...] + norm_back(grad, unit, scale, vec_ref[2:3, :])).astype(bf16)
    add_sums(sum_ref, (grad * unit, grad))


def grad_two(x, part, dus, wm, vecs, after=(), step=256):
    count, width = x.shape
    splits = wm.shape[0] // 2
    token = pl.BlockSpec((step, width), lambda i: (i, 0))
    return call(
        grad_two_body,
        8 * count * width * width,
        16 * count * width + 8 * width * width,
        after=after,
        grid=(count // step,),
        in_specs=[token, token]
        + [layers(v, step, width) for v in dus]
        + [resident(splits, width, 0), pl.BlockSpec(vecs.shape, lambda i: (0, 0))],
        out_specs=[token, pl.BlockSpec((2, 8, width), lambda i: (0, 0, 0))],
        out_shape=[jax.ShapeDtypeStruct((count, width), bf16), jax.ShapeDtypeStruct((2, 8, width), f32)],
    )(x, part, *[v[0] for v in dus], wm, vecs)


def grid_places():
    wide, narrow = lax.axis_index("wide"), lax.axis_index("narrow")
    return wide // 2, wide % 2, narrow // 2, narrow % 2


def to_place(move):
    pairs = []
    for z in range(4):
        for y in range(2):
            for x in range(2):
                for c in range(2):
                    a, b, d, e = move(z, y, x, c)
                    pairs.append((((z * 2 + y) * 2 + x) * 2 + c, ((a * 2 + b) * 2 + d) * 2 + e))
    return pairs


def over_c(value):
    return lax.ppermute(value, AXES, to_place(lambda z, y, x, c: (z, y, x, 1 - c)))


def over_x(value):
    return lax.ppermute(value, AXES, to_place(lambda z, y, x, c: (z, y, 1 - x, c)))


def over_y(value):
    return lax.ppermute(value, AXES, to_place(lambda z, y, x, c: (z, 1 - y, x, c)))


def over_z(value, by):
    return lax.ppermute(value, AXES, to_place(lambda z, y, x, c: ((z + by) % 4, y, x, c)))


def gather_staged(shards):
    own = jnp.stack([shards] + [over_z(shards, s) for s in (1, 2, 3)])
    by_x, by_y = over_x(own), over_y(own)
    lower, upper = over_y(by_x[:2]), over_x(by_y[2:])
    here = [own, by_x, by_y, lower, upper]
    return here + [over_c(v) for v in here]


class Reduction:
    def __init__(self, axes, made):
        self.axes, self.made = axes, made[0]
        self.held = [
            (keep, over_x(send) if axis == "x" else over_y(send))
            for axis, keep, send in zip(axes, made[::2], made[1::2])
        ]

    def second(self, made):
        self.made = made[0]
        self.held = [
            (keep, over_y(send) if axis == "x" else over_x(send))
            for axis, keep, send in zip(self.axes, made[::2], made[1::2])
        ]


def pair_body(place_ref, r, ins, outs):
    y, x = place_ref[1], place_ref[2]
    for n, axis in enumerate(r.axes):
        keep, got = ins[2 * n : 2 * n + 2]
        for ref, other in zip(outs[2 * n : 2 * n + 2], (0, 1)):
            at = (y if axis == "x" else x) ^ other
            ref[...] = (keep[:, :, at].astype(f32) + got[:, :, at].astype(f32)).astype(bf16)


def plane_body(place_ref, r, ins, outs):
    for m, ref in enumerate(outs):
        at = place_ref[0] ^ m
        for n in range(len(r.axes)):
            keep, got = ins[2 * n : 2 * n + 2]
            wide = keep.shape[-1]
            value = keep[:, at >> 1, at & 1].astype(f32) + got[:, at >> 1, at & 1].astype(f32)
            ref[:, :, n * wide : (n + 1) * wide] = value.astype(bf16)


def advance(place, pairs, planes, after=(), steps=2):
    blocks, *_, shard, wide = (pairs + planes)[0].held[0][0].shape
    width = wide * len((pairs + planes)[0].axes)
    shapes, places = [], []
    for r in pairs:
        shapes += [jax.ShapeDtypeStruct((blocks, 2, 2, shard, width // len(r.axes)), bf16)] * (2 * len(r.axes))
    places += [0] * len(shapes)
    if planes:
        shapes += [jax.ShapeDtypeStruct((len(planes), blocks, shard, width), bf16)] * 4
        places += [1] * 4
    operands = [v for r in pairs + planes for held in r.held for v in held]

    def spec(s, at=0):
        n = len(s.shape)
        block = tuple(d // steps if m == at else d for m, d in enumerate(s.shape))
        return pl.BlockSpec(block, lambda b, p: (0,) * at + (b,) + (0,) * (n - 1 - at))

    def body(place_ref, *refs):
        ins, outs = refs[: len(operands)], refs[len(operands) :]
        for r in pairs:
            count = 2 * len(r.axes)
            pair_body(place_ref, r, ins[:count], outs[:count])
            ins, outs = ins[count:], outs[count:]
        for n, r in enumerate(planes):
            count = 2 * len(r.axes)
            plane_body(place_ref, r, ins[:count], [ref.at[n] for ref in outs])
            ins = ins[count:]

    outs = call(
        body,
        0,
        sum(v.size * v.dtype.itemsize for v in operands) * 2,
        after=after,
        grid_spec=pltpu.PrefetchScalarGridSpec(
            num_scalar_prefetch=1,
            grid=(steps,),
            in_specs=[spec(v) for v in operands],
            out_specs=[spec(s, at) for s, at in zip(shapes, places)],
        ),
        out_shape=shapes,
    )(place, *operands)
    for r in pairs:
        count = 2 * len(r.axes)
        r.second(outs[:count])
        outs = outs[count:]
    terms = []
    for m, v in enumerate(outs):
        for r in planes:
            r.made = v
        v = v.reshape(-1, shard, width)
        terms.append(
            lax.ppermute(
                v, AXES, to_place(lambda z, y, x, c, m=m: (2 * c + ((z ^ m) >> 1), y, x, (z ^ m) & 1))
            )
        )
    return terms


def everywhere(value):
    for move in (
        lambda z, y, x, c: (z, y, x, 1 - c),
        lambda z, y, x, c: (z, y, 1 - x, c),
        lambda z, y, x, c: (z, 1 - y, x, c),
        lambda z, y, x, c: (z ^ 1, y, x, c),
        lambda z, y, x, c: (3 - z, y, x, c),
    ):
        value = value + lax.ppermute(value, AXES, to_place(move))
    return value


def pack_body(slot_ref, *refs, orders, per):
    terms, (shard_ref, out_ref, square_ref) = refs[: len(orders) * per], refs[len(orders) * per :]
    total = jnp.zeros(square_ref.shape, f32)
    for n, order in enumerate(orders):
        for m, b in enumerate(order):
            value = terms[n * per][m].astype(f32)
            for t in range(1, per):
                value = value + terms[n * per + t][m].astype(f32)
            shard_ref[b] = value
            total = total + value * value
    square_ref[...] = total

    def one(j, carry):
        b = slot_ref[j]

        @pl.when(b >= 0)
        def _():
            out_ref[j] = shard_ref[jnp.maximum(b, 0)].astype(bf16)

        @pl.when(b < 0)
        def _():
            out_ref[j] = jnp.zeros(out_ref.shape[1:], bf16)

        return carry

    lax.fori_loop(0, out_ref.shape[0], one, 0)


def pack(slots, terms, orders, after=()):
    per = len(terms[0])
    _, shard, width = terms[0][0].shape
    terms = [v for t in terms for v in t]
    vmem = pl.BlockSpec(memory_space=pltpu.VMEM)
    return call(
        functools.partial(pack_body, orders=orders, per=per),
        0,
        sum(v.size * v.dtype.itemsize for v in terms) * 2,
        after=after,
        in_specs=[pl.BlockSpec(memory_space=pltpu.SMEM)] + [vmem] * len(terms),
        out_specs=[vmem] * 3,
        out_shape=[
            jax.ShapeDtypeStruct((sum(map(len, orders)), shard, width), f32),
            jax.ShapeDtypeStruct((slots.shape[0], shard, width), bf16),
            jax.ShapeDtypeStruct((shard, width), f32),
        ],
    )(slots, *terms)


def to_low_body(l_ref, r_ref, l_low, r_low):
    l_low[...] = l_ref[...].astype(bf16)
    r_low[...] = r_ref[...].astype(bf16)


def to_low(left, right, after=(), step=384):
    width = left.shape[0]
    rows = pl.BlockSpec((step, width), lambda i: (i, 0))
    return call(
        to_low_body,
        0,
        12 * width**2,
        after=after,
        grid=(width // step,),
        in_specs=[rows, rows],
        out_specs=[rows, rows],
        out_shape=[jax.ShapeDtypeStruct((width, width), bf16)] * 2,
    )(left, right)


def precondition_body(scale_ref, s_ref, l_ref, r_ref, p_ref, s_low):
    @pl.when(pl.program_id(0) == 0)
    def _():
        s_low[...] = (s_ref[...].astype(f32) * scale_ref[0]).astype(bf16)

    left = mm(l_ref[...], s_low[...], NN)
    p_ref[...] = (scale_ref[1] * mm(left.astype(bf16), r_ref[...], NN)).astype(bf16)


def precondition(scales, block, left, right, step=384):
    width = block.shape[0]
    whole = pl.BlockSpec((width, width), lambda i: (0, 0))
    rows = pl.BlockSpec((step, width), lambda i: (i, 0))
    return call(
        precondition_body,
        4 * width**3,
        8 * width**2,
        grid=(width // step,),
        in_specs=[pl.BlockSpec(memory_space=pltpu.SMEM), whole, rows, whole],
        out_specs=rows,
        out_shape=jax.ShapeDtypeStruct((width, width), bf16),
        scratch_shapes=[pltpu.VMEM((width, width), bf16)],
    )(scales, block, left, right)


def statistics_body(has_ref, scale_ref, s_ref, l_ref, r_ref, nl_ref, nr_ref, s_low, *, step):
    i = pl.program_id(0)
    width = s_ref.shape[0]

    @pl.when(i == 0)
    def _():
        s_low[...] = (s_ref[...].astype(f32) * scale_ref[0]).astype(bf16)

    factor = (1.0 - decay_beta) * (scale_ref[1] * scale_ref[1] / width)
    at = pl.multiple_of(i * step, step)

    @pl.when(has_ref[0] != 0)
    def _():
        nl_ref[...] = decay_beta * l_ref[...] + factor * mm(s_low[pl.ds(at, step), :], s_low[...], NT)
        nr_ref[...] = decay_beta * r_ref[...] + factor * mm(s_low[:, pl.ds(at, step)], s_low[...], TN)

    @pl.when(has_ref[0] == 0)
    def _():
        nl_ref[...] = l_ref[...]
        nr_ref[...] = r_ref[...]


def statistics(has, scales, block, left, right, step=256):
    width = block.shape[0]
    whole = pl.BlockSpec((width, width), lambda i: (0, 0))
    rows = pl.BlockSpec((step, width), lambda i: (i, 0))
    smem = pl.BlockSpec(memory_space=pltpu.SMEM)
    return call(
        functools.partial(statistics_body, step=step),
        4 * width**3,
        18 * width**2,
        grid=(width // step,),
        in_specs=[smem, smem, whole, rows, rows],
        out_specs=[rows, rows],
        out_shape=[jax.ShapeDtypeStruct((width, width), f32)] * 2,
        scratch_shapes=[pltpu.VMEM((width, width), bf16)],
    )(has, scales, block, left, right)


def update_body(owner_ref, factor_ref, p_ref, shard_ref, block_ref, clip_ref, new_ref, copy_ref):
    for b in range(shard_ref.shape[0]):
        clip_ref[b] = shard_ref[b] * factor_ref[0]
        value = block_ref[b] - matrix_rate * p_ref[owner_ref[b]].astype(f32)
        new_ref[b] = value
        copy_ref[b] = value.astype(bf16)


def update(owners, factor, returned, shards, blocks):
    smem, vmem = pl.BlockSpec(memory_space=pltpu.SMEM), pl.BlockSpec(memory_space=pltpu.VMEM)
    return call(
        update_body,
        0,
        returned.size * 2 + shards.size * 18,
        in_specs=[smem, smem, vmem, vmem, vmem],
        out_specs=[vmem] * 3,
        out_shape=[
            jax.ShapeDtypeStruct(shards.shape, f32),
            jax.ShapeDtypeStruct(shards.shape, f32),
            jax.ShapeDtypeStruct(shards.shape, bf16),
        ],
    )(owners, factor, returned, shards, blocks)


def to_all(value):
    return lax.all_to_all(value, AXES, split_axis=0, concat_axis=0, tiled=True)


def per_device(
    tokens,
    segment_ids,
    cotangent,
    blocks,
    vectors,
    stat_left,
    stat_right,
    root_left,
    root_right,
    vec_stat,
    owners,
    *,
    paired,
):
    rows_here, seq_len, width = tokens.shape
    count = rows_here * seq_len
    splits = FF // width
    slot_count = lax.axis_size(AXES)
    my_index = lax.axis_index(AXES)
    shard = width // slot_count
    vec_rows = vectors.shape[0]

    low_blocks, low_vectors = blocks.astype(bf16), vectors.astype(bf16)
    everyone = jnp.broadcast_to(low_vectors.reshape(1, -1), (slot_count, vec_rows * shard))
    vecs = to_all(everyone).reshape(slot_count, vec_rows, shard)
    vecs = vecs.transpose(1, 0, 2).reshape(vec_rows, width).astype(f32)
    mlp_weights = lax.all_gather(low_blocks[4:], AXES, axis=1, tiled=True)

    flat_tokens = tokens.reshape(count, width)
    dy = cotangent.reshape(count, width)
    tables = rotary_tables(segment_ids)
    place = jnp.stack(grid_places()).astype(jnp.int32)
    if paired:
        pieces = gather_staged(low_blocks[:4])
    else:
        pieces = [lax.all_gather(low_blocks[:4], AXES, axis=1, tiled=True)]
    q, k, v, do, acts, attn_weights = project(place, flat_tokens, dy, pieces, vecs, tables)
    og, attn_sums, acts = attend(segment_ids, q, k, v, do, tables, acts)
    half = splits // 2
    orders = [list(range(4))]
    for first in (0, half):
        orders.append([base + first + j for base in (4, 4 + splits) for j in range(half)])
    if paired:
        acts_pair, og_pair = (acts, over_c(acts)), (og, over_c(og))
        dys = (acts_pair, 2, 1)
        ed0, up_sum0 = hidden(0, half, acts, mlp_weights, vecs)
        ed0_pair = (ed0, over_c(ed0))
        ed1, up_sum1 = hidden(half, half, acts, mlp_weights, vecs, after=(ed0, acts_pair[1]))
        ed1_pair = (ed1, over_c(ed1))

        def grads(left, two, one, after):
            operands = ((acts_pair, left, 1), two, one, dys, shard, "xy")
            return Reduction("xy", half_grads(place, *operands, after=after))

        attn = grads(0, (og_pair, 3, 1), (og_pair, 0, 3), (ed1,))
        low = grads(1, (ed0_pair, 0, half), (ed0_pair, half, half), (attn.made,))
        advance(place, [attn], [], after=(low.made,))
        high = grads(1, (ed1_pair, 0, half), (ed1_pair, half, half), (attn.made,))
        advance(place, [low], [], after=(high.made,))
        part, one_sums = grad_one(flat_tokens, dy, (og, 0, 3), attn_weights, vecs, after=(low.made,))
        terms = [advance(place, [high], [attn, low], after=(part,))]
        es, dus = [(v, 0, half) for v in (ed0, ed1)], [(v, half, half) for v in (ed0, ed1)]
        grad_in, two_sums = grad_two(flat_tokens, part, dus, mlp_weights, vecs, after=(high.made,))
        terms.append(advance(place, [], [high], after=(grad_in,)))
        orders = [orders[0] + orders[1], orders[2]]
    else:
        ed0, up_sum0 = hidden(0, half, acts, mlp_weights, vecs)
        ed1, up_sum1 = hidden(half, half, acts, mlp_weights, vecs)
        grads = [
            full_grads(acts[0], og[3:], og[:3], dy),
            full_grads(acts[1], ed0[:half], ed0[half:], dy),
            full_grads(acts[1], ed1[:half], ed1[half:], dy),
        ]
        terms = [[lax.psum_scatter(v, AXES, scatter_dimension=1, tiled=True)] for v in grads]
        es, dus = [(v, 0, half) for v in (ed0, ed1)], [(v, half, half) for v in (ed0, ed1)]
        part, one_sums = grad_one(flat_tokens, dy, (og, 0, 3), attn_weights, vecs)
        grad_in, two_sums = grad_two(flat_tokens, part, dus, mlp_weights, vecs)
    up_sums = [up_sum0, up_sum1]

    one_sums, two_sums = jnp.sum(one_sums, axis=1), jnp.sum(two_sums, axis=1)
    qkv_sums = jnp.sum(attn_sums, axis=1)
    up_sums = jnp.sum(jnp.concatenate(up_sums, axis=0), axis=1)
    bias_sum = one_sums[2:]
    grad_vectors = jnp.concatenate(
        [one_sums[:2], two_sums, qkv_sums, bias_sum, up_sums, bias_sum], axis=0
    )
    slot_ids = jnp.arange(slot_count, dtype=jnp.int32)
    match = owners[None, :] == slot_ids[:, None]
    slots = jnp.sum(jnp.where(match, jnp.arange(1, owners.shape[0] + 1, dtype=jnp.int32)[None], 0), axis=1) - 1
    has_block = jnp.any(owners == my_index)
    shards, outgoing, squares = pack(slots, terms, orders, after=(grad_in,))
    out = output(flat_tokens, (og, 3, 1), es, attn_weights, mlp_weights, vecs, after=(squares,))
    left_low, right_low = to_low(root_left[0], root_right[0], after=(out,))
    local = jnp.concatenate([grad_vectors, jnp.sum(squares, axis=0)[None], jnp.zeros((2, width), f32)])
    total = everywhere(local) if paired else lax.psum(local, AXES)
    vector_sums = total[:vec_rows]
    square_sum = jnp.sum(total[vec_rows]) + jnp.sum(vector_sums * vector_sums)
    shard_vectors = lax.dynamic_slice_in_dim(vector_sums, my_index * shard, shard, axis=1)
    grad_norm = jnp.sqrt(square_sum)
    factor = jnp.minimum(1.0, clip_level / grad_norm)
    root_count = math.sqrt(NPARAM)

    scale = factor * root_count
    power = jnp.exp2(jnp.floor(jnp.log2(jnp.maximum(scale, 1e-30)))).astype(bf16).astype(f32)
    scales = jnp.stack([power, scale / power])
    owned = to_all(outgoing).reshape(width, width)
    precond = precondition(scales, owned, left_low, right_low)
    returned = to_all(precond.reshape(slot_count, shard, width))
    new_left, new_right = statistics(
        has_block.astype(jnp.int32).reshape(1), scales, owned, stat_left[0], stat_right[0]
    )
    clipped_blocks, new_blocks, blocks_copy = update(owners, factor.reshape(1), returned, shards, blocks)
    clipped_vectors = shard_vectors * factor
    scaled_vectors = clipped_vectors * root_count
    new_vec_stat = decay_beta * vec_stat + (1.0 - decay_beta) * (scaled_vectors * scaled_vectors)
    new_vectors = vectors - vector_rate * scaled_vectors * lax.rsqrt(new_vec_stat)
    return (
        out.reshape(tokens.shape),
        grad_in.reshape(tokens.shape),
        clipped_blocks,
        clipped_vectors,
        grad_norm,
        new_left[None],
        new_right[None],
        new_vec_stat,
        new_blocks,
        new_vectors,
        blocks_copy,
        new_vectors.astype(bf16),
    )


def solution(mesh):
    rows = P(AXES, None, None)
    split_rows = P(None, AXES, None)
    split_columns = P(None, AXES)
    paired = dict(mesh.shape) == {"wide": 8, "narrow": 4}
    return jax.shard_map(
        functools.partial(per_device, paired=paired),
        mesh=mesh,
        in_specs=(
            rows, P(AXES, None), rows, split_rows, split_columns,
            rows, rows, rows, rows, split_columns, P(),
        ),
        out_specs=(
            rows, rows, split_rows, split_columns, P(), rows, rows,
            split_columns, split_rows, split_columns, split_rows, split_columns,
        ),
        check_vma=False,
    )
```

```python
import functools
import math

import jax
import jax.numpy as jnp
import numpy as np
from jax import lax
from jax.experimental import pallas as pl
from jax.experimental.pallas import tpu as pltpu
from jax.sharding import PartitionSpec as P

H = 12
FF = 3072
ROT = 16
NPARAM = 7087872
LONGEST = 256

clip_level = 1.0
matrix_rate = 0.03
vector_rate = 0.2
decay_beta = 0.5
norm_epsilon = 1e-05

f32 = jnp.float32
bf16 = jnp.bfloat16
AXES = ("wide", "narrow")
LANES = 128
MIB = 2**20

NN = (((1,), (0,)), ((), ()))
NT = (((1,), (1,)), ((), ()))
TN = (((0,), (0,)), ((), ()))


def mm(left, right, dims):
    return lax.dot_general(left, right, dims, preferred_element_type=f32)


def call(body, flops, moved, vmem=63, after=(), **rest):
    spec = rest.pop("grid_spec", None)
    grid = spec.grid if spec is not None else rest.get("grid", ())
    later = len(after)
    if later:
        held = [pl.BlockSpec(memory_space=pl.ANY)] * later
        if spec is not None:
            first = spec.num_scalar_prefetch + len(spec.in_specs)
            spec = pltpu.PrefetchScalarGridSpec(
                num_scalar_prefetch=spec.num_scalar_prefetch,
                grid=spec.grid,
                in_specs=list(spec.in_specs) + held,
                out_specs=spec.out_specs,
                scratch_shapes=spec.scratch_shapes,
            )
        else:
            first = len(rest["in_specs"])
            rest["in_specs"] = list(rest["in_specs"]) + held
        inner = body

        def body(*refs):
            inner(*refs[:first], *refs[first + later :])

    if spec is not None:
        rest["grid_spec"] = spec
    made = pl.pallas_call(
        body,
        compiler_params=pltpu.CompilerParams(
            vmem_limit_bytes=vmem * MIB,
            dimension_semantics=("arbitrary",) * len(grid),
        ),
        cost_estimate=pl.CostEstimate(
            flops=int(flops), bytes_accessed=int(moved), transcendentals=0
        ),
        **rest,
    )
    return lambda *operands: made(*operands, *after)


def sub_sum(values):
    return jnp.sum(values.reshape(-1, 8, values.shape[-1]), axis=0)


def rotary_tables(segment_ids):
    rows, length = segment_ids.shape
    start = jnp.sum(
        (segment_ids[:, None, :] < segment_ids[:, :, None]).astype(jnp.int32), axis=-1
    )
    offset = (jnp.arange(length, dtype=jnp.int32)[None] - start).astype(f32).reshape(-1, 1)
    half = ROT // 2
    lane = np.arange(LANES) % 64
    rates = np.where(lane < ROT, 10000.0 ** (-2.0 * (lane % half) / ROT), 0.0)
    angle = offset * jnp.asarray(rates, f32)[None]
    cosine, sine = jnp.cos(angle), jnp.sin(angle)
    first = sine * jnp.asarray(np.where(lane < half, -1.0, 0.0), f32)[None]
    second = sine * jnp.asarray(np.where((lane >= half) & (lane < ROT), 1.0, 0.0), f32)[None]
    return cosine, first, second


def rotate(values, cosine, first, second):
    parts = []
    for at in range(0, values.shape[1], LANES):
        part = values[:, at : at + LANES]
        parts.append(
            part * cosine
            + pltpu.roll(part, LANES - ROT // 2, 1) * first
            + pltpu.roll(part, ROT // 2, 1) * second
        )
    return jnp.concatenate(parts, axis=1)


def rotate_back(values, cosine, first, second):
    return (
        values * cosine
        - pltpu.roll(values, LANES - ROT // 2, 1) * first
        - pltpu.roll(values, ROT // 2, 1) * second
    )


def assemble(place_ref, pieces, w_ref):
    z, y, x, c = place_ref[0], place_ref[1], place_ref[2], place_ref[3]
    blocks, rows = w_ref.shape[0], 2 * pieces[0].shape[2]

    def plane(t, carry):
        apart = lax.rem(z - t + 4, 4)

        def put(here, there, at, ry, rx):
            chip = (t * 2 + (y ^ ry)) * 2 + (x ^ rx)
            where = pl.ds(pl.multiple_of(chip * rows, rows), rows)
            for order, wanted in (((here, there), c == 0), ((there, here), c != 0)):

                @pl.when(wanted)
                def _(order=order):
                    for n in range(blocks):
                        w_ref[n, where, :] = jnp.concatenate([ref[at, n] for ref in order], axis=0)

        for m, (ry, rx) in enumerate(((0, 0), (0, 1), (1, 0))):
            put(pieces[m], pieces[5 + m], apart, ry, rx)
        pl.when(apart < 2)(lambda: put(pieces[3], pieces[8], apart, 1, 1))
        pl.when(apart >= 2)(lambda: put(pieces[4], pieces[9], apart - 2, 1, 1))
        return carry

    lax.fori_loop(0, 4, plane, 0)


def project_body(place_ref, x_ref, dy_ref, vec_ref, c_ref, a_ref, b_ref, *refs):
    *pieces, q_ref, k_ref, v_ref, do_ref, acts_ref, w_ref = refs

    @pl.when(pl.program_id(0) == 0)
    def _():
        if len(pieces) > 1:
            assemble(place_ref, pieces, w_ref)
        else:
            w_ref[...] = pieces[0][...]

    unit, _ = normed(x_ref[...].astype(f32))
    a1 = (unit * vec_ref[0:1, :] + vec_ref[1:2, :]).astype(bf16)
    acts_ref[0] = a1
    acts_ref[1] = (unit * vec_ref[2:3, :] + vec_ref[3:4, :]).astype(bf16)
    acts_ref[2] = dy_ref[...]
    tables = (c_ref[...], a_ref[...], b_ref[...])
    q_ref[...] = rotate(mm(a1, w_ref[0], NN) + vec_ref[4:5, :], *tables).astype(bf16)
    k_ref[...] = rotate(mm(a1, w_ref[1], NN) + vec_ref[5:6, :], *tables).astype(bf16)
    v_ref[...] = (mm(a1, w_ref[2], NN) + vec_ref[6:7, :]).astype(bf16)
    do_ref[...] = mm(dy_ref[...], w_ref[3], NT).astype(bf16)


def project(place, x, dy, pieces, vecs, tables, step=256):
    count, width = x.shape
    token = pl.BlockSpec((step, width), lambda i, s: (i, 0))
    table = pl.BlockSpec((step, LANES), lambda i, s: (i, 0))
    once = pl.Buffered(1)
    return call(
        project_body,
        8 * count * width * width,
        20 * count * width + 16 * width * width,
        grid_spec=pltpu.PrefetchScalarGridSpec(
            num_scalar_prefetch=1,
            grid=(count // step,),
            in_specs=[token, token, pl.BlockSpec(vecs.shape, lambda i, s: (0, 0)), table, table, table]
            + [pl.BlockSpec(v.shape, lambda i, s, n=v.ndim: (0,) * n, pipeline_mode=once) for v in pieces],
            out_specs=[token] * 4
            + [
                pl.BlockSpec((3, step, width), lambda i, s: (0, i, 0)),
                pl.BlockSpec((4, width, width), lambda i, s: (0, 0, 0)),
            ],
        ),
        out_shape=[jax.ShapeDtypeStruct((count, width), bf16)] * 4
        + [jax.ShapeDtypeStruct((3, count, width), bf16), jax.ShapeDtypeStruct((4, width, width), bf16)],
    )(place, x, dy, vecs, *tables, *pieces)


def attend_body(
    acts_ref, col_ref, row_ref, q_ref, k_ref, v_ref, do_ref, c_ref, a_ref, b_ref,
    g_ref, sum_ref, acts_out_ref, mask_ref, *, block,
):
    length = q_ref.shape[0]
    steps = length // block

    def reach(i):
        return max(0, (i * block - (LONGEST - 1)) // block * block), (i + 1) * block

    @pl.when(pl.program_id(1) == 0)
    def _():
        for i in range(steps):
            lo, hi = reach(i)
            key = lax.broadcasted_iota(jnp.int32, (hi - lo, block), 0) + lo
            query = lax.broadcasted_iota(jnp.int32, (hi - lo, block), 1) + i * block
            same = col_ref[lo:hi, :] == row_ref[0, :, i * block : hi]
            mask = jnp.where(same & (key <= query), 0.0, -jnp.inf)
            mask_ref[i, 0 : hi - lo, 0:block] = mask
            mask_ref[i, 0 : hi - lo, block:] = mask

    low = lax.broadcasted_iota(jnp.int32, (1, LANES), 1) < 64
    eighth = jnp.asarray(0.125, bf16)
    zero = jnp.zeros((), bf16)

    def both(part):
        return jnp.concatenate([jnp.where(low, part, zero), jnp.where(low, zero, part)], axis=0)

    def unstack(part):
        return jnp.concatenate([part[0:64, 0:block], part[64:, block:]], axis=0).T

    pairs = []
    for at in range(0, q_ref.shape[1], LANES):
        lanes = slice(at, at + LANES)
        keys, values = k_ref[:, lanes], v_ref[:, lanes]
        pairs.append(
            (lanes, keys, values, (keys * eighth).T, values.T, q_ref[:, lanes] * eighth, do_ref[:, lanes])
        )
    q_sums = [jnp.zeros((8, LANES), f32) for _ in pairs]
    dks = [[None] * steps for _ in pairs]
    dvs = [[None] * steps for _ in pairs]

    def add(parts, n, value):
        parts[n] = value if parts[n] is None else parts[n] + value

    for i in range(steps):
        lo, hi = reach(i)
        here = slice(i * block, hi)
        for p, (lanes, keys, values, keys_t, values_t, queries, grads) in enumerate(pairs):
            q2, do2 = both(queries[here]), both(grads[here])
            scores = mm(keys[lo:hi], q2, NT) + mask_ref[i, 0 : hi - lo, :]
            d_soft = mm(values[lo:hi], do2, NT)
            raised = jnp.exp(scores - jnp.max(scores, axis=0, keepdims=True))
            soft = raised * (1.0 / jnp.sum(raised, axis=0, keepdims=True))
            inner = jnp.sum(soft * d_soft, axis=0, keepdims=True)
            soft_low = soft.astype(bf16)
            d_scores = (soft * (d_soft - inner)).astype(bf16)
            g_ref[3, here, lanes] = unstack(mm(values_t[:, lo:hi], soft_low, NN)).astype(bf16)
            dq = rotate_back(
                unstack(mm(keys_t[:, lo:hi], d_scores, NN)), c_ref[here, :], a_ref[here, :], b_ref[here, :]
            ).astype(bf16)
            g_ref[0, here, lanes] = dq
            q_sums[p] = q_sums[p] + sub_sum(dq.astype(f32))
            dk, dv = mm(d_scores, q2, NN), mm(soft_low, do2, NN)
            for n in range(lo // block, i + 1):
                rows = slice(n * block - lo, (n + 1) * block - lo)
                add(dks[p], n, dk[rows])
                add(dvs[p], n, dv[rows])
    for p, (lanes, *_) in enumerate(pairs):
        dk = rotate_back(jnp.concatenate(dks[p], axis=0), c_ref[...], a_ref[...], b_ref[...]).astype(bf16)
        dv = jnp.concatenate(dvs[p], axis=0).astype(bf16)
        g_ref[1, :, lanes] = dk
        g_ref[2, :, lanes] = dv
        sum_ref[0, :, lanes] = q_sums[p]
        sum_ref[1, :, lanes] = sub_sum(dk.astype(f32))
        sum_ref[2, :, lanes] = sub_sum(dv.astype(f32))


def attend(segment_ids, q, k, v, do, tables, acts, block=256, lanes=3 * LANES):
    rows, length = segment_ids.shape
    count, width = q.shape
    block = min(block, length)
    token = pl.BlockSpec((length, lanes), lambda r, h: (r, h))
    table = pl.BlockSpec((length, LANES), lambda r, h: (r, 0))
    return call(
        functools.partial(attend_body, block=block),
        24 * count * length * width,
        24 * count * width,
        grid=(rows, width // lanes),
        input_output_aliases={0: 2},
        in_specs=[
            pl.BlockSpec(memory_space=pl.ANY),
            pl.BlockSpec((length, 1), lambda r, h: (r, 0)),
            pl.BlockSpec((1, 1, length), lambda r, h: (r, 0, 0)),
            token,
            token,
            token,
            token,
            table,
            table,
            table,
        ],
        out_specs=[
            pl.BlockSpec((4, length, lanes), lambda r, h: (0, r, h)),
            pl.BlockSpec((3, 8, lanes), lambda r, h: (0, r, h)),
            pl.BlockSpec(memory_space=pl.ANY),
        ],
        out_shape=[
            jax.ShapeDtypeStruct((4, count, width), bf16),
            jax.ShapeDtypeStruct((3, 8 * rows, width), f32),
            jax.ShapeDtypeStruct(acts.shape, acts.dtype),
        ],
        scratch_shapes=[pltpu.VMEM((length // block, length, 2 * block), f32)],
    )(
        acts,
        segment_ids.reshape(-1, 1),
        segment_ids.reshape(rows, 1, length),
        q,
        k,
        v,
        do,
        *tables,
    )


def half_grads_body(place_ref, *refs, first, second, steps, axes):
    l1o, l1p, l2o, l2p, r1o, r1p, r2o, r2p, *outs, acc = refs
    i = pl.program_id(0)
    y, x = place_ref[1], place_ref[2]

    @pl.when(i == 0)
    def _():
        acc[...] = jnp.zeros_like(acc)

    for n in range(first + second):
        if n < first:
            part = mm(l1o[0], r1o[n], TN) + mm(l1p[0], r1p[n], TN)
        else:
            part = mm(l2o[n - first], r2o[0], TN) + mm(l2p[n - first], r2p[0], TN)
        acc[n] += part.reshape(acc.shape[1:])

    @pl.when(i == steps - 1)
    def _():
        for n in range(first + second):
            for r, axis in enumerate(axes):
                wide = outs[0].shape[-1]
                columns = slice(r * wide, (r + 1) * wide)
                for ref, other in zip(outs[2 * r : 2 * r + 2], (0, 1)):
                    if axis == "x":
                        value = acc[n, :, :, x ^ other, :, :, columns]
                    else:
                        value = acc[n, :, y ^ other, :, :, :, columns]
                    ref[n] = value.astype(bf16)


def layers(part, step, lanes, half=False):
    _, first, count = part
    return pl.BlockSpec((count, step, lanes), lambda i, *s: (first // count, i, s[0][3] if half else 0))


def half_grads(place, left_one, left_two, right_one, right_two, shard, axes, after=(), step=256):
    first, second = right_one[2], left_two[2]
    _, count, width = right_two[0][0].shape
    half = width // 2
    blocks = first + second
    steps = count // step
    shape = (blocks, 2, 2, 2, shard, width // len(axes))
    out = pl.BlockSpec(shape, lambda i, s: (0, 0, 0, 0, 0, 0))
    return call(
        functools.partial(half_grads_body, first=first, second=second, steps=steps, axes=axes),
        blocks * 2 * count * width * width,
        blocks * 4 * count * width,
        after=after,
        grid_spec=pltpu.PrefetchScalarGridSpec(
            num_scalar_prefetch=1,
            grid=(steps,),
            in_specs=[layers(left_one, step, half, True)] * 2
            + [layers(left_two, step, half, True)] * 2
            + [layers(right_one, step, width)] * 2
            + [layers(right_two, step, width)] * 2,
            out_specs=[out] * (2 * len(axes)),
            scratch_shapes=[pltpu.VMEM((blocks, 2, 2, 2, 2, shard, width), f32)],
        ),
        out_shape=[jax.ShapeDtypeStruct(shape, bf16)] * (2 * len(axes)),
    )(place, *left_one[0], *left_two[0], *right_one[0], *right_two[0])


def full_grads(left_one, left_two, right_one, right_two):
    one = jnp.einsum("td,nte->nde", left_one, right_one, preferred_element_type=f32)
    two = jnp.einsum("ntd,te->nde", left_two, right_two, preferred_element_type=f32)
    return jnp.concatenate([one, two], axis=0)


def gelu_parts(u):
    raised = jnp.exp(-0.5 * (u * u))
    t = 1.0 / (1.0 + (0.3275911 * math.sqrt(0.5)) * jnp.abs(u))
    poly = 1.061405429 * t - 1.453152027
    poly = poly * t + 1.421413741
    poly = poly * t - 0.284496736
    poly = (poly * t + 0.254829592) * t
    tail = 0.5 * poly * raised
    return jnp.where(u < 0, tail, 1.0 - tail), raised * (1.0 / math.sqrt(2.0 * math.pi))


def hidden_body(a2_ref, dy_ref, wu_ref, wd_ref, bu_ref, out_ref, sum_ref):
    u = mm(a2_ref[0], wu_ref[0], NN) + bu_ref[0]
    de = mm(dy_ref[0], wd_ref[0], NT)
    dist, density = gelu_parts(u)
    out_ref[0, 0] = (u * dist).astype(bf16)
    du = (de * (dist + u * density)).astype(bf16)
    out_ref[1, 0] = du
    part = sub_sum(du.astype(f32))

    @pl.when(pl.program_id(1) == 0)
    def _():
        sum_ref[0] = part

    @pl.when(pl.program_id(1) > 0)
    def _():
        sum_ref[0] += part


def hidden(first, acts, weights, vecs, after=(), step=512):
    _, count, width = acts.shape
    blocks = weights.shape[0] // 2
    both, sums = call(
        hidden_body,
        blocks * 4 * count * width * width,
        blocks * (8 * count * width + 4 * width * width),
        after=after,
        grid=(blocks, count // step),
        in_specs=[
            pl.BlockSpec((1, step, width), lambda j, i: (1, i, 0)),
            pl.BlockSpec((1, step, width), lambda j, i: (2, i, 0)),
            pl.BlockSpec((1, width, width), lambda j, i: (j, 0, 0)),
            pl.BlockSpec((1, width, width), lambda j, i: (blocks + j, 0, 0)),
            pl.BlockSpec((1, 1, width), lambda j, i: (first + j, 0, 0)),
        ],
        out_specs=[
            pl.BlockSpec((2, 1, step, width), lambda j, i: (0, j, i, 0)),
            pl.BlockSpec((1, 8, width), lambda j, i: (j, 0, 0)),
        ],
        out_shape=[
            jax.ShapeDtypeStruct((2, blocks, count, width), bf16),
            jax.ShapeDtypeStruct((blocks, 8, width), f32),
        ],
    )(acts, acts, weights, weights, vecs[:, None, :])
    return both.reshape(2 * blocks, count, width), sums


def norm_back(grad, unit, scale, gain):
    grad = grad * gain
    first = jnp.mean(grad, axis=1, keepdims=True)
    second = jnp.mean(grad * unit, axis=1, keepdims=True)
    return scale * (grad - first - unit * second)


def hidden_sum(hidden_refs, w_refs, dims, acc):
    for ref, w_ref in zip(hidden_refs, w_refs):
        for m in range(ref.shape[0]):
            part = mm(ref[m], w_ref[m], dims)
            acc = part if acc is None else acc + part
    return acc


def output_body(x_ref, o_ref, *refs, parts, splits):
    e_refs, wo_ref, w_refs, (vec_ref, out_ref) = refs[:parts], refs[parts], refs[parts + 1 : -2], refs[-2:]
    acc = hidden_sum(e_refs, w_refs, NN, mm(o_ref[0], wo_ref[0], NN))
    bias = vec_ref[7:8, :] + vec_ref[8 + splits : 9 + splits, :]
    out_ref[...] = (x_ref[...].astype(f32) + acc + bias).astype(bf16)


def resident(blocks, width, at):
    return pl.BlockSpec((blocks, width, width), lambda i: (at, 0, 0), pipeline_mode=pl.Buffered(1))


def output(x, o, es, wa, wm, vecs, after=(), step=256):
    count, width = x.shape
    half = wm[0].shape[0] // 2
    splits = half * len(wm)
    token = pl.BlockSpec((step, width), lambda i: (i, 0))
    return call(
        functools.partial(output_body, parts=len(es), splits=splits),
        10 * count * width * width,
        14 * count * width + 10 * width * width,
        after=after,
        grid=(count // step,),
        in_specs=[token]
        + [layers(v, step, width) for v in (o, *es)]
        + [resident(1, width, 3)]
        + [resident(half, width, 1)] * len(wm)
        + [pl.BlockSpec(vecs.shape, lambda i: (0, 0))],
        out_specs=token,
        out_shape=jax.ShapeDtypeStruct((count, width), bf16),
    )(x, *[v[0] for v in (o, *es)], wa, *wm, vecs)


def normed(x):
    centred = x - jnp.mean(x, axis=1, keepdims=True)
    scale = lax.rsqrt(jnp.mean(centred * centred, axis=1, keepdims=True) + norm_epsilon)
    return centred * scale, scale


def add_sums(sum_ref, sums):
    sums = [sub_sum(t) for t in sums]

    @pl.when(pl.program_id(0) == 0)
    def _():
        for n, s in enumerate(sums):
            sum_ref[n] = s

    @pl.when(pl.program_id(0) > 0)
    def _():
        for n, s in enumerate(sums):
            sum_ref[n] += s


def grad_one_body(x_ref, dy_ref, g_ref, wa_ref, vec_ref, part_ref, sum_ref):
    dy = dy_ref[...].astype(f32)
    grad = mm(g_ref[0], wa_ref[0], NT) + mm(g_ref[1], wa_ref[1], NT) + mm(g_ref[2], wa_ref[2], NT)
    unit, scale = normed(x_ref[...].astype(f32))
    part_ref[...] = dy + norm_back(grad, unit, scale, vec_ref[0:1, :])
    add_sums(sum_ref, (grad * unit, grad, dy))


def grad_one(x, dy, g, wa, vecs, after=(), step=256):
    count, width = x.shape
    token = pl.BlockSpec((step, width), lambda i: (i, 0))
    return call(
        grad_one_body,
        6 * count * width * width,
        14 * count * width + 6 * width * width,
        after=after,
        grid=(count // step,),
        in_specs=[
            token,
            token,
            layers(g, step, width),
            resident(3, width, 0),
            pl.BlockSpec(vecs.shape, lambda i: (0, 0)),
        ],
        out_specs=[token, pl.BlockSpec((3, 8, width), lambda i: (0, 0, 0))],
        out_shape=[jax.ShapeDtypeStruct((count, width), f32), jax.ShapeDtypeStruct((3, 8, width), f32)],
    )(x, dy, g[0], wa, vecs)


def grad_two_body(x_ref, part_ref, *refs):
    parts = (len(refs) - 3) // 2
    vec_ref, grad_ref, sum_ref = refs[2 * parts :]
    grad = hidden_sum(refs[:parts], refs[parts : 2 * parts], NT, None)
    unit, scale = normed(x_ref[...].astype(f32))
    grad_ref[...] = (part_ref[...] + norm_back(grad, unit, scale, vec_ref[2:3, :])).astype(bf16)
    add_sums(sum_ref, (grad * unit, grad))


def grad_two(x, part, dus, wm, vecs, after=(), step=256):
    count, width = x.shape
    token = pl.BlockSpec((step, width), lambda i: (i, 0))
    return call(
        grad_two_body,
        8 * count * width * width,
        16 * count * width + 8 * width * width,
        after=after,
        grid=(count // step,),
        in_specs=[token, token]
        + [layers(v, step, width) for v in dus]
        + [resident(w.shape[0] // 2, width, 0) for w in wm]
        + [pl.BlockSpec(vecs.shape, lambda i: (0, 0))],
        out_specs=[token, pl.BlockSpec((2, 8, width), lambda i: (0, 0, 0))],
        out_shape=[jax.ShapeDtypeStruct((count, width), bf16), jax.ShapeDtypeStruct((2, 8, width), f32)],
    )(x, part, *[v[0] for v in dus], *wm, vecs)


def grid_places():
    wide, narrow = lax.axis_index("wide"), lax.axis_index("narrow")
    return wide // 2, wide % 2, narrow // 2, narrow % 2


def to_place(move):
    pairs = []
    for z in range(4):
        for y in range(2):
            for x in range(2):
                for c in range(2):
                    a, b, d, e = move(z, y, x, c)
                    pairs.append((((z * 2 + y) * 2 + x) * 2 + c, ((a * 2 + b) * 2 + d) * 2 + e))
    return pairs


def over_c(value):
    return lax.ppermute(value, AXES, to_place(lambda z, y, x, c: (z, y, x, 1 - c)))


def over_x(value):
    return lax.ppermute(value, AXES, to_place(lambda z, y, x, c: (z, y, 1 - x, c)))


def over_y(value):
    return lax.ppermute(value, AXES, to_place(lambda z, y, x, c: (z, 1 - y, x, c)))


def over_z(value, by):
    return lax.ppermute(value, AXES, to_place(lambda z, y, x, c: ((z + by) % 4, y, x, c)))


def gather_staged(shards):
    own = jnp.stack([shards] + [over_z(shards, s) for s in (1, 2, 3)])
    by_x, by_y = over_x(own), over_y(own)
    lower, upper = over_y(by_x[:2]), over_x(by_y[2:])
    here = [own, by_x, by_y, lower, upper]
    return here + [over_c(v) for v in here]


class Reduction:
    def __init__(self, axes, made):
        self.axes, self.made = axes, made[0]
        self.held = [
            (keep, over_x(send) if axis == "x" else over_y(send))
            for axis, keep, send in zip(axes, made[::2], made[1::2])
        ]

    def second(self, made):
        self.made = made[0]
        self.held = [
            (keep, over_y(send) if axis == "x" else over_x(send))
            for axis, keep, send in zip(self.axes, made[::2], made[1::2])
        ]


def pair_body(place_ref, r, ins, outs):
    y, x = place_ref[1], place_ref[2]
    for n, axis in enumerate(r.axes):
        keep, got = ins[2 * n : 2 * n + 2]
        for ref, other in zip(outs[2 * n : 2 * n + 2], (0, 1)):
            at = (y if axis == "x" else x) ^ other
            ref[...] = (keep[:, :, at].astype(f32) + got[:, :, at].astype(f32)).astype(bf16)


def plane_body(place_ref, r, ins, outs):
    for m, ref in enumerate(outs):
        at = place_ref[0] ^ m
        for n in range(len(r.axes)):
            keep, got = ins[2 * n : 2 * n + 2]
            wide = keep.shape[-1]
            value = keep[:, at >> 1, at & 1].astype(f32) + got[:, at >> 1, at & 1].astype(f32)
            ref[:, :, n * wide : (n + 1) * wide] = value.astype(bf16)


def advance(place, pairs, planes, after=(), steps=2):
    blocks, *_, shard, wide = (pairs + planes)[0].held[0][0].shape
    width = wide * len((pairs + planes)[0].axes)
    shapes, places = [], []
    for r in pairs:
        shapes += [jax.ShapeDtypeStruct((blocks, 2, 2, shard, width // len(r.axes)), bf16)] * (2 * len(r.axes))
    places += [0] * len(shapes)
    if planes:
        shapes += [jax.ShapeDtypeStruct((len(planes), blocks, shard, width), bf16)] * 4
        places += [1] * 4
    operands = [v for r in pairs + planes for held in r.held for v in held]

    def spec(s, at=0):
        n = len(s.shape)
        block = tuple(d // steps if m == at else d for m, d in enumerate(s.shape))
        return pl.BlockSpec(block, lambda b, p: (0,) * at + (b,) + (0,) * (n - 1 - at))

    def body(place_ref, *refs):
        ins, outs = refs[: len(operands)], refs[len(operands) :]
        for r in pairs:
            count = 2 * len(r.axes)
            pair_body(place_ref, r, ins[:count], outs[:count])
            ins, outs = ins[count:], outs[count:]
        for n, r in enumerate(planes):
            count = 2 * len(r.axes)
            plane_body(place_ref, r, ins[:count], [ref.at[n] for ref in outs])
            ins = ins[count:]

    outs = call(
        body,
        0,
        sum(v.size * v.dtype.itemsize for v in operands) * 2,
        after=after,
        grid_spec=pltpu.PrefetchScalarGridSpec(
            num_scalar_prefetch=1,
            grid=(steps,),
            in_specs=[spec(v) for v in operands],
            out_specs=[spec(s, at) for s, at in zip(shapes, places)],
        ),
        out_shape=shapes,
    )(place, *operands)
    for r in pairs:
        count = 2 * len(r.axes)
        r.second(outs[:count])
        outs = outs[count:]
    terms = []
    for m, v in enumerate(outs):
        for r in planes:
            r.made = v
        v = v.reshape(-1, shard, width)
        terms.append(
            lax.ppermute(
                v, AXES, to_place(lambda z, y, x, c, m=m: (2 * c + ((z ^ m) >> 1), y, x, (z ^ m) & 1))
            )
        )
    return terms


def everywhere(value):
    def get(move):
        return lax.ppermute(value, AXES, to_place(move))

    value = value + over_c(value)
    by_x, by_y = over_x(value), over_y(value)
    across = get(lambda z, y, x, c: (z, 1 - y, 1 - x, c))
    value = (value + by_x) + (by_y + across)
    near = get(lambda z, y, x, c: (z ^ 1, y, x, c))
    far = get(lambda z, y, x, c: (z ^ 2, y, x, c))
    last = get(lambda z, y, x, c: (z ^ 3, y, x, c))
    return (value + near) + (far + last)


def pack_body(slot_ref, *refs, orders, per):
    terms, (shard_ref, out_ref, square_ref) = refs[: len(orders) * per], refs[len(orders) * per :]
    total = jnp.zeros(square_ref.shape, f32)
    for n, order in enumerate(orders):
        for m, b in enumerate(order):
            value = terms[n * per][m].astype(f32)
            for t in range(1, per):
                value = value + terms[n * per + t][m].astype(f32)
            shard_ref[b] = value
            total = total + value * value
    square_ref[...] = total

    def one(j, carry):
        b = slot_ref[j]

        @pl.when(b >= 0)
        def _():
            out_ref[j] = shard_ref[jnp.maximum(b, 0)].astype(bf16)

        @pl.when(b < 0)
        def _():
            out_ref[j] = jnp.zeros(out_ref.shape[1:], bf16)

        return carry

    lax.fori_loop(0, out_ref.shape[0], one, 0)


def pack(slots, terms, orders, after=()):
    per = len(terms[0])
    _, shard, width = terms[0][0].shape
    terms = [v for t in terms for v in t]
    vmem = pl.BlockSpec(memory_space=pltpu.VMEM)
    return call(
        functools.partial(pack_body, orders=orders, per=per),
        0,
        sum(v.size * v.dtype.itemsize for v in terms) * 2,
        after=after,
        in_specs=[pl.BlockSpec(memory_space=pltpu.SMEM)] + [vmem] * len(terms),
        out_specs=[vmem] * 3,
        out_shape=[
            jax.ShapeDtypeStruct((sum(map(len, orders)), shard, width), f32),
            jax.ShapeDtypeStruct((slots.shape[0], shard, width), bf16),
            jax.ShapeDtypeStruct((shard, width), f32),
        ],
    )(slots, *terms)


def to_low_body(l_ref, r_ref, l_low, r_low):
    l_low[...] = l_ref[...].astype(bf16)
    r_low[...] = r_ref[...].astype(bf16)


def to_low(left, right, after=(), step=384):
    width = left.shape[0]
    rows = pl.BlockSpec((step, width), lambda i: (i, 0))
    return call(
        to_low_body,
        0,
        12 * width**2,
        after=after,
        grid=(width // step,),
        in_specs=[rows, rows],
        out_specs=[rows, rows],
        out_shape=[jax.ShapeDtypeStruct((width, width), bf16)] * 2,
    )(left, right)


def precondition_body(scale_ref, s_ref, l_ref, r_ref, p_ref, s_low):
    @pl.when(pl.program_id(0) == 0)
    def _():
        s_low[...] = (s_ref[...].astype(f32) * scale_ref[0]).astype(bf16)

    left = mm(l_ref[...], s_low[...], NN)
    p_ref[...] = (scale_ref[1] * mm(left.astype(bf16), r_ref[...], NN)).astype(bf16)


def precondition(scales, block, left, right, step=384):
    width = block.shape[0]
    whole = pl.BlockSpec((width, width), lambda i: (0, 0))
    rows = pl.BlockSpec((step, width), lambda i: (i, 0))
    return call(
        precondition_body,
        4 * width**3,
        8 * width**2,
        grid=(width // step,),
        in_specs=[pl.BlockSpec(memory_space=pltpu.SMEM), whole, rows, whole],
        out_specs=rows,
        out_shape=jax.ShapeDtypeStruct((width, width), bf16),
        scratch_shapes=[pltpu.VMEM((width, width), bf16)],
    )(scales, block, left, right)


def statistics_body(has_ref, scale_ref, s_ref, l_ref, r_ref, nl_ref, nr_ref, s_low, *, step):
    i = pl.program_id(0)
    width = s_ref.shape[0]

    @pl.when(i == 0)
    def _():
        s_low[...] = (s_ref[...].astype(f32) * scale_ref[0]).astype(bf16)

    factor = (1.0 - decay_beta) * (scale_ref[1] * scale_ref[1] / width)
    at = pl.multiple_of(i * step, step)

    @pl.when(has_ref[0] != 0)
    def _():
        nl_ref[...] = decay_beta * l_ref[...] + factor * mm(s_low[pl.ds(at, step), :], s_low[...], NT)
        nr_ref[...] = decay_beta * r_ref[...] + factor * mm(s_low[:, pl.ds(at, step)], s_low[...], TN)

    @pl.when(has_ref[0] == 0)
    def _():
        nl_ref[...] = l_ref[...]
        nr_ref[...] = r_ref[...]


def statistics(has, scales, block, left, right, step=256):
    width = block.shape[0]
    whole = pl.BlockSpec((width, width), lambda i: (0, 0))
    rows = pl.BlockSpec((step, width), lambda i: (i, 0))
    smem = pl.BlockSpec(memory_space=pltpu.SMEM)
    return call(
        functools.partial(statistics_body, step=step),
        4 * width**3,
        18 * width**2,
        grid=(width // step,),
        in_specs=[smem, smem, whole, rows, rows],
        out_specs=[rows, rows],
        out_shape=[jax.ShapeDtypeStruct((width, width), f32)] * 2,
        scratch_shapes=[pltpu.VMEM((width, width), bf16)],
    )(has, scales, block, left, right)


def update_body(owner_ref, factor_ref, p_ref, shard_ref, block_ref, clip_ref, new_ref, copy_ref):
    for b in range(shard_ref.shape[0]):
        clip_ref[b] = shard_ref[b] * factor_ref[0]
        value = block_ref[b] - matrix_rate * p_ref[owner_ref[b]].astype(f32)
        new_ref[b] = value
        copy_ref[b] = value.astype(bf16)


def update(owners, factor, returned, shards, blocks):
    smem, vmem = pl.BlockSpec(memory_space=pltpu.SMEM), pl.BlockSpec(memory_space=pltpu.VMEM)
    return call(
        update_body,
        0,
        returned.size * 2 + shards.size * 18,
        in_specs=[smem, smem, vmem, vmem, vmem],
        out_specs=[vmem] * 3,
        out_shape=[
            jax.ShapeDtypeStruct(shards.shape, f32),
            jax.ShapeDtypeStruct(shards.shape, f32),
            jax.ShapeDtypeStruct(shards.shape, bf16),
        ],
    )(owners, factor, returned, shards, blocks)


def to_all(value):
    return lax.all_to_all(value, AXES, split_axis=0, concat_axis=0, tiled=True)


def per_device(
    tokens,
    segment_ids,
    cotangent,
    blocks,
    vectors,
    stat_left,
    stat_right,
    root_left,
    root_right,
    vec_stat,
    owners,
    *,
    paired,
):
    rows_here, seq_len, width = tokens.shape
    count = rows_here * seq_len
    splits = FF // width
    slot_count = lax.axis_size(AXES)
    my_index = lax.axis_index(AXES)
    shard = width // slot_count
    vec_rows = vectors.shape[0]

    low_blocks, low_vectors = blocks.astype(bf16), vectors.astype(bf16)
    everyone = jnp.broadcast_to(low_vectors.reshape(1, -1), (slot_count, vec_rows * shard))
    vecs = to_all(everyone).reshape(slot_count, vec_rows, shard)
    vecs = vecs.transpose(1, 0, 2).reshape(vec_rows, width).astype(f32)
    half = splits // 2
    mlp_weights = []
    for first in (4, 4 + half):
        part = jnp.concatenate([low_blocks[first : first + half], low_blocks[first + splits : first + splits + half]])
        mlp_weights.append(lax.all_gather(part, AXES, axis=1, tiled=True))

    flat_tokens = tokens.reshape(count, width)
    dy = cotangent.reshape(count, width)
    tables = rotary_tables(segment_ids)
    place = jnp.stack(grid_places()).astype(jnp.int32)
    if paired:
        pieces = gather_staged(low_blocks[:4])
    else:
        pieces = [lax.all_gather(low_blocks[:4], AXES, axis=1, tiled=True)]
    q, k, v, do, acts, attn_weights = project(place, flat_tokens, dy, pieces, vecs, tables)
    og, attn_sums, acts = attend(segment_ids, q, k, v, do, tables, acts)
    orders = [list(range(4))]
    for first in (0, half):
        orders.append([base + first + j for base in (4, 4 + splits) for j in range(half)])
    if paired:
        acts_pair, og_pair = (acts, over_c(acts)), (og, over_c(og))
        dys = (acts_pair, 2, 1)
        ed0, up_sum0 = hidden(8, acts, mlp_weights[0], vecs)
        ed0_pair = (ed0, over_c(ed0))
        ed1, up_sum1 = hidden(8 + half, acts, mlp_weights[1], vecs, after=(ed0, acts_pair[1]))
        ed1_pair = (ed1, over_c(ed1))

        def grads(left, two, one, after):
            operands = ((acts_pair, left, 1), two, one, dys, shard, "xy")
            return Reduction("xy", half_grads(place, *operands, after=after))

        attn = grads(0, (og_pair, 3, 1), (og_pair, 0, 3), (ed1,))
        low = grads(1, (ed0_pair, 0, half), (ed0_pair, half, half), (attn.made,))
        advance(place, [attn], [], after=(low.made,))
        high = grads(1, (ed1_pair, 0, half), (ed1_pair, half, half), (attn.made,))
        advance(place, [low], [], after=(high.made,))
        part, one_sums = grad_one(flat_tokens, dy, (og, 0, 3), attn_weights, vecs, after=(low.made,))
        terms = [advance(place, [high], [attn, low], after=(part,))]
        es, dus = [(v, 0, half) for v in (ed0, ed1)], [(v, half, half) for v in (ed0, ed1)]
        grad_in, two_sums = grad_two(flat_tokens, part, dus, mlp_weights, vecs, after=(high.made,))
        terms.append(advance(place, [], [high], after=(grad_in,)))
        last = high.made
        orders = [orders[0] + orders[1], orders[2]]
    else:
        ed0, up_sum0 = hidden(8, acts, mlp_weights[0], vecs)
        ed1, up_sum1 = hidden(8 + half, acts, mlp_weights[1], vecs)
        grads = [
            full_grads(acts[0], og[3:], og[:3], dy),
            full_grads(acts[1], ed0[:half], ed0[half:], dy),
            full_grads(acts[1], ed1[:half], ed1[half:], dy),
        ]
        terms = [[lax.psum_scatter(v, AXES, scatter_dimension=1, tiled=True)] for v in grads]
        es, dus = [(v, 0, half) for v in (ed0, ed1)], [(v, half, half) for v in (ed0, ed1)]
        part, one_sums = grad_one(flat_tokens, dy, (og, 0, 3), attn_weights, vecs)
        grad_in, two_sums = grad_two(flat_tokens, part, dus, mlp_weights, vecs)
        last = grad_in
    up_sums = [up_sum0, up_sum1]

    one_sums, two_sums = jnp.sum(one_sums, axis=1), jnp.sum(two_sums, axis=1)
    qkv_sums = jnp.sum(attn_sums, axis=1)
    up_sums = jnp.sum(jnp.concatenate(up_sums, axis=0), axis=1)
    bias_sum = one_sums[2:]
    grad_vectors = jnp.concatenate(
        [one_sums[:2], two_sums, qkv_sums, bias_sum, up_sums, bias_sum], axis=0
    )
    slot_ids = jnp.arange(slot_count, dtype=jnp.int32)
    match = owners[None, :] == slot_ids[:, None]
    slots = jnp.sum(jnp.where(match, jnp.arange(1, owners.shape[0] + 1, dtype=jnp.int32)[None], 0), axis=1) - 1
    has_block = jnp.any(owners == my_index)
    out = output(flat_tokens, (og, 3, 1), es, attn_weights, mlp_weights, vecs, after=(last,))
    shards, outgoing, squares = pack(slots, terms, orders, after=(out,))
    left_low, right_low = to_low(root_left[0], root_right[0], after=(squares,))
    local = jnp.concatenate([grad_vectors, jnp.sum(squares, axis=0)[None], jnp.zeros((2, width), f32)])
    total = everywhere(local) if paired else lax.psum(local, AXES)
    vector_sums = total[:vec_rows]
    square_sum = jnp.sum(total[vec_rows]) + jnp.sum(vector_sums * vector_sums)
    shard_vectors = lax.dynamic_slice_in_dim(vector_sums, my_index * shard, shard, axis=1)
    grad_norm = jnp.sqrt(square_sum)
    factor = jnp.minimum(1.0, clip_level / grad_norm)
    root_count = math.sqrt(NPARAM)

    scale = factor * root_count
    power = jnp.exp2(jnp.floor(jnp.log2(jnp.maximum(scale, 1e-30)))).astype(bf16).astype(f32)
    scales = jnp.stack([power, scale / power])
    owned = to_all(outgoing).reshape(width, width)
    precond = precondition(scales, owned, left_low, right_low)
    returned = to_all(precond.reshape(slot_count, shard, width))
    new_left, new_right = statistics(
        has_block.astype(jnp.int32).reshape(1), scales, owned, stat_left[0], stat_right[0]
    )
    clipped_blocks, new_blocks, blocks_copy = update(owners, factor.reshape(1), returned, shards, blocks)
    clipped_vectors = shard_vectors * factor
    scaled_vectors = clipped_vectors * root_count
    new_vec_stat = decay_beta * vec_stat + (1.0 - decay_beta) * (scaled_vectors * scaled_vectors)
    new_vectors = vectors - vector_rate * scaled_vectors * lax.rsqrt(new_vec_stat)
    return (
        out.reshape(tokens.shape),
        grad_in.reshape(tokens.shape),
        clipped_blocks,
        clipped_vectors,
        grad_norm,
        new_left[None],
        new_right[None],
        new_vec_stat,
        new_blocks,
        new_vectors,
        blocks_copy,
        new_vectors.astype(bf16),
    )


def solution(mesh):
    rows = P(AXES, None, None)
    split_rows = P(None, AXES, None)
    split_columns = P(None, AXES)
    paired = dict(mesh.shape) == {"wide": 8, "narrow": 4}
    return jax.shard_map(
        functools.partial(per_device, paired=paired),
        mesh=mesh,
        in_specs=(
            rows, P(AXES, None), rows, split_rows, split_columns,
            rows, rows, rows, rows, split_columns, P(),
        ),
        out_specs=(
            rows, rows, split_rows, split_columns, P(), rows, rows,
            split_columns, split_rows, split_columns, split_rows, split_columns,
        ),
        check_vma=False,
    )
```

```python
import functools
import math

import jax
import jax.numpy as jnp
import numpy as np
from jax import lax
from jax.experimental import pallas as pl
from jax.experimental.pallas import tpu as pltpu
from jax.sharding import PartitionSpec as P

H = 12
FF = 3072
ROT = 16
NPARAM = 7087872
LONGEST = 256

clip_level = 1.0
matrix_rate = 0.03
vector_rate = 0.2
decay_beta = 0.5
norm_epsilon = 1e-05

f32 = jnp.float32
bf16 = jnp.bfloat16
AXES = ("wide", "narrow")
LANES = 128
MIB = 2**20

NN = (((1,), (0,)), ((), ()))
NT = (((1,), (1,)), ((), ()))
TN = (((0,), (0,)), ((), ()))


def mm(left, right, dims):
    return lax.dot_general(left, right, dims, preferred_element_type=f32)


def call(body, flops, moved, vmem=64, after=(), **rest):
    spec = rest.pop("grid_spec", None)
    grid = spec.grid if spec is not None else rest.get("grid", ())
    later = len(after)
    if later:
        held = [pl.BlockSpec(memory_space=pl.ANY)] * later
        if spec is not None:
            first = spec.num_scalar_prefetch + len(spec.in_specs)
            spec = pltpu.PrefetchScalarGridSpec(
                num_scalar_prefetch=spec.num_scalar_prefetch,
                grid=spec.grid,
                in_specs=list(spec.in_specs) + held,
                out_specs=spec.out_specs,
                scratch_shapes=spec.scratch_shapes,
            )
        else:
            first = len(rest["in_specs"])
            rest["in_specs"] = list(rest["in_specs"]) + held
        inner = body

        def body(*refs):
            inner(*refs[:first], *refs[first + later :])

    if spec is not None:
        rest["grid_spec"] = spec
    made = pl.pallas_call(
        body,
        compiler_params=pltpu.CompilerParams(
            vmem_limit_bytes=vmem * MIB,
            dimension_semantics=("arbitrary",) * len(grid),
        ),
        cost_estimate=pl.CostEstimate(
            flops=int(flops), bytes_accessed=int(moved), transcendentals=0
        ),
        **rest,
    )
    return lambda *operands: made(*operands, *after)


def sub_sum(values):
    return jnp.sum(values.reshape(-1, 8, values.shape[-1]), axis=0)


def rotary_tables(segment_ids):
    rows, length = segment_ids.shape
    start = jnp.sum(
        (segment_ids[:, None, :] < segment_ids[:, :, None]).astype(jnp.int32), axis=-1
    )
    offset = (jnp.arange(length, dtype=jnp.int32)[None] - start).astype(f32).reshape(-1, 1)
    half = ROT // 2
    lane = np.arange(LANES) % 64
    rates = np.where(lane < ROT, 10000.0 ** (-2.0 * (lane % half) / ROT), 0.0)
    angle = offset * jnp.asarray(rates, f32)[None]
    cosine, sine = jnp.cos(angle), jnp.sin(angle)
    first = sine * jnp.asarray(np.where(lane < half, -1.0, 0.0), f32)[None]
    second = sine * jnp.asarray(np.where((lane >= half) & (lane < ROT), 1.0, 0.0), f32)[None]
    return cosine, first, second


def rotate(values, cosine, first, second):
    parts = []
    for at in range(0, values.shape[1], LANES):
        part = values[:, at : at + LANES]
        parts.append(
            part * cosine
            + pltpu.roll(part, LANES - ROT // 2, 1) * first
            + pltpu.roll(part, ROT // 2, 1) * second
        )
    return jnp.concatenate(parts, axis=1)


def rotate_back(values, cosine, first, second):
    return (
        values * cosine
        - pltpu.roll(values, LANES - ROT // 2, 1) * first
        - pltpu.roll(values, ROT // 2, 1) * second
    )


def assemble(place_ref, pieces, w_ref):
    z, y, x, c = place_ref[0], place_ref[1], place_ref[2], place_ref[3]
    blocks, rows = w_ref.shape[0], 2 * pieces[0].shape[2]

    def plane(t, carry):
        apart = lax.rem(z - t + 4, 4)

        def put(here, there, at, ry, rx):
            chip = (t * 2 + (y ^ ry)) * 2 + (x ^ rx)
            where = pl.ds(pl.multiple_of(chip * rows, rows), rows)
            for order, wanted in (((here, there), c == 0), ((there, here), c != 0)):

                @pl.when(wanted)
                def _(order=order):
                    for n in range(blocks):
                        w_ref[n, where, :] = jnp.concatenate([ref[at, n] for ref in order], axis=0)

        for m, (ry, rx) in enumerate(((0, 0), (0, 1), (1, 0))):
            put(pieces[m], pieces[5 + m], apart, ry, rx)
        pl.when(apart < 2)(lambda: put(pieces[3], pieces[8], apart, 1, 1))
        pl.when(apart >= 2)(lambda: put(pieces[4], pieces[9], apart - 2, 1, 1))
        return carry

    lax.fori_loop(0, 4, plane, 0)


def project_body(place_ref, x_ref, dy_ref, vec_ref, c_ref, a_ref, b_ref, *refs):
    *pieces, q_ref, k_ref, v_ref, do_ref, acts_ref, w_ref = refs

    @pl.when(pl.program_id(0) == 0)
    def _():
        if len(pieces) > 1:
            assemble(place_ref, pieces, w_ref)
        else:
            w_ref[...] = pieces[0][...]

    unit, _ = normed(x_ref[...].astype(f32))
    a1 = (unit * vec_ref[0:1, :] + vec_ref[1:2, :]).astype(bf16)
    acts_ref[0] = a1
    acts_ref[1] = (unit * vec_ref[2:3, :] + vec_ref[3:4, :]).astype(bf16)
    acts_ref[2] = dy_ref[...]
    tables = (c_ref[...], a_ref[...], b_ref[...])
    q_ref[...] = rotate(mm(a1, w_ref[0], NN) + vec_ref[4:5, :], *tables).astype(bf16)
    k_ref[...] = rotate(mm(a1, w_ref[1], NN) + vec_ref[5:6, :], *tables).astype(bf16)
    v_ref[...] = (mm(a1, w_ref[2], NN) + vec_ref[6:7, :]).astype(bf16)
    do_ref[...] = mm(dy_ref[...], w_ref[3], NT).astype(bf16)


def project(place, x, dy, pieces, vecs, tables, step=256):
    count, width = x.shape
    token = pl.BlockSpec((step, width), lambda i, s: (i, 0))
    table = pl.BlockSpec((step, LANES), lambda i, s: (i, 0))
    once = pl.Buffered(1)
    return call(
        project_body,
        8 * count * width * width,
        20 * count * width + 16 * width * width,
        grid_spec=pltpu.PrefetchScalarGridSpec(
            num_scalar_prefetch=1,
            grid=(count // step,),
            in_specs=[token, token, pl.BlockSpec(vecs.shape, lambda i, s: (0, 0)), table, table, table]
            + [pl.BlockSpec(v.shape, lambda i, s, n=v.ndim: (0,) * n, pipeline_mode=once) for v in pieces],
            out_specs=[token] * 4
            + [
                pl.BlockSpec((3, step, width), lambda i, s: (0, i, 0)),
                pl.BlockSpec((4, width, width), lambda i, s: (0, 0, 0)),
            ],
        ),
        out_shape=[jax.ShapeDtypeStruct((count, width), bf16)] * 4
        + [jax.ShapeDtypeStruct((3, count, width), bf16), jax.ShapeDtypeStruct((4, width, width), bf16)],
    )(place, x, dy, vecs, *tables, *pieces)


def attend_body(
    acts_ref, col_ref, row_ref, q_ref, k_ref, v_ref, do_ref, c_ref, a_ref, b_ref,
    g_ref, sum_ref, acts_out_ref, mask_ref, *, block,
):
    length = q_ref.shape[0]
    steps = length // block

    def reach(i):
        return max(0, (i * block - (LONGEST - 1)) // block * block), (i + 1) * block

    @pl.when(pl.program_id(1) == 0)
    def _():
        for i in range(steps):
            lo, hi = reach(i)
            key = lax.broadcasted_iota(jnp.int32, (hi - lo, block), 0) + lo
            query = lax.broadcasted_iota(jnp.int32, (hi - lo, block), 1) + i * block
            same = col_ref[lo:hi, :] == row_ref[0, :, i * block : hi]
            mask = jnp.where(same & (key <= query), 0.0, -jnp.inf)
            mask_ref[i, 0 : hi - lo, 0:block] = mask
            mask_ref[i, 0 : hi - lo, block:] = mask

    low = lax.broadcasted_iota(jnp.int32, (1, LANES), 1) < 64
    eighth = jnp.asarray(0.125, bf16)
    zero = jnp.zeros((), bf16)

    def both(part):
        return jnp.concatenate([jnp.where(low, part, zero), jnp.where(low, zero, part)], axis=0)

    def unstack(part):
        return jnp.concatenate([part[0:64, 0:block], part[64:, block:]], axis=0).T

    pairs = []
    for at in range(0, q_ref.shape[1], LANES):
        lanes = slice(at, at + LANES)
        keys, values = k_ref[:, lanes], v_ref[:, lanes]
        pairs.append(
            (lanes, keys, values, (keys * eighth).T, values.T, q_ref[:, lanes] * eighth, do_ref[:, lanes])
        )
    q_sums = [jnp.zeros((8, LANES), f32) for _ in pairs]
    dks = [[None] * steps for _ in pairs]
    dvs = [[None] * steps for _ in pairs]

    def add(parts, n, value):
        parts[n] = value if parts[n] is None else parts[n] + value

    for i in range(steps):
        lo, hi = reach(i)
        here = slice(i * block, hi)
        for p, (lanes, keys, values, keys_t, values_t, queries, grads) in enumerate(pairs):
            q2, do2 = both(queries[here]), both(grads[here])
            scores = mm(keys[lo:hi], q2, NT) + mask_ref[i, 0 : hi - lo, :]
            d_soft = mm(values[lo:hi], do2, NT)
            raised = jnp.exp(scores - jnp.max(scores, axis=0, keepdims=True))
            soft = raised * (1.0 / jnp.sum(raised, axis=0, keepdims=True))
            inner = jnp.sum(soft * d_soft, axis=0, keepdims=True)
            soft_low = soft.astype(bf16)
            d_scores = (soft * (d_soft - inner)).astype(bf16)
            g_ref[3, here, lanes] = unstack(mm(values_t[:, lo:hi], soft_low, NN)).astype(bf16)
            dq = rotate_back(
                unstack(mm(keys_t[:, lo:hi], d_scores, NN)), c_ref[here, :], a_ref[here, :], b_ref[here, :]
            ).astype(bf16)
            g_ref[0, here, lanes] = dq
            q_sums[p] = q_sums[p] + sub_sum(dq.astype(f32))
            dk, dv = mm(d_scores, q2, NN), mm(soft_low, do2, NN)
            for n in range(lo // block, i + 1):
                rows = slice(n * block - lo, (n + 1) * block - lo)
                add(dks[p], n, dk[rows])
                add(dvs[p], n, dv[rows])
    for p, (lanes, *_) in enumerate(pairs):
        dk = rotate_back(jnp.concatenate(dks[p], axis=0), c_ref[...], a_ref[...], b_ref[...]).astype(bf16)
        dv = jnp.concatenate(dvs[p], axis=0).astype(bf16)
        g_ref[1, :, lanes] = dk
        g_ref[2, :, lanes] = dv
        sum_ref[0, :, lanes] = q_sums[p]
        sum_ref[1, :, lanes] = sub_sum(dk.astype(f32))
        sum_ref[2, :, lanes] = sub_sum(dv.astype(f32))


def attend(segment_ids, q, k, v, do, tables, acts, block=256, lanes=3 * LANES):
    rows, length = segment_ids.shape
    count, width = q.shape
    block = min(block, length)
    token = pl.BlockSpec((length, lanes), lambda r, h: (r, h))
    table = pl.BlockSpec((length, LANES), lambda r, h: (r, 0))
    return call(
        functools.partial(attend_body, block=block),
        24 * count * length * width,
        24 * count * width,
        grid=(rows, width // lanes),
        input_output_aliases={0: 2},
        in_specs=[
            pl.BlockSpec(memory_space=pl.ANY),
            pl.BlockSpec((length, 1), lambda r, h: (r, 0)),
            pl.BlockSpec((1, 1, length), lambda r, h: (r, 0, 0)),
            token,
            token,
            token,
            token,
            table,
            table,
            table,
        ],
        out_specs=[
            pl.BlockSpec((4, length, lanes), lambda r, h: (0, r, h)),
            pl.BlockSpec((3, 8, lanes), lambda r, h: (0, r, h)),
            pl.BlockSpec(memory_space=pl.ANY),
        ],
        out_shape=[
            jax.ShapeDtypeStruct((4, count, width), bf16),
            jax.ShapeDtypeStruct((3, 8 * rows, width), f32),
            jax.ShapeDtypeStruct(acts.shape, acts.dtype),
        ],
        scratch_shapes=[pltpu.VMEM((length // block, length, 2 * block), f32)],
    )(
        acts,
        segment_ids.reshape(-1, 1),
        segment_ids.reshape(rows, 1, length),
        q,
        k,
        v,
        do,
        *tables,
    )


def half_grads_body(place_ref, *refs, first, second, steps, axes):
    l1o, l1p, l2o, l2p, r1o, r1p, r2o, r2p, *outs, acc = refs
    i = pl.program_id(0)
    y, x = place_ref[1], place_ref[2]

    @pl.when(i == 0)
    def _():
        acc[...] = jnp.zeros_like(acc)

    for n in range(first + second):
        if n < first:
            part = mm(l1o[0], r1o[n], TN) + mm(l1p[0], r1p[n], TN)
        else:
            part = mm(l2o[n - first], r2o[0], TN) + mm(l2p[n - first], r2p[0], TN)
        acc[n] += part.reshape(acc.shape[1:])

    @pl.when(i == steps - 1)
    def _():
        for n in range(first + second):
            for r, axis in enumerate(axes):
                wide = outs[0].shape[-1]
                columns = slice(r * wide, (r + 1) * wide)
                for ref, other in zip(outs[2 * r : 2 * r + 2], (0, 1)):
                    if axis == "x":
                        value = acc[n, :, :, x ^ other, :, :, columns]
                    else:
                        value = acc[n, :, y ^ other, :, :, :, columns]
                    ref[n] = value.astype(bf16)


def layers(part, step, lanes, half=False):
    _, first, count = part
    return pl.BlockSpec((count, step, lanes), lambda i, *s: (first // count, i, s[0][3] if half else 0))


def half_grads(place, left_one, left_two, right_one, right_two, shard, axes, after=(), step=256):
    first, second = right_one[2], left_two[2]
    _, count, width = right_two[0][0].shape
    half = width // 2
    blocks = first + second
    steps = count // step
    shape = (blocks, 2, 2, 2, shard, width // len(axes))
    out = pl.BlockSpec(shape, lambda i, s: (0, 0, 0, 0, 0, 0))
    return call(
        functools.partial(half_grads_body, first=first, second=second, steps=steps, axes=axes),
        blocks * 2 * count * width * width,
        blocks * 4 * count * width,
        after=after,
        grid_spec=pltpu.PrefetchScalarGridSpec(
            num_scalar_prefetch=1,
            grid=(steps,),
            in_specs=[layers(left_one, step, half, True)] * 2
            + [layers(left_two, step, half, True)] * 2
            + [layers(right_one, step, width)] * 2
            + [layers(right_two, step, width)] * 2,
            out_specs=[out] * (2 * len(axes)),
            scratch_shapes=[pltpu.VMEM((blocks, 2, 2, 2, 2, shard, width), f32)],
        ),
        out_shape=[jax.ShapeDtypeStruct(shape, bf16)] * (2 * len(axes)),
    )(place, *left_one[0], *left_two[0], *right_one[0], *right_two[0])


def full_grads(left_one, left_two, right_one, right_two):
    one = jnp.einsum("td,nte->nde", left_one, right_one, preferred_element_type=f32)
    two = jnp.einsum("ntd,te->nde", left_two, right_two, preferred_element_type=f32)
    return jnp.concatenate([one, two], axis=0)


def gelu_parts(u):
    raised = jnp.exp(-0.5 * (u * u))
    t = 1.0 / (1.0 + (0.3275911 * math.sqrt(0.5)) * jnp.abs(u))
    poly = 1.061405429 * t - 1.453152027
    poly = poly * t + 1.421413741
    poly = poly * t - 0.284496736
    poly = (poly * t + 0.254829592) * t
    tail = 0.5 * poly * raised
    return jnp.where(u < 0, tail, 1.0 - tail), raised * (1.0 / math.sqrt(2.0 * math.pi))


def hidden_body(a2_ref, dy_ref, wu_ref, wd_ref, bu_ref, out_ref, sum_ref):
    u = mm(a2_ref[0], wu_ref[0], NN) + bu_ref[0]
    de = mm(dy_ref[0], wd_ref[0], NT)
    dist, density = gelu_parts(u)
    out_ref[0, 0] = (u * dist).astype(bf16)
    du = (de * (dist + u * density)).astype(bf16)
    out_ref[1, 0] = du
    part = sub_sum(du.astype(f32))

    @pl.when(pl.program_id(1) == 0)
    def _():
        sum_ref[0] = part

    @pl.when(pl.program_id(1) > 0)
    def _():
        sum_ref[0] += part


def hidden(first, acts, weights, vecs, after=(), step=512):
    _, count, width = acts.shape
    splits = weights.shape[0] // 2
    blocks = splits // 2
    both, sums = call(
        hidden_body,
        blocks * 4 * count * width * width,
        blocks * (8 * count * width + 4 * width * width),
        after=after,
        grid=(blocks, count // step),
        in_specs=[
            pl.BlockSpec((1, step, width), lambda j, i: (1, i, 0)),
            pl.BlockSpec((1, step, width), lambda j, i: (2, i, 0)),
            pl.BlockSpec((1, width, width), lambda j, i: (first + j, 0, 0)),
            pl.BlockSpec((1, width, width), lambda j, i: (splits + first + j, 0, 0)),
            pl.BlockSpec((1, 1, width), lambda j, i: (8 + first + j, 0, 0)),
        ],
        out_specs=[
            pl.BlockSpec((2, 1, step, width), lambda j, i: (0, j, i, 0)),
            pl.BlockSpec((1, 8, width), lambda j, i: (j, 0, 0)),
        ],
        out_shape=[
            jax.ShapeDtypeStruct((2, blocks, count, width), bf16),
            jax.ShapeDtypeStruct((blocks, 8, width), f32),
        ],
    )(acts, acts, weights, weights, vecs[:, None, :])
    return both.reshape(2 * blocks, count, width), sums


def norm_back(grad, unit, scale, gain):
    grad = grad * gain
    first = jnp.mean(grad, axis=1, keepdims=True)
    second = jnp.mean(grad * unit, axis=1, keepdims=True)
    return scale * (grad - first - unit * second)


def hidden_sum(hidden_refs, w_ref, dims, acc):
    at = 0
    for ref in hidden_refs:
        for m in range(ref.shape[0]):
            part = mm(ref[m], w_ref[at], dims)
            acc = part if acc is None else acc + part
            at += 1
    return acc


def output_body(x_ref, o_ref, *refs, splits):
    *e_refs, wo_ref, w_ref, vec_ref, out_ref = refs
    acc = hidden_sum(e_refs, w_ref, NN, mm(o_ref[0], wo_ref[0], NN))
    bias = vec_ref[7:8, :] + vec_ref[8 + splits : 9 + splits, :]
    out_ref[...] = (x_ref[...].astype(f32) + acc + bias).astype(bf16)


def resident(blocks, width, at):
    return pl.BlockSpec((blocks, width, width), lambda i: (at, 0, 0), pipeline_mode=pl.Buffered(1))


def output(x, o, es, wa, wm, vecs, after=(), step=256):
    count, width = x.shape
    splits = wm.shape[0] // 2
    token = pl.BlockSpec((step, width), lambda i: (i, 0))
    return call(
        functools.partial(output_body, splits=splits),
        10 * count * width * width,
        14 * count * width + 10 * width * width,
        after=after,
        grid=(count // step,),
        in_specs=[token]
        + [layers(v, step, width) for v in (o, *es)]
        + [resident(1, width, 3), resident(splits, width, 1), pl.BlockSpec(vecs.shape, lambda i: (0, 0))],
        out_specs=token,
        out_shape=jax.ShapeDtypeStruct((count, width), bf16),
    )(x, *[v[0] for v in (o, *es)], wa, wm, vecs)


def normed(x):
    centred = x - jnp.mean(x, axis=1, keepdims=True)
    scale = lax.rsqrt(jnp.mean(centred * centred, axis=1, keepdims=True) + norm_epsilon)
    return centred * scale, scale


def add_sums(sum_ref, sums):
    sums = [sub_sum(t) for t in sums]

    @pl.when(pl.program_id(0) == 0)
    def _():
        for n, s in enumerate(sums):
            sum_ref[n] = s

    @pl.when(pl.program_id(0) > 0)
    def _():
        for n, s in enumerate(sums):
            sum_ref[n] += s


def grad_one_body(x_ref, dy_ref, g_ref, wa_ref, vec_ref, part_ref, sum_ref):
    dy = dy_ref[...].astype(f32)
    grad = mm(g_ref[0], wa_ref[0], NT) + mm(g_ref[1], wa_ref[1], NT) + mm(g_ref[2], wa_ref[2], NT)
    unit, scale = normed(x_ref[...].astype(f32))
    part_ref[...] = dy + norm_back(grad, unit, scale, vec_ref[0:1, :])
    add_sums(sum_ref, (grad * unit, grad, dy))


def grad_one(x, dy, g, wa, vecs, after=(), step=256):
    count, width = x.shape
    token = pl.BlockSpec((step, width), lambda i: (i, 0))
    return call(
        grad_one_body,
        6 * count * width * width,
        14 * count * width + 6 * width * width,
        after=after,
        grid=(count // step,),
        in_specs=[
            token,
            token,
            layers(g, step, width),
            resident(3, width, 0),
            pl.BlockSpec(vecs.shape, lambda i: (0, 0)),
        ],
        out_specs=[token, pl.BlockSpec((3, 8, width), lambda i: (0, 0, 0))],
        out_shape=[jax.ShapeDtypeStruct((count, width), f32), jax.ShapeDtypeStruct((3, 8, width), f32)],
    )(x, dy, g[0], wa, vecs)


def grad_two_body(x_ref, part_ref, *refs):
    *du_refs, w_ref, vec_ref, grad_ref, sum_ref = refs
    grad = hidden_sum(du_refs, w_ref, NT, None)
    unit, scale = normed(x_ref[...].astype(f32))
    grad_ref[...] = (part_ref[...] + norm_back(grad, unit, scale, vec_ref[2:3, :])).astype(bf16)
    add_sums(sum_ref, (grad * unit, grad))


def grad_two(x, part, dus, wm, vecs, after=(), step=256):
    count, width = x.shape
    token = pl.BlockSpec((step, width), lambda i: (i, 0))
    return call(
        grad_two_body,
        8 * count * width * width,
        16 * count * width + 8 * width * width,
        after=after,
        grid=(count // step,),
        in_specs=[token, token]
        + [layers(v, step, width) for v in dus]
        + [resident(wm.shape[0] // 2, width, 0), pl.BlockSpec(vecs.shape, lambda i: (0, 0))],
        out_specs=[token, pl.BlockSpec((2, 8, width), lambda i: (0, 0, 0))],
        out_shape=[jax.ShapeDtypeStruct((count, width), bf16), jax.ShapeDtypeStruct((2, 8, width), f32)],
    )(x, part, *[v[0] for v in dus], wm, vecs)


def grid_places():
    wide, narrow = lax.axis_index("wide"), lax.axis_index("narrow")
    return wide // 2, wide % 2, narrow // 2, narrow % 2


def to_place(move):
    pairs = []
    for z in range(4):
        for y in range(2):
            for x in range(2):
                for c in range(2):
                    a, b, d, e = move(z, y, x, c)
                    pairs.append((((z * 2 + y) * 2 + x) * 2 + c, ((a * 2 + b) * 2 + d) * 2 + e))
    return pairs


def over_c(value):
    return lax.ppermute(value, AXES, to_place(lambda z, y, x, c: (z, y, x, 1 - c)))


def over_x(value):
    return lax.ppermute(value, AXES, to_place(lambda z, y, x, c: (z, y, 1 - x, c)))


def over_y(value):
    return lax.ppermute(value, AXES, to_place(lambda z, y, x, c: (z, 1 - y, x, c)))


def over_z(value, by):
    return lax.ppermute(value, AXES, to_place(lambda z, y, x, c: ((z + by) % 4, y, x, c)))


def gather_staged(shards):
    own = jnp.stack([shards] + [over_z(shards, s) for s in (1, 2, 3)])
    by_x, by_y = over_x(own), over_y(own)
    lower, upper = over_y(by_x[:2]), over_x(by_y[2:])
    here = [own, by_x, by_y, lower, upper]
    return here + [over_c(v) for v in here]


class Reduction:
    def __init__(self, axes, made):
        self.axes, self.made = axes, made[0]
        self.held = [
            (keep, over_x(send) if axis == "x" else over_y(send))
            for axis, keep, send in zip(axes, made[::2], made[1::2])
        ]

    def second(self, made):
        self.made = made[0]
        self.held = [
            (keep, over_y(send) if axis == "x" else over_x(send))
            for axis, keep, send in zip(self.axes, made[::2], made[1::2])
        ]


def pair_body(place_ref, r, ins, outs):
    y, x = place_ref[1], place_ref[2]
    for n, axis in enumerate(r.axes):
        keep, got = ins[2 * n : 2 * n + 2]
        for ref, other in zip(outs[2 * n : 2 * n + 2], (0, 1)):
            at = (y if axis == "x" else x) ^ other
            ref[...] = (keep[:, :, at].astype(f32) + got[:, :, at].astype(f32)).astype(bf16)


def plane_body(place_ref, r, ins, outs):
    for m, ref in enumerate(outs):
        at = place_ref[0] ^ m
        for n in range(len(r.axes)):
            keep, got = ins[2 * n : 2 * n + 2]
            wide = keep.shape[-1]
            value = keep[:, at >> 1, at & 1].astype(f32) + got[:, at >> 1, at & 1].astype(f32)
            ref[:, :, n * wide : (n + 1) * wide] = value.astype(bf16)


def advance(place, pairs, planes, after=(), steps=2):
    blocks, *_, shard, wide = (pairs + planes)[0].held[0][0].shape
    width = wide * len((pairs + planes)[0].axes)
    shapes, places = [], []
    for r in pairs:
        shapes += [jax.ShapeDtypeStruct((blocks, 2, 2, shard, width // len(r.axes)), bf16)] * (2 * len(r.axes))
    places += [0] * len(shapes)
    if planes:
        shapes += [jax.ShapeDtypeStruct((len(planes), blocks, shard, width), bf16)] * 4
        places += [1] * 4
    operands = [v for r in pairs + planes for held in r.held for v in held]

    def spec(s, at=0):
        n = len(s.shape)
        block = tuple(d // steps if m == at else d for m, d in enumerate(s.shape))
        return pl.BlockSpec(block, lambda b, p: (0,) * at + (b,) + (0,) * (n - 1 - at))

    def body(place_ref, *refs):
        ins, outs = refs[: len(operands)], refs[len(operands) :]
        for r in pairs:
            count = 2 * len(r.axes)
            pair_body(place_ref, r, ins[:count], outs[:count])
            ins, outs = ins[count:], outs[count:]
        for n, r in enumerate(planes):
            count = 2 * len(r.axes)
            plane_body(place_ref, r, ins[:count], [ref.at[n] for ref in outs])
            ins = ins[count:]

    outs = call(
        body,
        0,
        sum(v.size * v.dtype.itemsize for v in operands) * 2,
        after=after,
        grid_spec=pltpu.PrefetchScalarGridSpec(
            num_scalar_prefetch=1,
            grid=(steps,),
            in_specs=[spec(v) for v in operands],
            out_specs=[spec(s, at) for s, at in zip(shapes, places)],
        ),
        out_shape=shapes,
    )(place, *operands)
    for r in pairs:
        count = 2 * len(r.axes)
        r.second(outs[:count])
        outs = outs[count:]
    terms = []
    for m, v in enumerate(outs):
        for r in planes:
            r.made = v
        v = v.reshape(-1, shard, width)
        terms.append(
            lax.ppermute(
                v, AXES, to_place(lambda z, y, x, c, m=m: (2 * c + ((z ^ m) >> 1), y, x, (z ^ m) & 1))
            )
        )
    return terms


def everywhere(value):
    def get(move):
        return lax.ppermute(value, AXES, to_place(move))

    near = get(lambda z, y, x, c: (z ^ 1, y, x, c))
    far = get(lambda z, y, x, c: (z ^ 2, y, x, c))
    last = get(lambda z, y, x, c: (z ^ 3, y, x, c))
    value = (value + near) + (far + last)
    by_x, by_y = over_x(value), over_y(value)
    across = get(lambda z, y, x, c: (z, 1 - y, 1 - x, c))
    value = (value + by_x) + (by_y + across)
    return value + over_c(value)


def pack_body(slot_ref, *refs, orders, per):
    terms, (shard_ref, out_ref, square_ref) = refs[: len(orders) * per], refs[len(orders) * per :]
    total = jnp.zeros(square_ref.shape, f32)
    for n, order in enumerate(orders):
        for m, b in enumerate(order):
            value = terms[n * per][m].astype(f32)
            for t in range(1, per):
                value = value + terms[n * per + t][m].astype(f32)
            shard_ref[b] = value
            total = total + value * value
    square_ref[...] = total

    def one(j, carry):
        b = slot_ref[j]

        @pl.when(b >= 0)
        def _():
            out_ref[j] = shard_ref[jnp.maximum(b, 0)].astype(bf16)

        @pl.when(b < 0)
        def _():
            out_ref[j] = jnp.zeros(out_ref.shape[1:], bf16)

        return carry

    lax.fori_loop(0, out_ref.shape[0], one, 0)


def pack(slots, terms, orders, after=()):
    per = len(terms[0])
    _, shard, width = terms[0][0].shape
    terms = [v for t in terms for v in t]
    vmem = pl.BlockSpec(memory_space=pltpu.VMEM)
    return call(
        functools.partial(pack_body, orders=orders, per=per),
        0,
        sum(v.size * v.dtype.itemsize for v in terms) * 2,
        after=after,
        in_specs=[pl.BlockSpec(memory_space=pltpu.SMEM)] + [vmem] * len(terms),
        out_specs=[vmem] * 3,
        out_shape=[
            jax.ShapeDtypeStruct((sum(map(len, orders)), shard, width), f32),
            jax.ShapeDtypeStruct((slots.shape[0], shard, width), bf16),
            jax.ShapeDtypeStruct((shard, width), f32),
        ],
    )(slots, *terms)


def to_low_body(l_ref, r_ref, l_low, r_low):
    l_low[...] = l_ref[...].astype(bf16)
    r_low[...] = r_ref[...].astype(bf16)


def to_low(left, right, after=(), step=384):
    width = left.shape[0]
    rows = pl.BlockSpec((step, width), lambda i: (i, 0))
    return call(
        to_low_body,
        0,
        12 * width**2,
        after=after,
        grid=(width // step,),
        in_specs=[rows, rows],
        out_specs=[rows, rows],
        out_shape=[jax.ShapeDtypeStruct((width, width), bf16)] * 2,
    )(left, right)


def precondition_body(scale_ref, s_ref, l_ref, r_ref, p_ref, s_low):
    @pl.when(pl.program_id(0) == 0)
    def _():
        s_low[...] = (s_ref[...].astype(f32) * scale_ref[0]).astype(bf16)

    left = mm(l_ref[...], s_low[...], NN)
    p_ref[...] = (scale_ref[1] * mm(left.astype(bf16), r_ref[...], NN)).astype(bf16)


def precondition(scales, block, left, right, step=384):
    width = block.shape[0]
    whole = pl.BlockSpec((width, width), lambda i: (0, 0))
    rows = pl.BlockSpec((step, width), lambda i: (i, 0))
    return call(
        precondition_body,
        4 * width**3,
        8 * width**2,
        grid=(width // step,),
        in_specs=[pl.BlockSpec(memory_space=pltpu.SMEM), whole, rows, whole],
        out_specs=rows,
        out_shape=jax.ShapeDtypeStruct((width, width), bf16),
        scratch_shapes=[pltpu.VMEM((width, width), bf16)],
    )(scales, block, left, right)


def statistics_body(has_ref, scale_ref, s_ref, l_ref, r_ref, nl_ref, nr_ref, s_low, *, step):
    i = pl.program_id(0)
    width = s_ref.shape[0]

    @pl.when(i == 0)
    def _():
        s_low[...] = (s_ref[...].astype(f32) * scale_ref[0]).astype(bf16)

    factor = (1.0 - decay_beta) * (scale_ref[1] * scale_ref[1] / width)
    at = pl.multiple_of(i * step, step)

    @pl.when(has_ref[0] != 0)
    def _():
        nl_ref[...] = decay_beta * l_ref[...] + factor * mm(s_low[pl.ds(at, step), :], s_low[...], NT)
        nr_ref[...] = decay_beta * r_ref[...] + factor * mm(s_low[:, pl.ds(at, step)], s_low[...], TN)

    @pl.when(has_ref[0] == 0)
    def _():
        nl_ref[...] = l_ref[...]
        nr_ref[...] = r_ref[...]


def statistics(has, scales, block, left, right, step=256):
    width = block.shape[0]
    whole = pl.BlockSpec((width, width), lambda i: (0, 0))
    rows = pl.BlockSpec((step, width), lambda i: (i, 0))
    smem = pl.BlockSpec(memory_space=pltpu.SMEM)
    return call(
        functools.partial(statistics_body, step=step),
        4 * width**3,
        18 * width**2,
        grid=(width // step,),
        in_specs=[smem, smem, whole, rows, rows],
        out_specs=[rows, rows],
        out_shape=[jax.ShapeDtypeStruct((width, width), f32)] * 2,
        scratch_shapes=[pltpu.VMEM((width, width), bf16)],
    )(has, scales, block, left, right)


def update_body(owner_ref, factor_ref, p_ref, shard_ref, block_ref, clip_ref, new_ref, copy_ref):
    for b in range(shard_ref.shape[0]):
        clip_ref[b] = shard_ref[b] * factor_ref[0]
        value = block_ref[b] - matrix_rate * p_ref[owner_ref[b]].astype(f32)
        new_ref[b] = value
        copy_ref[b] = value.astype(bf16)


def update(owners, factor, returned, shards, blocks):
    smem, vmem = pl.BlockSpec(memory_space=pltpu.SMEM), pl.BlockSpec(memory_space=pltpu.VMEM)
    return call(
        update_body,
        0,
        returned.size * 2 + shards.size * 18,
        in_specs=[smem, smem, vmem, vmem, vmem],
        out_specs=[vmem] * 3,
        out_shape=[
            jax.ShapeDtypeStruct(shards.shape, f32),
            jax.ShapeDtypeStruct(shards.shape, f32),
            jax.ShapeDtypeStruct(shards.shape, bf16),
        ],
    )(owners, factor, returned, shards, blocks)


def to_all(value):
    return lax.all_to_all(value, AXES, split_axis=0, concat_axis=0, tiled=True)


def per_device(
    tokens,
    segment_ids,
    cotangent,
    blocks,
    vectors,
    stat_left,
    stat_right,
    root_left,
    root_right,
    vec_stat,
    owners,
    *,
    paired,
):
    rows_here, seq_len, width = tokens.shape
    count = rows_here * seq_len
    splits = FF // width
    slot_count = lax.axis_size(AXES)
    my_index = lax.axis_index(AXES)
    shard = width // slot_count
    vec_rows = vectors.shape[0]

    low_blocks, low_vectors = blocks.astype(bf16), vectors.astype(bf16)
    everyone = jnp.broadcast_to(low_vectors.reshape(1, -1), (slot_count, vec_rows * shard))
    vecs = to_all(everyone).reshape(slot_count, vec_rows, shard)
    vecs = vecs.transpose(1, 0, 2).reshape(vec_rows, width).astype(f32)
    half = splits // 2
    mlp_weights = lax.all_gather(low_blocks[4:], AXES, axis=1, tiled=True)

    flat_tokens = tokens.reshape(count, width)
    dy = cotangent.reshape(count, width)
    tables = rotary_tables(segment_ids)
    place = jnp.stack(grid_places()).astype(jnp.int32)
    if paired:
        pieces = gather_staged(low_blocks[:4])
    else:
        pieces = [lax.all_gather(low_blocks[:4], AXES, axis=1, tiled=True)]
    q, k, v, do, acts, attn_weights = project(place, flat_tokens, dy, pieces, vecs, tables)
    og, attn_sums, acts = attend(segment_ids, q, k, v, do, tables, acts)
    orders = [list(range(4))]
    for first in (0, half):
        orders.append([base + first + j for base in (4, 4 + splits) for j in range(half)])
    if paired:
        acts_pair, og_pair = (acts, over_c(acts)), (og, over_c(og))
        dys = (acts_pair, 2, 1)
        ed0, up_sum0 = hidden(0, acts, mlp_weights, vecs)
        ed0_pair = (ed0, over_c(ed0))
        ed1, up_sum1 = hidden(half, acts, mlp_weights, vecs, after=(ed0, acts_pair[1]))
        ed1_pair = (ed1, over_c(ed1))

        def grads(left, two, one, after):
            operands = ((acts_pair, left, 1), two, one, dys, shard, "xy")
            return Reduction("xy", half_grads(place, *operands, after=after))

        attn = grads(0, (og_pair, 3, 1), (og_pair, 0, 3), (ed1,))
        low = grads(1, (ed0_pair, 0, half), (ed0_pair, half, half), (attn.made,))
        advance(place, [attn], [], after=(low.made,))
        high = grads(1, (ed1_pair, 0, half), (ed1_pair, half, half), (attn.made,))
        advance(place, [low], [], after=(high.made, *[got for _, got in attn.held]))
        part, one_sums = grad_one(flat_tokens, dy, (og, 0, 3), attn_weights, vecs, after=(low.made,))
        terms = [advance(place, [high], [attn, low], after=(part,))]
        es, dus = [(v, 0, half) for v in (ed0, ed1)], [(v, half, half) for v in (ed0, ed1)]
        grad_in, two_sums = grad_two(flat_tokens, part, dus, mlp_weights, vecs, after=(high.made,))
        terms.append(advance(place, [], [high], after=(grad_in,)))
        last = high.made
        orders = [orders[0] + orders[1], orders[2]]
    else:
        ed0, up_sum0 = hidden(0, acts, mlp_weights, vecs)
        ed1, up_sum1 = hidden(half, acts, mlp_weights, vecs)
        grads = [
            full_grads(acts[0], og[3:], og[:3], dy),
            full_grads(acts[1], ed0[:half], ed0[half:], dy),
            full_grads(acts[1], ed1[:half], ed1[half:], dy),
        ]
        terms = [[lax.psum_scatter(v, AXES, scatter_dimension=1, tiled=True)] for v in grads]
        es, dus = [(v, 0, half) for v in (ed0, ed1)], [(v, half, half) for v in (ed0, ed1)]
        part, one_sums = grad_one(flat_tokens, dy, (og, 0, 3), attn_weights, vecs)
        grad_in, two_sums = grad_two(flat_tokens, part, dus, mlp_weights, vecs)
        last = grad_in
    up_sums = [up_sum0, up_sum1]

    one_sums, two_sums = jnp.sum(one_sums, axis=1), jnp.sum(two_sums, axis=1)
    qkv_sums = jnp.sum(attn_sums, axis=1)
    up_sums = jnp.sum(jnp.concatenate(up_sums, axis=0), axis=1)
    bias_sum = one_sums[2:]
    grad_vectors = jnp.concatenate(
        [one_sums[:2], two_sums, qkv_sums, bias_sum, up_sums, bias_sum], axis=0
    )
    slot_ids = jnp.arange(slot_count, dtype=jnp.int32)
    match = owners[None, :] == slot_ids[:, None]
    slots = jnp.sum(jnp.where(match, jnp.arange(1, owners.shape[0] + 1, dtype=jnp.int32)[None], 0), axis=1) - 1
    has_block = jnp.any(owners == my_index)
    out = output(flat_tokens, (og, 3, 1), es, attn_weights, mlp_weights, vecs, after=(last,))
    shards, outgoing, squares = pack(slots, terms, orders, after=(out,))
    left_low, right_low = to_low(root_left[0], root_right[0], after=(squares,))
    local = jnp.concatenate([grad_vectors, jnp.sum(squares, axis=0)[None], jnp.zeros((2, width), f32)])
    total = everywhere(local) if paired else lax.psum(local, AXES)
    vector_sums = total[:vec_rows]
    square_sum = jnp.sum(total[vec_rows]) + jnp.sum(vector_sums * vector_sums)
    shard_vectors = lax.dynamic_slice_in_dim(vector_sums, my_index * shard, shard, axis=1)
    grad_norm = jnp.sqrt(square_sum)
    factor = jnp.minimum(1.0, clip_level / grad_norm)
    root_count = math.sqrt(NPARAM)

    scale = factor * root_count
    power = jnp.exp2(jnp.floor(jnp.log2(jnp.maximum(scale, 1e-30)))).astype(bf16).astype(f32)
    scales = jnp.stack([power, scale / power])
    owned = to_all(outgoing).reshape(width, width)
    precond = precondition(scales, owned, left_low, right_low)
    returned = to_all(precond.reshape(slot_count, shard, width))
    new_left, new_right = statistics(
        has_block.astype(jnp.int32).reshape(1), scales, owned, stat_left[0], stat_right[0]
    )
    clipped_blocks, new_blocks, blocks_copy = update(owners, factor.reshape(1), returned, shards, blocks)
    clipped_vectors = shard_vectors * factor
    scaled_vectors = clipped_vectors * root_count
    new_vec_stat = decay_beta * vec_stat + (1.0 - decay_beta) * (scaled_vectors * scaled_vectors)
    new_vectors = vectors - vector_rate * scaled_vectors * lax.rsqrt(new_vec_stat)
    return (
        out.reshape(tokens.shape),
        grad_in.reshape(tokens.shape),
        clipped_blocks,
        clipped_vectors,
        grad_norm,
        new_left[None],
        new_right[None],
        new_vec_stat,
        new_blocks,
        new_vectors,
        blocks_copy,
        new_vectors.astype(bf16),
    )


def solution(mesh):
    rows = P(AXES, None, None)
    split_rows = P(None, AXES, None)
    split_columns = P(None, AXES)
    paired = dict(mesh.shape) == {"wide": 8, "narrow": 4}
    return jax.shard_map(
        functools.partial(per_device, paired=paired),
        mesh=mesh,
        in_specs=(
            rows, P(AXES, None), rows, split_rows, split_columns,
            rows, rows, rows, rows, split_columns, P(),
        ),
        out_specs=(
            rows, rows, split_rows, split_columns, P(), rows, rows,
            split_columns, split_rows, split_columns, split_rows, split_columns,
        ),
        check_vma=False,
    )
```

```python
import functools
import math

import jax
import jax.numpy as jnp
import numpy as np
from jax import lax
from jax.experimental import pallas as pl
from jax.experimental.pallas import tpu as pltpu
from jax.sharding import PartitionSpec as P

H = 12
FF = 3072
ROT = 16
NPARAM = 7087872
LONGEST = 256

clip_level = 1.0
matrix_rate = 0.03
vector_rate = 0.2
decay_beta = 0.5
norm_epsilon = 1e-05

f32 = jnp.float32
bf16 = jnp.bfloat16
AXES = ("wide", "narrow")
LANES = 128
MIB = 2**20

NN = (((1,), (0,)), ((), ()))
NT = (((1,), (1,)), ((), ()))
TN = (((0,), (0,)), ((), ()))


def mm(left, right, dims):
    return lax.dot_general(left, right, dims, preferred_element_type=f32)


def call(body, flops, moved, vmem=64, after=(), **rest):
    spec = rest.pop("grid_spec", None)
    grid = spec.grid if spec is not None else rest.get("grid", ())
    later = len(after)
    if later:
        held = [pl.BlockSpec(memory_space=pl.ANY)] * later
        if spec is not None:
            first = spec.num_scalar_prefetch + len(spec.in_specs)
            spec = pltpu.PrefetchScalarGridSpec(
                num_scalar_prefetch=spec.num_scalar_prefetch,
                grid=spec.grid,
                in_specs=list(spec.in_specs) + held,
                out_specs=spec.out_specs,
                scratch_shapes=spec.scratch_shapes,
            )
        else:
            first = len(rest["in_specs"])
            rest["in_specs"] = list(rest["in_specs"]) + held
        inner = body

        def body(*refs):
            inner(*refs[:first], *refs[first + later :])

    if spec is not None:
        rest["grid_spec"] = spec
    made = pl.pallas_call(
        body,
        compiler_params=pltpu.CompilerParams(
            vmem_limit_bytes=vmem * MIB,
            dimension_semantics=("arbitrary",) * len(grid),
        ),
        cost_estimate=pl.CostEstimate(
            flops=int(flops), bytes_accessed=int(moved), transcendentals=0
        ),
        **rest,
    )
    return lambda *operands: made(*operands, *after)


def sub_sum(values):
    return jnp.sum(values.reshape(-1, 8, values.shape[-1]), axis=0)


def rotary_tables(segment_ids):
    rows, length = segment_ids.shape
    start = jnp.sum(
        (segment_ids[:, None, :] < segment_ids[:, :, None]).astype(jnp.int32), axis=-1
    )
    offset = (jnp.arange(length, dtype=jnp.int32)[None] - start).astype(f32).reshape(-1, 1)
    half = ROT // 2
    lane = np.arange(LANES) % 64
    rates = np.where(lane < ROT, 10000.0 ** (-2.0 * (lane % half) / ROT), 0.0)
    angle = offset * jnp.asarray(rates, f32)[None]
    cosine, sine = jnp.cos(angle), jnp.sin(angle)
    first = sine * jnp.asarray(np.where(lane < half, -1.0, 0.0), f32)[None]
    second = sine * jnp.asarray(np.where((lane >= half) & (lane < ROT), 1.0, 0.0), f32)[None]
    return cosine, first, second


def rotate(values, cosine, first, second):
    parts = []
    for at in range(0, values.shape[1], LANES):
        part = values[:, at : at + LANES]
        parts.append(
            part * cosine
            + pltpu.roll(part, LANES - ROT // 2, 1) * first
            + pltpu.roll(part, ROT // 2, 1) * second
        )
    return jnp.concatenate(parts, axis=1)


def rotate_back(values, cosine, first, second):
    return (
        values * cosine
        - pltpu.roll(values, LANES - ROT // 2, 1) * first
        - pltpu.roll(values, ROT // 2, 1) * second
    )


def assemble(place_ref, pieces, w_ref):
    z, y, x, c = place_ref[0], place_ref[1], place_ref[2], place_ref[3]
    blocks, rows = w_ref.shape[0], 2 * pieces[0].shape[2]

    def plane(t, carry):
        apart = lax.rem(z - t + 4, 4)

        def put(here, there, at, ry, rx):
            chip = (t * 2 + (y ^ ry)) * 2 + (x ^ rx)
            where = pl.ds(pl.multiple_of(chip * rows, rows), rows)
            for order, wanted in (((here, there), c == 0), ((there, here), c != 0)):

                @pl.when(wanted)
                def _(order=order):
                    for n in range(blocks):
                        w_ref[n, where, :] = jnp.concatenate([ref[at, n] for ref in order], axis=0)

        for m, (ry, rx) in enumerate(((0, 0), (0, 1), (1, 0))):
            put(pieces[m], pieces[5 + m], apart, ry, rx)
        pl.when(apart < 2)(lambda: put(pieces[3], pieces[8], apart, 1, 1))
        pl.when(apart >= 2)(lambda: put(pieces[4], pieces[9], apart - 2, 1, 1))
        return carry

    lax.fori_loop(0, 4, plane, 0)


def project_body(place_ref, x_ref, dy_ref, vec_ref, c_ref, a_ref, b_ref, *refs):
    *pieces, q_ref, k_ref, v_ref, do_ref, acts_ref, w_ref = refs

    @pl.when(pl.program_id(0) == 0)
    def _():
        if len(pieces) > 1:
            assemble(place_ref, pieces, w_ref)
        else:
            w_ref[...] = pieces[0][...]

    unit, _ = normed(x_ref[...].astype(f32))
    a1 = (unit * vec_ref[0:1, :] + vec_ref[1:2, :]).astype(bf16)
    acts_ref[0] = a1
    acts_ref[1] = (unit * vec_ref[2:3, :] + vec_ref[3:4, :]).astype(bf16)
    acts_ref[2] = dy_ref[...]
    tables = (c_ref[...], a_ref[...], b_ref[...])
    q_ref[...] = rotate(mm(a1, w_ref[0], NN) + vec_ref[4:5, :], *tables).astype(bf16)
    k_ref[...] = rotate(mm(a1, w_ref[1], NN) + vec_ref[5:6, :], *tables).astype(bf16)
    v_ref[...] = (mm(a1, w_ref[2], NN) + vec_ref[6:7, :]).astype(bf16)
    do_ref[...] = mm(dy_ref[...], w_ref[3], NT).astype(bf16)


def project(place, x, dy, pieces, vecs, tables, step=256):
    count, width = x.shape
    token = pl.BlockSpec((step, width), lambda i, s: (i, 0))
    table = pl.BlockSpec((step, LANES), lambda i, s: (i, 0))
    once = pl.Buffered(1)
    return call(
        project_body,
        8 * count * width * width,
        20 * count * width + 16 * width * width,
        grid_spec=pltpu.PrefetchScalarGridSpec(
            num_scalar_prefetch=1,
            grid=(count // step,),
            in_specs=[token, token, pl.BlockSpec(vecs.shape, lambda i, s: (0, 0)), table, table, table]
            + [pl.BlockSpec(v.shape, lambda i, s, n=v.ndim: (0,) * n, pipeline_mode=once) for v in pieces],
            out_specs=[token] * 4
            + [
                pl.BlockSpec((3, step, width), lambda i, s: (0, i, 0)),
                pl.BlockSpec((4, width, width), lambda i, s: (0, 0, 0)),
            ],
        ),
        out_shape=[jax.ShapeDtypeStruct((count, width), bf16)] * 4
        + [jax.ShapeDtypeStruct((3, count, width), bf16), jax.ShapeDtypeStruct((4, width, width), bf16)],
    )(place, x, dy, vecs, *tables, *pieces)


def attend_body(
    acts_ref, col_ref, row_ref, q_ref, k_ref, v_ref, do_ref, c_ref, a_ref, b_ref,
    g_ref, sum_ref, acts_out_ref, mask_ref, *, block,
):
    length = q_ref.shape[0]
    steps = length // block

    def reach(i):
        return max(0, (i * block - (LONGEST - 1)) // block * block), (i + 1) * block

    @pl.when(pl.program_id(1) == 0)
    def _():
        for i in range(steps):
            lo, hi = reach(i)
            key = lax.broadcasted_iota(jnp.int32, (hi - lo, block), 0) + lo
            query = lax.broadcasted_iota(jnp.int32, (hi - lo, block), 1) + i * block
            same = col_ref[lo:hi, :] == row_ref[0, :, i * block : hi]
            mask = jnp.where(same & (key <= query), 0.0, -jnp.inf)
            mask_ref[i, 0 : hi - lo, 0:block] = mask
            mask_ref[i, 0 : hi - lo, block:] = mask

    low = lax.broadcasted_iota(jnp.int32, (1, LANES), 1) < 64
    eighth = jnp.asarray(0.125, bf16)
    zero = jnp.zeros((), bf16)

    def both(part):
        return jnp.concatenate([jnp.where(low, part, zero), jnp.where(low, zero, part)], axis=0)

    def unstack(part):
        return jnp.concatenate([part[0:64, 0:block], part[64:, block:]], axis=0).T

    pairs = []
    for at in range(0, q_ref.shape[1], LANES):
        lanes = slice(at, at + LANES)
        keys, values = k_ref[:, lanes], v_ref[:, lanes]
        pairs.append(
            (lanes, keys, values, (keys * eighth).T, values.T, q_ref[:, lanes] * eighth, do_ref[:, lanes])
        )
    q_sums = [jnp.zeros((8, LANES), f32) for _ in pairs]
    dks = [[None] * steps for _ in pairs]
    dvs = [[None] * steps for _ in pairs]

    def add(parts, n, value):
        parts[n] = value if parts[n] is None else parts[n] + value

    for i in range(steps):
        lo, hi = reach(i)
        here = slice(i * block, hi)
        for p, (lanes, keys, values, keys_t, values_t, queries, grads) in enumerate(pairs):
            q2, do2 = both(queries[here]), both(grads[here])
            scores = mm(keys[lo:hi], q2, NT) + mask_ref[i, 0 : hi - lo, :]
            d_soft = mm(values[lo:hi], do2, NT)
            raised = jnp.exp(scores - jnp.max(scores, axis=0, keepdims=True))
            soft = raised * (1.0 / jnp.sum(raised, axis=0, keepdims=True))
            inner = jnp.sum(soft * d_soft, axis=0, keepdims=True)
            soft_low = soft.astype(bf16)
            d_scores = (soft * (d_soft - inner)).astype(bf16)
            g_ref[3, here, lanes] = unstack(mm(values_t[:, lo:hi], soft_low, NN)).astype(bf16)
            dq = rotate_back(
                unstack(mm(keys_t[:, lo:hi], d_scores, NN)), c_ref[here, :], a_ref[here, :], b_ref[here, :]
            ).astype(bf16)
            g_ref[0, here, lanes] = dq
            q_sums[p] = q_sums[p] + sub_sum(dq.astype(f32))
            dk, dv = mm(d_scores, q2, NN), mm(soft_low, do2, NN)
            for n in range(lo // block, i + 1):
                rows = slice(n * block - lo, (n + 1) * block - lo)
                add(dks[p], n, dk[rows])
                add(dvs[p], n, dv[rows])
    for p, (lanes, *_) in enumerate(pairs):
        dk = rotate_back(jnp.concatenate(dks[p], axis=0), c_ref[...], a_ref[...], b_ref[...]).astype(bf16)
        dv = jnp.concatenate(dvs[p], axis=0).astype(bf16)
        g_ref[1, :, lanes] = dk
        g_ref[2, :, lanes] = dv
        sum_ref[0, :, lanes] = q_sums[p]
        sum_ref[1, :, lanes] = sub_sum(dk.astype(f32))
        sum_ref[2, :, lanes] = sub_sum(dv.astype(f32))


def attend(segment_ids, q, k, v, do, tables, acts, block=256, lanes=3 * LANES):
    rows, length = segment_ids.shape
    count, width = q.shape
    block = min(block, length)
    token = pl.BlockSpec((length, lanes), lambda r, h: (r, h))
    table = pl.BlockSpec((length, LANES), lambda r, h: (r, 0))
    return call(
        functools.partial(attend_body, block=block),
        24 * count * length * width,
        24 * count * width,
        grid=(rows, width // lanes),
        input_output_aliases={0: 2},
        in_specs=[
            pl.BlockSpec(memory_space=pl.ANY),
            pl.BlockSpec((length, 1), lambda r, h: (r, 0)),
            pl.BlockSpec((1, 1, length), lambda r, h: (r, 0, 0)),
            token,
            token,
            token,
            token,
            table,
            table,
            table,
        ],
        out_specs=[
            pl.BlockSpec((4, length, lanes), lambda r, h: (0, r, h)),
            pl.BlockSpec((3, 8, lanes), lambda r, h: (0, r, h)),
            pl.BlockSpec(memory_space=pl.ANY),
        ],
        out_shape=[
            jax.ShapeDtypeStruct((4, count, width), bf16),
            jax.ShapeDtypeStruct((3, 8 * rows, width), f32),
            jax.ShapeDtypeStruct(acts.shape, acts.dtype),
        ],
        scratch_shapes=[pltpu.VMEM((length // block, length, 2 * block), f32)],
    )(
        acts,
        segment_ids.reshape(-1, 1),
        segment_ids.reshape(rows, 1, length),
        q,
        k,
        v,
        do,
        *tables,
    )


def half_grads_body(place_ref, *refs, first, second, steps, axes):
    l1o, l1p, l2o, l2p, r1o, r1p, r2o, r2p, *outs, acc = refs
    i = pl.program_id(0)
    y, x = place_ref[1], place_ref[2]

    def part(n):
        if n < first:
            value = mm(l1o[0], r1o[n], TN) + mm(l1p[0], r1p[n], TN)
        else:
            value = mm(l2o[n - first], r2o[0], TN) + mm(l2p[n - first], r2p[0], TN)
        return value.reshape(acc.shape[1:])

    @pl.when(i == 0)
    def _():
        for n in range(first + second):
            acc[n] = part(n)

    @pl.when(i > 0)
    def _():
        for n in range(first + second):
            acc[n] += part(n)

    @pl.when(i == steps - 1)
    def _():
        for n in range(first + second):
            for r, axis in enumerate(axes):
                wide = outs[0].shape[-1]
                columns = slice(r * wide, (r + 1) * wide)
                for ref, other in zip(outs[2 * r : 2 * r + 2], (0, 1)):
                    if axis == "x":
                        value = acc[n, :, :, x ^ other, :, :, columns]
                    else:
                        value = acc[n, :, y ^ other, :, :, :, columns]
                    ref[n] = value.astype(bf16)


def layers(part, step, lanes, half=False):
    _, first, count = part
    return pl.BlockSpec((count, step, lanes), lambda i, *s: (first // count, i, s[0][3] if half else 0))


def half_grads(place, left_one, left_two, right_one, right_two, shard, axes, after=(), step=256):
    first, second = right_one[2], left_two[2]
    _, count, width = right_two[0][0].shape
    half = width // 2
    blocks = first + second
    steps = count // step
    shape = (blocks, 2, 2, 2, shard, width // len(axes))
    out = pl.BlockSpec(shape, lambda i, s: (0, 0, 0, 0, 0, 0))
    return call(
        functools.partial(half_grads_body, first=first, second=second, steps=steps, axes=axes),
        blocks * 2 * count * width * width,
        blocks * 4 * count * width,
        after=after,
        grid_spec=pltpu.PrefetchScalarGridSpec(
            num_scalar_prefetch=1,
            grid=(steps,),
            in_specs=[layers(left_one, step, half, True)] * 2
            + [layers(left_two, step, half, True)] * 2
            + [layers(right_one, step, width)] * 2
            + [layers(right_two, step, width)] * 2,
            out_specs=[out] * (2 * len(axes)),
            scratch_shapes=[pltpu.VMEM((blocks, 2, 2, 2, 2, shard, width), f32)],
        ),
        out_shape=[jax.ShapeDtypeStruct(shape, bf16)] * (2 * len(axes)),
    )(place, *left_one[0], *left_two[0], *right_one[0], *right_two[0])


def full_grads(left_one, left_two, right_one, right_two):
    one = jnp.einsum("td,nte->nde", left_one, right_one, preferred_element_type=f32)
    two = jnp.einsum("ntd,te->nde", left_two, right_two, preferred_element_type=f32)
    return jnp.concatenate([one, two], axis=0)


def gelu_parts(u):
    raised = jnp.exp(-0.5 * (u * u))
    t = 1.0 / (1.0 + (0.3275911 * math.sqrt(0.5)) * jnp.abs(u))
    poly = 1.061405429 * t - 1.453152027
    poly = poly * t + 1.421413741
    poly = poly * t - 0.284496736
    poly = (poly * t + 0.254829592) * t
    tail = 0.5 * poly * raised
    return jnp.where(u < 0, tail, 1.0 - tail), raised * (1.0 / math.sqrt(2.0 * math.pi))


def hidden_body(a2_ref, dy_ref, wu_ref, wd_ref, vec_ref, out_ref, sum_ref, *, first):
    row = first + pl.program_id(0)
    u = mm(a2_ref[0], wu_ref[0], NN) + vec_ref[pl.ds(row, 1), :]
    de = mm(dy_ref[0], wd_ref[0], NT)
    dist, density = gelu_parts(u)
    out_ref[0, 0] = (u * dist).astype(bf16)
    du = (de * (dist + u * density)).astype(bf16)
    out_ref[1, 0] = du
    part = sub_sum(du.astype(f32))

    @pl.when(pl.program_id(1) == 0)
    def _():
        sum_ref[0] = part

    @pl.when(pl.program_id(1) > 0)
    def _():
        sum_ref[0] += part


def hidden(first, acts, weights, vecs, after=(), step=512):
    _, count, width = acts.shape
    splits = weights.shape[0] // 2
    blocks = splits // 2
    both, sums = call(
        functools.partial(hidden_body, first=8 + first),
        blocks * 4 * count * width * width,
        blocks * (8 * count * width + 4 * width * width),
        after=after,
        grid=(blocks, count // step),
        in_specs=[
            pl.BlockSpec((1, step, width), lambda j, i: (1, i, 0)),
            pl.BlockSpec((1, step, width), lambda j, i: (2, i, 0)),
            pl.BlockSpec((1, width, width), lambda j, i: (first + j, 0, 0)),
            pl.BlockSpec((1, width, width), lambda j, i: (splits + first + j, 0, 0)),
            pl.BlockSpec(vecs.shape, lambda j, i: (0, 0)),
        ],
        out_specs=[
            pl.BlockSpec((2, 1, step, width), lambda j, i: (0, j, i, 0)),
            pl.BlockSpec((1, 8, width), lambda j, i: (j, 0, 0)),
        ],
        out_shape=[
            jax.ShapeDtypeStruct((2, blocks, count, width), bf16),
            jax.ShapeDtypeStruct((blocks, 8, width), f32),
        ],
    )(acts, acts, weights, weights, vecs)
    return both.reshape(2 * blocks, count, width), sums


def norm_back(grad, unit, scale, gain):
    grad = grad * gain
    first = jnp.mean(grad, axis=1, keepdims=True)
    second = jnp.mean(grad * unit, axis=1, keepdims=True)
    return scale * (grad - first - unit * second)


def hidden_sum(hidden_refs, w_ref, dims, acc):
    at = 0
    for ref in hidden_refs:
        for m in range(ref.shape[0]):
            part = mm(ref[m], w_ref[at], dims)
            acc = part if acc is None else acc + part
            at += 1
    return acc


def output_body(x_ref, o_ref, *refs, splits):
    *e_refs, wo_ref, w_ref, vec_ref, out_ref = refs
    acc = hidden_sum(e_refs, w_ref, NN, mm(o_ref[0], wo_ref[0], NN))
    bias = vec_ref[7:8, :] + vec_ref[8 + splits : 9 + splits, :]
    out_ref[...] = (x_ref[...].astype(f32) + acc + bias).astype(bf16)


def resident(blocks, width, at):
    return pl.BlockSpec((blocks, width, width), lambda i: (at, 0, 0), pipeline_mode=pl.Buffered(1))


def output(x, o, es, wa, wm, vecs, after=(), step=256):
    count, width = x.shape
    splits = wm.shape[0] // 2
    token = pl.BlockSpec((step, width), lambda i: (i, 0))
    return call(
        functools.partial(output_body, splits=splits),
        10 * count * width * width,
        14 * count * width + 10 * width * width,
        after=after,
        grid=(count // step,),
        in_specs=[token]
        + [layers(v, step, width) for v in (o, *es)]
        + [resident(1, width, 3), resident(splits, width, 1), pl.BlockSpec(vecs.shape, lambda i: (0, 0))],
        out_specs=token,
        out_shape=jax.ShapeDtypeStruct((count, width), bf16),
    )(x, *[v[0] for v in (o, *es)], wa, wm, vecs)


def normed(x):
    centred = x - jnp.mean(x, axis=1, keepdims=True)
    scale = lax.rsqrt(jnp.mean(centred * centred, axis=1, keepdims=True) + norm_epsilon)
    return centred * scale, scale


def add_sums(sum_ref, sums):
    sums = [sub_sum(t) for t in sums]

    @pl.when(pl.program_id(0) == 0)
    def _():
        for n, s in enumerate(sums):
            sum_ref[n] = s

    @pl.when(pl.program_id(0) > 0)
    def _():
        for n, s in enumerate(sums):
            sum_ref[n] += s


def grad_one_body(x_ref, dy_ref, g_ref, wa_ref, vec_ref, part_ref, sum_ref):
    dy = dy_ref[...].astype(f32)
    grad = mm(g_ref[0], wa_ref[0], NT) + mm(g_ref[1], wa_ref[1], NT) + mm(g_ref[2], wa_ref[2], NT)
    unit, scale = normed(x_ref[...].astype(f32))
    part_ref[...] = dy + norm_back(grad, unit, scale, vec_ref[0:1, :])
    add_sums(sum_ref, (grad * unit, grad, dy))


def grad_one(x, dy, g, wa, vecs, after=(), step=256):
    count, width = x.shape
    token = pl.BlockSpec((step, width), lambda i: (i, 0))
    return call(
        grad_one_body,
        6 * count * width * width,
        14 * count * width + 6 * width * width,
        after=after,
        grid=(count // step,),
        in_specs=[
            token,
            token,
            layers(g, step, width),
            resident(3, width, 0),
            pl.BlockSpec(vecs.shape, lambda i: (0, 0)),
        ],
        out_specs=[token, pl.BlockSpec((3, 8, width), lambda i: (0, 0, 0))],
        out_shape=[jax.ShapeDtypeStruct((count, width), f32), jax.ShapeDtypeStruct((3, 8, width), f32)],
    )(x, dy, g[0], wa, vecs)


def grad_two_body(x_ref, part_ref, *refs):
    *du_refs, w_ref, vec_ref, grad_ref, sum_ref = refs
    grad = hidden_sum(du_refs, w_ref, NT, None)
    unit, scale = normed(x_ref[...].astype(f32))
    grad_ref[...] = (part_ref[...] + norm_back(grad, unit, scale, vec_ref[2:3, :])).astype(bf16)
    add_sums(sum_ref, (grad * unit, grad))


def grad_two(x, part, dus, wm, vecs, after=(), step=256):
    count, width = x.shape
    token = pl.BlockSpec((step, width), lambda i: (i, 0))
    return call(
        grad_two_body,
        8 * count * width * width,
        16 * count * width + 8 * width * width,
        after=after,
        grid=(count // step,),
        in_specs=[token, token]
        + [layers(v, step, width) for v in dus]
        + [resident(wm.shape[0] // 2, width, 0), pl.BlockSpec(vecs.shape, lambda i: (0, 0))],
        out_specs=[token, pl.BlockSpec((2, 8, width), lambda i: (0, 0, 0))],
        out_shape=[jax.ShapeDtypeStruct((count, width), bf16), jax.ShapeDtypeStruct((2, 8, width), f32)],
    )(x, part, *[v[0] for v in dus], wm, vecs)


def grid_places():
    wide, narrow = lax.axis_index("wide"), lax.axis_index("narrow")
    return wide // 2, wide % 2, narrow // 2, narrow % 2


def to_place(move):
    pairs = []
    for z in range(4):
        for y in range(2):
            for x in range(2):
                for c in range(2):
                    a, b, d, e = move(z, y, x, c)
                    pairs.append((((z * 2 + y) * 2 + x) * 2 + c, ((a * 2 + b) * 2 + d) * 2 + e))
    return pairs


def over_c(value):
    return lax.ppermute(value, AXES, to_place(lambda z, y, x, c: (z, y, x, 1 - c)))


def over_x(value):
    return lax.ppermute(value, AXES, to_place(lambda z, y, x, c: (z, y, 1 - x, c)))


def over_y(value):
    return lax.ppermute(value, AXES, to_place(lambda z, y, x, c: (z, 1 - y, x, c)))


def over_z(value, by):
    return lax.ppermute(value, AXES, to_place(lambda z, y, x, c: ((z + by) % 4, y, x, c)))


def gather_staged(shards):
    own = jnp.stack([shards] + [over_z(shards, s) for s in (1, 2, 3)])
    by_x, by_y = over_x(own), over_y(own)
    lower, upper = over_y(by_x[:2]), over_x(by_y[2:])
    here = [own, by_x, by_y, lower, upper]
    return here + [over_c(v) for v in here]


class Reduction:
    def __init__(self, axes, made):
        self.axes, self.made = axes, made[0]
        self.held = [
            (keep, over_x(send) if axis == "x" else over_y(send))
            for axis, keep, send in zip(axes, made[::2], made[1::2])
        ]

    def second(self, made):
        self.made = made[0]
        self.held = [
            (keep, over_y(send) if axis == "x" else over_x(send))
            for axis, keep, send in zip(self.axes, made[::2], made[1::2])
        ]


def pair_body(place_ref, r, ins, outs):
    y, x = place_ref[1], place_ref[2]
    for n, axis in enumerate(r.axes):
        keep, got = ins[2 * n : 2 * n + 2]
        for ref, other in zip(outs[2 * n : 2 * n + 2], (0, 1)):
            at = (y if axis == "x" else x) ^ other
            ref[...] = (keep[:, :, at].astype(f32) + got[:, :, at].astype(f32)).astype(bf16)


def plane_body(place_ref, r, ins, outs):
    for m, ref in enumerate(outs):
        at = place_ref[0] ^ m
        for n in range(len(r.axes)):
            keep, got = ins[2 * n : 2 * n + 2]
            wide = keep.shape[-1]
            value = keep[:, at >> 1, at & 1].astype(f32) + got[:, at >> 1, at & 1].astype(f32)
            ref[:, :, n * wide : (n + 1) * wide] = value.astype(bf16)


def advance(place, pairs, planes, after=(), steps=2):
    blocks, *_, shard, wide = (pairs + planes)[0].held[0][0].shape
    width = wide * len((pairs + planes)[0].axes)
    shapes, places = [], []
    for r in pairs:
        shapes += [jax.ShapeDtypeStruct((blocks, 2, 2, shard, width // len(r.axes)), bf16)] * (2 * len(r.axes))
    places += [0] * len(shapes)
    if planes:
        shapes += [jax.ShapeDtypeStruct((len(planes), blocks, shard, width), bf16)] * 4
        places += [1] * 4
    operands = [v for r in pairs + planes for held in r.held for v in held]

    def spec(s, at=0):
        n = len(s.shape)
        block = tuple(d // steps if m == at else d for m, d in enumerate(s.shape))
        return pl.BlockSpec(block, lambda b, p: (0,) * at + (b,) + (0,) * (n - 1 - at))

    def body(place_ref, *refs):
        ins, outs = refs[: len(operands)], refs[len(operands) :]
        for r in pairs:
            count = 2 * len(r.axes)
            pair_body(place_ref, r, ins[:count], outs[:count])
            ins, outs = ins[count:], outs[count:]
        for n, r in enumerate(planes):
            count = 2 * len(r.axes)
            plane_body(place_ref, r, ins[:count], [ref.at[n] for ref in outs])
            ins = ins[count:]

    outs = call(
        body,
        0,
        sum(v.size * v.dtype.itemsize for v in operands) * 2,
        after=after,
        grid_spec=pltpu.PrefetchScalarGridSpec(
            num_scalar_prefetch=1,
            grid=(steps,),
            in_specs=[spec(v) for v in operands],
            out_specs=[spec(s, at) for s, at in zip(shapes, places)],
        ),
        out_shape=shapes,
    )(place, *operands)
    for r in pairs:
        count = 2 * len(r.axes)
        r.second(outs[:count])
        outs = outs[count:]
    terms = []
    for m, v in enumerate(outs):
        for r in planes:
            r.made = v
        v = v.reshape(-1, shard, width)
        terms.append(
            lax.ppermute(
                v, AXES, to_place(lambda z, y, x, c, m=m: (2 * c + ((z ^ m) >> 1), y, x, (z ^ m) & 1))
            )
        )
    return terms


def everywhere(value):
    def get(move):
        return lax.ppermute(value, AXES, to_place(move))

    value = value + over_c(value)
    by_x, by_y = over_x(value), over_y(value)
    across = get(lambda z, y, x, c: (z, 1 - y, 1 - x, c))
    value = (value + by_x) + (by_y + across)
    near = get(lambda z, y, x, c: (z ^ 1, y, x, c))
    far = get(lambda z, y, x, c: (z ^ 2, y, x, c))
    last = get(lambda z, y, x, c: (z ^ 3, y, x, c))
    return (value + near) + (far + last)


def pack_body(slot_ref, *refs, orders, per):
    terms, (shard_ref, out_ref, square_ref) = refs[: len(orders) * per], refs[len(orders) * per :]
    total = jnp.zeros(square_ref.shape, f32)
    for n, order in enumerate(orders):
        for m, b in enumerate(order):
            value = terms[n * per][m].astype(f32)
            for t in range(1, per):
                value = value + terms[n * per + t][m].astype(f32)
            shard_ref[b] = value
            total = total + value * value
    square_ref[...] = total

    def one(j, carry):
        b = slot_ref[j]

        @pl.when(b >= 0)
        def _():
            out_ref[j] = shard_ref[jnp.maximum(b, 0)].astype(bf16)

        @pl.when(b < 0)
        def _():
            out_ref[j] = jnp.zeros(out_ref.shape[1:], bf16)

        return carry

    lax.fori_loop(0, out_ref.shape[0], one, 0)


def pack(slots, terms, orders, after=()):
    per = len(terms[0])
    _, shard, width = terms[0][0].shape
    terms = [v for t in terms for v in t]
    vmem = pl.BlockSpec(memory_space=pltpu.VMEM)
    return call(
        functools.partial(pack_body, orders=orders, per=per),
        0,
        sum(v.size * v.dtype.itemsize for v in terms) * 2,
        after=after,
        in_specs=[pl.BlockSpec(memory_space=pltpu.SMEM)] + [vmem] * len(terms),
        out_specs=[vmem] * 3,
        out_shape=[
            jax.ShapeDtypeStruct((sum(map(len, orders)), shard, width), f32),
            jax.ShapeDtypeStruct((slots.shape[0], shard, width), bf16),
            jax.ShapeDtypeStruct((shard, width), f32),
        ],
    )(slots, *terms)


def to_low_body(l_ref, r_ref, l_low, r_low):
    l_low[...] = l_ref[...].astype(bf16)
    r_low[...] = r_ref[...].astype(bf16)


def to_low(left, right, after=(), step=384):
    width = left.shape[0]
    rows = pl.BlockSpec((step, width), lambda i: (i, 0))
    return call(
        to_low_body,
        0,
        12 * width**2,
        after=after,
        grid=(width // step,),
        in_specs=[rows, rows],
        out_specs=[rows, rows],
        out_shape=[jax.ShapeDtypeStruct((width, width), bf16)] * 2,
    )(left, right)


def precondition_body(scale_ref, s_ref, l_ref, r_ref, p_ref, s_low):
    @pl.when(pl.program_id(0) == 0)
    def _():
        s_low[...] = (s_ref[...].astype(f32) * scale_ref[0]).astype(bf16)

    left = mm(l_ref[...], s_low[...], NN)
    p_ref[...] = (scale_ref[1] * mm(left.astype(bf16), r_ref[...], NN)).astype(bf16)


def precondition(scales, block, left, right, step=384):
    width = block.shape[0]
    whole = pl.BlockSpec((width, width), lambda i: (0, 0))
    rows = pl.BlockSpec((step, width), lambda i: (i, 0))
    return call(
        precondition_body,
        4 * width**3,
        8 * width**2,
        grid=(width // step,),
        in_specs=[pl.BlockSpec(memory_space=pltpu.SMEM), whole, rows, whole],
        out_specs=rows,
        out_shape=jax.ShapeDtypeStruct((width, width), bf16),
        scratch_shapes=[pltpu.VMEM((width, width), bf16)],
    )(scales, block, left, right)


def statistics_body(has_ref, scale_ref, s_ref, l_ref, r_ref, nl_ref, nr_ref, s_low, *, step):
    i = pl.program_id(0)
    width = s_ref.shape[0]

    @pl.when(i == 0)
    def _():
        s_low[...] = (s_ref[...].astype(f32) * scale_ref[0]).astype(bf16)

    factor = (1.0 - decay_beta) * (scale_ref[1] * scale_ref[1] / width)
    at = pl.multiple_of(i * step, step)

    @pl.when(has_ref[0] != 0)
    def _():
        nl_ref[...] = decay_beta * l_ref[...] + factor * mm(s_low[pl.ds(at, step), :], s_low[...], NT)
        nr_ref[...] = decay_beta * r_ref[...] + factor * mm(s_low[:, pl.ds(at, step)], s_low[...], TN)

    @pl.when(has_ref[0] == 0)
    def _():
        nl_ref[...] = l_ref[...]
        nr_ref[...] = r_ref[...]


def statistics(has, scales, block, left, right, step=256):
    width = block.shape[0]
    whole = pl.BlockSpec((width, width), lambda i: (0, 0))
    rows = pl.BlockSpec((step, width), lambda i: (i, 0))
    smem = pl.BlockSpec(memory_space=pltpu.SMEM)
    return call(
        functools.partial(statistics_body, step=step),
        4 * width**3,
        18 * width**2,
        grid=(width // step,),
        in_specs=[smem, smem, whole, rows, rows],
        out_specs=[rows, rows],
        out_shape=[jax.ShapeDtypeStruct((width, width), f32)] * 2,
        scratch_shapes=[pltpu.VMEM((width, width), bf16)],
    )(has, scales, block, left, right)


def update_body(owner_ref, factor_ref, p_ref, shard_ref, block_ref, clip_ref, new_ref, copy_ref):
    for b in range(shard_ref.shape[0]):
        clip_ref[b] = shard_ref[b] * factor_ref[0]
        value = block_ref[b] - matrix_rate * p_ref[owner_ref[b]].astype(f32)
        new_ref[b] = value
        copy_ref[b] = value.astype(bf16)


def update(owners, factor, returned, shards, blocks):
    smem, vmem = pl.BlockSpec(memory_space=pltpu.SMEM), pl.BlockSpec(memory_space=pltpu.VMEM)
    return call(
        update_body,
        0,
        returned.size * 2 + shards.size * 18,
        in_specs=[smem, smem, vmem, vmem, vmem],
        out_specs=[vmem] * 3,
        out_shape=[
            jax.ShapeDtypeStruct(shards.shape, f32),
            jax.ShapeDtypeStruct(shards.shape, f32),
            jax.ShapeDtypeStruct(shards.shape, bf16),
        ],
    )(owners, factor, returned, shards, blocks)


def to_all(value):
    return lax.all_to_all(value, AXES, split_axis=0, concat_axis=0, tiled=True)


def per_device(
    tokens,
    segment_ids,
    cotangent,
    blocks,
    vectors,
    stat_left,
    stat_right,
    root_left,
    root_right,
    vec_stat,
    owners,
    *,
    paired,
):
    rows_here, seq_len, width = tokens.shape
    count = rows_here * seq_len
    splits = FF // width
    slot_count = lax.axis_size(AXES)
    my_index = lax.axis_index(AXES)
    shard = width // slot_count
    vec_rows = vectors.shape[0]

    low_blocks, low_vectors = blocks.astype(bf16), vectors.astype(bf16)
    everyone = jnp.broadcast_to(low_vectors.reshape(1, -1), (slot_count, vec_rows * shard))
    vecs = to_all(everyone).reshape(slot_count, vec_rows, shard)
    vecs = vecs.transpose(1, 0, 2).reshape(vec_rows, width).astype(f32)
    half = splits // 2
    mlp_weights = lax.all_gather(low_blocks[4:], AXES, axis=1, tiled=True)

    flat_tokens = tokens.reshape(count, width)
    dy = cotangent.reshape(count, width)
    tables = rotary_tables(segment_ids)
    place = jnp.stack(grid_places()).astype(jnp.int32)
    if paired:
        pieces = gather_staged(low_blocks[:4])
    else:
        pieces = [lax.all_gather(low_blocks[:4], AXES, axis=1, tiled=True)]
    q, k, v, do, acts, attn_weights = project(place, flat_tokens, dy, pieces, vecs, tables)
    og, attn_sums, acts = attend(segment_ids, q, k, v, do, tables, acts)
    orders = [list(range(4))]
    for first in (0, half):
        orders.append([base + first + j for base in (4, 4 + splits) for j in range(half)])
    if paired:
        acts_pair, og_pair = (acts, over_c(acts)), (og, over_c(og))
        dys = (acts_pair, 2, 1)
        ed0, up_sum0 = hidden(0, acts, mlp_weights, vecs)
        ed0_pair = (ed0, over_c(ed0))
        ed1, up_sum1 = hidden(half, acts, mlp_weights, vecs, after=(ed0, acts_pair[1]))
        ed1_pair = (ed1, over_c(ed1))

        def grads(left, two, one, after):
            operands = ((acts_pair, left, 1), two, one, dys, shard, "xy")
            return Reduction("xy", half_grads(place, *operands, after=after))

        attn = grads(0, (og_pair, 3, 1), (og_pair, 0, 3), (ed1,))
        low = grads(1, (ed0_pair, 0, half), (ed0_pair, half, half), (attn.made,))
        advance(place, [attn], [], after=(low.made,))
        high = grads(1, (ed1_pair, 0, half), (ed1_pair, half, half), (attn.made,))
        advance(place, [low], [], after=(high.made, *[got for _, got in attn.held]))
        part, one_sums = grad_one(flat_tokens, dy, (og, 0, 3), attn_weights, vecs, after=(low.made,))
        terms = [advance(place, [high], [attn, low], after=(part,))]
        es, dus = [(v, 0, half) for v in (ed0, ed1)], [(v, half, half) for v in (ed0, ed1)]
        grad_in, two_sums = grad_two(flat_tokens, part, dus, mlp_weights, vecs, after=(high.made,))
        terms.append(advance(place, [], [high], after=(grad_in,)))
        orders = [orders[0] + orders[1], orders[2]]
    else:
        ed0, up_sum0 = hidden(0, acts, mlp_weights, vecs)
        ed1, up_sum1 = hidden(half, acts, mlp_weights, vecs)
        grads = [
            full_grads(acts[0], og[3:], og[:3], dy),
            full_grads(acts[1], ed0[:half], ed0[half:], dy),
            full_grads(acts[1], ed1[:half], ed1[half:], dy),
        ]
        terms = [[lax.psum_scatter(v, AXES, scatter_dimension=1, tiled=True)] for v in grads]
        es, dus = [(v, 0, half) for v in (ed0, ed1)], [(v, half, half) for v in (ed0, ed1)]
        part, one_sums = grad_one(flat_tokens, dy, (og, 0, 3), attn_weights, vecs)
        grad_in, two_sums = grad_two(flat_tokens, part, dus, mlp_weights, vecs)
    up_sums = [up_sum0, up_sum1]

    one_sums, two_sums = jnp.sum(one_sums, axis=1), jnp.sum(two_sums, axis=1)
    qkv_sums = jnp.sum(attn_sums, axis=1)
    up_sums = jnp.sum(jnp.concatenate(up_sums, axis=0), axis=1)
    bias_sum = one_sums[2:]
    grad_vectors = jnp.concatenate(
        [one_sums[:2], two_sums, qkv_sums, bias_sum, up_sums, bias_sum], axis=0
    )
    slot_ids = jnp.arange(slot_count, dtype=jnp.int32)
    match = owners[None, :] == slot_ids[:, None]
    slots = jnp.sum(jnp.where(match, jnp.arange(1, owners.shape[0] + 1, dtype=jnp.int32)[None], 0), axis=1) - 1
    has_block = jnp.any(owners == my_index)
    shards, outgoing, squares = pack(slots, terms, orders, after=(grad_in,))
    left_low, right_low = to_low(root_left[0], root_right[0], after=(squares,))
    out = output(flat_tokens, (og, 3, 1), es, attn_weights, mlp_weights, vecs, after=(left_low,))
    local = jnp.concatenate([grad_vectors, jnp.sum(squares, axis=0)[None], jnp.zeros((2, width), f32)])
    total = everywhere(local) if paired else lax.psum(local, AXES)
    vector_sums = total[:vec_rows]
    square_sum = jnp.sum(total[vec_rows]) + jnp.sum(vector_sums * vector_sums)
    shard_vectors = lax.dynamic_slice_in_dim(vector_sums, my_index * shard, shard, axis=1)
    grad_norm = jnp.sqrt(square_sum)
    factor = jnp.minimum(1.0, clip_level / grad_norm)
    root_count = math.sqrt(NPARAM)

    scale = factor * root_count
    power = jnp.exp2(jnp.floor(jnp.log2(jnp.maximum(scale, 1e-30)))).astype(bf16).astype(f32)
    scales = jnp.stack([power, scale / power])
    owned = to_all(outgoing).reshape(width, width)
    precond = precondition(scales, owned, left_low, right_low)
    returned = to_all(precond.reshape(slot_count, shard, width))
    new_left, new_right = statistics(
        has_block.astype(jnp.int32).reshape(1), scales, owned, stat_left[0], stat_right[0]
    )
    clipped_blocks, new_blocks, blocks_copy = update(owners, factor.reshape(1), returned, shards, blocks)
    clipped_vectors = shard_vectors * factor
    scaled_vectors = clipped_vectors * root_count
    new_vec_stat = decay_beta * vec_stat + (1.0 - decay_beta) * (scaled_vectors * scaled_vectors)
    new_vectors = vectors - vector_rate * scaled_vectors * lax.rsqrt(new_vec_stat)
    return (
        out.reshape(tokens.shape),
        grad_in.reshape(tokens.shape),
        clipped_blocks,
        clipped_vectors,
        grad_norm,
        new_left[None],
        new_right[None],
        new_vec_stat,
        new_blocks,
        new_vectors,
        blocks_copy,
        new_vectors.astype(bf16),
    )


def solution(mesh):
    rows = P(AXES, None, None)
    split_rows = P(None, AXES, None)
    split_columns = P(None, AXES)
    paired = dict(mesh.shape) == {"wide": 8, "narrow": 4}
    return jax.shard_map(
        functools.partial(per_device, paired=paired),
        mesh=mesh,
        in_specs=(
            rows, P(AXES, None), rows, split_rows, split_columns,
            rows, rows, rows, rows, split_columns, P(),
        ),
        out_specs=(
            rows, rows, split_rows, split_columns, P(), rows, rows,
            split_columns, split_rows, split_columns, split_rows, split_columns,
        ),
        check_vma=False,
    )
```

```python
import functools
import math

import jax
import jax.numpy as jnp
import numpy as np
from jax import lax
from jax.experimental import pallas as pl
from jax.experimental.pallas import tpu as pltpu
from jax.sharding import PartitionSpec as P

H = 12
FF = 3072
ROT = 16
NPARAM = 7087872
LONGEST = 256

clip_level = 1.0
matrix_rate = 0.03
vector_rate = 0.2
decay_beta = 0.5
norm_epsilon = 1e-05

f32 = jnp.float32
bf16 = jnp.bfloat16
AXES = ("wide", "narrow")
LANES = 128
MIB = 2**20

NN = (((1,), (0,)), ((), ()))
NT = (((1,), (1,)), ((), ()))
TN = (((0,), (0,)), ((), ()))


def mm(left, right, dims):
    return lax.dot_general(left, right, dims, preferred_element_type=f32)


def call(body, flops, moved, vmem=64, after=(), **rest):
    spec = rest.pop("grid_spec", None)
    grid = spec.grid if spec is not None else rest.get("grid", ())
    later = len(after)
    if later:
        held = [pl.BlockSpec(memory_space=pl.ANY)] * later
        if spec is not None:
            first = spec.num_scalar_prefetch + len(spec.in_specs)
            spec = pltpu.PrefetchScalarGridSpec(
                num_scalar_prefetch=spec.num_scalar_prefetch,
                grid=spec.grid,
                in_specs=list(spec.in_specs) + held,
                out_specs=spec.out_specs,
                scratch_shapes=spec.scratch_shapes,
            )
        else:
            first = len(rest["in_specs"])
            rest["in_specs"] = list(rest["in_specs"]) + held
        inner = body

        def body(*refs):
            inner(*refs[:first], *refs[first + later :])

    if spec is not None:
        rest["grid_spec"] = spec
    made = pl.pallas_call(
        body,
        compiler_params=pltpu.CompilerParams(
            vmem_limit_bytes=vmem * MIB,
            dimension_semantics=("arbitrary",) * len(grid),
        ),
        cost_estimate=pl.CostEstimate(
            flops=int(8 * flops), bytes_accessed=int(8 * moved), transcendentals=0
        ),
        **rest,
    )
    return lambda *operands: made(*operands, *after)


def sub_sum(values):
    return jnp.sum(values.reshape(-1, 8, values.shape[-1]), axis=0)


def rotary_tables(segment_ids):
    rows, length = segment_ids.shape
    start = jnp.sum(
        (segment_ids[:, None, :] < segment_ids[:, :, None]).astype(jnp.int32), axis=-1
    )
    offset = (jnp.arange(length, dtype=jnp.int32)[None] - start).astype(f32).reshape(-1, 1)
    half = ROT // 2
    lane = np.arange(LANES) % 64
    rates = np.where(lane < ROT, 10000.0 ** (-2.0 * (lane % half) / ROT), 0.0)
    angle = offset * jnp.asarray(rates, f32)[None]
    cosine, sine = jnp.cos(angle), jnp.sin(angle)
    first = sine * jnp.asarray(np.where(lane < half, -1.0, 0.0), f32)[None]
    second = sine * jnp.asarray(np.where((lane >= half) & (lane < ROT), 1.0, 0.0), f32)[None]
    return cosine, first, second


def rotate(values, cosine, first, second):
    parts = []
    for at in range(0, values.shape[1], LANES):
        part = values[:, at : at + LANES]
        parts.append(
            part * cosine
            + pltpu.roll(part, LANES - ROT // 2, 1) * first
            + pltpu.roll(part, ROT // 2, 1) * second
        )
    return jnp.concatenate(parts, axis=1)


def rotate_back(values, cosine, first, second):
    return (
        values * cosine
        - pltpu.roll(values, LANES - ROT // 2, 1) * first
        - pltpu.roll(values, ROT // 2, 1) * second
    )


def assemble(place_ref, pieces, w_ref):
    z, y, x, c = place_ref[0], place_ref[1], place_ref[2], place_ref[3]
    blocks, rows = w_ref.shape[0], 2 * pieces[0].shape[2]

    def plane(t, carry):
        apart = lax.rem(z - t + 4, 4)

        def put(here, there, at, ry, rx):
            chip = (t * 2 + (y ^ ry)) * 2 + (x ^ rx)
            where = pl.ds(pl.multiple_of(chip * rows, rows), rows)
            for order, wanted in (((here, there), c == 0), ((there, here), c != 0)):

                @pl.when(wanted)
                def _(order=order):
                    for n in range(blocks):
                        w_ref[n, where, :] = jnp.concatenate([ref[at, n] for ref in order], axis=0)

        for m, (ry, rx) in enumerate(((0, 0), (0, 1), (1, 0))):
            put(pieces[m], pieces[5 + m], apart, ry, rx)
        pl.when(apart < 2)(lambda: put(pieces[3], pieces[8], apart, 1, 1))
        pl.when(apart >= 2)(lambda: put(pieces[4], pieces[9], apart - 2, 1, 1))
        return carry

    lax.fori_loop(0, 4, plane, 0)


def project_body(place_ref, x_ref, dy_ref, vec_ref, c_ref, a_ref, b_ref, *refs):
    *pieces, q_ref, k_ref, v_ref, do_ref, acts_ref, a2_ref, w_ref = refs

    @pl.when(pl.program_id(0) == 0)
    def _():
        if len(pieces) > 1:
            assemble(place_ref, pieces, w_ref)
        else:
            w_ref[...] = pieces[0][...]

    unit, _ = normed(x_ref[...].astype(f32))
    a1 = (unit * vec_ref[0:1, :] + vec_ref[1:2, :]).astype(bf16)
    acts_ref[0] = a1
    acts_ref[1] = dy_ref[...]
    a2_ref[0] = (unit * vec_ref[2:3, :] + vec_ref[3:4, :]).astype(bf16)
    tables = (c_ref[...], a_ref[...], b_ref[...])
    q_ref[...] = rotate(mm(a1, w_ref[0], NN) + vec_ref[4:5, :], *tables).astype(bf16)
    k_ref[...] = rotate(mm(a1, w_ref[1], NN) + vec_ref[5:6, :], *tables).astype(bf16)
    v_ref[...] = (mm(a1, w_ref[2], NN) + vec_ref[6:7, :]).astype(bf16)
    do_ref[...] = mm(dy_ref[...], w_ref[3], NT).astype(bf16)


def project(place, x, dy, pieces, vecs, tables, step=256):
    count, width = x.shape
    token = pl.BlockSpec((step, width), lambda i, s: (i, 0))
    table = pl.BlockSpec((step, LANES), lambda i, s: (i, 0))
    once = pl.Buffered(1)
    return call(
        project_body,
        8 * count * width * width,
        20 * count * width + 16 * width * width,
        grid_spec=pltpu.PrefetchScalarGridSpec(
            num_scalar_prefetch=1,
            grid=(count // step,),
            in_specs=[token, token, pl.BlockSpec(vecs.shape, lambda i, s: (0, 0)), table, table, table]
            + [pl.BlockSpec(v.shape, lambda i, s, n=v.ndim: (0,) * n, pipeline_mode=once) for v in pieces],
            out_specs=[token] * 4
            + [
                pl.BlockSpec((2, step, width), lambda i, s: (0, i, 0)),
                pl.BlockSpec((1, step, width), lambda i, s: (0, i, 0)),
                pl.BlockSpec((4, width, width), lambda i, s: (0, 0, 0)),
            ],
        ),
        out_shape=[jax.ShapeDtypeStruct((count, width), bf16)] * 4
        + [
            jax.ShapeDtypeStruct((2, count, width), bf16),
            jax.ShapeDtypeStruct((1, count, width), bf16),
            jax.ShapeDtypeStruct((4, width, width), bf16),
        ],
    )(place, x, dy, vecs, *tables, *pieces)


def attend_body(
    acts_ref, a2_ref, col_ref, row_ref, q_ref, k_ref, v_ref, do_ref, c_ref, a_ref, b_ref,
    g_ref, sum_ref, acts_out_ref, a2_out_ref, mask_ref, *, block,
):
    length = q_ref.shape[0]
    steps = length // block

    def reach(i):
        return max(0, (i * block - (LONGEST - 1)) // block * block), (i + 1) * block

    @pl.when(pl.program_id(1) == 0)
    def _():
        for i in range(steps):
            lo, hi = reach(i)
            key = lax.broadcasted_iota(jnp.int32, (hi - lo, block), 0) + lo
            query = lax.broadcasted_iota(jnp.int32, (hi - lo, block), 1) + i * block
            same = col_ref[lo:hi, :] == row_ref[0, :, i * block : hi]
            mask = jnp.where(same & (key <= query), 0.0, -jnp.inf)
            mask_ref[i, 0 : hi - lo, 0:block] = mask
            mask_ref[i, 0 : hi - lo, block:] = mask

    low = lax.broadcasted_iota(jnp.int32, (1, LANES), 1) < 64
    eighth = jnp.asarray(0.125, bf16)
    zero = jnp.zeros((), bf16)

    def both(part):
        return jnp.concatenate([jnp.where(low, part, zero), jnp.where(low, zero, part)], axis=0)

    def unstack(part):
        return jnp.concatenate([part[0:64, 0:block], part[64:, block:]], axis=0).T

    pairs = []
    for at in range(0, q_ref.shape[1], LANES):
        lanes = slice(at, at + LANES)
        keys, values = k_ref[:, lanes], v_ref[:, lanes]
        pairs.append(
            (lanes, keys, values, (keys * eighth).T, values.T, q_ref[:, lanes] * eighth, do_ref[:, lanes])
        )
    q_sums = [jnp.zeros((8, LANES), f32) for _ in pairs]
    dks = [[None] * steps for _ in pairs]
    dvs = [[None] * steps for _ in pairs]

    def add(parts, n, value):
        parts[n] = value if parts[n] is None else parts[n] + value

    for i in range(steps):
        lo, hi = reach(i)
        here = slice(i * block, hi)
        for p, (lanes, keys, values, keys_t, values_t, queries, grads) in enumerate(pairs):
            q2, do2 = both(queries[here]), both(grads[here])
            scores = mm(keys[lo:hi], q2, NT) + mask_ref[i, 0 : hi - lo, :]
            d_soft = mm(values[lo:hi], do2, NT)
            raised = jnp.exp(scores - jnp.max(scores, axis=0, keepdims=True))
            soft = raised * (1.0 / jnp.sum(raised, axis=0, keepdims=True))
            inner = jnp.sum(soft * d_soft, axis=0, keepdims=True)
            soft_low = soft.astype(bf16)
            d_scores = (soft * (d_soft - inner)).astype(bf16)
            g_ref[3, here, lanes] = unstack(mm(values_t[:, lo:hi], soft_low, NN)).astype(bf16)
            dq = rotate_back(
                unstack(mm(keys_t[:, lo:hi], d_scores, NN)), c_ref[here, :], a_ref[here, :], b_ref[here, :]
            ).astype(bf16)
            g_ref[0, here, lanes] = dq
            q_sums[p] = q_sums[p] + sub_sum(dq.astype(f32))
            dk, dv = mm(d_scores, q2, NN), mm(soft_low, do2, NN)
            for n in range(lo // block, i + 1):
                rows = slice(n * block - lo, (n + 1) * block - lo)
                add(dks[p], n, dk[rows])
                add(dvs[p], n, dv[rows])
    for p, (lanes, *_) in enumerate(pairs):
        dk = rotate_back(jnp.concatenate(dks[p], axis=0), c_ref[...], a_ref[...], b_ref[...]).astype(bf16)
        dv = jnp.concatenate(dvs[p], axis=0).astype(bf16)
        g_ref[1, :, lanes] = dk
        g_ref[2, :, lanes] = dv
        sum_ref[0, :, lanes] = q_sums[p]
        sum_ref[1, :, lanes] = sub_sum(dk.astype(f32))
        sum_ref[2, :, lanes] = sub_sum(dv.astype(f32))


def attend(segment_ids, q, k, v, do, tables, acts, a2, block=256, lanes=3 * LANES):
    rows, length = segment_ids.shape
    count, width = q.shape
    block = min(block, length)
    token = pl.BlockSpec((length, lanes), lambda r, h: (r, h))
    table = pl.BlockSpec((length, LANES), lambda r, h: (r, 0))
    return call(
        functools.partial(attend_body, block=block),
        24 * count * length * width,
        24 * count * width,
        grid=(rows, width // lanes),
        input_output_aliases={0: 2, 1: 3},
        in_specs=[
            pl.BlockSpec(memory_space=pl.ANY),
            pl.BlockSpec(memory_space=pl.ANY),
            pl.BlockSpec((length, 1), lambda r, h: (r, 0)),
            pl.BlockSpec((1, 1, length), lambda r, h: (r, 0, 0)),
            token,
            token,
            token,
            token,
            table,
            table,
            table,
        ],
        out_specs=[
            pl.BlockSpec((4, length, lanes), lambda r, h: (0, r, h)),
            pl.BlockSpec((3, 8, lanes), lambda r, h: (0, r, h)),
            pl.BlockSpec(memory_space=pl.ANY),
            pl.BlockSpec(memory_space=pl.ANY),
        ],
        out_shape=[
            jax.ShapeDtypeStruct((4, count, width), bf16),
            jax.ShapeDtypeStruct((3, 8 * rows, width), f32),
            jax.ShapeDtypeStruct(acts.shape, acts.dtype),
            jax.ShapeDtypeStruct(a2.shape, a2.dtype),
        ],
        scratch_shapes=[pltpu.VMEM((length // block, length, 2 * block), f32)],
    )(
        acts,
        a2,
        segment_ids.reshape(-1, 1),
        segment_ids.reshape(rows, 1, length),
        q,
        k,
        v,
        do,
        *tables,
    )


def half_grads_body(place_ref, *refs, first, second, steps, axes):
    l1o, l1p, l2o, l2p, r1o, r1p, r2o, r2p, *outs, acc = refs
    i = pl.program_id(0)
    y, x = place_ref[1], place_ref[2]

    def part(n):
        if n < first:
            value = mm(l1o[0], r1o[n], TN) + mm(l1p[0], r1p[n], TN)
        else:
            value = mm(l2o[n - first], r2o[0], TN) + mm(l2p[n - first], r2p[0], TN)
        return value.reshape(acc.shape[1:])

    @pl.when(i == 0)
    def _():
        for n in range(first + second):
            acc[n] = part(n)

    @pl.when(i > 0)
    def _():
        for n in range(first + second):
            acc[n] += part(n)

    @pl.when(i == steps - 1)
    def _():
        for n in range(first + second):
            for r, axis in enumerate(axes):
                wide = outs[0].shape[-1]
                columns = slice(r * wide, (r + 1) * wide)
                for ref, other in zip(outs[2 * r : 2 * r + 2], (0, 1)):
                    if axis == "x":
                        value = acc[n, :, :, x ^ other, :, :, columns]
                    else:
                        value = acc[n, :, y ^ other, :, :, :, columns]
                    ref[n] = value.astype(bf16)


def layers(part, step, lanes, half=False):
    _, first, count = part
    return pl.BlockSpec((count, step, lanes), lambda i, *s: (first // count, i, s[0][3] if half else 0))


def half_grads(place, left_one, left_two, right_one, right_two, shard, axes, after=(), step=256):
    first, second = right_one[2], left_two[2]
    _, count, width = right_two[0][0].shape
    half = width // 2
    blocks = first + second
    steps = count // step
    shape = (blocks, 2, 2, 2, shard, width // len(axes))
    out = pl.BlockSpec(shape, lambda i, s: (0, 0, 0, 0, 0, 0))
    return call(
        functools.partial(half_grads_body, first=first, second=second, steps=steps, axes=axes),
        blocks * 2 * count * width * width,
        blocks * 4 * count * width,
        after=after,
        grid_spec=pltpu.PrefetchScalarGridSpec(
            num_scalar_prefetch=1,
            grid=(steps,),
            in_specs=[layers(left_one, step, half, True)] * 2
            + [layers(left_two, step, half, True)] * 2
            + [layers(right_one, step, width)] * 2
            + [layers(right_two, step, width)] * 2,
            out_specs=[out] * (2 * len(axes)),
            scratch_shapes=[pltpu.VMEM((blocks, 2, 2, 2, 2, shard, width), f32)],
        ),
        out_shape=[jax.ShapeDtypeStruct(shape, bf16)] * (2 * len(axes)),
    )(place, *left_one[0], *left_two[0], *right_one[0], *right_two[0])


def full_grads(left_one, left_two, right_one, right_two):
    one = jnp.einsum("td,nte->nde", left_one, right_one, preferred_element_type=f32)
    two = jnp.einsum("ntd,te->nde", left_two, right_two, preferred_element_type=f32)
    return jnp.concatenate([one, two], axis=0)


def gelu_parts(u):
    raised = jnp.exp(-0.5 * (u * u))
    t = 1.0 / (1.0 + (0.3275911 * math.sqrt(0.5)) * jnp.abs(u))
    poly = 1.061405429 * t - 1.453152027
    poly = poly * t + 1.421413741
    poly = poly * t - 0.284496736
    poly = (poly * t + 0.254829592) * t
    tail = 0.5 * poly * raised
    return jnp.where(u < 0, tail, 1.0 - tail), raised * (1.0 / math.sqrt(2.0 * math.pi))


def hidden_body(a2_ref, dy_ref, wu_ref, wd_ref, vec_ref, out_ref, sum_ref, *, first):
    row = first + pl.program_id(0)
    u = mm(a2_ref[0], wu_ref[0], NN) + vec_ref[pl.ds(row, 1), :]
    de = mm(dy_ref[0], wd_ref[0], NT)
    dist, density = gelu_parts(u)
    out_ref[0, 0] = (u * dist).astype(bf16)
    du = (de * (dist + u * density)).astype(bf16)
    out_ref[1, 0] = du
    part = sub_sum(du.astype(f32))

    @pl.when(pl.program_id(1) == 0)
    def _():
        sum_ref[0] = part

    @pl.when(pl.program_id(1) > 0)
    def _():
        sum_ref[0] += part


def hidden(first, acts, a2, weights, vecs, after=(), step=512):
    _, count, width = acts.shape
    splits = weights.shape[0] // 2
    blocks = splits // 2
    both, sums = call(
        functools.partial(hidden_body, first=8 + first),
        blocks * 4 * count * width * width,
        blocks * (8 * count * width + 4 * width * width),
        after=after,
        grid=(blocks, count // step),
        in_specs=[
            pl.BlockSpec((1, step, width), lambda j, i: (0, i, 0)),
            pl.BlockSpec((1, step, width), lambda j, i: (1, i, 0)),
            pl.BlockSpec((1, width, width), lambda j, i: (first + j, 0, 0)),
            pl.BlockSpec((1, width, width), lambda j, i: (splits + first + j, 0, 0)),
            pl.BlockSpec(vecs.shape, lambda j, i: (0, 0)),
        ],
        out_specs=[
            pl.BlockSpec((2, 1, step, width), lambda j, i: (0, j, i, 0)),
            pl.BlockSpec((1, 8, width), lambda j, i: (j, 0, 0)),
        ],
        out_shape=[
            jax.ShapeDtypeStruct((2, blocks, count, width), bf16),
            jax.ShapeDtypeStruct((blocks, 8, width), f32),
        ],
    )(a2, acts, weights, weights, vecs)
    return both.reshape(2 * blocks, count, width), sums


def norm_back(grad, unit, scale, gain):
    grad = grad * gain
    first = jnp.mean(grad, axis=1, keepdims=True)
    second = jnp.mean(grad * unit, axis=1, keepdims=True)
    return scale * (grad - first - unit * second)


def hidden_sum(hidden_refs, w_ref, dims, acc):
    at = 0
    for ref in hidden_refs:
        for m in range(ref.shape[0]):
            part = mm(ref[m], w_ref[at], dims)
            acc = part if acc is None else acc + part
            at += 1
    return acc


def output_body(x_ref, o_ref, *refs, splits):
    *e_refs, wo_ref, w_ref, vec_ref, out_ref = refs
    acc = hidden_sum(e_refs, w_ref, NN, mm(o_ref[0], wo_ref[0], NN))
    bias = vec_ref[7:8, :] + vec_ref[8 + splits : 9 + splits, :]
    out_ref[...] = (x_ref[...].astype(f32) + acc + bias).astype(bf16)


def resident(blocks, width, at):
    return pl.BlockSpec((blocks, width, width), lambda i: (at, 0, 0), pipeline_mode=pl.Buffered(1))


def output(x, o, es, wa, wm, vecs, after=(), step=256):
    count, width = x.shape
    splits = wm.shape[0] // 2
    token = pl.BlockSpec((step, width), lambda i: (i, 0))
    return call(
        functools.partial(output_body, splits=splits),
        10 * count * width * width,
        14 * count * width + 10 * width * width,
        after=after,
        grid=(count // step,),
        in_specs=[token]
        + [layers(v, step, width) for v in (o, *es)]
        + [resident(1, width, 3), resident(splits, width, 1), pl.BlockSpec(vecs.shape, lambda i: (0, 0))],
        out_specs=token,
        out_shape=jax.ShapeDtypeStruct((count, width), bf16),
    )(x, *[v[0] for v in (o, *es)], wa, wm, vecs)


def normed(x):
    centred = x - jnp.mean(x, axis=1, keepdims=True)
    scale = lax.rsqrt(jnp.mean(centred * centred, axis=1, keepdims=True) + norm_epsilon)
    return centred * scale, scale


def add_sums(sum_ref, sums):
    sums = [sub_sum(t) for t in sums]

    @pl.when(pl.program_id(0) == 0)
    def _():
        for n, s in enumerate(sums):
            sum_ref[n] = s

    @pl.when(pl.program_id(0) > 0)
    def _():
        for n, s in enumerate(sums):
            sum_ref[n] += s


def grad_one_body(x_ref, dy_ref, g_ref, wa_ref, vec_ref, part_ref, sum_ref):
    dy = dy_ref[...].astype(f32)
    grad = mm(g_ref[0], wa_ref[0], NT) + mm(g_ref[1], wa_ref[1], NT) + mm(g_ref[2], wa_ref[2], NT)
    unit, scale = normed(x_ref[...].astype(f32))
    part_ref[...] = dy + norm_back(grad, unit, scale, vec_ref[0:1, :])
    add_sums(sum_ref, (grad * unit, grad, dy))


def grad_one(x, dy, g, wa, vecs, after=(), step=256):
    count, width = x.shape
    token = pl.BlockSpec((step, width), lambda i: (i, 0))
    return call(
        grad_one_body,
        6 * count * width * width,
        14 * count * width + 6 * width * width,
        after=after,
        grid=(count // step,),
        in_specs=[
            token,
            token,
            layers(g, step, width),
            resident(3, width, 0),
            pl.BlockSpec(vecs.shape, lambda i: (0, 0)),
        ],
        out_specs=[token, pl.BlockSpec((3, 8, width), lambda i: (0, 0, 0))],
        out_shape=[jax.ShapeDtypeStruct((count, width), f32), jax.ShapeDtypeStruct((3, 8, width), f32)],
    )(x, dy, g[0], wa, vecs)


def grad_two_body(x_ref, part_ref, *refs):
    *du_refs, w_ref, vec_ref, grad_ref, sum_ref = refs
    grad = hidden_sum(du_refs, w_ref, NT, None)
    unit, scale = normed(x_ref[...].astype(f32))
    grad_ref[...] = (part_ref[...] + norm_back(grad, unit, scale, vec_ref[2:3, :])).astype(bf16)
    add_sums(sum_ref, (grad * unit, grad))


def grad_two(x, part, dus, wm, vecs, after=(), step=256):
    count, width = x.shape
    token = pl.BlockSpec((step, width), lambda i: (i, 0))
    return call(
        grad_two_body,
        8 * count * width * width,
        16 * count * width + 8 * width * width,
        after=after,
        grid=(count // step,),
        in_specs=[token, token]
        + [layers(v, step, width) for v in dus]
        + [resident(wm.shape[0] // 2, width, 0), pl.BlockSpec(vecs.shape, lambda i: (0, 0))],
        out_specs=[token, pl.BlockSpec((2, 8, width), lambda i: (0, 0, 0))],
        out_shape=[jax.ShapeDtypeStruct((count, width), bf16), jax.ShapeDtypeStruct((2, 8, width), f32)],
    )(x, part, *[v[0] for v in dus], wm, vecs)


def grid_places():
    wide, narrow = lax.axis_index("wide"), lax.axis_index("narrow")
    return wide // 2, wide % 2, narrow // 2, narrow % 2


def to_place(move):
    pairs = []
    for z in range(4):
        for y in range(2):
            for x in range(2):
                for c in range(2):
                    a, b, d, e = move(z, y, x, c)
                    pairs.append((((z * 2 + y) * 2 + x) * 2 + c, ((a * 2 + b) * 2 + d) * 2 + e))
    return pairs


def over_c(value):
    return lax.ppermute(value, AXES, to_place(lambda z, y, x, c: (z, y, x, 1 - c)))


def over_x(value):
    return lax.ppermute(value, AXES, to_place(lambda z, y, x, c: (z, y, 1 - x, c)))


def over_y(value):
    return lax.ppermute(value, AXES, to_place(lambda z, y, x, c: (z, 1 - y, x, c)))


def over_z(value, by):
    return lax.ppermute(value, AXES, to_place(lambda z, y, x, c: ((z + by) % 4, y, x, c)))


def gather_staged(shards):
    own = jnp.stack([shards] + [over_z(shards, s) for s in (1, 2, 3)])
    by_x, by_y = over_x(own), over_y(own)
    lower, upper = over_y(by_x[:2]), over_x(by_y[2:])
    here = [own, by_x, by_y, lower, upper]
    return here + [over_c(v) for v in here]


class Reduction:
    def __init__(self, axes, made):
        self.axes, self.made = axes, made[0]
        self.held = [
            (keep, over_x(send) if axis == "x" else over_y(send))
            for axis, keep, send in zip(axes, made[::2], made[1::2])
        ]

    def second(self, made):
        self.made = made[0]
        self.held = [
            (keep, over_y(send) if axis == "x" else over_x(send))
            for axis, keep, send in zip(self.axes, made[::2], made[1::2])
        ]


def pair_body(place_ref, r, ins, outs):
    y, x = place_ref[1], place_ref[2]
    for n, axis in enumerate(r.axes):
        keep, got = ins[2 * n : 2 * n + 2]
        for ref, other in zip(outs[2 * n : 2 * n + 2], (0, 1)):
            at = (y if axis == "x" else x) ^ other
            ref[...] = (keep[:, :, at].astype(f32) + got[:, :, at].astype(f32)).astype(bf16)


def plane_body(place_ref, r, ins, outs):
    for m, ref in enumerate(outs):
        at = place_ref[0] ^ m
        for n in range(len(r.axes)):
            keep, got = ins[2 * n : 2 * n + 2]
            wide = keep.shape[-1]
            value = keep[:, at >> 1, at & 1].astype(f32) + got[:, at >> 1, at & 1].astype(f32)
            ref[:, :, n * wide : (n + 1) * wide] = value.astype(bf16)


def advance(place, pairs, planes, after=(), steps=2):
    blocks, *_, shard, wide = (pairs + planes)[0].held[0][0].shape
    width = wide * len((pairs + planes)[0].axes)
    shapes, places = [], []
    for r in pairs:
        shapes += [jax.ShapeDtypeStruct((blocks, 2, 2, shard, width // len(r.axes)), bf16)] * (2 * len(r.axes))
    places += [0] * len(shapes)
    if planes:
        shapes += [jax.ShapeDtypeStruct((len(planes), blocks, shard, width), bf16)] * 4
        places += [1] * 4
    operands = [v for r in pairs + planes for held in r.held for v in held]

    def spec(s, at=0):
        n = len(s.shape)
        block = tuple(d // steps if m == at else d for m, d in enumerate(s.shape))
        return pl.BlockSpec(block, lambda b, p: (0,) * at + (b,) + (0,) * (n - 1 - at))

    def body(place_ref, *refs):
        ins, outs = refs[: len(operands)], refs[len(operands) :]
        for r in pairs:
            count = 2 * len(r.axes)
            pair_body(place_ref, r, ins[:count], outs[:count])
            ins, outs = ins[count:], outs[count:]
        for n, r in enumerate(planes):
            count = 2 * len(r.axes)
            plane_body(place_ref, r, ins[:count], [ref.at[n] for ref in outs])
            ins = ins[count:]

    outs = call(
        body,
        0,
        sum(v.size * v.dtype.itemsize for v in operands) * 2,
        after=after,
        grid_spec=pltpu.PrefetchScalarGridSpec(
            num_scalar_prefetch=1,
            grid=(steps,),
            in_specs=[spec(v) for v in operands],
            out_specs=[spec(s, at) for s, at in zip(shapes, places)],
        ),
        out_shape=shapes,
    )(place, *operands)
    for r in pairs:
        count = 2 * len(r.axes)
        r.second(outs[:count])
        outs = outs[count:]
    terms = []
    for m, v in enumerate(outs):
        for r in planes:
            r.made = v
        v = v.reshape(-1, shard, width)
        terms.append(
            lax.ppermute(
                v, AXES, to_place(lambda z, y, x, c, m=m: (2 * c + ((z ^ m) >> 1), y, x, (z ^ m) & 1))
            )
        )
    return terms


def everywhere(value):
    def get(move):
        return lax.ppermute(value, AXES, to_place(move))

    value = value + over_c(value)
    by_x, by_y = over_x(value), over_y(value)
    across = get(lambda z, y, x, c: (z, 1 - y, 1 - x, c))
    value = (value + by_x) + (by_y + across)
    near = get(lambda z, y, x, c: (z ^ 1, y, x, c))
    far = get(lambda z, y, x, c: (z ^ 2, y, x, c))
    last = get(lambda z, y, x, c: (z ^ 3, y, x, c))
    return [value, near, far, last]


def pack_body(slot_ref, *refs, orders, per):
    terms, (shard_ref, out_ref, square_ref) = refs[: len(orders) * per], refs[len(orders) * per :]
    total = jnp.zeros(square_ref.shape, f32)
    for n, order in enumerate(orders):
        for m, b in enumerate(order):
            value = terms[n * per][m].astype(f32)
            for t in range(1, per):
                value = value + terms[n * per + t][m].astype(f32)
            shard_ref[b] = value
            total = total + value * value
    square_ref[...] = total

    def one(j, carry):
        b = slot_ref[j]

        @pl.when(b >= 0)
        def _():
            out_ref[j] = shard_ref[jnp.maximum(b, 0)].astype(bf16)

        @pl.when(b < 0)
        def _():
            out_ref[j] = jnp.zeros(out_ref.shape[1:], bf16)

        return carry

    lax.fori_loop(0, out_ref.shape[0], one, 0)


def pack(slots, terms, orders, after=()):
    per = len(terms[0])
    _, shard, width = terms[0][0].shape
    terms = [v for t in terms for v in t]
    vmem = pl.BlockSpec(memory_space=pltpu.VMEM)
    return call(
        functools.partial(pack_body, orders=orders, per=per),
        0,
        sum(v.size * v.dtype.itemsize for v in terms) * 2,
        after=after,
        in_specs=[pl.BlockSpec(memory_space=pltpu.SMEM)] + [vmem] * len(terms),
        out_specs=[vmem] * 3,
        out_shape=[
            jax.ShapeDtypeStruct((sum(map(len, orders)), shard, width), f32),
            jax.ShapeDtypeStruct((slots.shape[0], shard, width), bf16),
            jax.ShapeDtypeStruct((shard, width), f32),
        ],
    )(slots, *terms)


def to_low_body(l_ref, r_ref, l_low, r_low):
    l_low[...] = l_ref[...].astype(bf16)
    r_low[...] = r_ref[...].astype(bf16)


def to_low(left, right, after=(), step=384):
    width = left.shape[0]
    rows = pl.BlockSpec((step, width), lambda i: (i, 0))
    return call(
        to_low_body,
        0,
        12 * width**2,
        after=after,
        grid=(width // step,),
        in_specs=[rows, rows],
        out_specs=[rows, rows],
        out_shape=[jax.ShapeDtypeStruct((width, width), bf16)] * 2,
    )(left, right)


def scale_parts(total, rows):
    vectors = total[:rows]
    squares = jnp.sum(vectors * vectors, keepdims=True) + jnp.sum(total[rows : rows + 1], keepdims=True)
    scale = jnp.minimum(1.0, clip_level / jnp.sqrt(squares)) * math.sqrt(NPARAM)
    power = jnp.exp2(jnp.floor(jnp.log2(jnp.maximum(scale, 1e-30)))).astype(bf16).astype(f32)
    return power, scale / power


def precondition_body(s_ref, l_ref, r_ref, *refs, rows):
    *part_refs, p_ref, s_low, rest = refs

    @pl.when(pl.program_id(0) == 0)
    def _():
        parts = [ref[...] for ref in part_refs]
        power, left = scale_parts(sum_parts(parts), rows)
        s_low[...] = (s_ref[...].astype(f32) * power).astype(bf16)
        rest[...] = jnp.broadcast_to(left, rest.shape)

    left = mm(l_ref[...], s_low[...], NN)
    p_ref[...] = (rest[0:1, 0:1] * mm(left.astype(bf16), r_ref[...], NN)).astype(bf16)


def sum_parts(parts):
    if len(parts) == 1:
        return parts[0]
    return (parts[0] + parts[1]) + (parts[2] + parts[3])


def precondition(parts, rows, block, left, right, step=384):
    width = block.shape[0]
    whole = pl.BlockSpec((width, width), lambda i: (0, 0))
    some = pl.BlockSpec((step, width), lambda i: (i, 0))
    return call(
        functools.partial(precondition_body, rows=rows),
        4 * width**3,
        8 * width**2,
        grid=(width // step,),
        in_specs=[whole, some, whole] + [pl.BlockSpec(v.shape, lambda i: (0, 0)) for v in parts],
        out_specs=some,
        out_shape=jax.ShapeDtypeStruct((width, width), bf16),
        scratch_shapes=[pltpu.VMEM((width, width), bf16), pltpu.VMEM((8, LANES), f32)],
    )(block, left, right, *parts)


def statistics_body(has_ref, scale_ref, s_ref, l_ref, r_ref, nl_ref, nr_ref, s_low, *, step):
    i = pl.program_id(0)
    width = s_ref.shape[0]

    @pl.when(i == 0)
    def _():
        s_low[...] = (s_ref[...].astype(f32) * scale_ref[0]).astype(bf16)

    factor = (1.0 - decay_beta) * (scale_ref[1] * scale_ref[1] / width)
    at = pl.multiple_of(i * step, step)

    @pl.when(has_ref[0] != 0)
    def _():
        nl_ref[...] = decay_beta * l_ref[...] + factor * mm(s_low[pl.ds(at, step), :], s_low[...], NT)
        nr_ref[...] = decay_beta * r_ref[...] + factor * mm(s_low[:, pl.ds(at, step)], s_low[...], TN)

    @pl.when(has_ref[0] == 0)
    def _():
        nl_ref[...] = l_ref[...]
        nr_ref[...] = r_ref[...]


def statistics(has, scales, block, left, right, step=256):
    width = block.shape[0]
    whole = pl.BlockSpec((width, width), lambda i: (0, 0))
    rows = pl.BlockSpec((step, width), lambda i: (i, 0))
    smem = pl.BlockSpec(memory_space=pltpu.SMEM)
    return call(
        functools.partial(statistics_body, step=step),
        4 * width**3,
        18 * width**2,
        grid=(width // step,),
        in_specs=[smem, smem, whole, rows, rows],
        out_specs=[rows, rows],
        out_shape=[jax.ShapeDtypeStruct((width, width), f32)] * 2,
        scratch_shapes=[pltpu.VMEM((width, width), bf16)],
    )(has, scales, block, left, right)


def update_body(owner_ref, factor_ref, p_ref, shard_ref, block_ref, clip_ref, new_ref, copy_ref):
    for b in range(shard_ref.shape[0]):
        clip_ref[b] = shard_ref[b] * factor_ref[0]
        value = block_ref[b] - matrix_rate * p_ref[owner_ref[b]].astype(f32)
        new_ref[b] = value
        copy_ref[b] = value.astype(bf16)


def update(owners, factor, returned, shards, blocks):
    smem, vmem = pl.BlockSpec(memory_space=pltpu.SMEM), pl.BlockSpec(memory_space=pltpu.VMEM)
    return call(
        update_body,
        0,
        returned.size * 2 + shards.size * 18,
        in_specs=[smem, smem, vmem, vmem, vmem],
        out_specs=[vmem] * 3,
        out_shape=[
            jax.ShapeDtypeStruct(shards.shape, f32),
            jax.ShapeDtypeStruct(shards.shape, f32),
            jax.ShapeDtypeStruct(shards.shape, bf16),
        ],
    )(owners, factor, returned, shards, blocks)


def to_all(value):
    return lax.all_to_all(value, AXES, split_axis=0, concat_axis=0, tiled=True)


def per_device(
    tokens,
    segment_ids,
    cotangent,
    blocks,
    vectors,
    stat_left,
    stat_right,
    root_left,
    root_right,
    vec_stat,
    owners,
    *,
    paired,
):
    rows_here, seq_len, width = tokens.shape
    count = rows_here * seq_len
    splits = FF // width
    slot_count = lax.axis_size(AXES)
    my_index = lax.axis_index(AXES)
    shard = width // slot_count
    vec_rows = vectors.shape[0]

    low_blocks, low_vectors = blocks.astype(bf16), vectors.astype(bf16)
    everyone = jnp.broadcast_to(low_vectors.reshape(1, -1), (slot_count, vec_rows * shard))
    vecs = to_all(everyone).reshape(slot_count, vec_rows, shard)
    vecs = vecs.transpose(1, 0, 2).reshape(vec_rows, width).astype(f32)
    half = splits // 2
    mlp_weights = lax.all_gather(low_blocks[4:], AXES, axis=1, tiled=True)

    flat_tokens = tokens.reshape(count, width)
    dy = cotangent.reshape(count, width)
    tables = rotary_tables(segment_ids)
    place = jnp.stack(grid_places()).astype(jnp.int32)
    if paired:
        pieces = gather_staged(low_blocks[:4])
    else:
        pieces = [lax.all_gather(low_blocks[:4], AXES, axis=1, tiled=True)]
    q, k, v, do, acts, a2, attn_weights = project(place, flat_tokens, dy, pieces, vecs, tables)
    og, attn_sums, acts, a2 = attend(segment_ids, q, k, v, do, tables, acts, a2)
    orders = [list(range(4))]
    for first in (0, half):
        orders.append([base + first + j for base in (4, 4 + splits) for j in range(half)])
    if paired:
        acts_pair, a2_pair, og_pair = [(v, over_c(v)) for v in (acts, a2, og)]
        ed0, up_sum0 = hidden(0, acts, a2, mlp_weights, vecs)
        ed0_pair = (ed0, over_c(ed0))

        def grads(left, two, one, after):
            operands = (left, two, one, (acts_pair, 1, 1), shard, "xy")
            return Reduction("xy", half_grads(place, *operands, after=after))

        attn = grads((acts_pair, 0, 1), (og_pair, 3, 1), (og_pair, 0, 3), (ed0,))
        ed1, up_sum1 = hidden(half, acts, a2, mlp_weights, vecs, after=(attn.made, a2_pair[1]))
        ed1_pair = (ed1, over_c(ed1))
        advance(place, [attn], [], after=(ed1,))
        low = grads((a2_pair, 0, 1), (ed0_pair, 0, half), (ed0_pair, half, half), (attn.made,))
        part, one_sums = grad_one(flat_tokens, dy, (og, 0, 3), attn_weights, vecs, after=(low.made,))
        terms = [advance(place, [low], [attn], after=(part,))]
        high = grads((a2_pair, 0, 1), (ed1_pair, 0, half), (ed1_pair, half, half), (low.made,))
        es, dus = [(v, 0, half) for v in (ed0, ed1)], [(v, half, half) for v in (ed0, ed1)]
        grad_in, two_sums = grad_two(
            flat_tokens, part, dus, mlp_weights, vecs, after=(high.made, *terms[0])
        )
        terms.append(advance(place, [high], [low], after=(grad_in,)))
        terms.append(advance(place, [], [high]))
    else:
        ed0, up_sum0 = hidden(0, acts, a2, mlp_weights, vecs)
        ed1, up_sum1 = hidden(half, acts, a2, mlp_weights, vecs)
        grads = [
            full_grads(acts[0], og[3:], og[:3], dy),
            full_grads(a2[0], ed0[:half], ed0[half:], dy),
            full_grads(a2[0], ed1[:half], ed1[half:], dy),
        ]
        terms = [[lax.psum_scatter(v, AXES, scatter_dimension=1, tiled=True)] for v in grads]
        es, dus = [(v, 0, half) for v in (ed0, ed1)], [(v, half, half) for v in (ed0, ed1)]
        part, one_sums = grad_one(flat_tokens, dy, (og, 0, 3), attn_weights, vecs)
        grad_in, two_sums = grad_two(flat_tokens, part, dus, mlp_weights, vecs)
    up_sums = [up_sum0, up_sum1]

    one_sums, two_sums = jnp.sum(one_sums, axis=1), jnp.sum(two_sums, axis=1)
    qkv_sums = jnp.sum(attn_sums, axis=1)
    up_sums = jnp.sum(jnp.concatenate(up_sums, axis=0), axis=1)
    bias_sum = one_sums[2:]
    grad_vectors = jnp.concatenate(
        [one_sums[:2], two_sums, qkv_sums, bias_sum, up_sums, bias_sum], axis=0
    )
    slot_ids = jnp.arange(slot_count, dtype=jnp.int32)
    match = owners[None, :] == slot_ids[:, None]
    slots = jnp.sum(jnp.where(match, jnp.arange(1, owners.shape[0] + 1, dtype=jnp.int32)[None], 0), axis=1) - 1
    has_block = jnp.any(owners == my_index)
    shards, outgoing, squares = pack(slots, terms, orders, after=(grad_in,))
    left_low, right_low = to_low(root_left[0], root_right[0], after=(squares,))
    out = output(flat_tokens, (og, 3, 1), es, attn_weights, mlp_weights, vecs, after=(left_low,))
    local = jnp.concatenate([grad_vectors, jnp.sum(squares, axis=0)[None], jnp.zeros((2, width), f32)])
    parts = everywhere(local) if paired else [lax.psum(local, AXES)]
    total = sum_parts(parts)
    vector_sums = total[:vec_rows]
    square_sum = jnp.sum(total[vec_rows]) + jnp.sum(vector_sums * vector_sums)
    shard_vectors = lax.dynamic_slice_in_dim(vector_sums, my_index * shard, shard, axis=1)
    grad_norm = jnp.sqrt(square_sum)
    factor = jnp.minimum(1.0, clip_level / grad_norm)
    root_count = math.sqrt(NPARAM)

    scale = factor * root_count
    power = jnp.exp2(jnp.floor(jnp.log2(jnp.maximum(scale, 1e-30)))).astype(bf16).astype(f32)
    scales = jnp.stack([power, scale / power])
    owned = to_all(outgoing).reshape(width, width)
    precond = precondition(parts, vec_rows, owned, left_low, right_low)
    returned = to_all(precond.reshape(slot_count, shard, width))
    new_left, new_right = statistics(
        has_block.astype(jnp.int32).reshape(1), scales, owned, stat_left[0], stat_right[0]
    )
    clipped_blocks, new_blocks, blocks_copy = update(owners, factor.reshape(1), returned, shards, blocks)
    clipped_vectors = shard_vectors * factor
    scaled_vectors = clipped_vectors * root_count
    new_vec_stat = decay_beta * vec_stat + (1.0 - decay_beta) * (scaled_vectors * scaled_vectors)
    new_vectors = vectors - vector_rate * scaled_vectors * lax.rsqrt(new_vec_stat)
    return (
        out.reshape(tokens.shape),
        grad_in.reshape(tokens.shape),
        clipped_blocks,
        clipped_vectors,
        grad_norm,
        new_left[None],
        new_right[None],
        new_vec_stat,
        new_blocks,
        new_vectors,
        blocks_copy,
        new_vectors.astype(bf16),
    )


def solution(mesh):
    rows = P(AXES, None, None)
    split_rows = P(None, AXES, None)
    split_columns = P(None, AXES)
    paired = dict(mesh.shape) == {"wide": 8, "narrow": 4}
    return jax.shard_map(
        functools.partial(per_device, paired=paired),
        mesh=mesh,
        in_specs=(
            rows, P(AXES, None), rows, split_rows, split_columns,
            rows, rows, rows, rows, split_columns, P(),
        ),
        out_specs=(
            rows, rows, split_rows, split_columns, P(), rows, rows,
            split_columns, split_rows, split_columns, split_rows, split_columns,
        ),
        check_vma=False,
    )
```

```python
import functools
import math

import jax
import jax.numpy as jnp
import numpy as np
from jax import lax
from jax.experimental import pallas as pl
from jax.experimental.pallas import tpu as pltpu
from jax.sharding import PartitionSpec as P

H = 12
FF = 3072
ROT = 16
NPARAM = 7087872
LONGEST = 256

clip_level = 1.0
matrix_rate = 0.03
vector_rate = 0.2
decay_beta = 0.5
norm_epsilon = 1e-05

f32 = jnp.float32
bf16 = jnp.bfloat16
AXES = ("wide", "narrow")
LANES = 128
MIB = 2**20

NN = (((1,), (0,)), ((), ()))
NT = (((1,), (1,)), ((), ()))
TN = (((0,), (0,)), ((), ()))


def mm(left, right, dims):
    return lax.dot_general(left, right, dims, preferred_element_type=f32)


def call(body, flops, moved, vmem=64, after=(), **rest):
    spec = rest.pop("grid_spec", None)
    grid = spec.grid if spec is not None else rest.get("grid", ())
    later = len(after)
    if later:
        held = [pl.BlockSpec(memory_space=pl.ANY)] * later
        if spec is not None:
            first = spec.num_scalar_prefetch + len(spec.in_specs)
            spec = pltpu.PrefetchScalarGridSpec(
                num_scalar_prefetch=spec.num_scalar_prefetch,
                grid=spec.grid,
                in_specs=list(spec.in_specs) + held,
                out_specs=spec.out_specs,
                scratch_shapes=spec.scratch_shapes,
            )
        else:
            first = len(rest["in_specs"])
            rest["in_specs"] = list(rest["in_specs"]) + held
        inner = body

        def body(*refs):
            inner(*refs[:first], *refs[first + later :])

    if spec is not None:
        rest["grid_spec"] = spec
    made = pl.pallas_call(
        body,
        compiler_params=pltpu.CompilerParams(
            vmem_limit_bytes=vmem * MIB,
            dimension_semantics=("arbitrary",) * len(grid),
        ),
        cost_estimate=pl.CostEstimate(
            flops=int(flops), bytes_accessed=int(moved), transcendentals=0
        ),
        **rest,
    )
    return lambda *operands: made(*operands, *after)


def sub_sum(values):
    return jnp.sum(values.reshape(-1, 8, values.shape[-1]), axis=0)


def rotary_tables(segment_ids):
    rows, length = segment_ids.shape
    start = jnp.sum(
        (segment_ids[:, None, :] < segment_ids[:, :, None]).astype(jnp.int32), axis=-1
    )
    offset = (jnp.arange(length, dtype=jnp.int32)[None] - start).astype(f32).reshape(-1, 1)
    half = ROT // 2
    lane = np.arange(LANES) % 64
    rates = np.where(lane < ROT, 10000.0 ** (-2.0 * (lane % half) / ROT), 0.0)
    angle = offset * jnp.asarray(rates, f32)[None]
    cosine, sine = jnp.cos(angle), jnp.sin(angle)
    first = sine * jnp.asarray(np.where(lane < half, -1.0, 0.0), f32)[None]
    second = sine * jnp.asarray(np.where((lane >= half) & (lane < ROT), 1.0, 0.0), f32)[None]
    return cosine, first, second


def rotate(values, cosine, first, second):
    parts = []
    for at in range(0, values.shape[1], LANES):
        part = values[:, at : at + LANES]
        parts.append(
            part * cosine
            + pltpu.roll(part, LANES - ROT // 2, 1) * first
            + pltpu.roll(part, ROT // 2, 1) * second
        )
    return jnp.concatenate(parts, axis=1)


def rotate_back(values, cosine, first, second):
    return (
        values * cosine
        - pltpu.roll(values, LANES - ROT // 2, 1) * first
        - pltpu.roll(values, ROT // 2, 1) * second
    )


def assemble(place_ref, pieces, w_ref):
    z, y, x, c = place_ref[0], place_ref[1], place_ref[2], place_ref[3]
    blocks, rows = w_ref.shape[0], 2 * pieces[0].shape[2]

    def plane(t, carry):
        apart = lax.rem(z - t + 4, 4)

        def put(here, there, at, ry, rx):
            chip = (t * 2 + (y ^ ry)) * 2 + (x ^ rx)
            where = pl.ds(pl.multiple_of(chip * rows, rows), rows)
            for order, wanted in (((here, there), c == 0), ((there, here), c != 0)):

                @pl.when(wanted)
                def _(order=order):
                    for n in range(blocks):
                        w_ref[n, where, :] = jnp.concatenate([ref[at, n] for ref in order], axis=0)

        for m, (ry, rx) in enumerate(((0, 0), (0, 1), (1, 0))):
            put(pieces[m], pieces[5 + m], apart, ry, rx)
        pl.when(apart < 2)(lambda: put(pieces[3], pieces[8], apart, 1, 1))
        pl.when(apart >= 2)(lambda: put(pieces[4], pieces[9], apart - 2, 1, 1))
        return carry

    lax.fori_loop(0, 4, plane, 0)


def project_body(place_ref, x_ref, dy_ref, vec_ref, c_ref, a_ref, b_ref, *refs):
    *pieces, q_ref, k_ref, v_ref, do_ref, acts_ref, w_ref = refs

    @pl.when(pl.program_id(0) == 0)
    def _():
        if len(pieces) > 1:
            assemble(place_ref, pieces, w_ref)
        else:
            w_ref[...] = pieces[0][...]

    unit, _ = normed(x_ref[...].astype(f32))
    a1 = (unit * vec_ref[0:1, :] + vec_ref[1:2, :]).astype(bf16)
    acts_ref[0] = a1
    acts_ref[1] = (unit * vec_ref[2:3, :] + vec_ref[3:4, :]).astype(bf16)
    acts_ref[2] = dy_ref[...]
    tables = (c_ref[...], a_ref[...], b_ref[...])
    q_ref[...] = rotate(mm(a1, w_ref[0], NN) + vec_ref[4:5, :], *tables).astype(bf16)
    k_ref[...] = rotate(mm(a1, w_ref[1], NN) + vec_ref[5:6, :], *tables).astype(bf16)
    v_ref[...] = (mm(a1, w_ref[2], NN) + vec_ref[6:7, :]).astype(bf16)
    do_ref[...] = mm(dy_ref[...], w_ref[3], NT).astype(bf16)


def project(place, x, dy, pieces, vecs, tables, step=256):
    count, width = x.shape
    token = pl.BlockSpec((step, width), lambda i, s: (i, 0))
    table = pl.BlockSpec((step, LANES), lambda i, s: (i, 0))
    once = pl.Buffered(1)
    return call(
        project_body,
        8 * count * width * width,
        20 * count * width + 16 * width * width,
        grid_spec=pltpu.PrefetchScalarGridSpec(
            num_scalar_prefetch=1,
            grid=(count // step,),
            in_specs=[token, token, pl.BlockSpec(vecs.shape, lambda i, s: (0, 0)), table, table, table]
            + [pl.BlockSpec(v.shape, lambda i, s, n=v.ndim: (0,) * n, pipeline_mode=once) for v in pieces],
            out_specs=[token] * 4
            + [
                pl.BlockSpec((3, step, width), lambda i, s: (0, i, 0)),
                pl.BlockSpec((4, width, width), lambda i, s: (0, 0, 0)),
            ],
        ),
        out_shape=[jax.ShapeDtypeStruct((count, width), bf16)] * 4
        + [jax.ShapeDtypeStruct((3, count, width), bf16), jax.ShapeDtypeStruct((4, width, width), bf16)],
    )(place, x, dy, vecs, *tables, *pieces)


def attend_body(
    acts_ref, col_ref, row_ref, q_ref, k_ref, v_ref, do_ref, c_ref, a_ref, b_ref,
    g_ref, sum_ref, acts_out_ref, mask_ref, *, block,
):
    length = q_ref.shape[0]
    steps = length // block

    def reach(i):
        return max(0, (i * block - (LONGEST - 1)) // block * block), (i + 1) * block

    @pl.when(pl.program_id(1) == 0)
    def _():
        for i in range(steps):
            lo, hi = reach(i)
            key = lax.broadcasted_iota(jnp.int32, (hi - lo, block), 0) + lo
            query = lax.broadcasted_iota(jnp.int32, (hi - lo, block), 1) + i * block
            same = col_ref[lo:hi, :] == row_ref[0, :, i * block : hi]
            mask = jnp.where(same & (key <= query), 0.0, -jnp.inf)
            mask_ref[i, 0 : hi - lo, 0:block] = mask
            mask_ref[i, 0 : hi - lo, block:] = mask

    low = lax.broadcasted_iota(jnp.int32, (1, LANES), 1) < 64
    eighth = jnp.asarray(0.125, bf16)
    zero = jnp.zeros((), bf16)

    def both(part):
        return jnp.concatenate([jnp.where(low, part, zero), jnp.where(low, zero, part)], axis=0)

    def unstack(part):
        return jnp.concatenate([part[0:64, 0:block], part[64:, block:]], axis=0).T

    pairs = []
    for at in range(0, q_ref.shape[1], LANES):
        lanes = slice(at, at + LANES)
        keys, values = k_ref[:, lanes], v_ref[:, lanes]
        pairs.append(
            (lanes, keys, values, (keys * eighth).T, values.T, q_ref[:, lanes] * eighth, do_ref[:, lanes])
        )
    q_sums = [jnp.zeros((8, LANES), f32) for _ in pairs]
    dks = [[None] * steps for _ in pairs]
    dvs = [[None] * steps for _ in pairs]

    def add(parts, n, value):
        parts[n] = value if parts[n] is None else parts[n] + value

    for i in range(steps):
        lo, hi = reach(i)
        here = slice(i * block, hi)
        for p, (lanes, keys, values, keys_t, values_t, queries, grads) in enumerate(pairs):
            q2, do2 = both(queries[here]), both(grads[here])
            scores = mm(keys[lo:hi], q2, NT) + mask_ref[i, 0 : hi - lo, :]
            d_soft = mm(values[lo:hi], do2, NT)
            raised = jnp.exp(scores - jnp.max(scores, axis=0, keepdims=True))
            soft = raised * (1.0 / jnp.sum(raised, axis=0, keepdims=True))
            inner = jnp.sum(soft * d_soft, axis=0, keepdims=True)
            soft_low = soft.astype(bf16)
            d_scores = (soft * (d_soft - inner)).astype(bf16)
            g_ref[3, here, lanes] = unstack(mm(values_t[:, lo:hi], soft_low, NN)).astype(bf16)
            dq = rotate_back(
                unstack(mm(keys_t[:, lo:hi], d_scores, NN)), c_ref[here, :], a_ref[here, :], b_ref[here, :]
            ).astype(bf16)
            g_ref[0, here, lanes] = dq
            q_sums[p] = q_sums[p] + sub_sum(dq.astype(f32))
            dk, dv = mm(d_scores, q2, NN), mm(soft_low, do2, NN)
            for n in range(lo // block, i + 1):
                rows = slice(n * block - lo, (n + 1) * block - lo)
                add(dks[p], n, dk[rows])
                add(dvs[p], n, dv[rows])
    for p, (lanes, *_) in enumerate(pairs):
        dk = rotate_back(jnp.concatenate(dks[p], axis=0), c_ref[...], a_ref[...], b_ref[...]).astype(bf16)
        dv = jnp.concatenate(dvs[p], axis=0).astype(bf16)
        g_ref[1, :, lanes] = dk
        g_ref[2, :, lanes] = dv
        sum_ref[0, :, lanes] = q_sums[p]
        sum_ref[1, :, lanes] = sub_sum(dk.astype(f32))
        sum_ref[2, :, lanes] = sub_sum(dv.astype(f32))


def attend(segment_ids, q, k, v, do, tables, acts, block=256, lanes=3 * LANES):
    rows, length = segment_ids.shape
    count, width = q.shape
    block = min(block, length)
    token = pl.BlockSpec((length, lanes), lambda r, h: (r, h))
    table = pl.BlockSpec((length, LANES), lambda r, h: (r, 0))
    return call(
        functools.partial(attend_body, block=block),
        24 * count * length * width,
        24 * count * width,
        grid=(rows, width // lanes),
        input_output_aliases={0: 2},
        in_specs=[
            pl.BlockSpec(memory_space=pl.ANY),
            pl.BlockSpec((length, 1), lambda r, h: (r, 0)),
            pl.BlockSpec((1, 1, length), lambda r, h: (r, 0, 0)),
            token,
            token,
            token,
            token,
            table,
            table,
            table,
        ],
        out_specs=[
            pl.BlockSpec((4, length, lanes), lambda r, h: (0, r, h)),
            pl.BlockSpec((3, 8, lanes), lambda r, h: (0, r, h)),
            pl.BlockSpec(memory_space=pl.ANY),
        ],
        out_shape=[
            jax.ShapeDtypeStruct((4, count, width), bf16),
            jax.ShapeDtypeStruct((3, 8 * rows, width), f32),
            jax.ShapeDtypeStruct(acts.shape, acts.dtype),
        ],
        scratch_shapes=[pltpu.VMEM((length // block, length, 2 * block), f32)],
    )(
        acts,
        segment_ids.reshape(-1, 1),
        segment_ids.reshape(rows, 1, length),
        q,
        k,
        v,
        do,
        *tables,
    )


def half_grads_body(place_ref, *refs, first, second, steps, axes):
    l1o, l1p, l2o, l2p, r1o, r1p, r2o, r2p, *outs, acc = refs
    i = pl.program_id(0)
    y, x = place_ref[1], place_ref[2]

    def part(n):
        if n < first:
            value = mm(l1o[0], r1o[n], TN) + mm(l1p[0], r1p[n], TN)
        else:
            value = mm(l2o[n - first], r2o[0], TN) + mm(l2p[n - first], r2p[0], TN)
        return value.reshape(acc.shape[1:])

    @pl.when(i == 0)
    def _():
        for n in range(first + second):
            acc[n] = part(n)

    @pl.when(i > 0)
    def _():
        for n in range(first + second):
            acc[n] += part(n)

    @pl.when(i == steps - 1)
    def _():
        for n in range(first + second):
            for r, axis in enumerate(axes):
                wide = outs[0].shape[-1]
                columns = slice(r * wide, (r + 1) * wide)
                for ref, other in zip(outs[2 * r : 2 * r + 2], (0, 1)):
                    if axis == "x":
                        value = acc[n, :, :, x ^ other, :, :, columns]
                    else:
                        value = acc[n, :, y ^ other, :, :, :, columns]
                    ref[n] = value.astype(bf16)


def layers(part, step, lanes, half=False):
    _, first, count = part
    return pl.BlockSpec((count, step, lanes), lambda i, *s: (first // count, i, s[0][3] if half else 0))


def half_grads(place, left_one, left_two, right_one, right_two, shard, axes, after=(), step=256):
    first, second = right_one[2], left_two[2]
    _, count, width = right_two[0][0].shape
    half = width // 2
    blocks = first + second
    steps = count // step
    shape = (blocks, 2, 2, 2, shard, width // len(axes))
    out = pl.BlockSpec(shape, lambda i, s: (0, 0, 0, 0, 0, 0))
    return call(
        functools.partial(half_grads_body, first=first, second=second, steps=steps, axes=axes),
        blocks * 2 * count * width * width,
        blocks * 4 * count * width,
        after=after,
        grid_spec=pltpu.PrefetchScalarGridSpec(
            num_scalar_prefetch=1,
            grid=(steps,),
            in_specs=[layers(left_one, step, half, True)] * 2
            + [layers(left_two, step, half, True)] * 2
            + [layers(right_one, step, width)] * 2
            + [layers(right_two, step, width)] * 2,
            out_specs=[out] * (2 * len(axes)),
            scratch_shapes=[pltpu.VMEM((blocks, 2, 2, 2, 2, shard, width), f32)],
        ),
        out_shape=[jax.ShapeDtypeStruct(shape, bf16)] * (2 * len(axes)),
    )(place, *left_one[0], *left_two[0], *right_one[0], *right_two[0])


def full_grads(left_one, left_two, right_one, right_two):
    one = jnp.einsum("td,nte->nde", left_one, right_one, preferred_element_type=f32)
    two = jnp.einsum("ntd,te->nde", left_two, right_two, preferred_element_type=f32)
    return jnp.concatenate([one, two], axis=0)


def gelu_parts(u):
    raised = jnp.exp(-0.5 * (u * u))
    t = 1.0 / (1.0 + (0.3275911 * math.sqrt(0.5)) * jnp.abs(u))
    poly = 1.061405429 * t - 1.453152027
    poly = poly * t + 1.421413741
    poly = poly * t - 0.284496736
    poly = (poly * t + 0.254829592) * t
    tail = 0.5 * poly * raised
    return jnp.where(u < 0, tail, 1.0 - tail), raised * (1.0 / math.sqrt(2.0 * math.pi))


def hidden_body(a2_ref, dy_ref, wu_ref, wd_ref, vec_ref, out_ref, sum_ref, *, first):
    row = first + pl.program_id(0)
    u = mm(a2_ref[0], wu_ref[0], NN) + vec_ref[pl.ds(row, 1), :]
    de = mm(dy_ref[0], wd_ref[0], NT)
    dist, density = gelu_parts(u)
    out_ref[0, 0] = (u * dist).astype(bf16)
    du = (de * (dist + u * density)).astype(bf16)
    out_ref[1, 0] = du
    part = sub_sum(du.astype(f32))

    @pl.when(pl.program_id(1) == 0)
    def _():
        sum_ref[0] = part

    @pl.when(pl.program_id(1) > 0)
    def _():
        sum_ref[0] += part


def hidden(first, acts, weights, vecs, after=(), step=512):
    _, count, width = acts.shape
    splits = weights.shape[0] // 2
    blocks = splits // 2
    both, sums = call(
        functools.partial(hidden_body, first=8 + first),
        blocks * 4 * count * width * width,
        blocks * (8 * count * width + 4 * width * width),
        after=after,
        grid=(blocks, count // step),
        in_specs=[
            pl.BlockSpec((1, step, width), lambda j, i: (1, i, 0)),
            pl.BlockSpec((1, step, width), lambda j, i: (2, i, 0)),
            pl.BlockSpec((1, width, width), lambda j, i: (first + j, 0, 0)),
            pl.BlockSpec((1, width, width), lambda j, i: (splits + first + j, 0, 0)),
            pl.BlockSpec(vecs.shape, lambda j, i: (0, 0)),
        ],
        out_specs=[
            pl.BlockSpec((2, 1, step, width), lambda j, i: (0, j, i, 0)),
            pl.BlockSpec((1, 8, width), lambda j, i: (j, 0, 0)),
        ],
        out_shape=[
            jax.ShapeDtypeStruct((2, blocks, count, width), bf16),
            jax.ShapeDtypeStruct((blocks, 8, width), f32),
        ],
    )(acts, acts, weights, weights, vecs)
    return both.reshape(2 * blocks, count, width), sums


def norm_back(grad, unit, scale, gain):
    grad = grad * gain
    first = jnp.mean(grad, axis=1, keepdims=True)
    second = jnp.mean(grad * unit, axis=1, keepdims=True)
    return scale * (grad - first - unit * second)


def hidden_sum(hidden_refs, w_ref, dims, acc):
    at = 0
    for ref in hidden_refs:
        for m in range(ref.shape[0]):
            part = mm(ref[m], w_ref[at], dims)
            acc = part if acc is None else acc + part
            at += 1
    return acc


def output_body(x_ref, o_ref, *refs, splits):
    *e_refs, wo_ref, w_ref, vec_ref, out_ref = refs
    acc = hidden_sum(e_refs, w_ref, NN, mm(o_ref[0], wo_ref[0], NN))
    bias = vec_ref[7:8, :] + vec_ref[8 + splits : 9 + splits, :]
    out_ref[...] = (x_ref[...].astype(f32) + acc + bias).astype(bf16)


def resident(blocks, width, at):
    return pl.BlockSpec((blocks, width, width), lambda i: (at, 0, 0), pipeline_mode=pl.Buffered(1))


def output(x, o, es, wa, wm, vecs, after=(), step=256):
    count, width = x.shape
    splits = wm.shape[0] // 2
    token = pl.BlockSpec((step, width), lambda i: (i, 0))
    return call(
        functools.partial(output_body, splits=splits),
        10 * count * width * width,
        14 * count * width + 10 * width * width,
        after=after,
        grid=(count // step,),
        in_specs=[token]
        + [layers(v, step, width) for v in (o, *es)]
        + [resident(1, width, 3), resident(splits, width, 1), pl.BlockSpec(vecs.shape, lambda i: (0, 0))],
        out_specs=token,
        out_shape=jax.ShapeDtypeStruct((count, width), bf16),
    )(x, *[v[0] for v in (o, *es)], wa, wm, vecs)


def normed(x):
    centred = x - jnp.mean(x, axis=1, keepdims=True)
    scale = lax.rsqrt(jnp.mean(centred * centred, axis=1, keepdims=True) + norm_epsilon)
    return centred * scale, scale


def add_sums(sum_ref, sums):
    sums = [sub_sum(t) for t in sums]

    @pl.when(pl.program_id(0) == 0)
    def _():
        for n, s in enumerate(sums):
            sum_ref[n] = s

    @pl.when(pl.program_id(0) > 0)
    def _():
        for n, s in enumerate(sums):
            sum_ref[n] += s


def grad_one_body(x_ref, dy_ref, g_ref, wa_ref, vec_ref, part_ref, sum_ref):
    dy = dy_ref[...].astype(f32)
    grad = mm(g_ref[0], wa_ref[0], NT) + mm(g_ref[1], wa_ref[1], NT) + mm(g_ref[2], wa_ref[2], NT)
    unit, scale = normed(x_ref[...].astype(f32))
    part_ref[...] = dy + norm_back(grad, unit, scale, vec_ref[0:1, :])
    add_sums(sum_ref, (grad * unit, grad, dy))


def grad_one(x, dy, g, wa, vecs, after=(), step=256):
    count, width = x.shape
    token = pl.BlockSpec((step, width), lambda i: (i, 0))
    return call(
        grad_one_body,
        6 * count * width * width,
        14 * count * width + 6 * width * width,
        after=after,
        grid=(count // step,),
        in_specs=[
            token,
            token,
            layers(g, step, width),
            resident(3, width, 0),
            pl.BlockSpec(vecs.shape, lambda i: (0, 0)),
        ],
        out_specs=[token, pl.BlockSpec((3, 8, width), lambda i: (0, 0, 0))],
        out_shape=[jax.ShapeDtypeStruct((count, width), f32), jax.ShapeDtypeStruct((3, 8, width), f32)],
    )(x, dy, g[0], wa, vecs)


def grad_two_body(x_ref, part_ref, *refs):
    *du_refs, w_ref, vec_ref, grad_ref, sum_ref = refs
    grad = hidden_sum(du_refs, w_ref, NT, None)
    unit, scale = normed(x_ref[...].astype(f32))
    grad_ref[...] = (part_ref[...] + norm_back(grad, unit, scale, vec_ref[2:3, :])).astype(bf16)
    add_sums(sum_ref, (grad * unit, grad))


def grad_two(x, part, dus, wm, vecs, after=(), step=256):
    count, width = x.shape
    token = pl.BlockSpec((step, width), lambda i: (i, 0))
    return call(
        grad_two_body,
        8 * count * width * width,
        16 * count * width + 8 * width * width,
        after=after,
        grid=(count // step,),
        in_specs=[token, token]
        + [layers(v, step, width) for v in dus]
        + [resident(wm.shape[0] // 2, width, 0), pl.BlockSpec(vecs.shape, lambda i: (0, 0))],
        out_specs=[token, pl.BlockSpec((2, 8, width), lambda i: (0, 0, 0))],
        out_shape=[jax.ShapeDtypeStruct((count, width), bf16), jax.ShapeDtypeStruct((2, 8, width), f32)],
    )(x, part, *[v[0] for v in dus], wm, vecs)


def grid_places():
    wide, narrow = lax.axis_index("wide"), lax.axis_index("narrow")
    return wide // 2, wide % 2, narrow // 2, narrow % 2


def to_place(move):
    pairs = []
    for z in range(4):
        for y in range(2):
            for x in range(2):
                for c in range(2):
                    a, b, d, e = move(z, y, x, c)
                    pairs.append((((z * 2 + y) * 2 + x) * 2 + c, ((a * 2 + b) * 2 + d) * 2 + e))
    return pairs


def over_c(value):
    return lax.ppermute(value, AXES, to_place(lambda z, y, x, c: (z, y, x, 1 - c)))


def over_x(value):
    return lax.ppermute(value, AXES, to_place(lambda z, y, x, c: (z, y, 1 - x, c)))


def over_y(value):
    return lax.ppermute(value, AXES, to_place(lambda z, y, x, c: (z, 1 - y, x, c)))


def over_z(value, by):
    return lax.ppermute(value, AXES, to_place(lambda z, y, x, c: ((z + by) % 4, y, x, c)))


def gather_staged(shards):
    own = jnp.stack([shards] + [over_z(shards, s) for s in (1, 2, 3)])
    by_x, by_y = over_x(own), over_y(own)
    lower, upper = over_y(by_x[:2]), over_x(by_y[2:])
    here = [own, by_x, by_y, lower, upper]
    return here + [over_c(v) for v in here]


class Reduction:
    def __init__(self, axes, made):
        self.axes, self.made = axes, made[0]
        self.held = [
            (keep, over_x(send) if axis == "x" else over_y(send))
            for axis, keep, send in zip(axes, made[::2], made[1::2])
        ]

    def second(self, made):
        self.made = made[0]
        self.held = [
            (keep, over_y(send) if axis == "x" else over_x(send))
            for axis, keep, send in zip(self.axes, made[::2], made[1::2])
        ]


def pair_body(place_ref, r, ins, outs):
    y, x = place_ref[1], place_ref[2]
    for n, axis in enumerate(r.axes):
        keep, got = ins[2 * n : 2 * n + 2]
        for ref, other in zip(outs[2 * n : 2 * n + 2], (0, 1)):
            at = (y if axis == "x" else x) ^ other
            ref[...] = (keep[:, :, at].astype(f32) + got[:, :, at].astype(f32)).astype(bf16)


def plane_body(place_ref, r, ins, outs):
    for m, ref in enumerate(outs):
        at = place_ref[0] ^ m
        for n in range(len(r.axes)):
            keep, got = ins[2 * n : 2 * n + 2]
            wide = keep.shape[-1]
            value = keep[:, at >> 1, at & 1].astype(f32) + got[:, at >> 1, at & 1].astype(f32)
            ref[:, :, n * wide : (n + 1) * wide] = value.astype(bf16)


def advance(place, pairs, planes, after=(), steps=2):
    blocks, *_, shard, wide = (pairs + planes)[0].held[0][0].shape
    width = wide * len((pairs + planes)[0].axes)
    shapes, places = [], []
    for r in pairs:
        shapes += [jax.ShapeDtypeStruct((blocks, 2, 2, shard, width // len(r.axes)), bf16)] * (2 * len(r.axes))
    places += [0] * len(shapes)
    if planes:
        shapes += [jax.ShapeDtypeStruct((len(planes), blocks, shard, width), bf16)] * 4
        places += [1] * 4
    operands = [v for r in pairs + planes for held in r.held for v in held]

    def spec(s, at=0):
        n = len(s.shape)
        block = tuple(d // steps if m == at else d for m, d in enumerate(s.shape))
        return pl.BlockSpec(block, lambda b, p: (0,) * at + (b,) + (0,) * (n - 1 - at))

    def body(place_ref, *refs):
        ins, outs = refs[: len(operands)], refs[len(operands) :]
        for r in pairs:
            count = 2 * len(r.axes)
            pair_body(place_ref, r, ins[:count], outs[:count])
            ins, outs = ins[count:], outs[count:]
        for n, r in enumerate(planes):
            count = 2 * len(r.axes)
            plane_body(place_ref, r, ins[:count], [ref.at[n] for ref in outs])
            ins = ins[count:]

    outs = call(
        body,
        0,
        sum(v.size * v.dtype.itemsize for v in operands) * 2,
        after=after,
        grid_spec=pltpu.PrefetchScalarGridSpec(
            num_scalar_prefetch=1,
            grid=(steps,),
            in_specs=[spec(v) for v in operands],
            out_specs=[spec(s, at) for s, at in zip(shapes, places)],
        ),
        out_shape=shapes,
    )(place, *operands)
    for r in pairs:
        count = 2 * len(r.axes)
        r.second(outs[:count])
        outs = outs[count:]
    terms = []
    for m, v in enumerate(outs):
        for r in planes:
            r.made = v
        v = v.reshape(-1, shard, width)
        terms.append(
            lax.ppermute(
                v, AXES, to_place(lambda z, y, x, c, m=m: (2 * c + ((z ^ m) >> 1), y, x, (z ^ m) & 1))
            )
        )
    return terms


def everywhere(value):
    def get(move):
        return lax.ppermute(value, AXES, to_place(move))

    value = value + over_c(value)
    by_x, by_y = over_x(value), over_y(value)
    across = get(lambda z, y, x, c: (z, 1 - y, 1 - x, c))
    value = (value + by_x) + (by_y + across)
    near = get(lambda z, y, x, c: (z ^ 1, y, x, c))
    far = get(lambda z, y, x, c: (z ^ 2, y, x, c))
    last = get(lambda z, y, x, c: (z ^ 3, y, x, c))
    return [value, near, far, last]


def pack_body(slot_ref, *refs, orders, per):
    terms, (shard_ref, out_ref, square_ref) = refs[: len(orders) * per], refs[len(orders) * per :]
    total = jnp.zeros(square_ref.shape, f32)
    for n, order in enumerate(orders):
        for m, b in enumerate(order):
            value = terms[n * per][m].astype(f32)
            for t in range(1, per):
                value = value + terms[n * per + t][m].astype(f32)
            shard_ref[b] = value
            total = total + value * value
    square_ref[...] = total

    def one(j, carry):
        b = slot_ref[j]

        @pl.when(b >= 0)
        def _():
            out_ref[j] = shard_ref[jnp.maximum(b, 0)].astype(bf16)

        @pl.when(b < 0)
        def _():
            out_ref[j] = jnp.zeros(out_ref.shape[1:], bf16)

        return carry

    lax.fori_loop(0, out_ref.shape[0], one, 0)


def pack(slots, terms, orders, after=()):
    per = len(terms[0])
    _, shard, width = terms[0][0].shape
    terms = [v for t in terms for v in t]
    vmem = pl.BlockSpec(memory_space=pltpu.VMEM)
    return call(
        functools.partial(pack_body, orders=orders, per=per),
        0,
        sum(v.size * v.dtype.itemsize for v in terms) * 2,
        after=after,
        in_specs=[pl.BlockSpec(memory_space=pltpu.SMEM)] + [vmem] * len(terms),
        out_specs=[vmem] * 3,
        out_shape=[
            jax.ShapeDtypeStruct((sum(map(len, orders)), shard, width), f32),
            jax.ShapeDtypeStruct((slots.shape[0], shard, width), bf16),
            jax.ShapeDtypeStruct((shard, width), f32),
        ],
    )(slots, *terms)


def to_low_body(l_ref, r_ref, l_low, r_low):
    l_low[...] = l_ref[...].astype(bf16)
    r_low[...] = r_ref[...].astype(bf16)


def to_low(left, right, after=(), step=384):
    width = left.shape[0]
    rows = pl.BlockSpec((step, width), lambda i: (i, 0))
    return call(
        to_low_body,
        0,
        12 * width**2,
        after=after,
        grid=(width // step,),
        in_specs=[rows, rows],
        out_specs=[rows, rows],
        out_shape=[jax.ShapeDtypeStruct((width, width), bf16)] * 2,
    )(left, right)


def scale_parts(total, rows):
    vectors = total[:rows]
    squares = jnp.sum(vectors * vectors, keepdims=True) + jnp.sum(total[rows : rows + 1], keepdims=True)
    scale = jnp.minimum(1.0, clip_level / jnp.sqrt(squares)) * math.sqrt(NPARAM)
    power = jnp.exp2(jnp.floor(jnp.log2(jnp.maximum(scale, 1e-30)))).astype(bf16).astype(f32)
    return power, scale / power


def precondition_body(s_ref, l_ref, r_ref, *refs, rows):
    *part_refs, p_ref, s_low, rest = refs

    @pl.when(pl.program_id(0) == 0)
    def _():
        parts = [ref[...] for ref in part_refs]
        power, left = scale_parts(sum_parts(parts), rows)
        s_low[...] = (s_ref[...].astype(f32) * power).astype(bf16)
        rest[...] = jnp.broadcast_to(left, rest.shape)

    left = mm(l_ref[...], s_low[...], NN)
    p_ref[...] = (rest[0:1, 0:1] * mm(left.astype(bf16), r_ref[...], NN)).astype(bf16)


def sum_parts(parts):
    if len(parts) == 1:
        return parts[0]
    return (parts[0] + parts[1]) + (parts[2] + parts[3])


def precondition(parts, rows, block, left, right, step=384):
    width = block.shape[0]
    whole = pl.BlockSpec((width, width), lambda i: (0, 0))
    some = pl.BlockSpec((step, width), lambda i: (i, 0))
    return call(
        functools.partial(precondition_body, rows=rows),
        4 * width**3,
        8 * width**2,
        grid=(width // step,),
        in_specs=[whole, some, whole] + [pl.BlockSpec(v.shape, lambda i: (0, 0)) for v in parts],
        out_specs=some,
        out_shape=jax.ShapeDtypeStruct((width, width), bf16),
        scratch_shapes=[pltpu.VMEM((width, width), bf16), pltpu.VMEM((8, LANES), f32)],
    )(block, left, right, *parts)


def statistics_body(has_ref, scale_ref, s_ref, l_ref, r_ref, nl_ref, nr_ref, s_low, *, step):
    i = pl.program_id(0)
    width = s_ref.shape[0]

    @pl.when(i == 0)
    def _():
        s_low[...] = (s_ref[...].astype(f32) * scale_ref[0]).astype(bf16)

    factor = (1.0 - decay_beta) * (scale_ref[1] * scale_ref[1] / width)
    at = pl.multiple_of(i * step, step)

    @pl.when(has_ref[0] != 0)
    def _():
        nl_ref[...] = decay_beta * l_ref[...] + factor * mm(s_low[pl.ds(at, step), :], s_low[...], NT)
        nr_ref[...] = decay_beta * r_ref[...] + factor * mm(s_low[:, pl.ds(at, step)], s_low[...], TN)

    @pl.when(has_ref[0] == 0)
    def _():
        nl_ref[...] = l_ref[...]
        nr_ref[...] = r_ref[...]


def statistics(has, scales, block, left, right, step=256):
    width = block.shape[0]
    whole = pl.BlockSpec((width, width), lambda i: (0, 0))
    rows = pl.BlockSpec((step, width), lambda i: (i, 0))
    smem = pl.BlockSpec(memory_space=pltpu.SMEM)
    return call(
        functools.partial(statistics_body, step=step),
        4 * width**3,
        18 * width**2,
        grid=(width // step,),
        in_specs=[smem, smem, whole, rows, rows],
        out_specs=[rows, rows],
        out_shape=[jax.ShapeDtypeStruct((width, width), f32)] * 2,
        scratch_shapes=[pltpu.VMEM((width, width), bf16)],
    )(has, scales, block, left, right)


def update_body(owner_ref, factor_ref, p_ref, shard_ref, block_ref, clip_ref, new_ref, copy_ref):
    for b in range(shard_ref.shape[0]):
        clip_ref[b] = shard_ref[b] * factor_ref[0]
        value = block_ref[b] - matrix_rate * p_ref[owner_ref[b]].astype(f32)
        new_ref[b] = value
        copy_ref[b] = value.astype(bf16)


def update(owners, factor, returned, shards, blocks):
    smem, vmem = pl.BlockSpec(memory_space=pltpu.SMEM), pl.BlockSpec(memory_space=pltpu.VMEM)
    return call(
        update_body,
        0,
        returned.size * 2 + shards.size * 18,
        in_specs=[smem, smem, vmem, vmem, vmem],
        out_specs=[vmem] * 3,
        out_shape=[
            jax.ShapeDtypeStruct(shards.shape, f32),
            jax.ShapeDtypeStruct(shards.shape, f32),
            jax.ShapeDtypeStruct(shards.shape, bf16),
        ],
    )(owners, factor, returned, shards, blocks)


def to_all(value):
    return lax.all_to_all(value, AXES, split_axis=0, concat_axis=0, tiled=True)


def per_device(
    tokens,
    segment_ids,
    cotangent,
    blocks,
    vectors,
    stat_left,
    stat_right,
    root_left,
    root_right,
    vec_stat,
    owners,
    *,
    paired,
):
    rows_here, seq_len, width = tokens.shape
    count = rows_here * seq_len
    splits = FF // width
    slot_count = lax.axis_size(AXES)
    my_index = lax.axis_index(AXES)
    shard = width // slot_count
    vec_rows = vectors.shape[0]

    low_blocks, low_vectors = blocks.astype(bf16), vectors.astype(bf16)
    everyone = jnp.broadcast_to(low_vectors.reshape(1, -1), (slot_count, vec_rows * shard))
    vecs = to_all(everyone).reshape(slot_count, vec_rows, shard)
    vecs = vecs.transpose(1, 0, 2).reshape(vec_rows, width).astype(f32)
    half = splits // 2
    mlp_weights = lax.all_gather(low_blocks[4:], AXES, axis=1, tiled=True)

    flat_tokens = tokens.reshape(count, width)
    dy = cotangent.reshape(count, width)
    tables = rotary_tables(segment_ids)
    place = jnp.stack(grid_places()).astype(jnp.int32)
    if paired:
        pieces = gather_staged(low_blocks[:4])
    else:
        pieces = [lax.all_gather(low_blocks[:4], AXES, axis=1, tiled=True)]
    q, k, v, do, acts, attn_weights = project(place, flat_tokens, dy, pieces, vecs, tables)
    og, attn_sums, acts = attend(segment_ids, q, k, v, do, tables, acts)
    orders = [list(range(4))]
    for first in (0, half):
        orders.append([base + first + j for base in (4, 4 + splits) for j in range(half)])
    if paired:
        acts_pair, og_pair = (acts, over_c(acts)), (og, over_c(og))
        dys = (acts_pair, 2, 1)
        ed0, up_sum0 = hidden(0, acts, mlp_weights, vecs)
        ed0_pair = (ed0, over_c(ed0))
        ed1, up_sum1 = hidden(half, acts, mlp_weights, vecs, after=(ed0, acts_pair[1]))
        ed1_pair = (ed1, over_c(ed1))

        def grads(left, two, one, after):
            operands = ((acts_pair, left, 1), two, one, dys, shard, "xy")
            return Reduction("xy", half_grads(place, *operands, after=after))

        attn = grads(0, (og_pair, 3, 1), (og_pair, 0, 3), (ed1,))
        low = grads(1, (ed0_pair, 0, half), (ed0_pair, half, half), (attn.made,))
        advance(place, [attn], [], after=(low.made,))
        high = grads(1, (ed1_pair, 0, half), (ed1_pair, half, half), (attn.made,))
        advance(place, [low], [], after=(high.made, *[got for _, got in attn.held]))
        part, one_sums = grad_one(flat_tokens, dy, (og, 0, 3), attn_weights, vecs, after=(low.made,))
        terms = [advance(place, [high], [attn, low], after=(part,))]
        es, dus = [(v, 0, half) for v in (ed0, ed1)], [(v, half, half) for v in (ed0, ed1)]
        grad_in, two_sums = grad_two(flat_tokens, part, dus, mlp_weights, vecs, after=(high.made,))
        terms.append(advance(place, [], [high], after=(grad_in,)))
        orders = [orders[0] + orders[1], orders[2]]
    else:
        ed0, up_sum0 = hidden(0, acts, mlp_weights, vecs)
        ed1, up_sum1 = hidden(half, acts, mlp_weights, vecs)
        grads = [
            full_grads(acts[0], og[3:], og[:3], dy),
            full_grads(acts[1], ed0[:half], ed0[half:], dy),
            full_grads(acts[1], ed1[:half], ed1[half:], dy),
        ]
        terms = [[lax.psum_scatter(v, AXES, scatter_dimension=1, tiled=True)] for v in grads]
        es, dus = [(v, 0, half) for v in (ed0, ed1)], [(v, half, half) for v in (ed0, ed1)]
        part, one_sums = grad_one(flat_tokens, dy, (og, 0, 3), attn_weights, vecs)
        grad_in, two_sums = grad_two(flat_tokens, part, dus, mlp_weights, vecs)
    up_sums = [up_sum0, up_sum1]

    one_sums, two_sums = jnp.sum(one_sums, axis=1), jnp.sum(two_sums, axis=1)
    qkv_sums = jnp.sum(attn_sums, axis=1)
    up_sums = jnp.sum(jnp.concatenate(up_sums, axis=0), axis=1)
    bias_sum = one_sums[2:]
    grad_vectors = jnp.concatenate(
        [one_sums[:2], two_sums, qkv_sums, bias_sum, up_sums, bias_sum], axis=0
    )
    slot_ids = jnp.arange(slot_count, dtype=jnp.int32)
    match = owners[None, :] == slot_ids[:, None]
    slots = jnp.sum(jnp.where(match, jnp.arange(1, owners.shape[0] + 1, dtype=jnp.int32)[None], 0), axis=1) - 1
    has_block = jnp.any(owners == my_index)
    shards, outgoing, squares = pack(slots, terms, orders, after=(grad_in,))
    left_low, right_low = to_low(root_left[0], root_right[0], after=(squares,))
    out = output(flat_tokens, (og, 3, 1), es, attn_weights, mlp_weights, vecs, after=(left_low,))
    local = jnp.concatenate([grad_vectors, jnp.sum(squares, axis=0)[None], jnp.zeros((2, width), f32)])
    parts = everywhere(local) if paired else [lax.psum(local, AXES)]
    total = sum_parts(parts)
    vector_sums = total[:vec_rows]
    square_sum = jnp.sum(total[vec_rows]) + jnp.sum(vector_sums * vector_sums)
    shard_vectors = lax.dynamic_slice_in_dim(vector_sums, my_index * shard, shard, axis=1)
    grad_norm = jnp.sqrt(square_sum)
    factor = jnp.minimum(1.0, clip_level / grad_norm)
    root_count = math.sqrt(NPARAM)

    scale = factor * root_count
    power = jnp.exp2(jnp.floor(jnp.log2(jnp.maximum(scale, 1e-30)))).astype(bf16).astype(f32)
    scales = jnp.stack([power, scale / power])
    owned = to_all(outgoing).reshape(width, width)
    precond = precondition(parts, vec_rows, owned, left_low, right_low)
    returned = to_all(precond.reshape(slot_count, shard, width))
    new_left, new_right = statistics(
        has_block.astype(jnp.int32).reshape(1), scales, owned, stat_left[0], stat_right[0]
    )
    clipped_blocks, new_blocks, blocks_copy = update(owners, factor.reshape(1), returned, shards, blocks)
    clipped_vectors = shard_vectors * factor
    scaled_vectors = clipped_vectors * root_count
    new_vec_stat = decay_beta * vec_stat + (1.0 - decay_beta) * (scaled_vectors * scaled_vectors)
    new_vectors = vectors - vector_rate * scaled_vectors * lax.rsqrt(new_vec_stat)
    return (
        out.reshape(tokens.shape),
        grad_in.reshape(tokens.shape),
        clipped_blocks,
        clipped_vectors,
        grad_norm,
        new_left[None],
        new_right[None],
        new_vec_stat,
        new_blocks,
        new_vectors,
        blocks_copy,
        new_vectors.astype(bf16),
    )


def solution(mesh):
    rows = P(AXES, None, None)
    split_rows = P(None, AXES, None)
    split_columns = P(None, AXES)
    paired = dict(mesh.shape) == {"wide": 8, "narrow": 4}
    return jax.shard_map(
        functools.partial(per_device, paired=paired),
        mesh=mesh,
        in_specs=(
            rows, P(AXES, None), rows, split_rows, split_columns,
            rows, rows, rows, rows, split_columns, P(),
        ),
        out_specs=(
            rows, rows, split_rows, split_columns, P(), rows, rows,
            split_columns, split_rows, split_columns, split_rows, split_columns,
        ),
        check_vma=False,
    )
```

```python
import functools
import math

import jax
import jax.numpy as jnp
import numpy as np
from jax import lax
from jax.experimental import pallas as pl
from jax.experimental.pallas import tpu as pltpu
from jax.sharding import PartitionSpec as P

H = 12
FF = 3072
ROT = 16
NPARAM = 7087872
LONGEST = 256

clip_level = 1.0
matrix_rate = 0.03
vector_rate = 0.2
decay_beta = 0.5
norm_epsilon = 1e-05

f32 = jnp.float32
bf16 = jnp.bfloat16
AXES = ("wide", "narrow")
LANES = 128
MIB = 2**20

NN = (((1,), (0,)), ((), ()))
NT = (((1,), (1,)), ((), ()))
TN = (((0,), (0,)), ((), ()))


def mm(left, right, dims):
    return lax.dot_general(left, right, dims, preferred_element_type=f32)


def call(body, flops, moved, vmem=64, after=(), **rest):
    spec = rest.pop("grid_spec", None)
    grid = spec.grid if spec is not None else rest.get("grid", ())
    later = len(after)
    if later:
        held = [pl.BlockSpec(memory_space=pl.ANY)] * later
        if spec is not None:
            first = spec.num_scalar_prefetch + len(spec.in_specs)
            spec = pltpu.PrefetchScalarGridSpec(
                num_scalar_prefetch=spec.num_scalar_prefetch,
                grid=spec.grid,
                in_specs=list(spec.in_specs) + held,
                out_specs=spec.out_specs,
                scratch_shapes=spec.scratch_shapes,
            )
        else:
            first = len(rest["in_specs"])
            rest["in_specs"] = list(rest["in_specs"]) + held
        inner = body

        def body(*refs):
            inner(*refs[:first], *refs[first + later :])

    if spec is not None:
        rest["grid_spec"] = spec
    made = pl.pallas_call(
        body,
        compiler_params=pltpu.CompilerParams(
            vmem_limit_bytes=vmem * MIB,
            dimension_semantics=("arbitrary",) * len(grid),
        ),
        cost_estimate=pl.CostEstimate(
            flops=int(flops), bytes_accessed=int(moved), transcendentals=0
        ),
        **rest,
    )
    return lambda *operands: made(*operands, *after)


def sub_sum(values):
    return jnp.sum(values.reshape(-1, 8, values.shape[-1]), axis=0)


def rotary_tables(segment_ids):
    rows, length = segment_ids.shape
    start = jnp.sum(
        (segment_ids[:, None, :] < segment_ids[:, :, None]).astype(jnp.int32), axis=-1
    )
    offset = (jnp.arange(length, dtype=jnp.int32)[None] - start).astype(f32).reshape(-1, 1)
    half = ROT // 2
    lane = np.arange(LANES) % 64
    rates = np.where(lane < ROT, 10000.0 ** (-2.0 * (lane % half) / ROT), 0.0)
    angle = offset * jnp.asarray(rates, f32)[None]
    cosine, sine = jnp.cos(angle), jnp.sin(angle)
    first = sine * jnp.asarray(np.where(lane < half, -1.0, 0.0), f32)[None]
    second = sine * jnp.asarray(np.where((lane >= half) & (lane < ROT), 1.0, 0.0), f32)[None]
    return cosine, first, second


def rotate(values, cosine, first, second):
    parts = []
    for at in range(0, values.shape[1], LANES):
        part = values[:, at : at + LANES]
        parts.append(
            part * cosine
            + pltpu.roll(part, LANES - ROT // 2, 1) * first
            + pltpu.roll(part, ROT // 2, 1) * second
        )
    return jnp.concatenate(parts, axis=1)


def rotate_back(values, cosine, first, second):
    return (
        values * cosine
        - pltpu.roll(values, LANES - ROT // 2, 1) * first
        - pltpu.roll(values, ROT // 2, 1) * second
    )


def assemble(place_ref, pieces, w_ref):
    z, y, x, c = place_ref[0], place_ref[1], place_ref[2], place_ref[3]
    blocks, rows = w_ref.shape[0], 2 * pieces[0].shape[2]

    def plane(t, carry):
        apart = lax.rem(z - t + 4, 4)

        def put(here, there, at, ry, rx):
            chip = (t * 2 + (y ^ ry)) * 2 + (x ^ rx)
            where = pl.ds(pl.multiple_of(chip * rows, rows), rows)
            for order, wanted in (((here, there), c == 0), ((there, here), c != 0)):

                @pl.when(wanted)
                def _(order=order):
                    for n in range(blocks):
                        w_ref[n, where, :] = jnp.concatenate([ref[at, n] for ref in order], axis=0)

        for m, (ry, rx) in enumerate(((0, 0), (0, 1), (1, 0))):
            put(pieces[m], pieces[5 + m], apart, ry, rx)
        pl.when(apart < 2)(lambda: put(pieces[3], pieces[8], apart, 1, 1))
        pl.when(apart >= 2)(lambda: put(pieces[4], pieces[9], apart - 2, 1, 1))
        return carry

    lax.fori_loop(0, 4, plane, 0)


def project_body(place_ref, x_ref, dy_ref, vec_ref, c_ref, a_ref, b_ref, *refs):
    *pieces, q_ref, k_ref, v_ref, do_ref, acts_ref, w_ref = refs

    @pl.when(pl.program_id(0) == 0)
    def _():
        if len(pieces) > 1:
            assemble(place_ref, pieces, w_ref)
        else:
            w_ref[...] = pieces[0][...]

    unit, _ = normed(x_ref[...].astype(f32))
    a1 = (unit * vec_ref[0:1, :] + vec_ref[1:2, :]).astype(bf16)
    acts_ref[0] = a1
    acts_ref[1] = (unit * vec_ref[2:3, :] + vec_ref[3:4, :]).astype(bf16)
    acts_ref[2] = dy_ref[...]
    tables = (c_ref[...], a_ref[...], b_ref[...])
    q_ref[...] = rotate(mm(a1, w_ref[0], NN) + vec_ref[4:5, :], *tables).astype(bf16)
    k_ref[...] = rotate(mm(a1, w_ref[1], NN) + vec_ref[5:6, :], *tables).astype(bf16)
    v_ref[...] = (mm(a1, w_ref[2], NN) + vec_ref[6:7, :]).astype(bf16)
    do_ref[...] = mm(dy_ref[...], w_ref[3], NT).astype(bf16)


def project(place, x, dy, pieces, vecs, tables, step=256):
    count, width = x.shape
    token = pl.BlockSpec((step, width), lambda i, s: (i, 0))
    table = pl.BlockSpec((step, LANES), lambda i, s: (i, 0))
    once = pl.Buffered(1)
    return call(
        project_body,
        8 * count * width * width,
        20 * count * width + 16 * width * width,
        grid_spec=pltpu.PrefetchScalarGridSpec(
            num_scalar_prefetch=1,
            grid=(count // step,),
            in_specs=[token, token, pl.BlockSpec(vecs.shape, lambda i, s: (0, 0)), table, table, table]
            + [pl.BlockSpec(v.shape, lambda i, s, n=v.ndim: (0,) * n, pipeline_mode=once) for v in pieces],
            out_specs=[token] * 4
            + [
                pl.BlockSpec((3, step, width), lambda i, s: (0, i, 0)),
                pl.BlockSpec((4, width, width), lambda i, s: (0, 0, 0)),
            ],
        ),
        out_shape=[jax.ShapeDtypeStruct((count, width), bf16)] * 4
        + [jax.ShapeDtypeStruct((3, count, width), bf16), jax.ShapeDtypeStruct((4, width, width), bf16)],
    )(place, x, dy, vecs, *tables, *pieces)


def attend_body(
    acts_ref, col_ref, row_ref, q_ref, k_ref, v_ref, do_ref, c_ref, a_ref, b_ref,
    g_ref, sum_ref, acts_out_ref, mask_ref, *, block,
):
    length = q_ref.shape[0]
    steps = length // block

    def reach(i):
        return max(0, (i * block - (LONGEST - 1)) // block * block), (i + 1) * block

    @pl.when(pl.program_id(1) == 0)
    def _():
        for i in range(steps):
            lo, hi = reach(i)
            key = lax.broadcasted_iota(jnp.int32, (hi - lo, block), 0) + lo
            query = lax.broadcasted_iota(jnp.int32, (hi - lo, block), 1) + i * block
            same = col_ref[lo:hi, :] == row_ref[0, :, i * block : hi]
            mask = jnp.where(same & (key <= query), 0.0, -jnp.inf)
            mask_ref[i, 0 : hi - lo, 0:block] = mask
            mask_ref[i, 0 : hi - lo, block:] = mask

    low = lax.broadcasted_iota(jnp.int32, (1, LANES), 1) < 64
    eighth = jnp.asarray(0.125, bf16)
    zero = jnp.zeros((), bf16)

    def both(part):
        return jnp.concatenate([jnp.where(low, part, zero), jnp.where(low, zero, part)], axis=0)

    def unstack(part):
        return jnp.concatenate([part[0:64, 0:block], part[64:, block:]], axis=0).T

    pairs = []
    for at in range(0, q_ref.shape[1], LANES):
        lanes = slice(at, at + LANES)
        keys, values = k_ref[:, lanes], v_ref[:, lanes]
        pairs.append(
            (lanes, keys, values, (keys * eighth).T, values.T, q_ref[:, lanes] * eighth, do_ref[:, lanes])
        )
    q_sums = [jnp.zeros((8, LANES), f32) for _ in pairs]
    dks = [[None] * steps for _ in pairs]
    dvs = [[None] * steps for _ in pairs]

    def add(parts, n, value):
        parts[n] = value if parts[n] is None else parts[n] + value

    for i in range(steps):
        lo, hi = reach(i)
        here = slice(i * block, hi)
        for p, (lanes, keys, values, keys_t, values_t, queries, grads) in enumerate(pairs):
            q2, do2 = both(queries[here]), both(grads[here])
            scores = mm(keys[lo:hi], q2, NT) + mask_ref[i, 0 : hi - lo, :]
            d_soft = mm(values[lo:hi], do2, NT)
            raised = jnp.exp(scores - jnp.max(scores, axis=0, keepdims=True))
            soft = raised * (1.0 / jnp.sum(raised, axis=0, keepdims=True))
            inner = jnp.sum(soft * d_soft, axis=0, keepdims=True)
            soft_low = soft.astype(bf16)
            d_scores = (soft * (d_soft - inner)).astype(bf16)
            g_ref[3, here, lanes] = unstack(mm(values_t[:, lo:hi], soft_low, NN)).astype(bf16)
            dq = rotate_back(
                unstack(mm(keys_t[:, lo:hi], d_scores, NN)), c_ref[here, :], a_ref[here, :], b_ref[here, :]
            ).astype(bf16)
            g_ref[0, here, lanes] = dq
            q_sums[p] = q_sums[p] + sub_sum(dq.astype(f32))
            dk, dv = mm(d_scores, q2, NN), mm(soft_low, do2, NN)
            for n in range(lo // block, i + 1):
                rows = slice(n * block - lo, (n + 1) * block - lo)
                add(dks[p], n, dk[rows])
                add(dvs[p], n, dv[rows])
    for p, (lanes, *_) in enumerate(pairs):
        dk = rotate_back(jnp.concatenate(dks[p], axis=0), c_ref[...], a_ref[...], b_ref[...]).astype(bf16)
        dv = jnp.concatenate(dvs[p], axis=0).astype(bf16)
        g_ref[1, :, lanes] = dk
        g_ref[2, :, lanes] = dv
        sum_ref[0, :, lanes] = q_sums[p]
        sum_ref[1, :, lanes] = sub_sum(dk.astype(f32))
        sum_ref[2, :, lanes] = sub_sum(dv.astype(f32))


def attend(segment_ids, q, k, v, do, tables, acts, block=256, lanes=3 * LANES):
    rows, length = segment_ids.shape
    count, width = q.shape
    block = min(block, length)
    token = pl.BlockSpec((length, lanes), lambda r, h: (r, h))
    table = pl.BlockSpec((length, LANES), lambda r, h: (r, 0))
    return call(
        functools.partial(attend_body, block=block),
        24 * count * length * width,
        24 * count * width,
        grid=(rows, width // lanes),
        input_output_aliases={0: 2},
        in_specs=[
            pl.BlockSpec(memory_space=pl.ANY),
            pl.BlockSpec((length, 1), lambda r, h: (r, 0)),
            pl.BlockSpec((1, 1, length), lambda r, h: (r, 0, 0)),
            token,
            token,
            token,
            token,
            table,
            table,
            table,
        ],
        out_specs=[
            pl.BlockSpec((4, length, lanes), lambda r, h: (0, r, h)),
            pl.BlockSpec((3, 8, lanes), lambda r, h: (0, r, h)),
            pl.BlockSpec(memory_space=pl.ANY),
        ],
        out_shape=[
            jax.ShapeDtypeStruct((4, count, width), bf16),
            jax.ShapeDtypeStruct((3, 8 * rows, width), f32),
            jax.ShapeDtypeStruct(acts.shape, acts.dtype),
        ],
        scratch_shapes=[pltpu.VMEM((length // block, length, 2 * block), f32)],
    )(
        acts,
        segment_ids.reshape(-1, 1),
        segment_ids.reshape(rows, 1, length),
        q,
        k,
        v,
        do,
        *tables,
    )


def half_grads_body(place_ref, *refs, first, second, steps, axes):
    l1o, l1p, l2o, l2p, r1o, r1p, r2o, r2p, *outs, acc = refs
    i = pl.program_id(0)
    y, x = place_ref[1], place_ref[2]

    def part(n):
        if n < first:
            value = mm(l1o[0], r1o[n], TN) + mm(l1p[0], r1p[n], TN)
        else:
            value = mm(l2o[n - first], r2o[0], TN) + mm(l2p[n - first], r2p[0], TN)
        return value.reshape(acc.shape[1:])

    @pl.when(i == 0)
    def _():
        for n in range(first + second):
            acc[n] = part(n)

    @pl.when(i > 0)
    def _():
        for n in range(first + second):
            acc[n] += part(n)

    @pl.when(i == steps - 1)
    def _():
        for n in range(first + second):
            for r, axis in enumerate(axes):
                wide = outs[0].shape[-1]
                columns = slice(r * wide, (r + 1) * wide)
                for ref, other in zip(outs[2 * r : 2 * r + 2], (0, 1)):
                    if axis == "x":
                        value = acc[n, :, :, x ^ other, :, :, columns]
                    else:
                        value = acc[n, :, y ^ other, :, :, :, columns]
                    ref[n] = value.astype(bf16)


def layers(part, step, lanes, half=False):
    _, first, count = part
    return pl.BlockSpec((count, step, lanes), lambda i, *s: (first // count, i, s[0][3] if half else 0))


def half_grads(place, left_one, left_two, right_one, right_two, shard, axes, after=(), step=256):
    first, second = right_one[2], left_two[2]
    _, count, width = right_two[0][0].shape
    half = width // 2
    blocks = first + second
    steps = count // step
    shape = (blocks, 2, 2, 2, shard, width // len(axes))
    out = pl.BlockSpec(shape, lambda i, s: (0, 0, 0, 0, 0, 0))
    return call(
        functools.partial(half_grads_body, first=first, second=second, steps=steps, axes=axes),
        blocks * 2 * count * width * width,
        blocks * 4 * count * width,
        after=after,
        grid_spec=pltpu.PrefetchScalarGridSpec(
            num_scalar_prefetch=1,
            grid=(steps,),
            in_specs=[layers(left_one, step, half, True)] * 2
            + [layers(left_two, step, half, True)] * 2
            + [layers(right_one, step, width)] * 2
            + [layers(right_two, step, width)] * 2,
            out_specs=[out] * (2 * len(axes)),
            scratch_shapes=[pltpu.VMEM((blocks, 2, 2, 2, 2, shard, width), f32)],
        ),
        out_shape=[jax.ShapeDtypeStruct(shape, bf16)] * (2 * len(axes)),
    )(place, *left_one[0], *left_two[0], *right_one[0], *right_two[0])


def full_grads(left_one, left_two, right_one, right_two):
    one = jnp.einsum("td,nte->nde", left_one, right_one, preferred_element_type=f32)
    two = jnp.einsum("ntd,te->nde", left_two, right_two, preferred_element_type=f32)
    return jnp.concatenate([one, two], axis=0)


def gelu_parts(u):
    raised = jnp.exp(-0.5 * (u * u))
    t = 1.0 / (1.0 + (0.3275911 * math.sqrt(0.5)) * jnp.abs(u))
    poly = 1.061405429 * t - 1.453152027
    poly = poly * t + 1.421413741
    poly = poly * t - 0.284496736
    poly = (poly * t + 0.254829592) * t
    tail = 0.5 * poly * raised
    return jnp.where(u < 0, tail, 1.0 - tail), raised * (1.0 / math.sqrt(2.0 * math.pi))


def hidden_body(a2_ref, dy_ref, wu_ref, wd_ref, vec_ref, out_ref, sum_ref, *, first):
    row = first + pl.program_id(0)
    u = mm(a2_ref[0], wu_ref[0], NN) + vec_ref[pl.ds(row, 1), :]
    de = mm(dy_ref[0], wd_ref[0], NT)
    dist, density = gelu_parts(u)
    out_ref[0, 0] = (u * dist).astype(bf16)
    du = (de * (dist + u * density)).astype(bf16)
    out_ref[1, 0] = du
    part = sub_sum(du.astype(f32))

    @pl.when(pl.program_id(1) == 0)
    def _():
        sum_ref[0] = part

    @pl.when(pl.program_id(1) > 0)
    def _():
        sum_ref[0] += part


def hidden(first, acts, weights, vecs, after=(), step=512):
    _, count, width = acts.shape
    splits = weights.shape[0] // 2
    blocks = splits // 2
    both, sums = call(
        functools.partial(hidden_body, first=8 + first),
        blocks * 4 * count * width * width,
        blocks * (8 * count * width + 4 * width * width),
        after=after,
        grid=(blocks, count // step),
        in_specs=[
            pl.BlockSpec((1, step, width), lambda j, i: (1, i, 0)),
            pl.BlockSpec((1, step, width), lambda j, i: (2, i, 0)),
            pl.BlockSpec((1, width, width), lambda j, i: (first + j, 0, 0)),
            pl.BlockSpec((1, width, width), lambda j, i: (splits + first + j, 0, 0)),
            pl.BlockSpec(vecs.shape, lambda j, i: (0, 0)),
        ],
        out_specs=[
            pl.BlockSpec((2, 1, step, width), lambda j, i: (0, j, i, 0)),
            pl.BlockSpec((1, 8, width), lambda j, i: (j, 0, 0)),
        ],
        out_shape=[
            jax.ShapeDtypeStruct((2, blocks, count, width), bf16),
            jax.ShapeDtypeStruct((blocks, 8, width), f32),
        ],
    )(acts, acts, weights, weights, vecs)
    return both.reshape(2 * blocks, count, width), sums


def norm_back(grad, unit, scale, gain):
    grad = grad * gain
    first = jnp.mean(grad, axis=1, keepdims=True)
    second = jnp.mean(grad * unit, axis=1, keepdims=True)
    return scale * (grad - first - unit * second)


def hidden_sum(hidden_refs, w_ref, dims, acc):
    at = 0
    for ref in hidden_refs:
        for m in range(ref.shape[0]):
            part = mm(ref[m], w_ref[at], dims)
            acc = part if acc is None else acc + part
            at += 1
    return acc


def output_body(x_ref, o_ref, *refs, splits):
    *e_refs, wo_ref, w_ref, vec_ref, out_ref = refs
    acc = hidden_sum(e_refs, w_ref, NN, mm(o_ref[0], wo_ref[0], NN))
    bias = vec_ref[7:8, :] + vec_ref[8 + splits : 9 + splits, :]
    out_ref[...] = (x_ref[...].astype(f32) + acc + bias).astype(bf16)


def resident(blocks, width, at):
    return pl.BlockSpec((blocks, width, width), lambda i: (at, 0, 0), pipeline_mode=pl.Buffered(1))


def output(x, o, es, wa, wm, vecs, after=(), step=256):
    count, width = x.shape
    splits = wm.shape[0] // 2
    token = pl.BlockSpec((step, width), lambda i: (i, 0))
    return call(
        functools.partial(output_body, splits=splits),
        10 * count * width * width,
        14 * count * width + 10 * width * width,
        after=after,
        grid=(count // step,),
        in_specs=[token]
        + [layers(v, step, width) for v in (o, *es)]
        + [resident(1, width, 3), resident(splits, width, 1), pl.BlockSpec(vecs.shape, lambda i: (0, 0))],
        out_specs=token,
        out_shape=jax.ShapeDtypeStruct((count, width), bf16),
    )(x, *[v[0] for v in (o, *es)], wa, wm, vecs)


def normed(x):
    centred = x - jnp.mean(x, axis=1, keepdims=True)
    scale = lax.rsqrt(jnp.mean(centred * centred, axis=1, keepdims=True) + norm_epsilon)
    return centred * scale, scale


def add_sums(sum_ref, sums):
    sums = [sub_sum(t) for t in sums]

    @pl.when(pl.program_id(0) == 0)
    def _():
        for n, s in enumerate(sums):
            sum_ref[n] = s

    @pl.when(pl.program_id(0) > 0)
    def _():
        for n, s in enumerate(sums):
            sum_ref[n] += s


def grad_one_body(x_ref, dy_ref, g_ref, wa_ref, vec_ref, part_ref, sum_ref):
    dy = dy_ref[...].astype(f32)
    grad = mm(g_ref[0], wa_ref[0], NT) + mm(g_ref[1], wa_ref[1], NT) + mm(g_ref[2], wa_ref[2], NT)
    unit, scale = normed(x_ref[...].astype(f32))
    part_ref[...] = dy + norm_back(grad, unit, scale, vec_ref[0:1, :])
    add_sums(sum_ref, (grad * unit, grad, dy))


def grad_one(x, dy, g, wa, vecs, after=(), step=256):
    count, width = x.shape
    token = pl.BlockSpec((step, width), lambda i: (i, 0))
    return call(
        grad_one_body,
        6 * count * width * width,
        14 * count * width + 6 * width * width,
        after=after,
        grid=(count // step,),
        in_specs=[
            token,
            token,
            layers(g, step, width),
            resident(3, width, 0),
            pl.BlockSpec(vecs.shape, lambda i: (0, 0)),
        ],
        out_specs=[token, pl.BlockSpec((3, 8, width), lambda i: (0, 0, 0))],
        out_shape=[jax.ShapeDtypeStruct((count, width), f32), jax.ShapeDtypeStruct((3, 8, width), f32)],
    )(x, dy, g[0], wa, vecs)


def grad_two_body(x_ref, part_ref, *refs):
    *du_refs, w_ref, vec_ref, grad_ref, sum_ref = refs
    grad = hidden_sum(du_refs, w_ref, NT, None)
    unit, scale = normed(x_ref[...].astype(f32))
    grad_ref[...] = (part_ref[...] + norm_back(grad, unit, scale, vec_ref[2:3, :])).astype(bf16)
    add_sums(sum_ref, (grad * unit, grad))


def grad_two(x, part, dus, wm, vecs, after=(), step=256):
    count, width = x.shape
    token = pl.BlockSpec((step, width), lambda i: (i, 0))
    return call(
        grad_two_body,
        8 * count * width * width,
        16 * count * width + 8 * width * width,
        after=after,
        grid=(count // step,),
        in_specs=[token, token]
        + [layers(v, step, width) for v in dus]
        + [resident(wm.shape[0] // 2, width, 0), pl.BlockSpec(vecs.shape, lambda i: (0, 0))],
        out_specs=[token, pl.BlockSpec((2, 8, width), lambda i: (0, 0, 0))],
        out_shape=[jax.ShapeDtypeStruct((count, width), bf16), jax.ShapeDtypeStruct((2, 8, width), f32)],
    )(x, part, *[v[0] for v in dus], wm, vecs)


def grid_places():
    wide, narrow = lax.axis_index("wide"), lax.axis_index("narrow")
    return wide // 2, wide % 2, narrow // 2, narrow % 2


def to_place(move):
    pairs = []
    for z in range(4):
        for y in range(2):
            for x in range(2):
                for c in range(2):
                    a, b, d, e = move(z, y, x, c)
                    pairs.append((((z * 2 + y) * 2 + x) * 2 + c, ((a * 2 + b) * 2 + d) * 2 + e))
    return pairs


def over_c(value):
    return lax.ppermute(value, AXES, to_place(lambda z, y, x, c: (z, y, x, 1 - c)))


def over_x(value):
    return lax.ppermute(value, AXES, to_place(lambda z, y, x, c: (z, y, 1 - x, c)))


def over_y(value):
    return lax.ppermute(value, AXES, to_place(lambda z, y, x, c: (z, 1 - y, x, c)))


def over_z(value, by):
    return lax.ppermute(value, AXES, to_place(lambda z, y, x, c: ((z + by) % 4, y, x, c)))


def gather_staged(shards):
    own = jnp.stack([shards] + [over_z(shards, s) for s in (1, 2, 3)])
    by_x, by_y = over_x(own), over_y(own)
    lower, upper = over_y(by_x[:2]), over_x(by_y[2:])
    here = [own, by_x, by_y, lower, upper]
    return here + [over_c(v) for v in here]


class Reduction:
    def __init__(self, axes, made):
        self.axes, self.made = axes, made[0]
        self.held = [
            (keep, over_x(send) if axis == "x" else over_y(send))
            for axis, keep, send in zip(axes, made[::2], made[1::2])
        ]

    def second(self, made):
        self.made = made[0]
        self.held = [
            (keep, over_y(send) if axis == "x" else over_x(send))
            for axis, keep, send in zip(self.axes, made[::2], made[1::2])
        ]


def pair_body(place_ref, r, ins, outs):
    y, x = place_ref[1], place_ref[2]
    for n, axis in enumerate(r.axes):
        keep, got = ins[2 * n : 2 * n + 2]
        for ref, other in zip(outs[2 * n : 2 * n + 2], (0, 1)):
            at = (y if axis == "x" else x) ^ other
            ref[...] = (keep[:, :, at].astype(f32) + got[:, :, at].astype(f32)).astype(bf16)


def plane_body(place_ref, r, ins, outs):
    for m, ref in enumerate(outs):
        at = place_ref[0] ^ m
        for n in range(len(r.axes)):
            keep, got = ins[2 * n : 2 * n + 2]
            wide = keep.shape[-1]
            value = keep[:, at >> 1, at & 1].astype(f32) + got[:, at >> 1, at & 1].astype(f32)
            ref[:, :, n * wide : (n + 1) * wide] = value.astype(bf16)


def advance(place, pairs, planes, after=(), steps=2):
    blocks, *_, shard, wide = (pairs + planes)[0].held[0][0].shape
    width = wide * len((pairs + planes)[0].axes)
    shapes, places = [], []
    for r in pairs:
        shapes += [jax.ShapeDtypeStruct((blocks, 2, 2, shard, width // len(r.axes)), bf16)] * (2 * len(r.axes))
    places += [0] * len(shapes)
    if planes:
        shapes += [jax.ShapeDtypeStruct((len(planes), blocks, shard, width), bf16)] * 4
        places += [1] * 4
    operands = [v for r in pairs + planes for held in r.held for v in held]

    def spec(s, at=0):
        n = len(s.shape)
        block = tuple(d // steps if m == at else d for m, d in enumerate(s.shape))
        return pl.BlockSpec(block, lambda b, p: (0,) * at + (b,) + (0,) * (n - 1 - at))

    def body(place_ref, *refs):
        ins, outs = refs[: len(operands)], refs[len(operands) :]
        for r in pairs:
            count = 2 * len(r.axes)
            pair_body(place_ref, r, ins[:count], outs[:count])
            ins, outs = ins[count:], outs[count:]
        for n, r in enumerate(planes):
            count = 2 * len(r.axes)
            plane_body(place_ref, r, ins[:count], [ref.at[n] for ref in outs])
            ins = ins[count:]

    outs = call(
        body,
        0,
        sum(v.size * v.dtype.itemsize for v in operands) * 2,
        after=after,
        grid_spec=pltpu.PrefetchScalarGridSpec(
            num_scalar_prefetch=1,
            grid=(steps,),
            in_specs=[spec(v) for v in operands],
            out_specs=[spec(s, at) for s, at in zip(shapes, places)],
        ),
        out_shape=shapes,
    )(place, *operands)
    for r in pairs:
        count = 2 * len(r.axes)
        r.second(outs[:count])
        outs = outs[count:]
    terms = []
    for m, v in enumerate(outs):
        for r in planes:
            r.made = v
        v = v.reshape(-1, shard, width)
        terms.append(
            lax.ppermute(
                v, AXES, to_place(lambda z, y, x, c, m=m: (2 * c + ((z ^ m) >> 1), y, x, (z ^ m) & 1))
            )
        )
    return terms


def everywhere(value):
    def get(move):
        return lax.ppermute(value, AXES, to_place(move))

    value = value + over_c(value)
    by_x, by_y = over_x(value), over_y(value)
    across = get(lambda z, y, x, c: (z, 1 - y, 1 - x, c))
    value = (value + by_x) + (by_y + across)
    near = get(lambda z, y, x, c: (z ^ 1, y, x, c))
    far = get(lambda z, y, x, c: (z ^ 2, y, x, c))
    last = get(lambda z, y, x, c: (z ^ 3, y, x, c))
    return [value, near, far, last]


def pack_body(slot_ref, *refs, orders, per):
    terms, (shard_ref, out_ref, square_ref) = refs[: len(orders) * per], refs[len(orders) * per :]
    total = jnp.zeros(square_ref.shape, f32)
    for n, order in enumerate(orders):
        for m, b in enumerate(order):
            value = terms[n * per][m].astype(f32)
            for t in range(1, per):
                value = value + terms[n * per + t][m].astype(f32)
            shard_ref[b] = value
            total = total + value * value
    square_ref[...] = total

    def one(j, carry):
        b = slot_ref[j]

        @pl.when(b >= 0)
        def _():
            out_ref[j] = shard_ref[jnp.maximum(b, 0)].astype(bf16)

        @pl.when(b < 0)
        def _():
            out_ref[j] = jnp.zeros(out_ref.shape[1:], bf16)

        return carry

    lax.fori_loop(0, out_ref.shape[0], one, 0)


def pack(slots, terms, orders, after=()):
    per = len(terms[0])
    _, shard, width = terms[0][0].shape
    terms = [v for t in terms for v in t]
    vmem = pl.BlockSpec(memory_space=pltpu.VMEM)
    return call(
        functools.partial(pack_body, orders=orders, per=per),
        0,
        sum(v.size * v.dtype.itemsize for v in terms) * 2,
        after=after,
        in_specs=[pl.BlockSpec(memory_space=pltpu.SMEM)] + [vmem] * len(terms),
        out_specs=[vmem] * 3,
        out_shape=[
            jax.ShapeDtypeStruct((sum(map(len, orders)), shard, width), f32),
            jax.ShapeDtypeStruct((slots.shape[0], shard, width), bf16),
            jax.ShapeDtypeStruct((shard, width), f32),
        ],
    )(slots, *terms)


def to_low_body(l_ref, r_ref, l_low, r_low):
    l_low[...] = l_ref[...].astype(bf16)
    r_low[...] = r_ref[...].astype(bf16)


def to_low(left, right, after=(), step=384):
    width = left.shape[0]
    rows = pl.BlockSpec((step, width), lambda i: (i, 0))
    return call(
        to_low_body,
        0,
        12 * width**2,
        after=after,
        grid=(width // step,),
        in_specs=[rows, rows],
        out_specs=[rows, rows],
        out_shape=[jax.ShapeDtypeStruct((width, width), bf16)] * 2,
    )(left, right)


def scale_parts(total, rows):
    vectors = total[:rows]
    squares = jnp.sum(vectors * vectors, keepdims=True) + jnp.sum(total[rows : rows + 1], keepdims=True)
    scale = jnp.minimum(1.0, clip_level / jnp.sqrt(squares)) * math.sqrt(NPARAM)
    power = jnp.exp2(jnp.floor(jnp.log2(jnp.maximum(scale, 1e-30)))).astype(bf16).astype(f32)
    return power, scale / power


def precondition_body(s_ref, l_ref, r_ref, *refs, rows):
    *part_refs, p_ref, s_low, rest = refs

    @pl.when(pl.program_id(0) == 0)
    def _():
        parts = [ref[...] for ref in part_refs]
        power, left = scale_parts(sum_parts(parts), rows)
        s_low[...] = (s_ref[...].astype(f32) * power).astype(bf16)
        rest[...] = jnp.broadcast_to(left, rest.shape)

    left = mm(l_ref[...], s_low[...], NN)
    p_ref[...] = (rest[0:1, 0:1] * mm(left.astype(bf16), r_ref[...], NN)).astype(bf16)


def sum_parts(parts):
    if len(parts) == 1:
        return parts[0]
    return (parts[0] + parts[1]) + (parts[2] + parts[3])


def precondition(parts, rows, block, left, right, step=384):
    width = block.shape[0]
    whole = pl.BlockSpec((width, width), lambda i: (0, 0))
    some = pl.BlockSpec((step, width), lambda i: (i, 0))
    return call(
        functools.partial(precondition_body, rows=rows),
        4 * width**3,
        8 * width**2,
        grid=(width // step,),
        in_specs=[whole, some, whole] + [pl.BlockSpec(v.shape, lambda i: (0, 0)) for v in parts],
        out_specs=some,
        out_shape=jax.ShapeDtypeStruct((width, width), bf16),
        scratch_shapes=[pltpu.VMEM((width, width), bf16), pltpu.VMEM((8, LANES), f32)],
    )(block, left, right, *parts)


def statistics_body(has_ref, scale_ref, s_ref, l_ref, r_ref, nl_ref, nr_ref, s_low, *, step):
    i = pl.program_id(0)
    width = s_ref.shape[0]

    @pl.when(i == 0)
    def _():
        s_low[...] = (s_ref[...].astype(f32) * scale_ref[0]).astype(bf16)

    factor = (1.0 - decay_beta) * (scale_ref[1] * scale_ref[1] / width)
    at = pl.multiple_of(i * step, step)

    @pl.when(has_ref[0] != 0)
    def _():
        nl_ref[...] = decay_beta * l_ref[...] + factor * mm(s_low[pl.ds(at, step), :], s_low[...], NT)
        nr_ref[...] = decay_beta * r_ref[...] + factor * mm(s_low[:, pl.ds(at, step)], s_low[...], TN)

    @pl.when(has_ref[0] == 0)
    def _():
        nl_ref[...] = l_ref[...]
        nr_ref[...] = r_ref[...]


def statistics(has, scales, block, left, right, step=256):
    width = block.shape[0]
    whole = pl.BlockSpec((width, width), lambda i: (0, 0))
    rows = pl.BlockSpec((step, width), lambda i: (i, 0))
    smem = pl.BlockSpec(memory_space=pltpu.SMEM)
    return call(
        functools.partial(statistics_body, step=step),
        4 * width**3,
        18 * width**2,
        grid=(width // step,),
        in_specs=[smem, smem, whole, rows, rows],
        out_specs=[rows, rows],
        out_shape=[jax.ShapeDtypeStruct((width, width), f32)] * 2,
        scratch_shapes=[pltpu.VMEM((width, width), bf16)],
    )(has, scales, block, left, right)


def update_body(owner_ref, factor_ref, p_ref, shard_ref, block_ref, clip_ref, new_ref, copy_ref):
    for b in range(shard_ref.shape[0]):
        clip_ref[b] = shard_ref[b] * factor_ref[0]
        value = block_ref[b] - matrix_rate * p_ref[owner_ref[b]].astype(f32)
        new_ref[b] = value
        copy_ref[b] = value.astype(bf16)


def update(owners, factor, returned, shards, blocks):
    smem, vmem = pl.BlockSpec(memory_space=pltpu.SMEM), pl.BlockSpec(memory_space=pltpu.VMEM)
    return call(
        update_body,
        0,
        returned.size * 2 + shards.size * 18,
        in_specs=[smem, smem, vmem, vmem, vmem],
        out_specs=[vmem] * 3,
        out_shape=[
            jax.ShapeDtypeStruct(shards.shape, f32),
            jax.ShapeDtypeStruct(shards.shape, f32),
            jax.ShapeDtypeStruct(shards.shape, bf16),
        ],
    )(owners, factor, returned, shards, blocks)


def to_all(value):
    return lax.all_to_all(value, AXES, split_axis=0, concat_axis=0, tiled=True)


def per_device(
    tokens,
    segment_ids,
    cotangent,
    blocks,
    vectors,
    stat_left,
    stat_right,
    root_left,
    root_right,
    vec_stat,
    owners,
    *,
    paired,
):
    rows_here, seq_len, width = tokens.shape
    count = rows_here * seq_len
    splits = FF // width
    slot_count = lax.axis_size(AXES)
    my_index = lax.axis_index(AXES)
    shard = width // slot_count
    vec_rows = vectors.shape[0]

    low_blocks, low_vectors = blocks.astype(bf16), vectors.astype(bf16)
    everyone = jnp.broadcast_to(low_vectors.reshape(1, -1), (slot_count, vec_rows * shard))
    vecs = to_all(everyone).reshape(slot_count, vec_rows, shard)
    vecs = vecs.transpose(1, 0, 2).reshape(vec_rows, width).astype(f32)
    half = splits // 2
    mlp_weights = lax.all_gather(low_blocks[4:], AXES, axis=1, tiled=True)

    flat_tokens = tokens.reshape(count, width)
    dy = cotangent.reshape(count, width)
    tables = rotary_tables(segment_ids)
    place = jnp.stack(grid_places()).astype(jnp.int32)
    if paired:
        pieces = gather_staged(low_blocks[:4])
    else:
        pieces = [lax.all_gather(low_blocks[:4], AXES, axis=1, tiled=True)]
    q, k, v, do, acts, attn_weights = project(place, flat_tokens, dy, pieces, vecs, tables)
    og, attn_sums, acts = attend(segment_ids, q, k, v, do, tables, acts)
    orders = [list(range(4))]
    for first in (0, half):
        orders.append([base + first + j for base in (4, 4 + splits) for j in range(half)])
    if paired:
        acts_pair, og_pair = (acts, over_c(acts)), (og, over_c(og))
        dys = (acts_pair, 2, 1)
        ed0, up_sum0 = hidden(0, acts, mlp_weights, vecs)
        ed0_pair = (ed0, over_c(ed0))
        ed1, up_sum1 = hidden(half, acts, mlp_weights, vecs, after=(ed0, acts_pair[1]))
        ed1_pair = (ed1, over_c(ed1))

        def grads(left, two, one, after):
            operands = ((acts_pair, left, 1), two, one, dys, shard, "xy")
            return Reduction("xy", half_grads(place, *operands, after=after))

        attn = grads(0, (og_pair, 3, 1), (og_pair, 0, 3), (ed1,))
        low = grads(1, (ed0_pair, 0, half), (ed0_pair, half, half), (attn.made,))
        advance(place, [attn], [], after=(low.made,))
        high = grads(1, (ed1_pair, 0, half), (ed1_pair, half, half), (attn.made,))
        advance(place, [low], [], after=(high.made, *[got for _, got in attn.held]))
        part, one_sums = grad_one(flat_tokens, dy, (og, 0, 3), attn_weights, vecs, after=(low.made,))
        terms = [advance(place, [high], [attn, low], after=(part,))]
        es, dus = [(v, 0, half) for v in (ed0, ed1)], [(v, half, half) for v in (ed0, ed1)]
        grad_in, two_sums = grad_two(flat_tokens, part, dus, mlp_weights, vecs, after=(high.made,))
        terms.append(advance(place, [], [high], after=(grad_in,)))
        orders = [orders[0] + orders[1], orders[2]]
    else:
        ed0, up_sum0 = hidden(0, acts, mlp_weights, vecs)
        ed1, up_sum1 = hidden(half, acts, mlp_weights, vecs)
        grads = [
            full_grads(acts[0], og[3:], og[:3], dy),
            full_grads(acts[1], ed0[:half], ed0[half:], dy),
            full_grads(acts[1], ed1[:half], ed1[half:], dy),
        ]
        terms = [[lax.psum_scatter(v, AXES, scatter_dimension=1, tiled=True)] for v in grads]
        es, dus = [(v, 0, half) for v in (ed0, ed1)], [(v, half, half) for v in (ed0, ed1)]
        part, one_sums = grad_one(flat_tokens, dy, (og, 0, 3), attn_weights, vecs)
        grad_in, two_sums = grad_two(flat_tokens, part, dus, mlp_weights, vecs)
    up_sums = [up_sum0, up_sum1]

    one_sums, two_sums = jnp.sum(one_sums, axis=1), jnp.sum(two_sums, axis=1)
    qkv_sums = jnp.sum(attn_sums, axis=1)
    up_sums = jnp.sum(jnp.concatenate(up_sums, axis=0), axis=1)
    bias_sum = one_sums[2:]
    grad_vectors = jnp.concatenate(
        [one_sums[:2], two_sums, qkv_sums, bias_sum, up_sums, bias_sum], axis=0
    )
    slot_ids = jnp.arange(slot_count, dtype=jnp.int32)
    match = owners[None, :] == slot_ids[:, None]
    slots = jnp.sum(jnp.where(match, jnp.arange(1, owners.shape[0] + 1, dtype=jnp.int32)[None], 0), axis=1) - 1
    has_block = jnp.any(owners == my_index)
    shards, outgoing, squares = pack(slots, terms, orders, after=(grad_in,))
    left_low, right_low = to_low(root_left[0], root_right[0], after=(squares,))
    local = jnp.concatenate([grad_vectors, jnp.sum(squares, axis=0)[None], jnp.zeros((2, width), f32)])
    parts = everywhere(local) if paired else [lax.psum(local, AXES)]
    total = sum_parts(parts)
    vector_sums = total[:vec_rows]
    square_sum = jnp.sum(total[vec_rows]) + jnp.sum(vector_sums * vector_sums)
    shard_vectors = lax.dynamic_slice_in_dim(vector_sums, my_index * shard, shard, axis=1)
    grad_norm = jnp.sqrt(square_sum)
    factor = jnp.minimum(1.0, clip_level / grad_norm)
    root_count = math.sqrt(NPARAM)

    scale = factor * root_count
    power = jnp.exp2(jnp.floor(jnp.log2(jnp.maximum(scale, 1e-30)))).astype(bf16).astype(f32)
    scales = jnp.stack([power, scale / power])
    out = output(flat_tokens, (og, 3, 1), es, attn_weights, mlp_weights, vecs, after=(left_low, scales, factor.reshape(1)))
    owned = to_all(outgoing).reshape(width, width)
    precond = precondition(parts, vec_rows, owned, left_low, right_low)
    returned = to_all(precond.reshape(slot_count, shard, width))
    new_left, new_right = statistics(
        has_block.astype(jnp.int32).reshape(1), scales, owned, stat_left[0], stat_right[0]
    )
    clipped_blocks, new_blocks, blocks_copy = update(owners, factor.reshape(1), returned, shards, blocks)
    clipped_vectors = shard_vectors * factor
    scaled_vectors = clipped_vectors * root_count
    new_vec_stat = decay_beta * vec_stat + (1.0 - decay_beta) * (scaled_vectors * scaled_vectors)
    new_vectors = vectors - vector_rate * scaled_vectors * lax.rsqrt(new_vec_stat)
    return (
        out.reshape(tokens.shape),
        grad_in.reshape(tokens.shape),
        clipped_blocks,
        clipped_vectors,
        grad_norm,
        new_left[None],
        new_right[None],
        new_vec_stat,
        new_blocks,
        new_vectors,
        blocks_copy,
        new_vectors.astype(bf16),
    )


def solution(mesh):
    rows = P(AXES, None, None)
    split_rows = P(None, AXES, None)
    split_columns = P(None, AXES)
    paired = dict(mesh.shape) == {"wide": 8, "narrow": 4}
    return jax.shard_map(
        functools.partial(per_device, paired=paired),
        mesh=mesh,
        in_specs=(
            rows, P(AXES, None), rows, split_rows, split_columns,
            rows, rows, rows, rows, split_columns, P(),
        ),
        out_specs=(
            rows, rows, split_rows, split_columns, P(), rows, rows,
            split_columns, split_rows, split_columns, split_rows, split_columns,
        ),
        check_vma=False,
    )
```

```python
import functools
import math

import jax
import jax.numpy as jnp
import numpy as np
from jax import lax
from jax.experimental import pallas as pl
from jax.experimental.pallas import tpu as pltpu
from jax.sharding import PartitionSpec as P

H = 12
FF = 3072
ROT = 16
NPARAM = 7087872
LONGEST = 256

clip_level = 1.0
matrix_rate = 0.03
vector_rate = 0.2
decay_beta = 0.5
norm_epsilon = 1e-05

f32 = jnp.float32
bf16 = jnp.bfloat16
AXES = ("wide", "narrow")
LANES = 128
MIB = 2**20

NN = (((1,), (0,)), ((), ()))
NT = (((1,), (1,)), ((), ()))
TN = (((0,), (0,)), ((), ()))


def mm(left, right, dims):
    return lax.dot_general(left, right, dims, preferred_element_type=f32)


def call(body, flops, moved, vmem=64, after=(), **rest):
    spec = rest.pop("grid_spec", None)
    grid = spec.grid if spec is not None else rest.get("grid", ())
    later = len(after)
    if later:
        held = [pl.BlockSpec(memory_space=pl.ANY)] * later
        if spec is not None:
            first = spec.num_scalar_prefetch + len(spec.in_specs)
            spec = pltpu.PrefetchScalarGridSpec(
                num_scalar_prefetch=spec.num_scalar_prefetch,
                grid=spec.grid,
                in_specs=list(spec.in_specs) + held,
                out_specs=spec.out_specs,
                scratch_shapes=spec.scratch_shapes,
            )
        else:
            first = len(rest["in_specs"])
            rest["in_specs"] = list(rest["in_specs"]) + held
        inner = body

        def body(*refs):
            inner(*refs[:first], *refs[first + later :])

    if spec is not None:
        rest["grid_spec"] = spec
    made = pl.pallas_call(
        body,
        compiler_params=pltpu.CompilerParams(
            vmem_limit_bytes=vmem * MIB,
            dimension_semantics=("arbitrary",) * len(grid),
        ),
        cost_estimate=pl.CostEstimate(
            flops=int(flops), bytes_accessed=int(moved), transcendentals=0
        ),
        **rest,
    )
    return lambda *operands: made(*operands, *after)


def sub_sum(values):
    return jnp.sum(values.reshape(-1, 8, values.shape[-1]), axis=0)


def rotary_tables(segment_ids):
    rows, length = segment_ids.shape
    start = jnp.sum(
        (segment_ids[:, None, :] < segment_ids[:, :, None]).astype(jnp.int32), axis=-1
    )
    offset = (jnp.arange(length, dtype=jnp.int32)[None] - start).astype(f32).reshape(-1, 1)
    half = ROT // 2
    lane = np.arange(LANES) % 64
    rates = np.where(lane < ROT, 10000.0 ** (-2.0 * (lane % half) / ROT), 0.0)
    angle = offset * jnp.asarray(rates, f32)[None]
    cosine, sine = jnp.cos(angle), jnp.sin(angle)
    first = sine * jnp.asarray(np.where(lane < half, -1.0, 0.0), f32)[None]
    second = sine * jnp.asarray(np.where((lane >= half) & (lane < ROT), 1.0, 0.0), f32)[None]
    return cosine, first, second


def rotate(values, cosine, first, second):
    parts = []
    for at in range(0, values.shape[1], LANES):
        part = values[:, at : at + LANES]
        parts.append(
            part * cosine
            + pltpu.roll(part, LANES - ROT // 2, 1) * first
            + pltpu.roll(part, ROT // 2, 1) * second
        )
    return jnp.concatenate(parts, axis=1)


def rotate_back(values, cosine, first, second):
    return (
        values * cosine
        - pltpu.roll(values, LANES - ROT // 2, 1) * first
        - pltpu.roll(values, ROT // 2, 1) * second
    )


def assemble(place_ref, pieces, w_ref):
    z, y, x, c = place_ref[0], place_ref[1], place_ref[2], place_ref[3]
    blocks, rows = w_ref.shape[0], 2 * pieces[0].shape[2]

    def plane(t, carry):
        apart = lax.rem(z - t + 4, 4)

        def put(here, there, at, ry, rx):
            chip = (t * 2 + (y ^ ry)) * 2 + (x ^ rx)
            where = pl.ds(pl.multiple_of(chip * rows, rows), rows)
            for order, wanted in (((here, there), c == 0), ((there, here), c != 0)):

                @pl.when(wanted)
                def _(order=order):
                    for n in range(blocks):
                        w_ref[n, where, :] = jnp.concatenate([ref[at, n] for ref in order], axis=0)

        for m, (ry, rx) in enumerate(((0, 0), (0, 1), (1, 0))):
            put(pieces[m], pieces[5 + m], apart, ry, rx)
        pl.when(apart < 2)(lambda: put(pieces[3], pieces[8], apart, 1, 1))
        pl.when(apart >= 2)(lambda: put(pieces[4], pieces[9], apart - 2, 1, 1))
        return carry

    lax.fori_loop(0, 4, plane, 0)


def project_body(place_ref, x_ref, dy_ref, vec_ref, c_ref, a_ref, b_ref, *refs):
    *pieces, q_ref, k_ref, v_ref, do_ref, acts_ref, w_ref = refs

    @pl.when(pl.program_id(0) == 0)
    def _():
        if len(pieces) > 1:
            assemble(place_ref, pieces, w_ref)
        else:
            w_ref[...] = pieces[0][...]

    unit, _ = normed(x_ref[...].astype(f32))
    a1 = (unit * vec_ref[0:1, :] + vec_ref[1:2, :]).astype(bf16)
    acts_ref[0] = a1
    acts_ref[1] = (unit * vec_ref[2:3, :] + vec_ref[3:4, :]).astype(bf16)
    acts_ref[2] = dy_ref[...]
    tables = (c_ref[...], a_ref[...], b_ref[...])
    q_ref[...] = rotate(mm(a1, w_ref[0], NN) + vec_ref[4:5, :], *tables).astype(bf16)
    k_ref[...] = rotate(mm(a1, w_ref[1], NN) + vec_ref[5:6, :], *tables).astype(bf16)
    v_ref[...] = (mm(a1, w_ref[2], NN) + vec_ref[6:7, :]).astype(bf16)
    do_ref[...] = mm(dy_ref[...], w_ref[3], NT).astype(bf16)


def project(place, x, dy, pieces, vecs, tables, step=256):
    count, width = x.shape
    token = pl.BlockSpec((step, width), lambda i, s: (i, 0))
    table = pl.BlockSpec((step, LANES), lambda i, s: (i, 0))
    once = pl.Buffered(1)
    return call(
        project_body,
        8 * count * width * width,
        20 * count * width + 16 * width * width,
        grid_spec=pltpu.PrefetchScalarGridSpec(
            num_scalar_prefetch=1,
            grid=(count // step,),
            in_specs=[token, token, pl.BlockSpec(vecs.shape, lambda i, s: (0, 0)), table, table, table]
            + [pl.BlockSpec(v.shape, lambda i, s, n=v.ndim: (0,) * n, pipeline_mode=once) for v in pieces],
            out_specs=[token] * 4
            + [
                pl.BlockSpec((3, step, width), lambda i, s: (0, i, 0)),
                pl.BlockSpec((4, width, width), lambda i, s: (0, 0, 0)),
            ],
        ),
        out_shape=[jax.ShapeDtypeStruct((count, width), bf16)] * 4
        + [jax.ShapeDtypeStruct((3, count, width), bf16), jax.ShapeDtypeStruct((4, width, width), bf16)],
    )(place, x, dy, vecs, *tables, *pieces)


def attend_body(
    acts_ref, col_ref, row_ref, q_ref, k_ref, v_ref, do_ref, c_ref, a_ref, b_ref,
    g_ref, sum_ref, acts_out_ref, mask_ref, *, block,
):
    length = q_ref.shape[0]
    steps = length // block

    def reach(i):
        return max(0, (i * block - (LONGEST - 1)) // block * block), (i + 1) * block

    @pl.when(pl.program_id(1) == 0)
    def _():
        for i in range(steps):
            lo, hi = reach(i)
            key = lax.broadcasted_iota(jnp.int32, (hi - lo, block), 0) + lo
            query = lax.broadcasted_iota(jnp.int32, (hi - lo, block), 1) + i * block
            same = col_ref[lo:hi, :] == row_ref[0, :, i * block : hi]
            mask = jnp.where(same & (key <= query), 0.0, -jnp.inf)
            mask_ref[i, 0 : hi - lo, 0:block] = mask
            mask_ref[i, 0 : hi - lo, block:] = mask

    low = lax.broadcasted_iota(jnp.int32, (1, LANES), 1) < 64
    eighth = jnp.asarray(0.125, bf16)
    zero = jnp.zeros((), bf16)

    def both(part):
        return jnp.concatenate([jnp.where(low, part, zero), jnp.where(low, zero, part)], axis=0)

    def unstack(part):
        return jnp.concatenate([part[0:64, 0:block], part[64:, block:]], axis=0).T

    pairs = []
    for at in range(0, q_ref.shape[1], LANES):
        lanes = slice(at, at + LANES)
        keys, values = k_ref[:, lanes], v_ref[:, lanes]
        pairs.append(
            (lanes, keys, values, (keys * eighth).T, values.T, q_ref[:, lanes] * eighth, do_ref[:, lanes])
        )
    q_sums = [jnp.zeros((8, LANES), f32) for _ in pairs]
    dks = [[None] * steps for _ in pairs]
    dvs = [[None] * steps for _ in pairs]

    def add(parts, n, value):
        parts[n] = value if parts[n] is None else parts[n] + value

    for i in range(steps):
        lo, hi = reach(i)
        here = slice(i * block, hi)
        for p, (lanes, keys, values, keys_t, values_t, queries, grads) in enumerate(pairs):
            q2, do2 = both(queries[here]), both(grads[here])
            scores = mm(keys[lo:hi], q2, NT) + mask_ref[i, 0 : hi - lo, :]
            d_soft = mm(values[lo:hi], do2, NT)
            raised = jnp.exp(scores - jnp.max(scores, axis=0, keepdims=True))
            soft = raised * (1.0 / jnp.sum(raised, axis=0, keepdims=True))
            inner = jnp.sum(soft * d_soft, axis=0, keepdims=True)
            soft_low = soft.astype(bf16)
            d_scores = (soft * (d_soft - inner)).astype(bf16)
            g_ref[3, here, lanes] = unstack(mm(values_t[:, lo:hi], soft_low, NN)).astype(bf16)
            dq = rotate_back(
                unstack(mm(keys_t[:, lo:hi], d_scores, NN)), c_ref[here, :], a_ref[here, :], b_ref[here, :]
            ).astype(bf16)
            g_ref[0, here, lanes] = dq
            q_sums[p] = q_sums[p] + sub_sum(dq.astype(f32))
            dk, dv = mm(d_scores, q2, NN), mm(soft_low, do2, NN)
            for n in range(lo // block, i + 1):
                rows = slice(n * block - lo, (n + 1) * block - lo)
                add(dks[p], n, dk[rows])
                add(dvs[p], n, dv[rows])
    for p, (lanes, *_) in enumerate(pairs):
        dk = rotate_back(jnp.concatenate(dks[p], axis=0), c_ref[...], a_ref[...], b_ref[...]).astype(bf16)
        dv = jnp.concatenate(dvs[p], axis=0).astype(bf16)
        g_ref[1, :, lanes] = dk
        g_ref[2, :, lanes] = dv
        sum_ref[0, :, lanes] = q_sums[p]
        sum_ref[1, :, lanes] = sub_sum(dk.astype(f32))
        sum_ref[2, :, lanes] = sub_sum(dv.astype(f32))


def attend(segment_ids, q, k, v, do, tables, acts, block=256, lanes=3 * LANES):
    rows, length = segment_ids.shape
    count, width = q.shape
    block = min(block, length)
    token = pl.BlockSpec((length, lanes), lambda r, h: (r, h))
    table = pl.BlockSpec((length, LANES), lambda r, h: (r, 0))
    return call(
        functools.partial(attend_body, block=block),
        24 * count * length * width,
        24 * count * width,
        grid=(rows, width // lanes),
        input_output_aliases={0: 2},
        in_specs=[
            pl.BlockSpec(memory_space=pl.ANY),
            pl.BlockSpec((length, 1), lambda r, h: (r, 0)),
            pl.BlockSpec((1, 1, length), lambda r, h: (r, 0, 0)),
            token,
            token,
            token,
            token,
            table,
            table,
            table,
        ],
        out_specs=[
            pl.BlockSpec((4, length, lanes), lambda r, h: (0, r, h)),
            pl.BlockSpec((3, 8, lanes), lambda r, h: (0, r, h)),
            pl.BlockSpec(memory_space=pl.ANY),
        ],
        out_shape=[
            jax.ShapeDtypeStruct((4, count, width), bf16),
            jax.ShapeDtypeStruct((3, 8 * rows, width), f32),
            jax.ShapeDtypeStruct(acts.shape, acts.dtype),
        ],
        scratch_shapes=[pltpu.VMEM((length // block, length, 2 * block), f32)],
    )(
        acts,
        segment_ids.reshape(-1, 1),
        segment_ids.reshape(rows, 1, length),
        q,
        k,
        v,
        do,
        *tables,
    )


def half_grads_body(place_ref, *refs, first, second, steps, axes):
    l1o, l1p, l2o, l2p, r1o, r1p, r2o, r2p, *outs, acc = refs
    i = pl.program_id(0)
    y, x = place_ref[1], place_ref[2]

    @pl.when(i == 0)
    def _():
        acc[...] = jnp.zeros_like(acc)

    for n in range(first + second):
        if n < first:
            part = mm(l1o[0], r1o[n], TN) + mm(l1p[0], r1p[n], TN)
        else:
            part = mm(l2o[n - first], r2o[0], TN) + mm(l2p[n - first], r2p[0], TN)
        acc[n] += part.reshape(acc.shape[1:])

    @pl.when(i == steps - 1)
    def _():
        for n in range(first + second):
            for r, axis in enumerate(axes):
                wide = outs[0].shape[-1]
                columns = slice(r * wide, (r + 1) * wide)
                for ref, other in zip(outs[2 * r : 2 * r + 2], (0, 1)):
                    if axis == "x":
                        value = acc[n, :, :, x ^ other, :, :, columns]
                    else:
                        value = acc[n, :, y ^ other, :, :, :, columns]
                    ref[n] = value.astype(bf16)


def layers(part, step, lanes, half=False):
    _, first, count = part
    return pl.BlockSpec((count, step, lanes), lambda i, *s: (first // count, i, s[0][3] if half else 0))


def half_grads(place, left_one, left_two, right_one, right_two, shard, axes, after=(), step=256):
    first, second = right_one[2], left_two[2]
    _, count, width = right_two[0][0].shape
    half = width // 2
    blocks = first + second
    steps = count // step
    shape = (blocks, 2, 2, 2, shard, width // len(axes))
    out = pl.BlockSpec(shape, lambda i, s: (0, 0, 0, 0, 0, 0))
    return call(
        functools.partial(half_grads_body, first=first, second=second, steps=steps, axes=axes),
        blocks * 2 * count * width * width,
        blocks * 4 * count * width,
        after=after,
        grid_spec=pltpu.PrefetchScalarGridSpec(
            num_scalar_prefetch=1,
            grid=(steps,),
            in_specs=[layers(left_one, step, half, True)] * 2
            + [layers(left_two, step, half, True)] * 2
            + [layers(right_one, step, width)] * 2
            + [layers(right_two, step, width)] * 2,
            out_specs=[out] * (2 * len(axes)),
            scratch_shapes=[pltpu.VMEM((blocks, 2, 2, 2, 2, shard, width), f32)],
        ),
        out_shape=[jax.ShapeDtypeStruct(shape, bf16)] * (2 * len(axes)),
    )(place, *left_one[0], *left_two[0], *right_one[0], *right_two[0])


def full_grads(left_one, left_two, right_one, right_two):
    one = jnp.einsum("td,nte->nde", left_one, right_one, preferred_element_type=f32)
    two = jnp.einsum("ntd,te->nde", left_two, right_two, preferred_element_type=f32)
    return jnp.concatenate([one, two], axis=0)


def gelu_parts(u):
    raised = jnp.exp(-0.5 * (u * u))
    t = 1.0 / (1.0 + (0.3275911 * math.sqrt(0.5)) * jnp.abs(u))
    poly = 1.061405429 * t - 1.453152027
    poly = poly * t + 1.421413741
    poly = poly * t - 0.284496736
    poly = (poly * t + 0.254829592) * t
    tail = 0.5 * poly * raised
    return jnp.where(u < 0, tail, 1.0 - tail), raised * (1.0 / math.sqrt(2.0 * math.pi))


def hidden_body(a2_ref, dy_ref, wu_ref, wd_ref, vec_ref, out_ref, sum_ref, *, first):
    row = first + pl.program_id(0)
    u = mm(a2_ref[0], wu_ref[0], NN) + vec_ref[pl.ds(row, 1), :]
    de = mm(dy_ref[0], wd_ref[0], NT)
    dist, density = gelu_parts(u)
    out_ref[0, 0] = (u * dist).astype(bf16)
    du = (de * (dist + u * density)).astype(bf16)
    out_ref[1, 0] = du
    part = sub_sum(du.astype(f32))

    @pl.when(pl.program_id(1) == 0)
    def _():
        sum_ref[0] = part

    @pl.when(pl.program_id(1) > 0)
    def _():
        sum_ref[0] += part


def hidden(first, acts, weights, vecs, after=(), step=512):
    _, count, width = acts.shape
    splits = weights.shape[0] // 2
    blocks = splits // 2
    both, sums = call(
        functools.partial(hidden_body, first=8 + first),
        blocks * 4 * count * width * width,
        blocks * (8 * count * width + 4 * width * width),
        after=after,
        grid=(blocks, count // step),
        in_specs=[
            pl.BlockSpec((1, step, width), lambda j, i: (1, i, 0)),
            pl.BlockSpec((1, step, width), lambda j, i: (2, i, 0)),
            pl.BlockSpec((1, width, width), lambda j, i: (first + j, 0, 0)),
            pl.BlockSpec((1, width, width), lambda j, i: (splits + first + j, 0, 0)),
            pl.BlockSpec(vecs.shape, lambda j, i: (0, 0)),
        ],
        out_specs=[
            pl.BlockSpec((2, 1, step, width), lambda j, i: (0, j, i, 0)),
            pl.BlockSpec((1, 8, width), lambda j, i: (j, 0, 0)),
        ],
        out_shape=[
            jax.ShapeDtypeStruct((2, blocks, count, width), bf16),
            jax.ShapeDtypeStruct((blocks, 8, width), f32),
        ],
    )(acts, acts, weights, weights, vecs)
    return both.reshape(2 * blocks, count, width), sums


def norm_back(grad, unit, scale, gain):
    grad = grad * gain
    first = jnp.mean(grad, axis=1, keepdims=True)
    second = jnp.mean(grad * unit, axis=1, keepdims=True)
    return scale * (grad - first - unit * second)


def hidden_sum(hidden_refs, w_ref, dims, acc):
    at = 0
    for ref in hidden_refs:
        for m in range(ref.shape[0]):
            part = mm(ref[m], w_ref[at], dims)
            acc = part if acc is None else acc + part
            at += 1
    return acc


def output_body(x_ref, o_ref, *refs, splits):
    *e_refs, wo_ref, w_ref, vec_ref, out_ref = refs
    acc = hidden_sum(e_refs, w_ref, NN, mm(o_ref[0], wo_ref[0], NN))
    bias = vec_ref[7:8, :] + vec_ref[8 + splits : 9 + splits, :]
    out_ref[...] = (x_ref[...].astype(f32) + acc + bias).astype(bf16)


def resident(blocks, width, at):
    return pl.BlockSpec((blocks, width, width), lambda i: (at, 0, 0), pipeline_mode=pl.Buffered(1))


def output(x, o, es, wa, wm, vecs, after=(), step=256):
    count, width = x.shape
    splits = wm.shape[0] // 2
    token = pl.BlockSpec((step, width), lambda i: (i, 0))
    return call(
        functools.partial(output_body, splits=splits),
        10 * count * width * width,
        14 * count * width + 10 * width * width,
        after=after,
        grid=(count // step,),
        in_specs=[token]
        + [layers(v, step, width) for v in (o, *es)]
        + [resident(1, width, 3), resident(splits, width, 1), pl.BlockSpec(vecs.shape, lambda i: (0, 0))],
        out_specs=token,
        out_shape=jax.ShapeDtypeStruct((count, width), bf16),
    )(x, *[v[0] for v in (o, *es)], wa, wm, vecs)


def normed(x):
    centred = x - jnp.mean(x, axis=1, keepdims=True)
    scale = lax.rsqrt(jnp.mean(centred * centred, axis=1, keepdims=True) + norm_epsilon)
    return centred * scale, scale


def add_sums(sum_ref, sums):
    sums = [sub_sum(t) for t in sums]

    @pl.when(pl.program_id(0) == 0)
    def _():
        for n, s in enumerate(sums):
            sum_ref[n] = s

    @pl.when(pl.program_id(0) > 0)
    def _():
        for n, s in enumerate(sums):
            sum_ref[n] += s


def grad_one_body(x_ref, dy_ref, g_ref, wa_ref, vec_ref, part_ref, sum_ref):
    dy = dy_ref[...].astype(f32)
    grad = mm(g_ref[0], wa_ref[0], NT) + mm(g_ref[1], wa_ref[1], NT) + mm(g_ref[2], wa_ref[2], NT)
    unit, scale = normed(x_ref[...].astype(f32))
    part_ref[...] = dy + norm_back(grad, unit, scale, vec_ref[0:1, :])
    add_sums(sum_ref, (grad * unit, grad, dy))


def grad_one(x, dy, g, wa, vecs, after=(), step=256):
    count, width = x.shape
    token = pl.BlockSpec((step, width), lambda i: (i, 0))
    return call(
        grad_one_body,
        6 * count * width * width,
        14 * count * width + 6 * width * width,
        after=after,
        grid=(count // step,),
        in_specs=[
            token,
            token,
            layers(g, step, width),
            resident(3, width, 0),
            pl.BlockSpec(vecs.shape, lambda i: (0, 0)),
        ],
        out_specs=[token, pl.BlockSpec((3, 8, width), lambda i: (0, 0, 0))],
        out_shape=[jax.ShapeDtypeStruct((count, width), f32), jax.ShapeDtypeStruct((3, 8, width), f32)],
    )(x, dy, g[0], wa, vecs)


def grad_two_body(x_ref, part_ref, *refs):
    *du_refs, w_ref, vec_ref, grad_ref, sum_ref = refs
    grad = hidden_sum(du_refs, w_ref, NT, None)
    unit, scale = normed(x_ref[...].astype(f32))
    grad_ref[...] = (part_ref[...] + norm_back(grad, unit, scale, vec_ref[2:3, :])).astype(bf16)
    add_sums(sum_ref, (grad * unit, grad))


def grad_two(x, part, dus, wm, vecs, after=(), step=256):
    count, width = x.shape
    token = pl.BlockSpec((step, width), lambda i: (i, 0))
    return call(
        grad_two_body,
        8 * count * width * width,
        16 * count * width + 8 * width * width,
        after=after,
        grid=(count // step,),
        in_specs=[token, token]
        + [layers(v, step, width) for v in dus]
        + [resident(wm.shape[0] // 2, width, 0), pl.BlockSpec(vecs.shape, lambda i: (0, 0))],
        out_specs=[token, pl.BlockSpec((2, 8, width), lambda i: (0, 0, 0))],
        out_shape=[jax.ShapeDtypeStruct((count, width), bf16), jax.ShapeDtypeStruct((2, 8, width), f32)],
    )(x, part, *[v[0] for v in dus], wm, vecs)


def grid_places():
    wide, narrow = lax.axis_index("wide"), lax.axis_index("narrow")
    return wide // 2, wide % 2, narrow // 2, narrow % 2


def to_place(move):
    pairs = []
    for z in range(4):
        for y in range(2):
            for x in range(2):
                for c in range(2):
                    a, b, d, e = move(z, y, x, c)
                    pairs.append((((z * 2 + y) * 2 + x) * 2 + c, ((a * 2 + b) * 2 + d) * 2 + e))
    return pairs


def over_c(value):
    return lax.ppermute(value, AXES, to_place(lambda z, y, x, c: (z, y, x, 1 - c)))


def over_x(value):
    return lax.ppermute(value, AXES, to_place(lambda z, y, x, c: (z, y, 1 - x, c)))


def over_y(value):
    return lax.ppermute(value, AXES, to_place(lambda z, y, x, c: (z, 1 - y, x, c)))


def over_z(value, by):
    return lax.ppermute(value, AXES, to_place(lambda z, y, x, c: ((z + by) % 4, y, x, c)))


def gather_staged(shards):
    own = jnp.stack([shards] + [over_z(shards, s) for s in (1, 2, 3)])
    by_x, by_y = over_x(own), over_y(own)
    lower, upper = over_y(by_x[:2]), over_x(by_y[2:])
    here = [own, by_x, by_y, lower, upper]
    return here + [over_c(v) for v in here]


class Reduction:
    def __init__(self, axes, made):
        self.axes, self.made = axes, made[0]
        self.held = [
            (keep, over_x(send) if axis == "x" else over_y(send))
            for axis, keep, send in zip(axes, made[::2], made[1::2])
        ]

    def second(self, made):
        self.made = made[0]
        self.held = [
            (keep, over_y(send) if axis == "x" else over_x(send))
            for axis, keep, send in zip(self.axes, made[::2], made[1::2])
        ]


def pair_body(place_ref, r, ins, outs):
    y, x = place_ref[1], place_ref[2]
    for n, axis in enumerate(r.axes):
        keep, got = ins[2 * n : 2 * n + 2]
        for ref, other in zip(outs[2 * n : 2 * n + 2], (0, 1)):
            at = (y if axis == "x" else x) ^ other
            ref[...] = (keep[:, :, at].astype(f32) + got[:, :, at].astype(f32)).astype(bf16)


def plane_body(place_ref, r, ins, outs):
    for m, ref in enumerate(outs):
        at = place_ref[0] ^ m
        for n in range(len(r.axes)):
            keep, got = ins[2 * n : 2 * n + 2]
            wide = keep.shape[-1]
            value = keep[:, at >> 1, at & 1].astype(f32) + got[:, at >> 1, at & 1].astype(f32)
            ref[:, :, n * wide : (n + 1) * wide] = value.astype(bf16)


def advance(place, pairs, planes, after=(), steps=2):
    blocks, *_, shard, wide = (pairs + planes)[0].held[0][0].shape
    width = wide * len((pairs + planes)[0].axes)
    shapes, places = [], []
    for r in pairs:
        shapes += [jax.ShapeDtypeStruct((blocks, 2, 2, shard, width // len(r.axes)), bf16)] * (2 * len(r.axes))
    places += [0] * len(shapes)
    if planes:
        shapes += [jax.ShapeDtypeStruct((len(planes), blocks, shard, width), bf16)] * 4
        places += [1] * 4
    operands = [v for r in pairs + planes for held in r.held for v in held]

    def spec(s, at=0):
        n = len(s.shape)
        block = tuple(d // steps if m == at else d for m, d in enumerate(s.shape))
        return pl.BlockSpec(block, lambda b, p: (0,) * at + (b,) + (0,) * (n - 1 - at))

    def body(place_ref, *refs):
        ins, outs = refs[: len(operands)], refs[len(operands) :]
        for r in pairs:
            count = 2 * len(r.axes)
            pair_body(place_ref, r, ins[:count], outs[:count])
            ins, outs = ins[count:], outs[count:]
        for n, r in enumerate(planes):
            count = 2 * len(r.axes)
            plane_body(place_ref, r, ins[:count], [ref.at[n] for ref in outs])
            ins = ins[count:]

    outs = call(
        body,
        0,
        sum(v.size * v.dtype.itemsize for v in operands) * 2,
        after=after,
        grid_spec=pltpu.PrefetchScalarGridSpec(
            num_scalar_prefetch=1,
            grid=(steps,),
            in_specs=[spec(v) for v in operands],
            out_specs=[spec(s, at) for s, at in zip(shapes, places)],
        ),
        out_shape=shapes,
    )(place, *operands)
    for r in pairs:
        count = 2 * len(r.axes)
        r.second(outs[:count])
        outs = outs[count:]
    terms = []
    for m, v in enumerate(outs):
        for r in planes:
            r.made = v
        v = v.reshape(-1, shard, width)
        terms.append(
            lax.ppermute(
                v, AXES, to_place(lambda z, y, x, c, m=m: (2 * c + ((z ^ m) >> 1), y, x, (z ^ m) & 1))
            )
        )
    return terms


def everywhere(value):
    def get(move):
        return lax.ppermute(value, AXES, to_place(move))

    value = value + over_c(value)
    by_x, by_y = over_x(value), over_y(value)
    across = get(lambda z, y, x, c: (z, 1 - y, 1 - x, c))
    value = (value + by_x) + (by_y + across)
    near = get(lambda z, y, x, c: (z ^ 1, y, x, c))
    far = get(lambda z, y, x, c: (z ^ 2, y, x, c))
    last = get(lambda z, y, x, c: (z ^ 3, y, x, c))
    return [value, near, far, last]


def pack_body(slot_ref, *refs, orders, per):
    terms, (shard_ref, out_ref, square_ref) = refs[: len(orders) * per], refs[len(orders) * per :]
    total = jnp.zeros(square_ref.shape, f32)
    for n, order in enumerate(orders):
        for m, b in enumerate(order):
            value = terms[n * per][m].astype(f32)
            for t in range(1, per):
                value = value + terms[n * per + t][m].astype(f32)
            shard_ref[b] = value
            total = total + value * value
    square_ref[...] = total

    def one(j, carry):
        b = slot_ref[j]

        @pl.when(b >= 0)
        def _():
            out_ref[j] = shard_ref[jnp.maximum(b, 0)].astype(bf16)

        @pl.when(b < 0)
        def _():
            out_ref[j] = jnp.zeros(out_ref.shape[1:], bf16)

        return carry

    lax.fori_loop(0, out_ref.shape[0], one, 0)


def pack(slots, terms, orders, after=()):
    per = len(terms[0])
    _, shard, width = terms[0][0].shape
    terms = [v for t in terms for v in t]
    vmem = pl.BlockSpec(memory_space=pltpu.VMEM)
    return call(
        functools.partial(pack_body, orders=orders, per=per),
        0,
        sum(v.size * v.dtype.itemsize for v in terms) * 2,
        after=after,
        in_specs=[pl.BlockSpec(memory_space=pltpu.SMEM)] + [vmem] * len(terms),
        out_specs=[vmem] * 3,
        out_shape=[
            jax.ShapeDtypeStruct((sum(map(len, orders)), shard, width), f32),
            jax.ShapeDtypeStruct((slots.shape[0], shard, width), bf16),
            jax.ShapeDtypeStruct((shard, width), f32),
        ],
    )(slots, *terms)


def to_low_body(l_ref, r_ref, l_low, r_low):
    l_low[...] = l_ref[...].astype(bf16)
    r_low[...] = r_ref[...].astype(bf16)


def to_low(left, right, after=(), step=384):
    width = left.shape[0]
    rows = pl.BlockSpec((step, width), lambda i: (i, 0))
    return call(
        to_low_body,
        0,
        12 * width**2,
        after=after,
        grid=(width // step,),
        in_specs=[rows, rows],
        out_specs=[rows, rows],
        out_shape=[jax.ShapeDtypeStruct((width, width), bf16)] * 2,
    )(left, right)


def scale_parts(total, rows):
    vectors = total[:rows]
    squares = jnp.sum(vectors * vectors, keepdims=True) + jnp.sum(total[rows : rows + 1], keepdims=True)
    scale = jnp.minimum(1.0, clip_level / jnp.sqrt(squares)) * math.sqrt(NPARAM)
    power = jnp.exp2(jnp.floor(jnp.log2(jnp.maximum(scale, 1e-30)))).astype(bf16).astype(f32)
    return power, scale / power


def precondition_body(s_ref, l_ref, r_ref, *refs, rows):
    *part_refs, p_ref, s_low, rest = refs

    @pl.when(pl.program_id(0) == 0)
    def _():
        parts = [ref[...] for ref in part_refs]
        power, left = scale_parts(sum_parts(parts), rows)
        s_low[...] = (s_ref[...].astype(f32) * power).astype(bf16)
        rest[...] = jnp.broadcast_to(left, rest.shape)

    left = mm(l_ref[...], s_low[...], NN)
    p_ref[...] = (rest[0:1, 0:1] * mm(left.astype(bf16), r_ref[...], NN)).astype(bf16)


def sum_parts(parts):
    if len(parts) == 1:
        return parts[0]
    return (parts[0] + parts[1]) + (parts[2] + parts[3])


def precondition(parts, rows, block, left, right, step=384):
    width = block.shape[0]
    whole = pl.BlockSpec((width, width), lambda i: (0, 0))
    some = pl.BlockSpec((step, width), lambda i: (i, 0))
    return call(
        functools.partial(precondition_body, rows=rows),
        4 * width**3,
        8 * width**2,
        grid=(width // step,),
        in_specs=[whole, some, whole] + [pl.BlockSpec(v.shape, lambda i: (0, 0)) for v in parts],
        out_specs=some,
        out_shape=jax.ShapeDtypeStruct((width, width), bf16),
        scratch_shapes=[pltpu.VMEM((width, width), bf16), pltpu.VMEM((8, LANES), f32)],
    )(block, left, right, *parts)


def statistics_body(has_ref, scale_ref, s_ref, l_ref, r_ref, nl_ref, nr_ref, s_low, *, step):
    i = pl.program_id(0)
    width = s_ref.shape[0]

    @pl.when(i == 0)
    def _():
        s_low[...] = (s_ref[...].astype(f32) * scale_ref[0]).astype(bf16)

    factor = (1.0 - decay_beta) * (scale_ref[1] * scale_ref[1] / width)
    at = pl.multiple_of(i * step, step)

    @pl.when(has_ref[0] != 0)
    def _():
        nl_ref[...] = decay_beta * l_ref[...] + factor * mm(s_low[pl.ds(at, step), :], s_low[...], NT)
        nr_ref[...] = decay_beta * r_ref[...] + factor * mm(s_low[:, pl.ds(at, step)], s_low[...], TN)

    @pl.when(has_ref[0] == 0)
    def _():
        nl_ref[...] = l_ref[...]
        nr_ref[...] = r_ref[...]


def statistics(has, scales, block, left, right, step=256):
    width = block.shape[0]
    whole = pl.BlockSpec((width, width), lambda i: (0, 0))
    rows = pl.BlockSpec((step, width), lambda i: (i, 0))
    smem = pl.BlockSpec(memory_space=pltpu.SMEM)
    return call(
        functools.partial(statistics_body, step=step),
        4 * width**3,
        18 * width**2,
        grid=(width // step,),
        in_specs=[smem, smem, whole, rows, rows],
        out_specs=[rows, rows],
        out_shape=[jax.ShapeDtypeStruct((width, width), f32)] * 2,
        scratch_shapes=[pltpu.VMEM((width, width), bf16)],
    )(has, scales, block, left, right)


def update_body(owner_ref, factor_ref, p_ref, shard_ref, block_ref, clip_ref, new_ref, copy_ref):
    for b in range(shard_ref.shape[0]):
        clip_ref[b] = shard_ref[b] * factor_ref[0]
        value = block_ref[b] - matrix_rate * p_ref[owner_ref[b]].astype(f32)
        new_ref[b] = value
        copy_ref[b] = value.astype(bf16)


def update(owners, factor, returned, shards, blocks):
    smem, vmem = pl.BlockSpec(memory_space=pltpu.SMEM), pl.BlockSpec(memory_space=pltpu.VMEM)
    return call(
        update_body,
        0,
        returned.size * 2 + shards.size * 18,
        in_specs=[smem, smem, vmem, vmem, vmem],
        out_specs=[vmem] * 3,
        out_shape=[
            jax.ShapeDtypeStruct(shards.shape, f32),
            jax.ShapeDtypeStruct(shards.shape, f32),
            jax.ShapeDtypeStruct(shards.shape, bf16),
        ],
    )(owners, factor, returned, shards, blocks)


def to_all(value):
    return lax.all_to_all(value, AXES, split_axis=0, concat_axis=0, tiled=True)


def per_device(
    tokens,
    segment_ids,
    cotangent,
    blocks,
    vectors,
    stat_left,
    stat_right,
    root_left,
    root_right,
    vec_stat,
    owners,
    *,
    paired,
):
    rows_here, seq_len, width = tokens.shape
    count = rows_here * seq_len
    splits = FF // width
    slot_count = lax.axis_size(AXES)
    my_index = lax.axis_index(AXES)
    shard = width // slot_count
    vec_rows = vectors.shape[0]

    low_blocks, low_vectors = blocks.astype(bf16), vectors.astype(bf16)
    everyone = jnp.broadcast_to(low_vectors.reshape(1, -1), (slot_count, vec_rows * shard))
    vecs = to_all(everyone).reshape(slot_count, vec_rows, shard)
    vecs = vecs.transpose(1, 0, 2).reshape(vec_rows, width).astype(f32)
    half = splits // 2
    mlp_weights = lax.all_gather(low_blocks[4:], AXES, axis=1, tiled=True)

    flat_tokens = tokens.reshape(count, width)
    dy = cotangent.reshape(count, width)
    tables = rotary_tables(segment_ids)
    place = jnp.stack(grid_places()).astype(jnp.int32)
    if paired:
        pieces = gather_staged(low_blocks[:4])
    else:
        pieces = [lax.all_gather(low_blocks[:4], AXES, axis=1, tiled=True)]
    q, k, v, do, acts, attn_weights = project(place, flat_tokens, dy, pieces, vecs, tables)
    og, attn_sums, acts = attend(segment_ids, q, k, v, do, tables, acts)
    orders = [list(range(4))]
    for first in (0, half):
        orders.append([base + first + j for base in (4, 4 + splits) for j in range(half)])
    if paired:
        acts_pair, og_pair = (acts, over_c(acts)), (og, over_c(og))
        dys = (acts_pair, 2, 1)
        ed0, up_sum0 = hidden(0, acts, mlp_weights, vecs)
        ed0_pair = (ed0, over_c(ed0))
        ed1, up_sum1 = hidden(half, acts, mlp_weights, vecs, after=(ed0, acts_pair[1]))
        ed1_pair = (ed1, over_c(ed1))

        def grads(left, two, one, after):
            operands = ((acts_pair, left, 1), two, one, dys, shard, "xy")
            return Reduction("xy", half_grads(place, *operands, after=after))

        attn = grads(0, (og_pair, 3, 1), (og_pair, 0, 3), (ed1,))
        low = grads(1, (ed0_pair, 0, half), (ed0_pair, half, half), (attn.made,))
        advance(place, [attn], [], after=(low.made,))
        high = grads(1, (ed1_pair, 0, half), (ed1_pair, half, half), (attn.made,))
        advance(place, [low], [], after=(high.made, *[got for _, got in attn.held]))
        part, one_sums = grad_one(flat_tokens, dy, (og, 0, 3), attn_weights, vecs, after=(low.made,))
        terms = [advance(place, [high], [attn, low], after=(part,))]
        es, dus = [(v, 0, half) for v in (ed0, ed1)], [(v, half, half) for v in (ed0, ed1)]
        grad_in, two_sums = grad_two(flat_tokens, part, dus, mlp_weights, vecs, after=(high.made,))
        terms.append(advance(place, [], [high], after=(grad_in,)))
        orders = [orders[0] + orders[1], orders[2]]
    else:
        ed0, up_sum0 = hidden(0, acts, mlp_weights, vecs)
        ed1, up_sum1 = hidden(half, acts, mlp_weights, vecs)
        grads = [
            full_grads(acts[0], og[3:], og[:3], dy),
            full_grads(acts[1], ed0[:half], ed0[half:], dy),
            full_grads(acts[1], ed1[:half], ed1[half:], dy),
        ]
        terms = [[lax.psum_scatter(v, AXES, scatter_dimension=1, tiled=True)] for v in grads]
        es, dus = [(v, 0, half) for v in (ed0, ed1)], [(v, half, half) for v in (ed0, ed1)]
        part, one_sums = grad_one(flat_tokens, dy, (og, 0, 3), attn_weights, vecs)
        grad_in, two_sums = grad_two(flat_tokens, part, dus, mlp_weights, vecs)
    up_sums = [up_sum0, up_sum1]

    one_sums, two_sums = jnp.sum(one_sums, axis=1), jnp.sum(two_sums, axis=1)
    qkv_sums = jnp.sum(attn_sums, axis=1)
    up_sums = jnp.sum(jnp.concatenate(up_sums, axis=0), axis=1)
    bias_sum = one_sums[2:]
    grad_vectors = jnp.concatenate(
        [one_sums[:2], two_sums, qkv_sums, bias_sum, up_sums, bias_sum], axis=0
    )
    slot_ids = jnp.arange(slot_count, dtype=jnp.int32)
    match = owners[None, :] == slot_ids[:, None]
    slots = jnp.sum(jnp.where(match, jnp.arange(1, owners.shape[0] + 1, dtype=jnp.int32)[None], 0), axis=1) - 1
    has_block = jnp.any(owners == my_index)
    shards, outgoing, squares = pack(slots, terms, orders, after=(grad_in,))
    left_low, right_low = to_low(root_left[0], root_right[0], after=(squares,))
    local = jnp.concatenate([grad_vectors, jnp.sum(squares, axis=0)[None], jnp.zeros((2, width), f32)])
    parts = everywhere(local) if paired else [lax.psum(local, AXES)]
    total = sum_parts(parts)
    vector_sums = total[:vec_rows]
    square_sum = jnp.sum(total[vec_rows]) + jnp.sum(vector_sums * vector_sums)
    shard_vectors = lax.dynamic_slice_in_dim(vector_sums, my_index * shard, shard, axis=1)
    grad_norm = jnp.sqrt(square_sum)
    factor = jnp.minimum(1.0, clip_level / grad_norm)
    root_count = math.sqrt(NPARAM)

    scale = factor * root_count
    power = jnp.exp2(jnp.floor(jnp.log2(jnp.maximum(scale, 1e-30)))).astype(bf16).astype(f32)
    scales = jnp.stack([power, scale / power])
    out = output(flat_tokens, (og, 3, 1), es, attn_weights, mlp_weights, vecs, after=(left_low, scales, factor.reshape(1)))
    owned = to_all(outgoing).reshape(width, width)
    precond = precondition(parts, vec_rows, owned, left_low, right_low)
    returned = to_all(precond.reshape(slot_count, shard, width))
    new_left, new_right = statistics(
        has_block.astype(jnp.int32).reshape(1), scales, owned, stat_left[0], stat_right[0]
    )
    clipped_blocks, new_blocks, blocks_copy = update(owners, factor.reshape(1), returned, shards, blocks)
    clipped_vectors = shard_vectors * factor
    scaled_vectors = clipped_vectors * root_count
    new_vec_stat = decay_beta * vec_stat + (1.0 - decay_beta) * (scaled_vectors * scaled_vectors)
    new_vectors = vectors - vector_rate * scaled_vectors * lax.rsqrt(new_vec_stat)
    return (
        out.reshape(tokens.shape),
        grad_in.reshape(tokens.shape),
        clipped_blocks,
        clipped_vectors,
        grad_norm,
        new_left[None],
        new_right[None],
        new_vec_stat,
        new_blocks,
        new_vectors,
        blocks_copy,
        new_vectors.astype(bf16),
    )


def solution(mesh):
    rows = P(AXES, None, None)
    split_rows = P(None, AXES, None)
    split_columns = P(None, AXES)
    paired = dict(mesh.shape) == {"wide": 8, "narrow": 4}
    return jax.shard_map(
        functools.partial(per_device, paired=paired),
        mesh=mesh,
        in_specs=(
            rows, P(AXES, None), rows, split_rows, split_columns,
            rows, rows, rows, rows, split_columns, P(),
        ),
        out_specs=(
            rows, rows, split_rows, split_columns, P(), rows, rows,
            split_columns, split_rows, split_columns, split_rows, split_columns,
        ),
        check_vma=False,
    )
```

```python
import functools
import math

import jax
import jax.numpy as jnp
import numpy as np
from jax import lax
from jax.experimental import pallas as pl
from jax.experimental.pallas import tpu as pltpu
from jax.sharding import PartitionSpec as P

H = 12
FF = 3072
ROT = 16
NPARAM = 7087872
LONGEST = 256

clip_level = 1.0
matrix_rate = 0.03
vector_rate = 0.2
decay_beta = 0.5
norm_epsilon = 1e-05

f32 = jnp.float32
bf16 = jnp.bfloat16
AXES = ("wide", "narrow")
LANES = 128
MIB = 2**20

NN = (((1,), (0,)), ((), ()))
NT = (((1,), (1,)), ((), ()))
TN = (((0,), (0,)), ((), ()))


def mm(left, right, dims):
    return lax.dot_general(left, right, dims, preferred_element_type=f32)


def call(body, flops, moved, vmem=64, after=(), **rest):
    spec = rest.pop("grid_spec", None)
    grid = spec.grid if spec is not None else rest.get("grid", ())
    later = len(after)
    if later:
        held = [pl.BlockSpec(memory_space=pl.ANY)] * later
        if spec is not None:
            first = spec.num_scalar_prefetch + len(spec.in_specs)
            spec = pltpu.PrefetchScalarGridSpec(
                num_scalar_prefetch=spec.num_scalar_prefetch,
                grid=spec.grid,
                in_specs=list(spec.in_specs) + held,
                out_specs=spec.out_specs,
                scratch_shapes=spec.scratch_shapes,
            )
        else:
            first = len(rest["in_specs"])
            rest["in_specs"] = list(rest["in_specs"]) + held
        inner = body

        def body(*refs):
            inner(*refs[:first], *refs[first + later :])

    if spec is not None:
        rest["grid_spec"] = spec
    made = pl.pallas_call(
        body,
        compiler_params=pltpu.CompilerParams(
            vmem_limit_bytes=vmem * MIB,
            dimension_semantics=("arbitrary",) * len(grid),
        ),
        cost_estimate=pl.CostEstimate(
            flops=int(flops), bytes_accessed=int(moved), transcendentals=0
        ),
        **rest,
    )
    return lambda *operands: made(*operands, *after)


def sub_sum(values):
    return jnp.sum(values.reshape(-1, 8, values.shape[-1]), axis=0)


def rotary_tables(segment_ids):
    rows, length = segment_ids.shape
    start = jnp.sum(
        (segment_ids[:, None, :] < segment_ids[:, :, None]).astype(jnp.int32), axis=-1
    )
    offset = (jnp.arange(length, dtype=jnp.int32)[None] - start).astype(f32).reshape(-1, 1)
    half = ROT // 2
    lane = np.arange(LANES) % 64
    rates = np.where(lane < ROT, 10000.0 ** (-2.0 * (lane % half) / ROT), 0.0)
    angle = offset * jnp.asarray(rates, f32)[None]
    cosine, sine = jnp.cos(angle), jnp.sin(angle)
    first = sine * jnp.asarray(np.where(lane < half, -1.0, 0.0), f32)[None]
    second = sine * jnp.asarray(np.where((lane >= half) & (lane < ROT), 1.0, 0.0), f32)[None]
    return cosine, first, second


def rotate(values, cosine, first, second):
    parts = []
    for at in range(0, values.shape[1], LANES):
        part = values[:, at : at + LANES]
        parts.append(
            part * cosine
            + pltpu.roll(part, LANES - ROT // 2, 1) * first
            + pltpu.roll(part, ROT // 2, 1) * second
        )
    return jnp.concatenate(parts, axis=1)


def rotate_back(values, cosine, first, second):
    return (
        values * cosine
        - pltpu.roll(values, LANES - ROT // 2, 1) * first
        - pltpu.roll(values, ROT // 2, 1) * second
    )


def assemble(place_ref, pieces, w_ref):
    z, y, x, c = place_ref[0], place_ref[1], place_ref[2], place_ref[3]
    blocks, rows = w_ref.shape[0], 2 * pieces[0].shape[2]

    def plane(t, carry):
        apart = lax.rem(z - t + 4, 4)

        def put(here, there, at, ry, rx):
            chip = (t * 2 + (y ^ ry)) * 2 + (x ^ rx)
            where = pl.ds(pl.multiple_of(chip * rows, rows), rows)
            for order, wanted in (((here, there), c == 0), ((there, here), c != 0)):

                @pl.when(wanted)
                def _(order=order):
                    for n in range(blocks):
                        w_ref[n, where, :] = jnp.concatenate([ref[at, n] for ref in order], axis=0)

        for m, (ry, rx) in enumerate(((0, 0), (0, 1), (1, 0))):
            put(pieces[m], pieces[5 + m], apart, ry, rx)
        pl.when(apart < 2)(lambda: put(pieces[3], pieces[8], apart, 1, 1))
        pl.when(apart >= 2)(lambda: put(pieces[4], pieces[9], apart - 2, 1, 1))
        return carry

    lax.fori_loop(0, 4, plane, 0)


def project_body(place_ref, x_ref, dy_ref, vec_ref, c_ref, a_ref, b_ref, *refs):
    *pieces, q_ref, k_ref, v_ref, do_ref, acts_ref, w_ref = refs

    @pl.when(pl.program_id(0) == 0)
    def _():
        if len(pieces) > 1:
            assemble(place_ref, pieces, w_ref)
        else:
            w_ref[...] = pieces[0][...]

    unit, _ = normed(x_ref[...].astype(f32))
    a1 = (unit * vec_ref[0:1, :] + vec_ref[1:2, :]).astype(bf16)
    acts_ref[0] = a1
    acts_ref[1] = (unit * vec_ref[2:3, :] + vec_ref[3:4, :]).astype(bf16)
    acts_ref[2] = dy_ref[...]
    tables = (c_ref[...], a_ref[...], b_ref[...])
    q_ref[...] = rotate(mm(a1, w_ref[0], NN) + vec_ref[4:5, :], *tables).astype(bf16)
    k_ref[...] = rotate(mm(a1, w_ref[1], NN) + vec_ref[5:6, :], *tables).astype(bf16)
    v_ref[...] = (mm(a1, w_ref[2], NN) + vec_ref[6:7, :]).astype(bf16)
    do_ref[...] = mm(dy_ref[...], w_ref[3], NT).astype(bf16)


def project(place, x, dy, pieces, vecs, tables, step=256):
    count, width = x.shape
    token = pl.BlockSpec((step, width), lambda i, s: (i, 0))
    table = pl.BlockSpec((step, LANES), lambda i, s: (i, 0))
    once = pl.Buffered(1)
    return call(
        project_body,
        8 * count * width * width,
        20 * count * width + 16 * width * width,
        grid_spec=pltpu.PrefetchScalarGridSpec(
            num_scalar_prefetch=1,
            grid=(count // step,),
            in_specs=[token, token, pl.BlockSpec(vecs.shape, lambda i, s: (0, 0)), table, table, table]
            + [pl.BlockSpec(v.shape, lambda i, s, n=v.ndim: (0,) * n, pipeline_mode=once) for v in pieces],
            out_specs=[token] * 4
            + [
                pl.BlockSpec((3, step, width), lambda i, s: (0, i, 0)),
                pl.BlockSpec((4, width, width), lambda i, s: (0, 0, 0)),
            ],
        ),
        out_shape=[jax.ShapeDtypeStruct((count, width), bf16)] * 4
        + [jax.ShapeDtypeStruct((3, count, width), bf16), jax.ShapeDtypeStruct((4, width, width), bf16)],
    )(place, x, dy, vecs, *tables, *pieces)


def attend_body(
    acts_ref, col_ref, row_ref, q_ref, k_ref, v_ref, do_ref, c_ref, a_ref, b_ref,
    g_ref, sum_ref, acts_out_ref, mask_ref, *, block,
):
    length = q_ref.shape[0]
    steps = length // block

    def reach(i):
        return max(0, (i * block - (LONGEST - 1)) // block * block), (i + 1) * block

    @pl.when(pl.program_id(1) == 0)
    def _():
        for i in range(steps):
            lo, hi = reach(i)
            key = lax.broadcasted_iota(jnp.int32, (hi - lo, block), 0) + lo
            query = lax.broadcasted_iota(jnp.int32, (hi - lo, block), 1) + i * block
            same = col_ref[lo:hi, :] == row_ref[0, :, i * block : hi]
            mask = jnp.where(same & (key <= query), 0.0, -jnp.inf)
            mask_ref[i, 0 : hi - lo, 0:block] = mask
            mask_ref[i, 0 : hi - lo, block:] = mask

    low = lax.broadcasted_iota(jnp.int32, (1, LANES), 1) < 64
    eighth = jnp.asarray(0.125, bf16)
    zero = jnp.zeros((), bf16)

    def both(part):
        return jnp.concatenate([jnp.where(low, part, zero), jnp.where(low, zero, part)], axis=0)

    def unstack(part):
        return jnp.concatenate([part[0:64, 0:block], part[64:, block:]], axis=0).T

    pairs = []
    for at in range(0, q_ref.shape[1], LANES):
        lanes = slice(at, at + LANES)
        keys, values = k_ref[:, lanes], v_ref[:, lanes]
        pairs.append(
            (lanes, keys, values, (keys * eighth).T, values.T, q_ref[:, lanes] * eighth, do_ref[:, lanes])
        )
    q_sums = [jnp.zeros((8, LANES), f32) for _ in pairs]
    dks = [[None] * steps for _ in pairs]
    dvs = [[None] * steps for _ in pairs]

    def add(parts, n, value):
        parts[n] = value if parts[n] is None else parts[n] + value

    for i in range(steps):
        lo, hi = reach(i)
        here = slice(i * block, hi)
        for p, (lanes, keys, values, keys_t, values_t, queries, grads) in enumerate(pairs):
            q2, do2 = both(queries[here]), both(grads[here])
            scores = mm(keys[lo:hi], q2, NT) + mask_ref[i, 0 : hi - lo, :]
            d_soft = mm(values[lo:hi], do2, NT)
            raised = jnp.exp(scores - jnp.max(scores, axis=0, keepdims=True))
            soft = raised * (1.0 / jnp.sum(raised, axis=0, keepdims=True))
            inner = jnp.sum(soft * d_soft, axis=0, keepdims=True)
            soft_low = soft.astype(bf16)
            d_scores = (soft * (d_soft - inner)).astype(bf16)
            g_ref[3, here, lanes] = unstack(mm(values_t[:, lo:hi], soft_low, NN)).astype(bf16)
            dq = rotate_back(
                unstack(mm(keys_t[:, lo:hi], d_scores, NN)), c_ref[here, :], a_ref[here, :], b_ref[here, :]
            ).astype(bf16)
            g_ref[0, here, lanes] = dq
            q_sums[p] = q_sums[p] + sub_sum(dq.astype(f32))
            dk, dv = mm(d_scores, q2, NN), mm(soft_low, do2, NN)
            for n in range(lo // block, i + 1):
                rows = slice(n * block - lo, (n + 1) * block - lo)
                add(dks[p], n, dk[rows])
                add(dvs[p], n, dv[rows])
    for p, (lanes, *_) in enumerate(pairs):
        dk = rotate_back(jnp.concatenate(dks[p], axis=0), c_ref[...], a_ref[...], b_ref[...]).astype(bf16)
        dv = jnp.concatenate(dvs[p], axis=0).astype(bf16)
        g_ref[1, :, lanes] = dk
        g_ref[2, :, lanes] = dv
        sum_ref[0, :, lanes] = q_sums[p]
        sum_ref[1, :, lanes] = sub_sum(dk.astype(f32))
        sum_ref[2, :, lanes] = sub_sum(dv.astype(f32))


def attend(segment_ids, q, k, v, do, tables, acts, block=256, lanes=3 * LANES):
    rows, length = segment_ids.shape
    count, width = q.shape
    block = min(block, length)
    token = pl.BlockSpec((length, lanes), lambda r, h: (r, h))
    table = pl.BlockSpec((length, LANES), lambda r, h: (r, 0))
    return call(
        functools.partial(attend_body, block=block),
        24 * count * length * width,
        24 * count * width,
        grid=(rows, width // lanes),
        input_output_aliases={0: 2},
        in_specs=[
            pl.BlockSpec(memory_space=pl.ANY),
            pl.BlockSpec((length, 1), lambda r, h: (r, 0)),
            pl.BlockSpec((1, 1, length), lambda r, h: (r, 0, 0)),
            token,
            token,
            token,
            token,
            table,
            table,
            table,
        ],
        out_specs=[
            pl.BlockSpec((4, length, lanes), lambda r, h: (0, r, h)),
            pl.BlockSpec((3, 8, lanes), lambda r, h: (0, r, h)),
            pl.BlockSpec(memory_space=pl.ANY),
        ],
        out_shape=[
            jax.ShapeDtypeStruct((4, count, width), bf16),
            jax.ShapeDtypeStruct((3, 8 * rows, width), f32),
            jax.ShapeDtypeStruct(acts.shape, acts.dtype),
        ],
        scratch_shapes=[pltpu.VMEM((length // block, length, 2 * block), f32)],
    )(
        acts,
        segment_ids.reshape(-1, 1),
        segment_ids.reshape(rows, 1, length),
        q,
        k,
        v,
        do,
        *tables,
    )


def half_grads_body(place_ref, *refs, first, second, steps, axes):
    l1o, l1p, l2o, l2p, r1o, r1p, r2o, r2p, *outs, acc = refs
    i = pl.program_id(0)
    y, x = place_ref[1], place_ref[2]

    @pl.when(i == 0)
    def _():
        acc[...] = jnp.zeros_like(acc)

    for n in range(first + second):
        if n < first:
            part = mm(l1o[0], r1o[n], TN) + mm(l1p[0], r1p[n], TN)
        else:
            part = mm(l2o[n - first], r2o[0], TN) + mm(l2p[n - first], r2p[0], TN)
        acc[n] += part.reshape(acc.shape[1:])

    @pl.when(i == steps - 1)
    def _():
        for n in range(first + second):
            for r, axis in enumerate(axes):
                wide = outs[0].shape[-1]
                columns = slice(r * wide, (r + 1) * wide)
                for ref, other in zip(outs[2 * r : 2 * r + 2], (0, 1)):
                    if axis == "x":
                        value = acc[n, :, :, x ^ other, :, :, columns]
                    else:
                        value = acc[n, :, y ^ other, :, :, :, columns]
                    ref[n] = value.astype(bf16)


def layers(part, step, lanes, half=False):
    _, first, count = part
    return pl.BlockSpec((count, step, lanes), lambda i, *s: (first // count, i, s[0][3] if half else 0))


def half_grads(place, left_one, left_two, right_one, right_two, shard, axes, after=(), step=256):
    first, second = right_one[2], left_two[2]
    _, count, width = right_two[0][0].shape
    half = width // 2
    blocks = first + second
    steps = count // step
    shape = (blocks, 2, 2, 2, shard, width // len(axes))
    out = pl.BlockSpec(shape, lambda i, s: (0, 0, 0, 0, 0, 0))
    return call(
        functools.partial(half_grads_body, first=first, second=second, steps=steps, axes=axes),
        blocks * 2 * count * width * width,
        blocks * 4 * count * width,
        after=after,
        grid_spec=pltpu.PrefetchScalarGridSpec(
            num_scalar_prefetch=1,
            grid=(steps,),
            in_specs=[layers(left_one, step, half, True)] * 2
            + [layers(left_two, step, half, True)] * 2
            + [layers(right_one, step, width)] * 2
            + [layers(right_two, step, width)] * 2,
            out_specs=[out] * (2 * len(axes)),
            scratch_shapes=[pltpu.VMEM((blocks, 2, 2, 2, 2, shard, width), f32)],
        ),
        out_shape=[jax.ShapeDtypeStruct(shape, bf16)] * (2 * len(axes)),
    )(place, *left_one[0], *left_two[0], *right_one[0], *right_two[0])


def full_grads(left_one, left_two, right_one, right_two):
    one = jnp.einsum("td,nte->nde", left_one, right_one, preferred_element_type=f32)
    two = jnp.einsum("ntd,te->nde", left_two, right_two, preferred_element_type=f32)
    return jnp.concatenate([one, two], axis=0)


def gelu_parts(u):
    raised = jnp.exp(-0.5 * (u * u))
    t = 1.0 / (1.0 + (0.3275911 * math.sqrt(0.5)) * jnp.abs(u))
    poly = 1.061405429 * t - 1.453152027
    poly = poly * t + 1.421413741
    poly = poly * t - 0.284496736
    poly = (poly * t + 0.254829592) * t
    tail = 0.5 * poly * raised
    return jnp.where(u < 0, tail, 1.0 - tail), raised * (1.0 / math.sqrt(2.0 * math.pi))


def hidden_body(a2_ref, dy_ref, wu_ref, wd_ref, vec_ref, out_ref, sum_ref, *, first):
    row = first + pl.program_id(0)
    u = mm(a2_ref[0], wu_ref[0], NN) + vec_ref[pl.ds(row, 1), :]
    de = mm(dy_ref[0], wd_ref[0], NT)
    dist, density = gelu_parts(u)
    out_ref[0, 0] = (u * dist).astype(bf16)
    du = (de * (dist + u * density)).astype(bf16)
    out_ref[1, 0] = du
    part = sub_sum(du.astype(f32))

    @pl.when(pl.program_id(1) == 0)
    def _():
        sum_ref[0] = part

    @pl.when(pl.program_id(1) > 0)
    def _():
        sum_ref[0] += part


def hidden(first, acts, weights, vecs, after=(), step=512):
    _, count, width = acts.shape
    splits = weights.shape[0] // 2
    blocks = splits // 2
    both, sums = call(
        functools.partial(hidden_body, first=8 + first),
        blocks * 4 * count * width * width,
        blocks * (8 * count * width + 4 * width * width),
        after=after,
        grid=(blocks, count // step),
        in_specs=[
            pl.BlockSpec((1, step, width), lambda j, i: (1, i, 0)),
            pl.BlockSpec((1, step, width), lambda j, i: (2, i, 0)),
            pl.BlockSpec((1, width, width), lambda j, i: (first + j, 0, 0)),
            pl.BlockSpec((1, width, width), lambda j, i: (splits + first + j, 0, 0)),
            pl.BlockSpec(vecs.shape, lambda j, i: (0, 0)),
        ],
        out_specs=[
            pl.BlockSpec((2, 1, step, width), lambda j, i: (0, j, i, 0)),
            pl.BlockSpec((1, 8, width), lambda j, i: (j, 0, 0)),
        ],
        out_shape=[
            jax.ShapeDtypeStruct((2, blocks, count, width), bf16),
            jax.ShapeDtypeStruct((blocks, 8, width), f32),
        ],
    )(acts, acts, weights, weights, vecs)
    return both.reshape(2 * blocks, count, width), sums


def norm_back(grad, unit, scale, gain):
    grad = grad * gain
    first = jnp.mean(grad, axis=1, keepdims=True)
    second = jnp.mean(grad * unit, axis=1, keepdims=True)
    return scale * (grad - first - unit * second)


def hidden_sum(hidden_refs, w_ref, dims, acc):
    at = 0
    for ref in hidden_refs:
        for m in range(ref.shape[0]):
            part = mm(ref[m], w_ref[at], dims)
            acc = part if acc is None else acc + part
            at += 1
    return acc


def output_body(x_ref, o_ref, *refs, splits):
    *e_refs, wo_ref, w_ref, vec_ref, out_ref = refs
    acc = hidden_sum(e_refs, w_ref, NN, mm(o_ref[0], wo_ref[0], NN))
    bias = vec_ref[7:8, :] + vec_ref[8 + splits : 9 + splits, :]
    out_ref[...] = (x_ref[...].astype(f32) + acc + bias).astype(bf16)


def resident(blocks, width, at):
    return pl.BlockSpec((blocks, width, width), lambda i: (at, 0, 0), pipeline_mode=pl.Buffered(1))


def output(x, o, es, wa, wm, vecs, after=(), step=256):
    count, width = x.shape
    splits = wm.shape[0] // 2
    token = pl.BlockSpec((step, width), lambda i: (i, 0))
    return call(
        functools.partial(output_body, splits=splits),
        10 * count * width * width,
        14 * count * width + 10 * width * width,
        after=after,
        grid=(count // step,),
        in_specs=[token]
        + [layers(v, step, width) for v in (o, *es)]
        + [resident(1, width, 3), resident(splits, width, 1), pl.BlockSpec(vecs.shape, lambda i: (0, 0))],
        out_specs=token,
        out_shape=jax.ShapeDtypeStruct((count, width), bf16),
    )(x, *[v[0] for v in (o, *es)], wa, wm, vecs)


def normed(x):
    centred = x - jnp.mean(x, axis=1, keepdims=True)
    scale = lax.rsqrt(jnp.mean(centred * centred, axis=1, keepdims=True) + norm_epsilon)
    return centred * scale, scale


def add_sums(sum_ref, sums):
    sums = [sub_sum(t) for t in sums]

    @pl.when(pl.program_id(0) == 0)
    def _():
        for n, s in enumerate(sums):
            sum_ref[n] = s

    @pl.when(pl.program_id(0) > 0)
    def _():
        for n, s in enumerate(sums):
            sum_ref[n] += s


def grad_one_body(x_ref, dy_ref, g_ref, wa_ref, vec_ref, part_ref, sum_ref):
    dy = dy_ref[...].astype(f32)
    grad = mm(g_ref[0], wa_ref[0], NT) + mm(g_ref[1], wa_ref[1], NT) + mm(g_ref[2], wa_ref[2], NT)
    unit, scale = normed(x_ref[...].astype(f32))
    part_ref[...] = dy + norm_back(grad, unit, scale, vec_ref[0:1, :])
    add_sums(sum_ref, (grad * unit, grad, dy))


def grad_one(x, dy, g, wa, vecs, after=(), step=256):
    count, width = x.shape
    token = pl.BlockSpec((step, width), lambda i: (i, 0))
    return call(
        grad_one_body,
        6 * count * width * width,
        14 * count * width + 6 * width * width,
        after=after,
        grid=(count // step,),
        in_specs=[
            token,
            token,
            layers(g, step, width),
            resident(3, width, 0),
            pl.BlockSpec(vecs.shape, lambda i: (0, 0)),
        ],
        out_specs=[token, pl.BlockSpec((3, 8, width), lambda i: (0, 0, 0))],
        out_shape=[jax.ShapeDtypeStruct((count, width), f32), jax.ShapeDtypeStruct((3, 8, width), f32)],
    )(x, dy, g[0], wa, vecs)


def grad_two_body(x_ref, part_ref, *refs):
    *du_refs, w_ref, vec_ref, grad_ref, sum_ref = refs
    grad = hidden_sum(du_refs, w_ref, NT, None)
    unit, scale = normed(x_ref[...].astype(f32))
    grad_ref[...] = (part_ref[...] + norm_back(grad, unit, scale, vec_ref[2:3, :])).astype(bf16)
    add_sums(sum_ref, (grad * unit, grad))


def grad_two(x, part, dus, wm, vecs, after=(), step=256):
    count, width = x.shape
    token = pl.BlockSpec((step, width), lambda i: (i, 0))
    return call(
        grad_two_body,
        8 * count * width * width,
        16 * count * width + 8 * width * width,
        after=after,
        grid=(count // step,),
        in_specs=[token, token]
        + [layers(v, step, width) for v in dus]
        + [resident(wm.shape[0] // 2, width, 0), pl.BlockSpec(vecs.shape, lambda i: (0, 0))],
        out_specs=[token, pl.BlockSpec((2, 8, width), lambda i: (0, 0, 0))],
        out_shape=[jax.ShapeDtypeStruct((count, width), bf16), jax.ShapeDtypeStruct((2, 8, width), f32)],
    )(x, part, *[v[0] for v in dus], wm, vecs)


def grid_places():
    wide, narrow = lax.axis_index("wide"), lax.axis_index("narrow")
    return wide // 2, wide % 2, narrow // 2, narrow % 2


def to_place(move):
    pairs = []
    for z in range(4):
        for y in range(2):
            for x in range(2):
                for c in range(2):
                    a, b, d, e = move(z, y, x, c)
                    pairs.append((((z * 2 + y) * 2 + x) * 2 + c, ((a * 2 + b) * 2 + d) * 2 + e))
    return pairs


def over_c(value):
    return lax.ppermute(value, AXES, to_place(lambda z, y, x, c: (z, y, x, 1 - c)))


def over_x(value):
    return lax.ppermute(value, AXES, to_place(lambda z, y, x, c: (z, y, 1 - x, c)))


def over_y(value):
    return lax.ppermute(value, AXES, to_place(lambda z, y, x, c: (z, 1 - y, x, c)))


def over_z(value, by):
    return lax.ppermute(value, AXES, to_place(lambda z, y, x, c: ((z + by) % 4, y, x, c)))


def gather_staged(shards):
    own = jnp.stack([shards] + [over_z(shards, s) for s in (1, 2, 3)])
    by_x, by_y = over_x(own), over_y(own)
    lower, upper = over_y(by_x[:2]), over_x(by_y[2:])
    here = [own, by_x, by_y, lower, upper]
    return here + [over_c(v) for v in here]


class Reduction:
    def __init__(self, axes, made):
        self.axes, self.made = axes, made[0]
        self.held = [
            (keep, over_x(send) if axis == "x" else over_y(send))
            for axis, keep, send in zip(axes, made[::2], made[1::2])
        ]

    def second(self, made):
        self.made = made[0]
        self.held = [
            (keep, over_y(send) if axis == "x" else over_x(send))
            for axis, keep, send in zip(self.axes, made[::2], made[1::2])
        ]


def pair_body(place_ref, r, ins, outs):
    y, x = place_ref[1], place_ref[2]
    for n, axis in enumerate(r.axes):
        keep, got = ins[2 * n : 2 * n + 2]
        for ref, other in zip(outs[2 * n : 2 * n + 2], (0, 1)):
            at = (y if axis == "x" else x) ^ other
            ref[...] = (keep[:, :, at].astype(f32) + got[:, :, at].astype(f32)).astype(bf16)


def plane_body(place_ref, r, ins, outs):
    for m, ref in enumerate(outs):
        at = place_ref[0] ^ m
        for n in range(len(r.axes)):
            keep, got = ins[2 * n : 2 * n + 2]
            wide = keep.shape[-1]
            value = keep[:, at >> 1, at & 1].astype(f32) + got[:, at >> 1, at & 1].astype(f32)
            ref[:, :, n * wide : (n + 1) * wide] = value.astype(bf16)


def advance(place, pairs, planes, after=(), steps=2):
    blocks, *_, shard, wide = (pairs + planes)[0].held[0][0].shape
    width = wide * len((pairs + planes)[0].axes)
    shapes, places = [], []
    for r in pairs:
        shapes += [jax.ShapeDtypeStruct((blocks, 2, 2, shard, width // len(r.axes)), bf16)] * (2 * len(r.axes))
    places += [0] * len(shapes)
    if planes:
        shapes += [jax.ShapeDtypeStruct((len(planes), blocks, shard, width), bf16)] * 4
        places += [1] * 4
    operands = [v for r in pairs + planes for held in r.held for v in held]

    def spec(s, at=0):
        n = len(s.shape)
        block = tuple(d // steps if m == at else d for m, d in enumerate(s.shape))
        return pl.BlockSpec(block, lambda b, p: (0,) * at + (b,) + (0,) * (n - 1 - at))

    def body(place_ref, *refs):
        ins, outs = refs[: len(operands)], refs[len(operands) :]
        for r in pairs:
            count = 2 * len(r.axes)
            pair_body(place_ref, r, ins[:count], outs[:count])
            ins, outs = ins[count:], outs[count:]
        for n, r in enumerate(planes):
            count = 2 * len(r.axes)
            plane_body(place_ref, r, ins[:count], [ref.at[n] for ref in outs])
            ins = ins[count:]

    outs = call(
        body,
        0,
        sum(v.size * v.dtype.itemsize for v in operands) * 2,
        after=after,
        grid_spec=pltpu.PrefetchScalarGridSpec(
            num_scalar_prefetch=1,
            grid=(steps,),
            in_specs=[spec(v) for v in operands],
            out_specs=[spec(s, at) for s, at in zip(shapes, places)],
        ),
        out_shape=shapes,
    )(place, *operands)
    for r in pairs:
        count = 2 * len(r.axes)
        r.second(outs[:count])
        outs = outs[count:]
    terms = []
    for m, v in enumerate(outs):
        for r in planes:
            r.made = v
        v = v.reshape(-1, shard, width)
        terms.append(
            lax.ppermute(
                v, AXES, to_place(lambda z, y, x, c, m=m: (2 * c + ((z ^ m) >> 1), y, x, (z ^ m) & 1))
            )
        )
    return terms


def everywhere(value):
    def get(move):
        return lax.ppermute(value, AXES, to_place(move))

    value = value + over_c(value)
    by_x, by_y = over_x(value), over_y(value)
    across = get(lambda z, y, x, c: (z, 1 - y, 1 - x, c))
    value = (value + by_x) + (by_y + across)
    near = get(lambda z, y, x, c: (z ^ 1, y, x, c))
    far = get(lambda z, y, x, c: (z ^ 2, y, x, c))
    last = get(lambda z, y, x, c: (z ^ 3, y, x, c))
    return [value, near, far, last]


def pack_body(slot_ref, *refs, orders, per):
    terms, (shard_ref, out_ref, square_ref) = refs[: len(orders) * per], refs[len(orders) * per :]
    total = jnp.zeros(square_ref.shape, f32)
    for n, order in enumerate(orders):
        for m, b in enumerate(order):
            value = terms[n * per][m].astype(f32)
            for t in range(1, per):
                value = value + terms[n * per + t][m].astype(f32)
            shard_ref[b] = value
            total = total + value * value
    square_ref[...] = total

    def one(j, carry):
        b = slot_ref[j]

        @pl.when(b >= 0)
        def _():
            out_ref[j] = shard_ref[jnp.maximum(b, 0)].astype(bf16)

        @pl.when(b < 0)
        def _():
            out_ref[j] = jnp.zeros(out_ref.shape[1:], bf16)

        return carry

    lax.fori_loop(0, out_ref.shape[0], one, 0)


def pack(slots, terms, orders, after=()):
    per = len(terms[0])
    _, shard, width = terms[0][0].shape
    terms = [v for t in terms for v in t]
    vmem = pl.BlockSpec(memory_space=pltpu.VMEM)
    return call(
        functools.partial(pack_body, orders=orders, per=per),
        0,
        sum(v.size * v.dtype.itemsize for v in terms) * 2,
        after=after,
        in_specs=[pl.BlockSpec(memory_space=pltpu.SMEM)] + [vmem] * len(terms),
        out_specs=[vmem] * 3,
        out_shape=[
            jax.ShapeDtypeStruct((sum(map(len, orders)), shard, width), f32),
            jax.ShapeDtypeStruct((slots.shape[0], shard, width), bf16),
            jax.ShapeDtypeStruct((shard, width), f32),
        ],
    )(slots, *terms)


def to_low_body(l_ref, r_ref, l_low, r_low):
    l_low[...] = l_ref[...].astype(bf16)
    r_low[...] = r_ref[...].astype(bf16)


def to_low(left, right, after=(), step=384):
    width = left.shape[0]
    rows = pl.BlockSpec((step, width), lambda i: (i, 0))
    return call(
        to_low_body,
        0,
        12 * width**2,
        after=after,
        grid=(width // step,),
        in_specs=[rows, rows],
        out_specs=[rows, rows],
        out_shape=[jax.ShapeDtypeStruct((width, width), bf16)] * 2,
    )(left, right)


def scale_parts(total, rows):
    vectors = total[:rows]
    squares = jnp.sum(vectors * vectors, keepdims=True) + jnp.sum(total[rows : rows + 1], keepdims=True)
    scale = jnp.minimum(1.0, clip_level / jnp.sqrt(squares)) * math.sqrt(NPARAM)
    power = jnp.exp2(jnp.floor(jnp.log2(jnp.maximum(scale, 1e-30)))).astype(bf16).astype(f32)
    return power, scale / power


def precondition_body(s_ref, l_ref, r_ref, *refs, rows):
    *part_refs, p_ref, s_low, rest = refs

    @pl.when(pl.program_id(0) == 0)
    def _():
        parts = [ref[...] for ref in part_refs]
        power, left = scale_parts(sum_parts(parts), rows)
        s_low[...] = (s_ref[...].astype(f32) * power).astype(bf16)
        rest[...] = jnp.broadcast_to(left, rest.shape)

    left = mm(l_ref[...], s_low[...], NN)
    p_ref[...] = (rest[0:1, 0:1] * mm(left.astype(bf16), r_ref[...], NN)).astype(bf16)


def sum_parts(parts):
    if len(parts) == 1:
        return parts[0]
    return (parts[0] + parts[1]) + (parts[2] + parts[3])


def precondition(parts, rows, block, left, right, step=384):
    width = block.shape[0]
    whole = pl.BlockSpec((width, width), lambda i: (0, 0))
    some = pl.BlockSpec((step, width), lambda i: (i, 0))
    return call(
        functools.partial(precondition_body, rows=rows),
        4 * width**3,
        8 * width**2,
        grid=(width // step,),
        in_specs=[whole, some, whole] + [pl.BlockSpec(v.shape, lambda i: (0, 0)) for v in parts],
        out_specs=some,
        out_shape=jax.ShapeDtypeStruct((width, width), bf16),
        scratch_shapes=[pltpu.VMEM((width, width), bf16), pltpu.VMEM((8, LANES), f32)],
    )(block, left, right, *parts)


def statistics_body(has_ref, scale_ref, s_ref, l_ref, r_ref, nl_ref, nr_ref, s_low, *, step):
    i = pl.program_id(0)
    width = s_ref.shape[0]

    @pl.when(i == 0)
    def _():
        s_low[...] = (s_ref[...].astype(f32) * scale_ref[0]).astype(bf16)

    factor = (1.0 - decay_beta) * (scale_ref[1] * scale_ref[1] / width)
    at = pl.multiple_of(i * step, step)

    @pl.when(has_ref[0] != 0)
    def _():
        nl_ref[...] = decay_beta * l_ref[...] + factor * mm(s_low[pl.ds(at, step), :], s_low[...], NT)
        nr_ref[...] = decay_beta * r_ref[...] + factor * mm(s_low[:, pl.ds(at, step)], s_low[...], TN)

    @pl.when(has_ref[0] == 0)
    def _():
        nl_ref[...] = l_ref[...]
        nr_ref[...] = r_ref[...]


def statistics(has, scales, block, left, right, step=256):
    width = block.shape[0]
    whole = pl.BlockSpec((width, width), lambda i: (0, 0))
    rows = pl.BlockSpec((step, width), lambda i: (i, 0))
    smem = pl.BlockSpec(memory_space=pltpu.SMEM)
    return call(
        functools.partial(statistics_body, step=step),
        4 * width**3,
        18 * width**2,
        grid=(width // step,),
        in_specs=[smem, smem, whole, rows, rows],
        out_specs=[rows, rows],
        out_shape=[jax.ShapeDtypeStruct((width, width), f32)] * 2,
        scratch_shapes=[pltpu.VMEM((width, width), bf16)],
    )(has, scales, block, left, right)


def update_body(owner_ref, factor_ref, p_ref, shard_ref, block_ref, clip_ref, new_ref, copy_ref):
    for b in range(shard_ref.shape[0]):
        clip_ref[b] = shard_ref[b] * factor_ref[0]
        value = block_ref[b] - matrix_rate * p_ref[owner_ref[b]].astype(f32)
        new_ref[b] = value
        copy_ref[b] = value.astype(bf16)


def update(owners, factor, returned, shards, blocks):
    smem, vmem = pl.BlockSpec(memory_space=pltpu.SMEM), pl.BlockSpec(memory_space=pltpu.VMEM)
    return call(
        update_body,
        0,
        returned.size * 2 + shards.size * 18,
        in_specs=[smem, smem, vmem, vmem, vmem],
        out_specs=[vmem] * 3,
        out_shape=[
            jax.ShapeDtypeStruct(shards.shape, f32),
            jax.ShapeDtypeStruct(shards.shape, f32),
            jax.ShapeDtypeStruct(shards.shape, bf16),
        ],
    )(owners, factor, returned, shards, blocks)


def to_all(value):
    return lax.all_to_all(value, AXES, split_axis=0, concat_axis=0, tiled=True)


def per_device(
    tokens,
    segment_ids,
    cotangent,
    blocks,
    vectors,
    stat_left,
    stat_right,
    root_left,
    root_right,
    vec_stat,
    owners,
    *,
    paired,
):
    rows_here, seq_len, width = tokens.shape
    count = rows_here * seq_len
    splits = FF // width
    slot_count = lax.axis_size(AXES)
    my_index = lax.axis_index(AXES)
    shard = width // slot_count
    vec_rows = vectors.shape[0]

    low_blocks, low_vectors = blocks.astype(bf16), vectors.astype(bf16)
    everyone = jnp.broadcast_to(low_vectors.reshape(1, -1), (slot_count, vec_rows * shard))
    vecs = to_all(everyone).reshape(slot_count, vec_rows, shard)
    vecs = vecs.transpose(1, 0, 2).reshape(vec_rows, width).astype(f32)
    half = splits // 2
    mlp_weights = lax.all_gather(low_blocks[4:], AXES, axis=1, tiled=True)

    flat_tokens = tokens.reshape(count, width)
    dy = cotangent.reshape(count, width)
    tables = rotary_tables(segment_ids)
    place = jnp.stack(grid_places()).astype(jnp.int32)
    if paired:
        pieces = gather_staged(low_blocks[:4])
    else:
        pieces = [lax.all_gather(low_blocks[:4], AXES, axis=1, tiled=True)]
    q, k, v, do, acts, attn_weights = project(place, flat_tokens, dy, pieces, vecs, tables)
    og, attn_sums, acts = attend(segment_ids, q, k, v, do, tables, acts)
    orders = [list(range(4))]
    for first in (0, half):
        orders.append([base + first + j for base in (4, 4 + splits) for j in range(half)])
    if paired:
        acts_pair, og_pair = (acts, over_c(acts)), (og, over_c(og))
        dys = (acts_pair, 2, 1)
        ed0, up_sum0 = hidden(0, acts, mlp_weights, vecs)
        ed0_pair = (ed0, over_c(ed0))
        ed1, up_sum1 = hidden(half, acts, mlp_weights, vecs, after=(ed0, acts_pair[1]))
        ed1_pair = (ed1, over_c(ed1))

        def grads(left, two, one, after):
            operands = ((acts_pair, left, 1), two, one, dys, shard, "xy")
            return Reduction("xy", half_grads(place, *operands, after=after))

        attn = grads(0, (og_pair, 3, 1), (og_pair, 0, 3), (ed1,))
        low = grads(1, (ed0_pair, 0, half), (ed0_pair, half, half), (attn.made,))
        advance(place, [attn], [], after=(low.made,))
        high = grads(1, (ed1_pair, 0, half), (ed1_pair, half, half), (attn.made,))
        advance(place, [low], [], after=(high.made, *[got for _, got in attn.held]))
        part, one_sums = grad_one(flat_tokens, dy, (og, 0, 3), attn_weights, vecs, after=(low.made,))
        terms = [advance(place, [high], [attn, low], after=(part,))]
        es, dus = [(v, 0, half) for v in (ed0, ed1)], [(v, half, half) for v in (ed0, ed1)]
        terms.append(advance(place, [], [high]))
        grad_in, two_sums = grad_two(flat_tokens, part, dus, mlp_weights, vecs, after=(high.made,))
        orders = [orders[0] + orders[1], orders[2]]
    else:
        ed0, up_sum0 = hidden(0, acts, mlp_weights, vecs)
        ed1, up_sum1 = hidden(half, acts, mlp_weights, vecs)
        grads = [
            full_grads(acts[0], og[3:], og[:3], dy),
            full_grads(acts[1], ed0[:half], ed0[half:], dy),
            full_grads(acts[1], ed1[:half], ed1[half:], dy),
        ]
        terms = [[lax.psum_scatter(v, AXES, scatter_dimension=1, tiled=True)] for v in grads]
        es, dus = [(v, 0, half) for v in (ed0, ed1)], [(v, half, half) for v in (ed0, ed1)]
        part, one_sums = grad_one(flat_tokens, dy, (og, 0, 3), attn_weights, vecs)
        grad_in, two_sums = grad_two(flat_tokens, part, dus, mlp_weights, vecs)
    up_sums = [up_sum0, up_sum1]

    one_sums, two_sums = jnp.sum(one_sums, axis=1), jnp.sum(two_sums, axis=1)
    qkv_sums = jnp.sum(attn_sums, axis=1)
    up_sums = jnp.sum(jnp.concatenate(up_sums, axis=0), axis=1)
    bias_sum = one_sums[2:]
    grad_vectors = jnp.concatenate(
        [one_sums[:2], two_sums, qkv_sums, bias_sum, up_sums, bias_sum], axis=0
    )
    slot_ids = jnp.arange(slot_count, dtype=jnp.int32)
    match = owners[None, :] == slot_ids[:, None]
    slots = jnp.sum(jnp.where(match, jnp.arange(1, owners.shape[0] + 1, dtype=jnp.int32)[None], 0), axis=1) - 1
    has_block = jnp.any(owners == my_index)
    shards, outgoing, squares = pack(slots, terms, orders, after=(grad_in,))
    left_low, right_low = to_low(root_left[0], root_right[0], after=(squares,))
    local = jnp.concatenate([grad_vectors, jnp.sum(squares, axis=0)[None], jnp.zeros((2, width), f32)])
    parts = everywhere(local) if paired else [lax.psum(local, AXES)]
    total = sum_parts(parts)
    vector_sums = total[:vec_rows]
    square_sum = jnp.sum(total[vec_rows]) + jnp.sum(vector_sums * vector_sums)
    shard_vectors = lax.dynamic_slice_in_dim(vector_sums, my_index * shard, shard, axis=1)
    grad_norm = jnp.sqrt(square_sum)
    factor = jnp.minimum(1.0, clip_level / grad_norm)
    root_count = math.sqrt(NPARAM)

    scale = factor * root_count
    power = jnp.exp2(jnp.floor(jnp.log2(jnp.maximum(scale, 1e-30)))).astype(bf16).astype(f32)
    scales = jnp.stack([power, scale / power])
    out = output(flat_tokens, (og, 3, 1), es, attn_weights, mlp_weights, vecs, after=(left_low, scales, factor.reshape(1)))
    owned = to_all(outgoing).reshape(width, width)
    precond = precondition(parts, vec_rows, owned, left_low, right_low)
    returned = to_all(precond.reshape(slot_count, shard, width))
    new_left, new_right = statistics(
        has_block.astype(jnp.int32).reshape(1), scales, owned, stat_left[0], stat_right[0]
    )
    clipped_blocks, new_blocks, blocks_copy = update(owners, factor.reshape(1), returned, shards, blocks)
    clipped_vectors = shard_vectors * factor
    scaled_vectors = clipped_vectors * root_count
    new_vec_stat = decay_beta * vec_stat + (1.0 - decay_beta) * (scaled_vectors * scaled_vectors)
    new_vectors = vectors - vector_rate * scaled_vectors * lax.rsqrt(new_vec_stat)
    return (
        out.reshape(tokens.shape),
        grad_in.reshape(tokens.shape),
        clipped_blocks,
        clipped_vectors,
        grad_norm,
        new_left[None],
        new_right[None],
        new_vec_stat,
        new_blocks,
        new_vectors,
        blocks_copy,
        new_vectors.astype(bf16),
    )


def solution(mesh):
    rows = P(AXES, None, None)
    split_rows = P(None, AXES, None)
    split_columns = P(None, AXES)
    paired = dict(mesh.shape) == {"wide": 8, "narrow": 4}
    return jax.shard_map(
        functools.partial(per_device, paired=paired),
        mesh=mesh,
        in_specs=(
            rows, P(AXES, None), rows, split_rows, split_columns,
            rows, rows, rows, rows, split_columns, P(),
        ),
        out_specs=(
            rows, rows, split_rows, split_columns, P(), rows, rows,
            split_columns, split_rows, split_columns, split_rows, split_columns,
        ),
        check_vma=False,
    )
```
